32 devices in a mesh: dp: 8 (over y, x, core), tensor: 4 (over z).
Axes of the slice: x: 2, y: 2, z: 4, core: 2. Of those that a mesh axis runs over, the one named last changes fastest.
Arguments:
- block_in: bfloat16 [8, 2048, 1024], P('dp', 'tensor'), may hold values from -6 to 6
- segments: int32 [8, 2048], P('dp'), may hold values from 0 to 15, never falling along the last dimension, each value on 1 to 512 neighbouring positions
- retrieved: int32 [8, 4, 8], P('dp'), may hold values from 0 to 255, as said below
- partner: int32 [8], P('dp'), may hold values from 0 to 7, as said below
- memory_keys: bfloat16 [8, 128, 128, 1024], P(None, 'dp', None, 'tensor'), may hold values from -6 to 6
- memory_values: bfloat16 [8, 128, 128, 1024], P(None, 'dp', None, 'tensor'), may hold values from -6 to 6
- gain_attn: bfloat16 [1024], P('dp'), may hold values from 0.5 to 1.5
- w_query: bfloat16 [1024, 1024], P('dp', 'tensor'), may hold values from -0.375 to 0.375
- w_key: bfloat16 [1024, 1024], P('dp', 'tensor'), may hold values from -0.1875 to 0.1875
- w_value: bfloat16 [1024, 1024], P('dp', 'tensor'), may hold values from -0.1875 to 0.1875
- w_out: bfloat16 [1024, 1024], P('tensor', 'dp'), may hold values from -2 to 2
- gain_ffn: bfloat16 [1024], P('dp'), may hold values from 0.5 to 1.5
- w_gate: bfloat16 [1024, 2816], P('dp', 'tensor'), may hold values from -0.1875 to 0.1875
- w_up: bfloat16 [1024, 2816], P('dp', 'tensor'), may hold values from -0.1875 to 0.1875
- w_down: bfloat16 [2816, 1024], P('tensor', 'dp'), may hold values from -0.21875 to 0.21875
- cotangent: bfloat16 [8, 2048, 1024], P('dp', 'tensor'), may hold values from -6 to 6
Outputs:
- block_out: float32 [8, 2048, 1024], P('dp', 'tensor')
- grad_in: float32 [8, 2048, 1024], P('dp', 'tensor')
- grad_gain_attn: float32 [1024], P('dp')
- grad_query: float32 [1024, 1024], P('dp', 'tensor')
- grad_key: float32 [1024, 1024], P('dp', 'tensor')
- grad_value: float32 [1024, 1024], P('dp', 'tensor')
- grad_out: float32 [1024, 1024], P('tensor', 'dp')
- grad_gain_ffn: float32 [1024], P('dp')
- grad_gate: float32 [1024, 2816], P('dp', 'tensor')
- grad_up: float32 [1024, 2816], P('dp', 'tensor')
- grad_down: float32 [2816, 1024], P('tensor', 'dp')
The draws below stay inside these ranges and needn't reach their ends.
Inputs may be any that keep to these rules, and one draw needn't show every extreme that they name: `retrieved`: entry v names block v of the combined memory: below 128 the sequence's own block v, else the partner's block v - 128. Block j of any sequence lies on data device j // 16. All 32 entries of one sequence are different, at most 8 of them name blocks on one data device, and for some device exactly 8. partner[s] differs from s.
All inputs are finite; a program needn't handle non-finite values.
Results may differ from the reference program's by a relative error of at most 0.025.
Values may be sent and summed in bfloat16 or wider, within the bound.
A program may use at most 192 MiB of HBM per device.

```python
import math
import jax
import jax.numpy as jnp
import numpy as np
from jax import lax

D = 1024
HEADS = 8
HD = 128
FF = 2816
QB = 512
MEMB = 128
MBLK = 128
KSEL = 8
DOCS = 16
LEN = 2048
SEQS = 8
NQB = 4
NREQ = 32
MB_DEV = 16
CAP = 8


def draw_partner(key, part):
    offsets = jax.random.randint(key, (SEQS,), 1, SEQS)
    return ((jnp.arange(SEQS) + offsets) % SEQS).astype(jnp.int32)


def retrieved_one(key):
    slot_total = SEQS * CAP
    key_order, key_shuffle, key_offset = jax.random.split(key, 3)
    order = jax.random.permutation(key_order, slot_total)
    owners = order // CAP
    ranking = jnp.where(owners == owners[0], 0, 1 + jnp.arange(slot_total))
    chosen = order[jnp.argsort(ranking, stable=True)][:NREQ]
    chosen = chosen[jax.random.permutation(key_shuffle, NREQ)]
    owner_dev = chosen // CAP
    within = chosen % CAP
    offsets = jax.random.randint(key_offset, (SEQS,), 0, 2 * MB_DEV)
    code_value = (offsets[owner_dev] + within) % (2 * MB_DEV)
    from_partner = code_value // MB_DEV
    local_block = code_value % MB_DEV
    return (from_partner * MEMB + owner_dev * MB_DEV + local_block).reshape(NQB, KSEL).astype(jnp.int32)


def draw_retrieved(key, part):
    keys_all = jax.random.split(key, SEQS)
    return jax.vmap(retrieved_one)(keys_all)


def raised(entries, own_key, source, target, parts, factor):
    def block_of(dim):
        return (jnp.arange(entries.shape[dim]) // (entries.shape[dim] // parts)).reshape((-1,) + (1,) * (entries.ndim - 1 - dim))

    first = jax.random.permutation(own_key, parts)[block_of(target)]
    other_side = (block_of(target) + parts // 2) % parts
    return jnp.where((block_of(source) == first) | (block_of(source) == other_side), factor * entries, entries)


def block_levels(key, shape, cuts, smallest, top_value):
    gain, own = 1.0, jax.random.fold_in(key, 6)
    for axis_at, parts in cuts:
        heights = jnp.exp(jax.random.uniform(jax.random.fold_in(own, axis_at), (parts,), jnp.float32, smallest / len(cuts), top_value / len(cuts)))
        gain = gain * jnp.repeat(heights, shape[axis_at] // parts).reshape([-1 if axis == axis_at else 1 for axis in range(len(shape))])
    return gain


def split_up(count, total, reach, lean):
    loads = [(1 << 20) // math.isqrt(grade ** lean) + 1 for grade in range(2, count + 1)]
    rest, given = total - reach - (count - 1), [1] * (count - 1)
    while rest > 0:
        free = [i for i in range(count - 1) if given[i] < reach]
        pool, remaining = sum([loads[i] for i in free]), rest
        for i in free:
            more = min(reach - given[i], max(1, remaining * loads[i] // pool), rest)
            given[i] = given[i] + more
            rest = rest - more
    return np.array([reach] + given)


def ragged(rng, count, total, bound, skew):
    if count == 2:
        one = jax.random.randint(rng, (), max(1, total - bound), min(bound, total - 1) + 1)
        return jnp.stack([one, total - one])
    sizes = jnp.asarray(split_up(count, total, bound, skew), jnp.int32)
    twos = (count - 1) // 2
    donor, receiver = sizes[1:1 + 2 * twos:2], sizes[2:2 + 2 * twos:2]
    slack = jnp.minimum(donor - 1, bound - receiver)
    passed = jax.random.randint(jax.random.fold_in(rng, 1), (twos,), 0, 1 << 20) % (slack + 1)
    sizes = sizes.at[1:1 + 2 * twos:2].set(donor - passed).at[2:2 + 2 * twos:2].set(receiver + passed)
    return sizes[jax.random.permutation(jax.random.fold_in(rng, 2), count)]


def normal_values(key, extent, spread, most, cuts=(), kind=jnp.bfloat16):
    array = spread * jax.random.normal(key, extent, jnp.float32)
    if cuts:
        array = array * block_levels(key, extent, cuts, -0.22, 0.18)
    return jnp.clip(array, -most, most).astype(kind)


def gaussian_with(own_key, dims, spread, most, cuts, heavy, kind=jnp.bfloat16):
    entries = spread * jax.random.normal(own_key, dims, jnp.float32)
    if cuts:
        entries = entries * block_levels(own_key, dims, cuts, -0.22, 0.18)
    return jnp.clip(raised(entries, jax.random.fold_in(own_key, 3), *heavy), -most, most).astype(kind)


def setup_inputs(seed: int = 0) -> dict:
    splits = jax.random.split(jax.random.key(seed), 17)
    block_in = gaussian_with(splits[0], (SEQS, LEN, D), 1.0, 6.0, ((0, 8), (1, 4)), (0, 2, 8, 2.0))
    segments = jax.vmap(lambda own: jnp.searchsorted(jnp.cumsum(ragged(own, DOCS, LEN, LEN // 4, 2)), jnp.arange(LEN), side="right"))(jax.random.split(splits[1], SEQS)).reshape((SEQS, LEN)).astype(jnp.int32)
    retrieved = draw_retrieved(jax.random.fold_in(splits[16], 71), 0)
    partner = draw_partner(jax.random.fold_in(splits[16], 71), 0)
    memory_keys = normal_values(splits[4], (SEQS, MEMB, MBLK, D), 1.0, 6.0, ((1, 8), (3, 4)))
    memory_values = normal_values(splits[5], (SEQS, MEMB, MBLK, D), 1.0, 6.0, ((1, 8), (3, 4)))
    gain_attn = jnp.clip(1.0 + 0.1 * jax.random.normal(splits[6], (D,), jnp.float32), 0.5, 1.5).astype(jnp.bfloat16)
    w_query = normal_values(splits[7], (D, D), (D // 4) ** -0.5, 0.375, ((0, 8), (1, 4)))
    w_key = normal_values(splits[8], (D, D), D ** -0.5, 0.1875, ((0, 8), (1, 4)))
    w_value = normal_values(splits[9], (D, D), D ** -0.5, 0.1875, ((0, 8), (1, 4)))
    w_out = gaussian_with(splits[10], (D, D), (D // 64) ** -0.5, 2.0, ((0, 4), (1, 8)), (0, 1, 8, 2.0))
    gain_ffn = jnp.clip(1.0 + 0.1 * jax.random.normal(splits[11], (D,), jnp.float32), 0.5, 1.5).astype(jnp.bfloat16)
    w_gate = normal_values(splits[12], (D, FF), D ** -0.5, 0.1875, ((0, 8), (1, 4)))
    w_up = normal_values(splits[13], (D, FF), D ** -0.5, 0.1875, ((0, 8), (1, 4)))
    w_down = normal_values(splits[14], (FF, D), (FF // 4) ** -0.5, 0.21875, ((0, 4), (1, 8)))
    cotangent = gaussian_with(splits[15], (SEQS, LEN, D), 1.0, 6.0, ((0, 8), (1, 4)), (0, 2, 8, 2.0))
    return {"block_in": block_in, "segments": segments, "retrieved": retrieved, "partner": partner, "memory_keys": memory_keys, "memory_values": memory_values, "gain_attn": gain_attn, "w_query": w_query, "w_key": w_key, "w_value": w_value, "w_out": w_out, "gain_ffn": gain_ffn, "w_gate": w_gate, "w_up": w_up, "w_down": w_down, "cotangent": cotangent}


@jax.custom_vjp
def low(v):
    return lax.optimization_barrier(v.astype(jnp.bfloat16)).astype(jnp.float32)

@jax.custom_vjp
def low_back(v):
    return v

def low_keep(v):
    return (low(v), None)

def low_pass(kept, grad):
    return (grad,)

def back_keep(v):
    return (v, None)

def back_low(kept, grad):
    return (low(grad),)
low.defvjp(low_keep, low_pass)
low_back.defvjp(back_keep, back_low)
EPSILON = 1e-05
MASKED = -1e+30
HIGHEST_PRECISION = lax.Precision.HIGHEST

def normalize(field, gain_vec):
    return field * lax.rsqrt(lax.optimization_barrier(jnp.mean(field * field, axis=-1, keepdims=True)) + EPSILON) * gain_vec

def rotate(field):
    head_size = field.shape[-1]
    half_width = head_size // 2
    frequencies = 10000.0 ** (-jnp.arange(half_width, dtype=jnp.float32) * 2.0 / head_size)
    angles = jnp.arange(field.shape[0], dtype=jnp.float32)[:, None] * frequencies[None, :]
    cosine = jnp.cos(angles)[:, None, :]
    sine_table = jnp.sin(angles)[:, None, :]
    first_half = field[..., :half_width]
    second_half = field[..., half_width:]
    return jnp.concatenate([first_half * cosine - second_half * sine_table, second_half * cosine + first_half * sine_table], axis=-1)

def matmul(left, right):
    return jnp.dot(left, right, precision=HIGHEST_PRECISION)

def layer(stream_in, params, memory_k, memory_v, seg_row):
    gain_attn, w_query, w_key, w_value, w_out, gain_ffn, w_gate, w_up, w_down = params
    positions = jnp.arange(LEN)
    normed = low(normalize(stream_in, gain_attn))
    queries = low(rotate(low_back(matmul(normed, w_query)).reshape(LEN, HEADS, HD)))
    keys_local = low(rotate(low_back(matmul(normed, w_key)).reshape(LEN, HEADS, HD)))
    values_local = low(low_back(matmul(normed, w_value))).reshape(LEN, HEADS, HD)
    score_scale = HD ** (-0.5)

    def attend(pieces):
        query_blk, seg_blk, pos_blk, key_mem, value_mem = pieces
        local_scores = jnp.einsum('qhd,khd->hqk', query_blk, keys_local, precision=HIGHEST_PRECISION)
        memory_scores = jnp.einsum('qhd,khd->hqk', query_blk, key_mem, precision=HIGHEST_PRECISION)
        scores = low_back(jnp.concatenate([local_scores, memory_scores], axis=-1) * score_scale)
        allowed = (seg_blk[:, None] == seg_row[None, :]) & (positions[None, :] <= pos_blk[:, None])
        allowed = jnp.concatenate([allowed, jnp.ones((QB, KSEL * MBLK), dtype=jnp.bool_)], axis=1)
        weights_soft = low(jax.nn.softmax(jnp.where(allowed[None], scores, MASKED), axis=-1))
        values_all = jnp.concatenate([values_local, value_mem], axis=0)
        return jnp.einsum('hqk,khd->qhd', weights_soft, values_all, precision=HIGHEST_PRECISION)
    attended = lax.map(jax.checkpoint(attend), (queries.reshape(NQB, QB, HEADS, HD), seg_row.reshape(NQB, QB), positions.reshape(NQB, QB), memory_k, memory_v))
    mixed = low(low_back(attended.reshape(LEN, D)))
    stream = stream_in + low_back(matmul(mixed, w_out))
    normed_ffn = low(normalize(stream, gain_ffn))
    gate_pre = low_back(matmul(normed_ffn, w_gate))
    up_pre = low_back(matmul(normed_ffn, w_up))
    hidden = low(jax.nn.silu(gate_pre) * up_pre)
    return stream + matmul(hidden, w_down)

def reference(block_in, segments, retrieved, partner, memory_keys, memory_values, gain_attn, w_query, w_key, w_value, w_out, gain_ffn, w_gate, w_up, w_down, cotangent):
    params = tuple((param_one.astype(jnp.float32) for param_one in (gain_attn, w_query, w_key, w_value, w_out, gain_ffn, w_gate, w_up, w_down)))

    def per_sequence(sums, seq_index):
        chosen = retrieved[seq_index].reshape(-1)
        other = partner[seq_index]
        memory_k = jnp.concatenate([memory_keys[seq_index], memory_keys[other]], axis=0)[chosen]
        memory_k = memory_k.astype(jnp.float32).reshape(NQB, KSEL * MBLK, HEADS, HD)
        memory_v = jnp.concatenate([memory_values[seq_index], memory_values[other]], axis=0)[chosen]
        memory_v = memory_v.astype(jnp.float32).reshape(NQB, KSEL * MBLK, HEADS, HD)
        seg_row = segments[seq_index]

        def forward(stream_in, *weights_in):
            return layer(stream_in, weights_in, memory_k, memory_v, seg_row)
        result, pull = jax.vjp(forward, block_in[seq_index].astype(jnp.float32), *params)
        grads = pull(cotangent[seq_index].astype(jnp.float32))
        sums = tuple((total_one + grad_one for total_one, grad_one in zip(sums, grads[1:])))
        return (sums, (result, grads[0]))
    zeros = tuple((jnp.zeros_like(param_one) for param_one in params))
    sums, (outputs, input_grads) = lax.scan(per_sequence, zeros, jnp.arange(SEQS, dtype=jnp.int32))
    return (outputs, input_grads, sums[0], sums[1], sums[2], sums[3], sums[4], sums[5], sums[6], sums[7], sums[8])
```

```python
import functools
import math

import jax
import jax.numpy as jnp
from jax import lax
from jax.experimental import pallas as pl
from jax.experimental.pallas import tpu as pltpu
from jax.sharding import PartitionSpec as P

MESH = pl.DeviceIdType.MESH
MEMB = 128


class Grid:
    def __init__(self, dp, tensor):
        side = math.isqrt(dp // 2)
        assert side * side * 2 == dp
        self.na, self.nb, self.nc, self.nz, self.dp = side, side, 2, tensor, dp


def coords(g):
    me = lax.axis_index("dp")
    t = lax.axis_index("tensor")
    return me // (2 * g.nb), (me // 2) % g.nb, me % 2, t, me


def send(src, dst, ssem, rsem, dp, t):
    return pltpu.make_async_remote_copy(
        src_ref=src, dst_ref=dst, send_sem=ssem, recv_sem=rsem, device_id=(dp, t), device_id_type=MESH
    )


def greet(g, me, t):
    bar = pltpu.get_barrier_semaphore()
    for k in range(1, g.dp):
        pl.semaphore_signal(bar, inc=1, device_id=((me + k) % g.dp, t), device_id_type=MESH)
    for k in range(1, g.nz):
        pl.semaphore_signal(bar, inc=1, device_id=(me, (t + k) % g.nz), device_id_type=MESH)
    pl.semaphore_wait(bar, g.dp - 1 + g.nz - 1)


class Gather:
    def __init__(self, g, shard, buf, rows, b_first, sems, base):
        self.g, self.shard, self.buf, self.rows, self.b_first = g, shard, buf, rows, b_first
        self.sems, self.next = sems, base
        self.sent = []

    def _sem(self):
        i = self.next
        self.next += 1
        return self.sems[0].at[i], self.sems[1].at[i]

    def at(self, dp, t=None):
        lo, n = self.rows
        if t is None:
            return self.buf.at[dp, :, pl.ds(lo, n), :]
        return self.buf.at[dp, t, pl.ds(lo, n), :]

    def start_z(self):
        g = self.g
        a, b, c, t, me = coords(g)
        lo, n = self.rows
        src = self.shard.at[pl.ds(lo, n), :]
        self.z = []
        for k in range(1, g.nz):
            s, r = self._sem()
            d = send(src, self.at(me, t), s, r, me, (t + k) % g.nz)
            d.start()
            self.z.append(d)
        s, _ = self._sem()
        self.own = pltpu.make_async_copy(src, self.at(me, t), s)
        self.own.start()
        self.sent += self.z

    def _dp(self, a, b, c):
        return (a * self.g.nb + b) * 2 + c

    def _core(self, dp, c):
        s, r = self._sem()
        d = send(self.at(dp), self.at(dp), s, r, coords(self.g)[4] + 1 - 2 * c, coords(self.g)[3])
        d.start()
        self.core.append(d)
        self.sent.append(d)

    def start_first(self):
        g = self.g
        a, b, c, t, me = coords(g)
        self.own.wait()
        for d in self.z:
            d.wait_recv()
        self.first, self.core = [], []
        n1 = g.nb if self.b_first else g.na
        for k in range(1, n1):
            to = self._dp(a, (b + k) % n1, c) if self.b_first else self._dp((a + k) % n1, b, c)
            s, r = self._sem()
            d = send(self.at(me), self.at(me), s, r, to, t)
            d.start()
            self.first.append(d)
        self.sent += self.first
        self._core(me, c)

    def start_second(self):
        g = self.g
        a, b, c, t, me = coords(g)
        n1, n2 = (g.nb, g.na) if self.b_first else (g.na, g.nb)
        for d in self.first:
            d.wait_recv()
        held = [self._dp(a, (b - k) % n1, c) if self.b_first else self._dp((a - k) % n1, b, c) for k in range(n1)]
        self.second = []
        for slot in held:
            for k in range(1, n2):
                to = self._dp((a + k) % n2, b, c) if self.b_first else self._dp(a, (b + k) % n2, c)
                s, r = self._sem()
                d = send(self.at(slot), self.at(slot), s, r, to, t)
                d.start()
                self.second.append(d)
        for slot in held[1:]:
            self._core(slot, c)
        self.sent += self.second

    def start_core(self):
        g = self.g
        a, b, c, t, me = coords(g)
        n1, n2 = (g.nb, g.na) if self.b_first else (g.na, g.nb)
        for d in self.second:
            d.wait_recv()
        for k1 in range(n1):
            for k in range(1, n2):
                slot = (
                    self._dp((a - k) % n2, (b - k1) % n1, c)
                    if self.b_first
                    else self._dp((a - k1) % n1, (b - k) % n2, c)
                )
                self._core(slot, c)

    def finish(self):
        for d in self.core:
            d.wait_recv()
        for d in self.sent:
            d.wait_send()


def gather_sems(g):
    return g.nz + (g.na - 1) + g.na * (g.na - 1) + g.na * g.nb


def k1_kernel(g, cap, nq, ksel, halo, units, n_w, *refs):
    refs = list(refs)
    take = lambda n: [refs.pop(0) for _ in range(n)]
    requests, sel = take(2)
    x, gains, mem_k, mem_v = take(4)
    shards = take(n_w)
    bufs = take(n_w)
    xh, gains_all, mk, mv = take(4)
    loc_k, loc_v, stage_k, stage_v, rec_k, rec_v, zst_k, zst_v = take(8)
    req_in, req_s = take(2)
    ss, rs, msl, mss, mrs, zss, zrs, xss, xrs, qss, qrs, gss, grs = take(13)
    a, b, c, t, me = coords(g)
    greet(g, me, t)
    rq, gn = [], []
    for k in range(1, g.dp):
        to = (me + k) % g.dp
        d = send(requests.at[to], req_in.at[me], qss.at[k], qrs.at[k], to, t)
        d.start()
        rq.append(d)
    for k in range(1, g.dp):
        to = (me + k) % g.dp
        d = send(gains, gains_all.at[me], gss.at[k], grs.at[k], to, t)
        d.start()
        gn.append(d)
    own_r = pltpu.make_async_copy(requests.at[me], req_in.at[me], qss.at[0])
    own_r.start()
    own_g = pltpu.make_async_copy(gains, gains_all.at[me], gss.at[0])
    own_g.start()
    lk = pltpu.make_async_copy(mem_k, loc_k, msl.at[0])
    lv = pltpu.make_async_copy(mem_v, loc_v, msl.at[1])
    lk.start()
    lv.start()
    per = gather_sems(g)
    gs = [Gather(g, shards[w], bufs[w], rows, bf, (ss, rs), i * per) for i, (w, rows, bf) in enumerate(units)]
    for u in gs[:4]:
        u.start_z()
    xs = []
    for k in range(1, halo + 1):
        d = send(x, xh.at[k - 1], xss.at[k - 1], xrs.at[k - 1], me, (t + k) % g.nz)
        xs.append(d)

        @pl.when(t + k < g.nz)
        def _():
            d.start()

    own_r.wait()
    own_g.wait()
    for d in rq:
        d.wait()
    cp = pltpu.make_async_copy(req_in, req_s, qrs.at[0])
    cp.start()
    cp.wait()

    def exchange(loc, stage, rec, i, load):
        load.wait()

        @pl.loop(0, g.dp)
        def _(s):
            for k in range(cap):
                stage[s, k] = loc[req_s[s, 0, k]]

        out = []
        for k in range(1, g.dp):
            to = (me + k) % g.dp
            d = send(stage.at[to], rec.at[me], mss.at[i, k], mrs.at[i, k], to, t)
            d.start()
            out.append(d)
        own = pltpu.make_async_copy(stage.at[me], rec.at[me], mss.at[i, 0])
        own.start()
        return out + [own]

    ek = exchange(loc_k, stage_k, rec_k, 0, lk)
    for u in gs[:4]:
        u.start_first()
    ev = exchange(loc_v, stage_v, rec_v, 1, lv)
    for u in gs[4:]:
        u.start_z()
    for u in gs[:4]:
        u.start_second()
    for u in gs[:4]:
        u.start_core()

    def spread(moves, rec, zst, out, i):
        for d in moves:
            d.wait()

        @pl.loop(0, nq)
        def _(q):
            for j in range(ksel):
                zst[q, j] = rec[sel[q * ksel + j] // cap, sel[q * ksel + j] % cap]

        res = []
        for k in range(1, g.nz):
            to = (t + k) % g.nz
            d = send(zst.at[to], out.at[t], zss.at[i, k], zrs.at[i, k], me, to)
            d.start()
            res.append(d)
        own = pltpu.make_async_copy(zst.at[t], out.at[t], zss.at[i, 0])
        own.start()
        return res + [own]

    zk = spread(ek, rec_k, zst_k, mk, 0)
    for u in gs[4:]:
        u.start_first()
    zv = spread(ev, rec_v, zst_v, mv, 1)
    for u in gs[4:]:
        u.start_second()
    for u in gs[4:]:
        u.start_core()
    for d in zk + zv + gn:
        d.wait()
    for u in gs:
        u.finish()
    for k, d in enumerate(xs):

        @pl.when(t + k + 1 < g.nz)
        def _():
            d.wait_send()

        @pl.when(t >= k + 1)
        def _():
            d.wait_recv()


def k1(g, cap, halo, requests, sel, x, gains, mem_k, mem_v, shards, nq, ksel):
    bf = jnp.bfloat16
    blk = mem_k.shape[1:]
    units = []
    for w, s in enumerate(shards):
        r = s.shape[0]
        kind = w % 7
        if w in (0, 4):
            units.append((w, (0, r), True))
        elif w in (1, 5):
            units.append((w, (0, r), False))
        else:
            units.append((w, (0, r // 2), True))
            units.append((w, (r // 2, r - r // 2), False))
    n_w = len(shards)
    any_ = pl.BlockSpec(memory_space=pl.ANY)
    nsem = len(units) * gather_sems(g)
    dma = lambda *n: pltpu.SemaphoreType.DMA(n)
    out_shape = (
        [jax.ShapeDtypeStruct((g.dp, g.nz) + s.shape, bf) for s in shards]
        + [jax.ShapeDtypeStruct((halo,) + x.shape, bf), jax.ShapeDtypeStruct((g.dp,) + gains.shape, gains.dtype)]
        + [jax.ShapeDtypeStruct((g.nz, ksel) + blk, bf)] * 2
    )
    scratch = (
        [pltpu.VMEM(mem_k.shape, bf)] * 2
        + [pltpu.VMEM((g.dp, cap) + blk, bf)] * 4
        + [pltpu.VMEM((nq, ksel) + blk, bf)] * 2
        + [pltpu.VMEM((g.dp, 8, 128), jnp.int32), pltpu.SMEM((g.dp, 8, 128), jnp.int32)]
        + [dma(nsem), dma(nsem), dma(2), dma(2, g.dp), dma(2, g.dp), dma(2, g.nz), dma(2, g.nz)]
        + [dma(halo), dma(halo), dma(g.dp), dma(g.dp), dma(g.dp), dma(g.dp)]
    )
    return pl.pallas_call(
        functools.partial(k1_kernel, g, cap, nq, ksel, halo, units, n_w),
        out_shape=out_shape,
        in_specs=[pl.BlockSpec(memory_space=pltpu.VMEM), pl.BlockSpec(memory_space=pltpu.SMEM)] + [any_] * (4 + n_w),
        out_specs=[any_] * len(out_shape),
        scratch_shapes=scratch,
        compiler_params=pltpu.CompilerParams(collective_id=0, has_side_effects=True, vmem_limit_bytes=60 * 2**20),
        name="fwd_exchange",
    )(requests, sel, x, gains, mem_k, mem_v, *shards)


def plan_requests(retrieved, partner, dp_size, blocks_dev, cap):
    wanted = retrieved.reshape(-1)
    n = wanted.shape[0]
    from_partner = wanted // MEMB
    block_index = wanted % MEMB
    owner = block_index // blocks_dev
    local = block_index % blocks_dev
    seq = jnp.where(from_partner == 0, lax.axis_index("dp"), partner)
    flat = seq * blocks_dev + local
    i = jnp.arange(n)
    slot = jnp.sum(((owner[:, None] == owner[None, :]) & (i[None, :] < i[:, None])).astype(jnp.int32), axis=1)
    hit = (owner[None, None, :] == jnp.arange(dp_size)[:, None, None]) & (
        slot[None, None, :] == jnp.arange(128)[None, :, None]
    )
    req = jnp.sum(jnp.where(hit, flat[None, None, :], 0), axis=2)
    return jnp.broadcast_to(req[:, None, :], (dp_size, 8, 128)).astype(jnp.int32), (owner * cap + slot).astype(jnp.int32)

HD = 128
EPSILON = 1e-05
MASKED = -1e30
F32, BF16 = jnp.float32, jnp.bfloat16


def dot_nn(x, y):
    return lax.dot_general(x, y, (((1,), (0,)), ((), ())), preferred_element_type=F32)


def dot_nt(x, y):
    return lax.dot_general(x, y, (((1,), (1,)), ((), ())), preferred_element_type=F32)


def dot_tn(x, y):
    return lax.dot_general(x, y, (((0,), (0,)), ((), ())), preferred_element_type=F32)


def inv_rms(v):
    return lax.rsqrt(jnp.mean(v * v, axis=-1, keepdims=True) + EPSILON)


def gain_row(gains_ref, which):
    n = gains_ref.shape[0]
    return jnp.concatenate([gains_ref[d, which : which + 1, :] for d in range(n)], axis=1)


def turn(v, cos, sin):
    return v * cos + pltpu.roll(v, HD // 2, axis=1) * sin


def lanes(ref):
    return jnp.concatenate([ref[d, 0] for d in range(ref.shape[0])], axis=1)


def rows(ref):
    return jnp.concatenate([ref[d, 0] for d in range(ref.shape[0])], axis=0)


VL = 60 * 2**20


def full(shape, buffers=None):
    n = len(shape)
    kw = {} if buffers is None else dict(pipeline_mode=pl.Buffered(buffers))
    return pl.BlockSpec(shape, lambda *i: (0,) * n, **kw)


def project(halo, first, x, xh, gains, cos, sin, wq, wk, wv):
    r, d = x.shape
    dp, nz, _, cols = wq.shape
    rt = (halo + 1) * r

    def kern(x_ref, xh_ref, gn_ref, cos_ref, sin_ref, wq_ref, wk_ref, wv_ref, n_ref, q_ref, k_ref, v_ref, w_s):
        @pl.when(pl.program_id(0) == 0)
        def _():
            g = gain_row(gn_ref, 0)
            t = lax.axis_index("tensor")
            for j in range(halo):
                v = xh_ref[j].astype(F32)
                n = (v * inv_rms(v) * g).astype(BF16)
                n_ref[pl.ds((halo - 1 - j) * r, r), :] = jnp.where(t >= j + 1, n, jnp.zeros_like(n))
            v = x_ref[...].astype(F32)
            n_ref[pl.ds(halo * r, r), :] = (v * inv_rms(v) * g).astype(BF16)

        w_s[:, 0:cols] = rows(wq_ref)
        w_s[:, cols : 2 * cols] = rows(wk_ref)
        w_s[:, 2 * cols :] = rows(wv_ref)

        tile = 256

        @pl.loop(0, rt // tile)
        def _(i):
            at = pl.ds(pl.multiple_of(i * tile, tile), tile)
            n = n_ref[at, :]
            y = dot_nn(n, w_s[:, cols:])
            cs, sn = cos_ref[at, :], sin_ref[at, :]
            for h in range(cols // HD):
                k_ref[at, h * HD : (h + 1) * HD] = turn(y[:, h * HD : (h + 1) * HD], cs, sn).astype(BF16)
            v_ref[at, :] = y[:, cols:].astype(BF16)

            @pl.when(i >= halo * r // tile)
            def _():
                z = dot_nn(n, w_s[:, 0:cols])
                to = pl.ds(pl.multiple_of(i * tile - halo * r, tile), tile)
                for h in range(cols // HD):
                    q_ref[to, h * HD : (h + 1) * HD] = turn(z[:, h * HD : (h + 1) * HD], cs, sn).astype(BF16)

    wspec = pl.BlockSpec((dp, 1, wq.shape[2], cols), lambda t: (0, t, 0, 0))
    col = lambda n: pl.BlockSpec((n, cols), lambda t: (0, t))
    return pl.pallas_call(
        kern,
        grid=(nz,),
        in_specs=[full((r, d)), full((halo, r, d)), full(gains.shape), full((rt, HD)), full((rt, HD))] + [wspec] * 3,
        out_specs=[full((rt, d)), col(r), col(rt), col(rt)],
        out_shape=[
            jax.ShapeDtypeStruct((rt, d), BF16),
            jax.ShapeDtypeStruct((r, d), BF16),
            jax.ShapeDtypeStruct((rt, d), BF16),
            jax.ShapeDtypeStruct((rt, d), BF16),
        ],
        scratch_shapes=[pltpu.VMEM((d, 3 * cols), BF16)],
        compiler_params=pltpu.CompilerParams(vmem_limit_bytes=VL, dimension_semantics=("arbitrary",)),
        name="project",
    )(x, xh, gains, cos, sin, wq, wk, wv)


def allowed_of(seg_q, seg_k, q0, k0):
    n, m = seg_q.shape[0], seg_k.shape[1]
    qp = lax.broadcasted_iota(jnp.int32, (n, m), 0) + q0
    kp = lax.broadcasted_iota(jnp.int32, (n, m), 1) + k0
    return (seg_q == seg_k) & (kp <= qp)


QT = 256
C2 = HD**-0.5 * math.log2(math.e)


def attend(halo, window, q, k, v, mk, mv, seg_q, seg_k):
    r, d = q.shape
    rt = k.shape[0]
    nz, ksel, blk, cols = mk.shape
    per = cols // HD
    nm = ksel * blk

    def kern(q_ref, k_ref, v_ref, mk_ref, mv_ref, sq_ref, sk_ref, o_ref, l_ref):
        km = mk_ref[0].reshape(nm, HD)
        vm = mv_ref[0].reshape(nm, HD)
        for i in range(r // QT):
            at = slice(i * QT, (i + 1) * QT)
            k0 = halo * r - window + i * QT
            ks = slice(k0, k0 + window + QT)
            qq = q_ref[at, :]
            ok = allowed_of(sq_ref[at, :], sk_ref[:, ks], halo * r + i * QT, k0)
            sl = jnp.where(ok, dot_nt(qq, k_ref[ks, :]), MASKED)
            sm = dot_nt(qq, km)
            m = jnp.maximum(jnp.max(sl, axis=1, keepdims=True), jnp.max(sm, axis=1, keepdims=True))
            mc = m * C2
            el = jnp.exp2(sl * C2 - mc)
            em = jnp.exp2(sm * C2 - mc)
            tot = jnp.sum(el, axis=1, keepdims=True) + jnp.sum(em, axis=1, keepdims=True)
            acc = dot_nn(el.astype(BF16), v_ref[ks, :]) + dot_nn(em.astype(BF16), vm)
            o_ref[at, :] = (acc / tot).astype(BF16)
            l_ref[0, at, :] = mc + jnp.log2(tot)

    head = lambda n: pl.BlockSpec((n, HD), lambda h: (0, h))
    mem = pl.BlockSpec((1, ksel, blk, HD), lambda h: (h // per, 0, 0, h % per))
    return pl.pallas_call(
        kern,
        grid=(d // HD,),
        in_specs=[head(r), head(rt), head(rt), mem, mem, full((r, 1)), full((1, rt))],
        out_specs=[head(r), pl.BlockSpec((1, r, 1), lambda h: (h, 0, 0))],
        out_shape=[jax.ShapeDtypeStruct((r, d), BF16), jax.ShapeDtypeStruct((d // HD, r, 1), F32)],
        compiler_params=pltpu.CompilerParams(vmem_limit_bytes=VL, dimension_semantics=("arbitrary",)),
        name="attend",
    )(q, k, v, mk, mv, seg_q, seg_k)


def attend_back(halo, window, q, k, v, mk, mv, seg_q, seg_k, o, lse, do, cos, sin):
    r, d = q.shape
    rt = k.shape[0]
    nz, ksel, blk, cols = mk.shape
    per = cols // HD
    nm = ksel * blk
    scale = HD**-0.5

    def kern(q_ref, k_ref, v_ref, mk_ref, mv_ref, sq_ref, sk_ref, o_ref, l_ref, do_ref, cos_ref, sin_ref,
             dq_ref, dk_ref, dv_ref, sdk, sdv):
        km = mk_ref[0].reshape(nm, HD)
        vm = mv_ref[0].reshape(nm, HD)
        sdk[...] = jnp.zeros_like(sdk)
        sdv[...] = jnp.zeros_like(sdv)
        for i in range(r // QT):
            at = slice(i * QT, (i + 1) * QT)
            k0 = halo * r - window + i * QT
            ks = slice(k0, k0 + window + QT)
            own = slice(halo * r + i * QT, halo * r + (i + 1) * QT)
            qq, dd = q_ref[at, :], do_ref[at, :]
            lse_c = l_ref[0, at, :]
            delta = jnp.sum(dd.astype(F32) * o_ref[at, :].astype(F32), axis=1, keepdims=True)
            ok = allowed_of(sq_ref[at, :], sk_ref[:, ks], halo * r + i * QT, k0)
            pm = jnp.exp2(dot_nt(qq, km) * C2 - lse_c)
            dsm = (pm * (dot_nt(dd, vm) - delta)).astype(BF16)
            plo = jnp.where(ok, jnp.exp2(dot_nt(qq, k_ref[ks, :]) * C2 - lse_c), 0.0)
            dsl = (plo * (dot_nt(dd, v_ref[ks, :]) - delta)).astype(BF16)
            dq = (dot_nn(dsm, km) + dot_nn(dsl, k_ref[ks, :])) * scale
            dq_ref[at, :] = turn(dq, cos_ref[own, :], -sin_ref[own, :]).astype(BF16)
            sdk[ks, :] += dot_tn(dsl, qq)
            sdv[ks, :] += dot_tn(plo.astype(BF16), dd)
        dk_ref[...] = turn(sdk[...] * scale, cos_ref[...], -sin_ref[...]).astype(BF16)
        dv_ref[...] = sdv[...].astype(BF16)

    head = lambda n: pl.BlockSpec((n, HD), lambda h: (0, h))
    mem = pl.BlockSpec((1, ksel, blk, HD), lambda h: (h // per, 0, 0, h % per))
    return pl.pallas_call(
        kern,
        grid=(d // HD,),
        in_specs=[head(r), head(rt), head(rt), mem, mem, full((r, 1)), full((1, rt)), head(r),
                  pl.BlockSpec((1, r, 1), lambda h: (h, 0, 0)), head(r), full((rt, HD)), full((rt, HD))],
        out_specs=[head(r), head(rt), head(rt)],
        out_shape=[jax.ShapeDtypeStruct((n, d), BF16) for n in (r, rt, rt)],
        scratch_shapes=[pltpu.VMEM((rt, HD), F32)] * 2,
        compiler_params=pltpu.CompilerParams(vmem_limit_bytes=VL, dimension_semantics=("arbitrary",)),
        name="attend_back",
    )(q, k, v, mk, mv, seg_q, seg_k, o, lse, do, cos, sin)


def out_norm(x, o, wo, gains):
    r, d = x.shape
    dp, nz, kk, _ = wo.shape

    def kern(x_ref, o_ref, w_ref, gn_ref, h_ref, n_ref):
        t = pl.program_id(0)

        @pl.when(t == 0)
        def _():
            h_ref[...] = x_ref[...].astype(F32)

        w = lanes(w_ref)
        tile = 256

        @pl.loop(0, r // tile)
        def _(i):
            at = pl.ds(pl.multiple_of(i * tile, tile), tile)
            h_ref[at, :] += dot_nn(o_ref[at, :], w)

        @pl.when(t == pl.num_programs(0) - 1)
        def _():
            h = h_ref[...]
            n_ref[...] = (h * inv_rms(h) * gain_row(gn_ref, 1)).astype(BF16)

    return pl.pallas_call(
        kern,
        grid=(nz,),
        in_specs=[full((r, d)), pl.BlockSpec((r, kk), lambda t: (0, t)),
                  pl.BlockSpec((dp, 1, kk, wo.shape[3]), lambda t: (0, t, 0, 0)), full(gains.shape)],
        out_specs=[full((r, d)), full((r, d))],
        out_shape=[jax.ShapeDtypeStruct((r, d), F32), jax.ShapeDtypeStruct((r, d), BF16)],
        compiler_params=pltpu.CompilerParams(vmem_limit_bytes=VL, dimension_semantics=("arbitrary",)),
        name="out_norm",
    )(x, o, wo, gains)


def feed(h, n2, c, gains, wg, wu, wd, wo):
    r, d = h.shape
    dp, nz, ff, _ = wg.shape
    kk = wo.shape[2]

    def kern(h_ref, n_ref, c_ref, gn_ref, wg_ref, wu_ref, wd_ref, wo_ref,
             hid_ref, dg_ref, du_ref, out_ref, dh_ref, dhb_ref, do_ref, gg_ref, sg, su, sd, acc):
        t = pl.program_id(0)
        last = pl.num_programs(0) - 1
        sg[...] = lanes(wg_ref)
        su[...] = lanes(wu_ref)
        sd[...] = lanes(wd_ref)

        @pl.when(t == 0)
        def _():
            out_ref[...] = h_ref[...]
            acc[...] = jnp.zeros_like(acc)

        tile = 128

        @pl.loop(0, r // tile)
        def _(i):
            at = pl.ds(pl.multiple_of(i * tile, tile), tile)
            n = n_ref[at, :]
            gate = dot_nt(n, sg[...])
            up = dot_nt(n, su[...])
            dhid = dot_nt(c_ref[at, :], sd[...])
            sig = 1.0 / (1.0 + jnp.exp(-gate))
            act = gate * sig
            hid = (act * up).astype(BF16)
            hid_ref[0, at, :] = hid
            dg = (dhid * up * (sig * (1.0 + gate * (1.0 - sig)))).astype(BF16)
            du = (dhid * act).astype(BF16)
            dg_ref[0, at, :] = dg
            du_ref[0, at, :] = du
            out_ref[at, :] += dot_nn(hid, sd[...])
            acc[at, :] += dot_nn(dg, sg[...]) + dot_nn(du, su[...])

        @pl.when(t == last)
        def _():
            g = gain_row(gn_ref, 1)
            h = h_ref[...]
            dn = acc[...]
            iv = inv_rms(h)
            gg_ref[...] = jnp.sum(dn * h * iv, axis=0, keepdims=True)
            gd = dn * g
            dh = c_ref[...].astype(F32) + iv * gd - h * (iv * iv * iv * jnp.mean(h * gd, axis=1, keepdims=True))
            dh_ref[...] = dh
            dhb_ref[...] = dh.astype(BF16)

            @pl.loop(0, nz)
            def _(u):
                w = jnp.concatenate([wo_ref[e, u] for e in range(dp)], axis=1)
                do_ref[u] = dot_nt(dhb_ref[...], w).astype(BF16)

    wspec = pl.BlockSpec((dp, 1, ff, wg.shape[3]), lambda t: (0, t, 0, 0))
    piece = pl.BlockSpec((1, r, ff), lambda t: (t, 0, 0))
    one = lambda s: full(s, 1)
    return pl.pallas_call(
        kern,
        grid=(nz,),
        in_specs=[one((r, d)), one((r, d)), one((r, d)), one(gains.shape), wspec, wspec, wspec, one(wo.shape)],
        out_specs=[piece, piece, piece, full((r, d)), full((r, d)), full((r, d)), full((nz, r, kk)), full((1, d))],
        out_shape=[jax.ShapeDtypeStruct((nz, r, ff), BF16)] * 3
        + [jax.ShapeDtypeStruct((r, d), F32), jax.ShapeDtypeStruct((r, d), F32), jax.ShapeDtypeStruct((r, d), BF16),
           jax.ShapeDtypeStruct((nz, r, kk), BF16), jax.ShapeDtypeStruct((1, d), F32)],
        scratch_shapes=[pltpu.VMEM((ff, d), BF16)] * 3 + [pltpu.VMEM((r, d), F32)],
        compiler_params=pltpu.CompilerParams(vmem_limit_bytes=VL, dimension_semantics=("arbitrary",)),
        name="feed",
    )(h, n2, c, gains, wg, wu, wd, wo)


def project_back(halo, x, xh, dq, dk, dv, wq, wk, wv):
    r, d = x.shape
    dp, nz, _, cols = wq.shape
    rt = (halo + 1) * r

    def kern(x_ref, xh_ref, dq_ref, dk_ref, dv_ref, wq_ref, wk_ref, wv_ref, own_ref, hb_ref, gg_ref, acc, w_s):
        t = pl.program_id(0)
        w_s[:, 0:cols] = rows(wk_ref)
        w_s[:, cols : 2 * cols] = rows(wv_ref)
        w_s[:, 2 * cols :] = rows(wq_ref)

        @pl.when(t == 0)
        def _():
            acc[...] = jnp.zeros_like(acc)

        tile = 256

        @pl.loop(0, rt // tile)
        def _(i):
            at = pl.ds(pl.multiple_of(i * tile, tile), tile)
            acc[at, :] += dot_nt(jnp.concatenate([dk_ref[at, :], dv_ref[at, :]], axis=1), w_s[:, 0 : 2 * cols])

        @pl.loop(0, r // tile)
        def _(i):
            at = pl.ds(pl.multiple_of(i * tile, tile), tile)
            to = pl.ds(pl.multiple_of(i * tile + halo * r, tile), tile)
            acc[to, :] += dot_nt(dq_ref[at, :], w_s[:, 2 * cols :])

        @pl.when(t == pl.num_programs(0) - 1)
        def _():
            me = lax.axis_index("tensor")
            own_ref[...] = acc[halo * r :, :]
            hb_ref[...] = acc[: halo * r, :].astype(BF16)
            v = x_ref[...].astype(F32)
            g = jnp.sum(acc[halo * r :, :] * v * inv_rms(v), axis=0, keepdims=True)
            for j in range(halo):
                v = xh_ref[j].astype(F32)
                lo = (halo - 1 - j) * r
                more = jnp.sum(acc[lo : lo + r, :] * v * inv_rms(v), axis=0, keepdims=True)
                g = g + jnp.where(me >= j + 1, more, jnp.zeros_like(more))
            gg_ref[...] = g

    wspec = pl.BlockSpec((dp, 1, wq.shape[2], cols), lambda t: (0, t, 0, 0))
    col = lambda n: pl.BlockSpec((n, cols), lambda t: (0, t))
    return pl.pallas_call(
        kern,
        grid=(nz,),
        in_specs=[full((r, d)), full((halo, r, d)), col(r), col(rt), col(rt)] + [wspec] * 3,
        out_specs=[full((r, d)), full((halo * r, d)), full((1, d))],
        out_shape=[jax.ShapeDtypeStruct((r, d), F32), jax.ShapeDtypeStruct((halo * r, d), BF16),
                   jax.ShapeDtypeStruct((1, d), F32)],
        scratch_shapes=[pltpu.VMEM((rt, d), F32), pltpu.VMEM((d, 3 * cols), BF16)],
        compiler_params=pltpu.CompilerParams(vmem_limit_bytes=VL, dimension_semantics=("arbitrary",)),
        name="project_back",
    )(x, xh, dq, dk, dv, wq, wk, wv)


def feed_grads(hid, dg, du, n2, c):
    nz, r, ff = hid[0].shape
    half = n2[0].shape[1]
    nb = half // 128

    def kern(h0, h1, g0, g1, u0, u1, n0, n1, c0, c1, gg, gu, gd):
        def put(out, a0, a1, b0, b1):
            y = (dot_tn(a0[0], b0[...]) + dot_tn(a1[0], b1[...])).astype(BF16)
            for e in range(nb):
                out[e, 0] = y[:, e * 128 : (e + 1) * 128]

        put(gg, g0, g1, n0, n1)
        put(gu, u0, u1, n0, n1)
        put(gd, h0, h1, c0, c1)

    piece = pl.BlockSpec((1, r, ff), lambda t: (t, 0, 0))
    out = pl.BlockSpec((nb, 1, ff, 128), lambda t: (0, t, 0, 0))
    return pl.pallas_call(
        kern,
        grid=(nz,),
        in_specs=[piece] * 6 + [full((r, half))] * 4,
        out_specs=[out] * 3,
        out_shape=[jax.ShapeDtypeStruct((nb, nz, ff, 128), BF16)] * 3,
        compiler_params=pltpu.CompilerParams(vmem_limit_bytes=VL, dimension_semantics=("arbitrary",)),
        name="feed_grads",
    )(*hid, *dg, *du, *n2, *c)


def attn_grads(halo, nz, o, dhb, n1, dq, dk, dv):
    r, d = o[0].shape
    half = dhb[0].shape[1]
    rt = (halo + 1) * r
    nb, cols = half // 128, d // nz

    def kern(o0, o1, b0, b1, n0, m1, q0, q1, k0, k1, v0, v1, go, gq, gk, gv):
        y = (dot_tn(o0[...], b0[...]) + dot_tn(o1[...], b1[...])).astype(BF16)
        for e in range(nb):
            go[e, 0] = y[:, e * 128 : (e + 1) * 128]
        own = pl.ds(halo * r, r)
        for out, p0, p1, a0, a1 in (
            (gq, q0, q1, n0.at[own], m1.at[own]),
            (gk, k0, k1, n0, m1),
            (gv, v0, v1, n0, m1),
        ):
            y = (dot_tn(a0[...], p0[...]) + dot_tn(a1[...], p1[...])).astype(BF16)
            for e in range(nb):
                out[e, 0] = y[e * 128 : (e + 1) * 128, :]

    col = lambda n: pl.BlockSpec((n, cols), lambda t: (0, t))
    out1 = pl.BlockSpec((nb, 1, cols, 128), lambda t: (0, t, 0, 0))
    out2 = pl.BlockSpec((nb, 1, 128, cols), lambda t: (0, t, 0, 0))
    return pl.pallas_call(
        kern,
        grid=(nz,),
        in_specs=[col(r)] * 2 + [full((r, half))] * 2 + [full((rt, half))] * 2 + [col(r)] * 2 + [col(rt)] * 4,
        out_specs=[out1, out2, out2, out2],
        out_shape=[jax.ShapeDtypeStruct((nb, nz, cols, 128), BF16)]
        + [jax.ShapeDtypeStruct((nb, nz, 128, cols), BF16)] * 3,
        compiler_params=pltpu.CompilerParams(vmem_limit_bytes=VL, dimension_semantics=("arbitrary",)),
        name="attn_grads",
    )(*o, *dhb, *n1, *dq, *dk, *dv)


def input_grad(halo, x, gains, dn1, more, dh):
    r, d = x.shape
    tile = 256

    def kern(x_ref, gn_ref, dn_ref, m_ref, dh_ref, out_ref):
        t = lax.axis_index("tensor")
        nz = lax.axis_size("tensor")
        dn = dn_ref[...]
        for j in range(halo):
            v = m_ref[j].astype(F32)
            dn = dn + jnp.where(t + j + 1 < nz, v, jnp.zeros_like(v))
        v = x_ref[...].astype(F32)
        iv = inv_rms(v)
        gd = dn * gain_row(gn_ref, 0)
        out_ref[...] = dh_ref[...] + iv * gd - v * (iv * iv * iv * jnp.mean(v * gd, axis=1, keepdims=True))

    row = pl.BlockSpec((tile, d), lambda i: (i, 0))
    return pl.pallas_call(
        kern,
        grid=(r // tile,),
        in_specs=[row, full(gains.shape), row, pl.BlockSpec((halo, tile, d), lambda i: (0, i, 0)), row],
        out_specs=row,
        out_shape=jax.ShapeDtypeStruct((r, d), F32),
        compiler_params=pltpu.CompilerParams(vmem_limit_bytes=VL, dimension_semantics=("arbitrary",)),
        name="input_grad",
    )(x, gains, dn1, more, dh)


class Scatter:
    def __init__(self, g, src, rows, b_first, bufs, sems, out):
        self.g, self.src, self.rows, self.b_first, self.out = g, src, rows, b_first, out
        self.acc, self.r1, self.r2, self.r3 = bufs
        self.sems, self.next = sems, 0
        self.sent = []

    def _sem(self):
        i = self.next
        self.next += 1
        return self.sems[0].at[i], self.sems[1].at[i]

    def _e(self, f, s):
        return s * self.g.nb + f if self.b_first else f * self.g.nb + s

    def _dp(self, f, s, c):
        return self._e(f, s) * 2 + c

    def _mine(self):
        a, b, c, t, me = coords(self.g)
        f, s = (b, a) if self.b_first else (a, b)
        n1, n2 = (self.g.nb, self.g.na) if self.b_first else (self.g.na, self.g.nb)
        return f, s, c, t, me, n1, n2

    def start_first(self):
        f, s, c, t, me, n1, n2 = self._mine()
        lo, n = self.rows
        self.own, self.first = [], []
        for k in range(1, n1):
            to = (f + k) % n1
            for j in range(n2):
                x, y = self._sem()
                d = send(self.src.at[self._e(to, j), :, pl.ds(lo, n), :], self.r1.at[k - 1, j], x, y, self._dp(to, s, c), t)
                d.start()
                self.first.append(d)
        for j in range(n2):
            x, _ = self._sem()
            d = pltpu.make_async_copy(self.src.at[self._e(f, j), :, pl.ds(lo, n), :], self.acc.at[j], x)
            d.start()
            self.own.append(d)
        self.sent += self.first

    def start_second(self):
        f, s, c, t, me, n1, n2 = self._mine()
        for d in self.own:
            d.wait()
        for d in self.first:
            d.wait_recv()
        for j in range(n2):

            @pl.loop(0, self.g.nz)
            def _(u):
                v = self.acc[j, u].astype(F32)
                for k in range(n1 - 1):
                    v = v + self.r1[k, j, u].astype(F32)
                self.acc[j, u] = v.astype(BF16)

        self.second = []
        for k in range(1, n2):
            to = (s + k) % n2
            x, y = self._sem()
            d = send(self.acc.at[to], self.r2.at[k - 1], x, y, self._dp(f, to, c), t)
            d.start()
            self.second.append(d)
        self.sent += self.second

    def start_z(self):
        f, s, c, t, me, n1, n2 = self._mine()
        for d in self.second:
            d.wait_recv()

        @pl.loop(0, self.g.nz)
        def _(u):
            v = self.acc[s, u].astype(F32)
            for k in range(n2 - 1):
                v = v + self.r2[k, u].astype(F32)
            self.acc[s, u] = v.astype(BF16)

        self.third = []
        for k in range(1, self.g.nz):
            to = (t + k) % self.g.nz
            x, y = self._sem()
            d = send(self.acc.at[s, to], self.r3.at[k - 1], x, y, me, to)
            d.start()
            self.third.append(d)
        self.sent += self.third

    def finish(self):
        f, s, c, t, me, n1, n2 = self._mine()
        lo, n = self.rows
        for d in self.third:
            d.wait_recv()
        v = self.acc[s, t].astype(F32)
        for k in range(self.g.nz - 1):
            v = v + self.r3[k].astype(F32)
        self.out[pl.ds(lo, n), :] = v
        for d in self.sent:
            d.wait_send()


def scatter_sems(g):
    return (g.na - 1) * g.na + g.na + (g.na - 1) + (g.nz - 1)


def k2_kernel(g, halo, units, n_w, *refs):
    refs = list(refs)
    take = lambda n: [refs.pop(0) for _ in range(n)]
    gains, hb = take(2)
    srcs = take(n_w)
    gout, more = take(2)
    outs = take(n_w)
    bufs = [take(4) for _ in units]
    sems = [take(2) for _ in units]
    gz, gs, gd = take(3)
    zss, zrs, dss, drs, hss, hrs = take(6)
    a, b, c, t, me = coords(g)
    greet(g, me, t)
    us = [
        Scatter(g, srcs[w], rows, bf, bufs[i], sems[i], outs[w]) for i, (w, rows, bf) in enumerate(units)
    ]
    pairs = [us[i : i + 2] for i in range(0, len(us), 2)]
    np_ = len(pairs)
    r = more.shape[1]
    hd = []
    for j in range(halo):
        d = send(hb.at[pl.ds((halo - 1 - j) * r, r), :], more.at[j], hss.at[j], hrs.at[j], me, (t + g.nz - 1 - j) % g.nz)
        hd.append(d)

        @pl.when(t >= j + 1)
        def _():
            d.start()

    zg = []
    for k in range(1, g.nz):
        d = send(gains, gz.at[k - 1], zss.at[k - 1], zrs.at[k - 1], me, (t + k) % g.nz)
        d.start()
        zg.append(d)
    for p in range(min(2, np_)):
        for u in pairs[p]:
            u.start_first()
    for d in zg:
        d.wait()
    tot = gains[...]
    for k in range(g.nz - 1):
        tot = tot + gz[k]
    for e in range(g.dp):
        gs[e] = tot[:, e * 128 : (e + 1) * 128]
    dg = []
    for k in range(1, g.dp):
        to = (me + k) % g.dp
        d = send(gs.at[to], gd.at[me], dss.at[k], drs.at[k], to, t)
        d.start()
        dg.append(d)
    own = pltpu.make_async_copy(gs.at[me], gd.at[me], dss.at[0])
    own.start()
    for p in range(np_):
        for u in pairs[p]:
            u.start_second()
        if p + 2 < np_:
            for u in pairs[p + 2]:
                u.start_first()
        if p >= 1:
            for u in pairs[p - 1]:
                u.start_z()
    for u in pairs[-1]:
        u.start_z()
    own.wait()
    for d in dg:
        d.wait()
    v = gd[0]
    for e in range(1, g.dp):
        v = v + gd[e]
    gout[...] = v
    for u in us:
        u.finish()
    for j, d in enumerate(hd):

        @pl.when(t >= j + 1)
        def _():
            d.wait_send()

        @pl.when(t + j + 1 < g.nz)
        def _():
            d.wait_recv()


def halves(srcs_rows):
    units = []
    for item in srcs_rows:
        if len(item) == 2:
            (w0, n0), (w1, n1) = item
            units += [(w0, (0, n0), True), (w1, (0, n1), False)]
        else:
            ((w, n),) = item
            units += [(w, (0, n // 2), True), (w, (n // 2, n - n // 2), False)]
    return units


def k2(g, halo, gains, hb, srcs, units, r):
    any_ = pl.BlockSpec(memory_space=pl.ANY)
    vm = pl.BlockSpec(memory_space=pltpu.VMEM)
    dma = lambda *n: pltpu.SemaphoreType.DMA(n)
    d = hb.shape[1]
    n_w = len(srcs)
    scratch = []
    for w, (lo, n), bf in units:
        cols = srcs[w].shape[3]
        n1, n2 = (g.nb, g.na) if bf else (g.na, g.nb)
        scratch += [
            pltpu.VMEM((n2, g.nz, n, cols), BF16),
            pltpu.VMEM((n1 - 1, n2, g.nz, n, cols), BF16),
            pltpu.VMEM((n2 - 1, g.nz, n, cols), BF16),
            pltpu.VMEM((g.nz - 1, n, cols), BF16),
        ]
    scratch += [dma(scatter_sems(g))] * (2 * len(units))
    scratch += [pltpu.VMEM((g.nz - 1,) + gains.shape, F32), pltpu.VMEM((g.dp, 2, 128), F32), pltpu.VMEM((g.dp, 2, 128), F32)]
    scratch += [dma(g.nz), dma(g.nz), dma(g.dp), dma(g.dp), dma(halo), dma(halo)]
    out_shape = [jax.ShapeDtypeStruct((2, 128), F32), jax.ShapeDtypeStruct((halo, r, d), BF16)] + [
        jax.ShapeDtypeStruct(s.shape[2:], F32) for s in srcs
    ]
    return pl.pallas_call(
        functools.partial(k2_kernel, g, halo, units, n_w),
        out_shape=out_shape,
        in_specs=[vm, any_] + [any_] * n_w,
        out_specs=[vm, any_] + [vm] * n_w,
        scratch_shapes=scratch,
        compiler_params=pltpu.CompilerParams(collective_id=1, has_side_effects=True, vmem_limit_bytes=60 * 2**20),
        name="bwd_exchange",
    )(gains, hb, *srcs)


HEADS = 8
QB = 512


def normalize(field, gain_vec):
    return field * lax.rsqrt(jnp.mean(field * field, axis=-1, keepdims=True) + EPSILON) * gain_vec


def rotate(field, heads_here):
    row_total = field.shape[0]
    head_size = field.shape[1] // heads_here
    half_width = head_size // 2
    frequencies = 10000.0 ** (-jnp.arange(half_width, dtype=jnp.float32) * 2.0 / head_size)
    angles = jnp.arange(row_total, dtype=jnp.float32)[:, None] * frequencies[None, :]
    cosine = jnp.cos(angles)[:, None, :]
    sine_table = jnp.sin(angles)[:, None, :]
    split_heads = field.reshape(row_total, heads_here, head_size)
    first_half = split_heads[..., :half_width]
    second_half = split_heads[..., half_width:]
    turned = jnp.concatenate(
        [
            first_half * cosine - second_half * sine_table,
            second_half * cosine + first_half * sine_table,
        ],
        axis=-1,
    )
    return turned.reshape(row_total, heads_here * head_size)


def contract_rows(left, right):
    return lax.dot_general(
        left, right, (((0,), (0,)), ((), ())), preferred_element_type=jnp.float32
    )


def against(left, right):
    return lax.dot_general(
        left, right, (((1,), (1,)), ((), ())), preferred_element_type=jnp.float32
    )


def spread_rows(local_rows, matrices):
    piece_rows = lax.all_gather(local_rows, "tensor", axis=0, tiled=True)
    return jnp.concatenate(
        [jnp.dot(piece_rows, matrix, preferred_element_type=jnp.float32) for matrix in matrices],
        axis=1,
    )


def reduce_rows(left, right):
    return lax.psum_scatter(
        jnp.dot(left, right, preferred_element_type=jnp.float32).astype(jnp.bfloat16),
        "tensor",
        scatter_dimension=0,
        tiled=True,
    ).astype(jnp.float32)


def return_rows(pairs):
    summed = against(pairs[0][0], pairs[0][1])
    for grad_block, matrix in pairs[1:]:
        summed = summed + against(grad_block, matrix)
    return lax.psum_scatter(
        summed.astype(jnp.bfloat16), "tensor", scatter_dimension=0, tiled=True
    ).astype(jnp.float32)


def weight_grads(local_rows, grads_list):
    piece_rows = lax.all_gather(local_rows, "tensor", axis=0, tiled=True)
    return tuple((contract_rows(piece_rows, grad_one) for grad_one in grads_list))


def all_rows(local_grad):
    return lax.all_gather(local_grad, "tensor", axis=0, tiled=True)


def on_device_any(
    block_in,
    segments,
    retrieved,
    partner,
    memory_keys,
    memory_values,
    gain_attn,
    w_query,
    w_key,
    w_value,
    w_out,
    gain_ffn,
    w_gate,
    w_up,
    w_down,
    cotangent,
):
    tensor_size = lax.axis_size("tensor")
    dp_size = lax.axis_size("dp")
    heads_here = HEADS // tensor_size
    head_width = heads_here * HD
    score_scale = HD ** (-0.5)
    seq_len = segments.shape[1]
    query_blocks = seq_len // QB
    stream_in = block_in[0].astype(jnp.float32)
    seg_row = segments[0]
    positions = jnp.arange(seq_len)
    gathered = (
        lax.all_gather(gain_attn, "dp", axis=0, tiled=True),
        lax.all_gather(w_query, "dp", axis=0, tiled=True),
        lax.all_gather(w_key, "dp", axis=0, tiled=True),
        lax.all_gather(w_value, "dp", axis=0, tiled=True),
        lax.all_gather(w_out, "dp", axis=1, tiled=True),
        lax.all_gather(gain_ffn, "dp", axis=0, tiled=True),
        lax.all_gather(w_gate, "dp", axis=0, tiled=True),
        lax.all_gather(w_up, "dp", axis=0, tiled=True),
        lax.all_gather(w_down, "dp", axis=1, tiled=True),
    )
    gain_one, query_w, key_w, value_w, out_w, gain_two, gate_w, up_w, down_w = gathered
    wanted = retrieved[0].reshape(-1)
    request_total = wanted.shape[0]
    capacity = max(2, (2 * request_total + dp_size - 1) // dp_size)
    blocks_dev = memory_keys.shape[1]
    from_partner = wanted // MEMB
    block_index = wanted % MEMB
    owner_dev = block_index // blocks_dev
    local_block = block_index % blocks_dev
    seq_id = jnp.where(from_partner == 0, lax.axis_index("dp"), partner[0])
    owner_hits = (owner_dev[:, None] == jnp.arange(dp_size)[None, :]).astype(jnp.int32)
    slot_index = jnp.sum((jnp.cumsum(owner_hits, axis=0) - 1) * owner_hits, axis=1)
    requests = (
        jnp.zeros((dp_size, capacity, 2), jnp.int32)
        .at[owner_dev, slot_index]
        .set(jnp.stack([seq_id, local_block], axis=-1))
    )
    received = lax.all_to_all(requests, "dp", split_axis=0, concat_axis=0, tiled=True)
    picked_keys = memory_keys[received[..., 0], received[..., 1]]
    picked_values = memory_values[received[..., 0], received[..., 1]]
    fetched_keys = lax.all_to_all(picked_keys, "dp", split_axis=0, concat_axis=0, tiled=True)
    fetched_values = lax.all_to_all(picked_values, "dp", split_axis=0, concat_axis=0, tiled=True)
    memory_k = fetched_keys[owner_dev, slot_index].reshape(query_blocks, -1, heads_here, HD)
    memory_v = fetched_values[owner_dev, slot_index].reshape(query_blocks, -1, heads_here, HD)
    normed = normalize(stream_in, gain_one.astype(jnp.float32)).astype(jnp.bfloat16)
    qkv_rows = spread_rows(normed, [query_w, key_w, value_w])
    query_raw = qkv_rows[:, :head_width]
    key_raw = qkv_rows[:, head_width : 2 * head_width]
    queries = rotate(query_raw, heads_here).astype(jnp.bfloat16)
    keys_all = rotate(key_raw, heads_here).astype(jnp.bfloat16).reshape(seq_len, heads_here, HD)
    values_all = qkv_rows[:, 2 * head_width :].astype(jnp.bfloat16).reshape(seq_len, heads_here, HD)
    query_tiles = queries.reshape(query_blocks, QB, heads_here, HD)
    seg_tiles = seg_row.reshape(query_blocks, QB)
    pos_tiles = positions.reshape(query_blocks, QB)

    def scores_of(query_blk, seg_blk, pos_blk, key_mem):
        local_scores = jnp.einsum(
            "qhd,khd->hqk", query_blk, keys_all, preferred_element_type=jnp.float32
        )
        memory_scores = jnp.einsum(
            "qhd,khd->hqk", query_blk, key_mem, preferred_element_type=jnp.float32
        )
        raw_scores = jnp.concatenate([local_scores, memory_scores], axis=-1) * score_scale
        allowed = (seg_blk[:, None] == seg_row[None, :]) & (positions[None, :] <= pos_blk[:, None])
        allowed = jnp.concatenate(
            [allowed, jnp.ones((query_blk.shape[0], key_mem.shape[0]), dtype=jnp.bool_)], axis=1
        )
        return (raw_scores, allowed)

    def forward_block(pieces):
        query_blk, seg_blk, pos_blk, key_mem, value_mem = pieces
        raw_scores, allowed = scores_of(query_blk, seg_blk, pos_blk, key_mem)
        masked = jnp.where(allowed[None], raw_scores, MASKED)
        row_max = jnp.max(masked, axis=-1, keepdims=True)
        expo = jnp.exp(masked - row_max)
        row_total = jnp.sum(expo, axis=-1, keepdims=True)
        weights_soft = (expo / row_total).astype(jnp.bfloat16)
        values_both = jnp.concatenate([values_all, value_mem], axis=0)
        result = jnp.einsum(
            "hqk,khd->qhd", weights_soft, values_both, preferred_element_type=jnp.float32
        )
        return (result, (row_max + jnp.log(row_total))[..., 0])

    attended, log_totals = lax.map(
        forward_block, (query_tiles, seg_tiles, pos_tiles, memory_k, memory_v)
    )
    mixed = attended.reshape(seq_len, head_width).astype(jnp.bfloat16)
    stream = stream_in + reduce_rows(mixed, out_w)
    normed_ffn = normalize(stream, gain_two.astype(jnp.float32)).astype(jnp.bfloat16)
    gate_up = spread_rows(normed_ffn, [gate_w, up_w])
    hidden_width = gate_w.shape[1]
    gate_pre = gate_up[:, :hidden_width]
    up_pre = gate_up[:, hidden_width:]
    hidden = (jax.nn.silu(gate_pre) * up_pre).astype(jnp.bfloat16)
    block_out = stream + reduce_rows(hidden, down_w)
    gathered_back = (
        lax.all_gather(gain_attn, "dp", axis=0, tiled=True),
        lax.all_gather(w_query, "dp", axis=0, tiled=True),
        lax.all_gather(w_key, "dp", axis=0, tiled=True),
        lax.all_gather(w_value, "dp", axis=0, tiled=True),
        lax.all_gather(w_out, "dp", axis=1, tiled=True),
        lax.all_gather(gain_ffn, "dp", axis=0, tiled=True),
        lax.all_gather(w_gate, "dp", axis=0, tiled=True),
        lax.all_gather(w_up, "dp", axis=0, tiled=True),
        lax.all_gather(w_down, "dp", axis=1, tiled=True),
    )
    gain_one, query_w, key_w, value_w, out_w, gain_two, gate_w, up_w, down_w = gathered_back
    dout_rows = cotangent[0]

    def gated(gate_in, up_in):
        return jax.nn.silu(gate_in) * up_in

    dout_full = all_rows(dout_rows)
    grad_down = contract_rows(hidden, dout_full)
    d_hidden = against(dout_full, down_w)
    gated_value, pull_gated = jax.vjp(gated, gate_pre, up_pre)
    d_gate, d_up = pull_gated(d_hidden)
    d_gate = d_gate.astype(jnp.bfloat16)
    d_up = d_up.astype(jnp.bfloat16)
    d_norm_ffn = return_rows([(d_gate, gate_w), (d_up, up_w)])
    grad_gate, grad_up = weight_grads(normed_ffn, [d_gate, d_up])
    norm_value, pull_norm_ffn = jax.vjp(normalize, stream, gain_two.astype(jnp.float32))
    d_stream_norm, grad_gain_ffn = pull_norm_ffn(d_norm_ffn)
    d_stream = dout_rows.astype(jnp.float32) + d_stream_norm
    d_stream_full = all_rows(d_stream.astype(jnp.bfloat16))
    grad_out = contract_rows(mixed, d_stream_full)
    d_mixed = against(d_stream_full, out_w).astype(jnp.bfloat16)
    d_mixed_tiles = d_mixed.reshape(query_blocks, QB, heads_here, HD)

    def backward_block(carry_sums, pieces):
        key_sum, value_sum = carry_sums
        query_blk, seg_blk, pos_blk, key_mem, value_mem, log_blk, grad_blk = pieces
        raw_scores, allowed = scores_of(query_blk, seg_blk, pos_blk, key_mem)
        probs = jnp.where(allowed[None], jnp.exp(raw_scores - log_blk[..., None]), 0.0)
        values_both = jnp.concatenate([values_all, value_mem], axis=0)
        d_probs = jnp.einsum(
            "qhd,khd->hqk", grad_blk, values_both, preferred_element_type=jnp.float32
        )
        shared = jnp.sum(probs * d_probs, axis=-1, keepdims=True)
        d_scores = (probs * (d_probs - shared)).astype(jnp.bfloat16)
        probs_low = probs.astype(jnp.bfloat16)
        keys_both = jnp.concatenate([keys_all, key_mem], axis=0)
        d_query = (
            jnp.einsum("hqk,khd->qhd", d_scores, keys_both, preferred_element_type=jnp.float32)
            * score_scale
        )
        key_sum = (
            key_sum
            + jnp.einsum(
                "hqk,qhd->khd",
                d_scores[..., :seq_len],
                query_blk,
                preferred_element_type=jnp.float32,
            )
            * score_scale
        )
        value_sum = value_sum + jnp.einsum(
            "hqk,qhd->khd", probs_low[..., :seq_len], grad_blk, preferred_element_type=jnp.float32
        )
        return ((key_sum, value_sum), d_query)

    zero_grads = jnp.zeros((seq_len, heads_here, HD), jnp.float32)
    (d_keys, d_values), d_queries = lax.scan(
        backward_block,
        (zero_grads, zero_grads),
        (query_tiles, seg_tiles, pos_tiles, memory_k, memory_v, log_totals, d_mixed_tiles),
    )

    def turn(field):
        return rotate(field, heads_here)

    turned_value, pull_turn = jax.vjp(turn, query_raw)
    d_query_raw = pull_turn(d_queries.reshape(seq_len, head_width))[0].astype(jnp.bfloat16)
    d_key_raw = pull_turn(d_keys.reshape(seq_len, head_width))[0].astype(jnp.bfloat16)
    d_value_raw = d_values.reshape(seq_len, head_width).astype(jnp.bfloat16)
    d_norm_attn = return_rows([(d_query_raw, query_w), (d_key_raw, key_w), (d_value_raw, value_w)])
    grad_query, grad_key, grad_value = weight_grads(normed, [d_query_raw, d_key_raw, d_value_raw])
    norm_first, pull_norm_attn = jax.vjp(normalize, stream_in, gain_one.astype(jnp.float32))
    d_input_norm, grad_gain_attn = pull_norm_attn(d_norm_attn)
    grad_in = d_stream + d_input_norm
    grad_gain_attn, grad_gain_ffn = lax.psum((grad_gain_attn, grad_gain_ffn), "tensor")
    results = (
        lax.psum_scatter(
            grad_gain_attn.astype(jnp.bfloat16), "dp", scatter_dimension=0, tiled=True
        ).astype(jnp.float32),
        lax.psum_scatter(
            grad_query.astype(jnp.bfloat16), "dp", scatter_dimension=0, tiled=True
        ).astype(jnp.float32),
        lax.psum_scatter(
            grad_key.astype(jnp.bfloat16), "dp", scatter_dimension=0, tiled=True
        ).astype(jnp.float32),
        lax.psum_scatter(
            grad_value.astype(jnp.bfloat16), "dp", scatter_dimension=0, tiled=True
        ).astype(jnp.float32),
        lax.psum_scatter(
            grad_out.astype(jnp.bfloat16), "dp", scatter_dimension=1, tiled=True
        ).astype(jnp.float32),
        lax.psum_scatter(
            grad_gain_ffn.astype(jnp.bfloat16), "dp", scatter_dimension=0, tiled=True
        ).astype(jnp.float32),
        lax.psum_scatter(
            grad_gate.astype(jnp.bfloat16), "dp", scatter_dimension=0, tiled=True
        ).astype(jnp.float32),
        lax.psum_scatter(
            grad_up.astype(jnp.bfloat16), "dp", scatter_dimension=0, tiled=True
        ).astype(jnp.float32),
        lax.psum_scatter(
            grad_down.astype(jnp.bfloat16), "dp", scatter_dimension=1, tiled=True
        ).astype(jnp.float32),
    )
    return (block_out[None], grad_in[None]) + results


def cover(halo, r, t):
    half = HD // 2
    freq = 10000.0 ** (-jnp.arange(half, dtype=F32) * 2.0 / HD)
    pos = (t * r - halo * r + jnp.arange((halo + 1) * r)).astype(F32)
    ang = pos[:, None] * freq[None, :]
    cos, sin = jnp.cos(ang), jnp.sin(ang)
    return jnp.concatenate([cos, cos], axis=1), jnp.concatenate([-sin, sin], axis=1)


def on_device(*args):
    x, dp = args[0], lax.axis_size("dp")
    side = math.isqrt(dp // 2)
    if 2 * side * side == dp and x.shape[2] % (128 * dp) == 0:
        return on_device_rows(*args)
    return on_device_any(*args)


def on_device_rows(
    block_in, segments, retrieved, partner, memory_keys, memory_values,
    gain_attn, w_query, w_key, w_value, w_out, gain_ffn, w_gate, w_up, w_down, cotangent,
):
    g = Grid(lax.axis_size("dp"), lax.axis_size("tensor"))
    t, me = lax.axis_index("tensor"), lax.axis_index("dp")
    x, c = block_in[0], cotangent[0]
    r, d = x.shape
    seq_len = segments.shape[1]
    window = seq_len // 4
    halo = -(-window // r)
    nq, ksel = retrieved.shape[1:]
    cap = max(2, -(-2 * nq * ksel // g.dp))
    req, sel = plan_requests(retrieved[0], partner[0], g.dp, memory_keys.shape[1], cap)
    gains = jnp.stack([gain_attn, gain_ffn]).astype(F32)
    flat = lambda m: m.reshape((-1,) + m.shape[2:])
    shards = [w_query, w_key, w_value, w_out, w_gate.T, w_up.T, w_down]
    wq, wk, wv, wo, wg, wu, wd, xh, gn, mk, mv = k1(
        g, cap, halo, req, sel, x, gains, flat(memory_keys), flat(memory_values), shards, nq, ksel
    )
    cos, sin = cover(halo, r, t)
    padded = jnp.concatenate([jnp.full((halo * r,), -1, jnp.int32), segments[0]])
    seg = lax.dynamic_slice(padded, (t * r,), ((halo + 1) * r,))
    seg_k, seg_q = seg[None, :], seg[halo * r :, None]

    n1, q, k, v = project(halo, None, x, xh, gn, cos, sin, wq, wk, wv)
    o, lse = attend(halo, window, q, k, v, mk, mv, seg_q, seg_k)
    h, n2 = out_norm(x, o, wo, gn)
    hid, dg, du, block_out, dh, dhb, do, gg_ffn = feed(h, n2, c, gn, wg, wu, wd, wo)
    do = jnp.transpose(do, (1, 0, 2)).reshape(r, d)
    dq, dk, dv = attend_back(halo, window, q, k, v, mk, mv, seg_q, seg_k, o, lse, do, cos, sin)
    dn1, hb, gg_attn = project_back(halo, x, xh, dq, dk, dv, wq, wk, wv)

    core = me % 2
    pairs = [(i, i ^ 1) for i in range(g.dp)]
    other = lambda y: lax.ppermute(y, "dp", pairs)

    def cut(y):
        z = y.reshape(y.shape[0], d // 256, 2, 128)
        mine = lax.dynamic_index_in_dim(z, core, 2, False).reshape(y.shape[0], d // 2)
        theirs = lax.dynamic_index_in_dim(z, 1 - core, 2, False).reshape(y.shape[0], d // 2)
        return mine, other(theirs)

    both = lambda y: (y, other(y))
    ggt, gut, gdn = feed_grads(both(hid), both(dg), both(du), cut(n2), cut(c))
    go, gq, gk, gv = attn_grads(halo, g.nz, both(o), cut(dhb), cut(n1), both(dq), both(dk), both(dv))
    srcs = [ggt, gut, gdn, go, gq, gk, gv]
    n = lambda w: (w, srcs[w].shape[2])
    units = halves([(n(0), n(1)), (n(2),), (n(3),), (n(4), n(5)), (n(6),)])
    gains_part = jnp.concatenate([gg_attn, gg_ffn], axis=0)
    gout, more, o_gate, o_up, o_down, o_out, o_q, o_k, o_v = k2(g, halo, gains_part, hb, srcs, units, r)
    grad_in = input_grad(halo, x, gn, dn1, more, dh)
    return (
        block_out[None], grad_in[None], gout[0], o_q, o_k, o_v, o_out, gout[1], o_gate.T, o_up.T, o_down,
    )


def solution(mesh):
    return jax.shard_map(
        on_device,
        mesh=mesh,
        in_specs=(
            P("dp", "tensor", None), P("dp", None), P("dp", None, None), P("dp"),
            P(None, "dp", None, "tensor"), P(None, "dp", None, "tensor"),
            P("dp"), P("dp", "tensor"), P("dp", "tensor"), P("dp", "tensor"), P("tensor", "dp"),
            P("dp"), P("dp", "tensor"), P("dp", "tensor"), P("tensor", "dp"), P("dp", "tensor", None),
        ),
        out_specs=(
            P("dp", "tensor", None), P("dp", "tensor", None),
            P("dp"), P("dp", "tensor"), P("dp", "tensor"), P("dp", "tensor"), P("tensor", "dp"),
            P("dp"), P("dp", "tensor"), P("dp", "tensor"), P("tensor", "dp"),
        ),
        check_vma=False,
    )
```

```python
import functools
import math

import jax
import jax.numpy as jnp
from jax import lax
from jax.experimental import pallas as pl
from jax.experimental.pallas import tpu as pltpu
from jax.sharding import PartitionSpec as P

MESH = pl.DeviceIdType.MESH
MEMB = 128


class Grid:
    def __init__(self, dp, tensor):
        side = math.isqrt(dp // 2)
        assert side * side * 2 == dp
        self.na, self.nb, self.nc, self.nz, self.dp = side, side, 2, tensor, dp


def coords(g):
    me = lax.axis_index("dp")
    t = lax.axis_index("tensor")
    return me // (2 * g.nb), (me // 2) % g.nb, me % 2, t, me


def send(src, dst, ssem, rsem, dp, t):
    return pltpu.make_async_remote_copy(
        src_ref=src, dst_ref=dst, send_sem=ssem, recv_sem=rsem, device_id=(dp, t), device_id_type=MESH
    )


def greet(g, me, t):
    bar = pltpu.get_barrier_semaphore()
    for k in range(1, g.dp):
        pl.semaphore_signal(bar, inc=1, device_id=((me + k) % g.dp, t), device_id_type=MESH)
    for k in range(1, g.nz):
        pl.semaphore_signal(bar, inc=1, device_id=(me, (t + k) % g.nz), device_id_type=MESH)
    pl.semaphore_wait(bar, g.dp - 1 + g.nz - 1)


class Gather:
    def __init__(self, g, shard, buf, rows, b_first, sems, base):
        self.g, self.shard, self.buf, self.rows, self.b_first = g, shard, buf, rows, b_first
        self.sems, self.next = sems, base
        self.sent = []

    def _sem(self):
        i = self.next
        self.next += 1
        return self.sems[0].at[i], self.sems[1].at[i]

    def at(self, dp, t=None):
        lo, n = self.rows
        if t is None:
            return self.buf.at[dp, :, pl.ds(lo, n), :]
        return self.buf.at[dp, t, pl.ds(lo, n), :]

    def start_z(self):
        g = self.g
        a, b, c, t, me = coords(g)
        lo, n = self.rows
        src = self.shard.at[pl.ds(lo, n), :]
        self.z = []
        for k in range(1, g.nz):
            s, r = self._sem()
            d = send(src, self.at(me, t), s, r, me, (t + k) % g.nz)
            d.start()
            self.z.append(d)
        s, _ = self._sem()
        self.own = pltpu.make_async_copy(src, self.at(me, t), s)
        self.own.start()
        self.sent += self.z

    def _dp(self, a, b, c):
        return (a * self.g.nb + b) * 2 + c

    def _core(self, dp, c):
        s, r = self._sem()
        d = send(self.at(dp), self.at(dp), s, r, coords(self.g)[4] + 1 - 2 * c, coords(self.g)[3])
        d.start()
        self.core.append(d)
        self.sent.append(d)

    def start_first(self):
        g = self.g
        a, b, c, t, me = coords(g)
        self.own.wait()
        for d in self.z:
            d.wait_recv()
        self.first, self.core = [], []
        n1 = g.nb if self.b_first else g.na
        for k in range(1, n1):
            to = self._dp(a, (b + k) % n1, c) if self.b_first else self._dp((a + k) % n1, b, c)
            s, r = self._sem()
            d = send(self.at(me), self.at(me), s, r, to, t)
            d.start()
            self.first.append(d)
        self.sent += self.first
        self._core(me, c)

    def start_second(self):
        g = self.g
        a, b, c, t, me = coords(g)
        n1, n2 = (g.nb, g.na) if self.b_first else (g.na, g.nb)
        for d in self.first:
            d.wait_recv()
        held = [self._dp(a, (b - k) % n1, c) if self.b_first else self._dp((a - k) % n1, b, c) for k in range(n1)]
        self.second = []
        for slot in held:
            for k in range(1, n2):
                to = self._dp((a + k) % n2, b, c) if self.b_first else self._dp(a, (b + k) % n2, c)
                s, r = self._sem()
                d = send(self.at(slot), self.at(slot), s, r, to, t)
                d.start()
                self.second.append(d)
        for slot in held[1:]:
            self._core(slot, c)
        self.sent += self.second

    def start_core(self):
        g = self.g
        a, b, c, t, me = coords(g)
        n1, n2 = (g.nb, g.na) if self.b_first else (g.na, g.nb)
        for d in self.second:
            d.wait_recv()
        for k1 in range(n1):
            for k in range(1, n2):
                slot = (
                    self._dp((a - k) % n2, (b - k1) % n1, c)
                    if self.b_first
                    else self._dp((a - k1) % n1, (b - k) % n2, c)
                )
                self._core(slot, c)

    def finish(self):
        for d in self.core:
            d.wait_recv()
        for d in self.sent:
            d.wait_send()


def gather_sems(g):
    return g.nz + (g.na - 1) + g.na * (g.na - 1) + g.na * g.nb


def plan_requests(retrieved, partner, dp_size, blocks_dev, cap):
    wanted = retrieved.reshape(-1)
    n = wanted.shape[0]
    from_partner = wanted // MEMB
    block_index = wanted % MEMB
    owner = block_index // blocks_dev
    local = block_index % blocks_dev
    seq = jnp.where(from_partner == 0, lax.axis_index("dp"), partner)
    flat = seq * blocks_dev + local
    i = jnp.arange(n)
    slot = jnp.sum(((owner[:, None] == owner[None, :]) & (i[None, :] < i[:, None])).astype(jnp.int32), axis=1)
    hit = (owner[None, None, :] == jnp.arange(dp_size)[:, None, None]) & (
        slot[None, None, :] == jnp.arange(128)[None, :, None]
    )
    req = jnp.sum(jnp.where(hit, flat[None, None, :], 0), axis=2)
    return jnp.broadcast_to(req[:, None, :], (dp_size, 8, 128)).astype(jnp.int32), (owner * cap + slot).astype(jnp.int32)

HD = 128
EPSILON = 1e-05
MASKED = -1e30
F32, BF16 = jnp.float32, jnp.bfloat16


def dot_nn(x, y):
    return lax.dot_general(x, y, (((1,), (0,)), ((), ())), preferred_element_type=F32)


def dot_nt(x, y):
    return lax.dot_general(x, y, (((1,), (1,)), ((), ())), preferred_element_type=F32)


def dot_tn(x, y):
    return lax.dot_general(x, y, (((0,), (0,)), ((), ())), preferred_element_type=F32)


def inv_rms(v):
    return lax.rsqrt(jnp.mean(v * v, axis=-1, keepdims=True) + EPSILON)


def gain_row(gains_ref, which):
    n = gains_ref.shape[0]
    return jnp.concatenate([gains_ref[d, which : which + 1, :] for d in range(n)], axis=1)


def turn(v, cos, sin):
    return v * cos + pltpu.roll(v, HD // 2, axis=1) * sin


def lanes(ref):
    return jnp.concatenate([ref[d, 0] for d in range(ref.shape[0])], axis=1)


def rows(ref):
    return jnp.concatenate([ref[d, 0] for d in range(ref.shape[0])], axis=0)


VL = 60 * 2**20


def full(shape, buffers=None):
    n = len(shape)
    kw = {} if buffers is None else dict(pipeline_mode=pl.Buffered(buffers))
    return pl.BlockSpec(shape, lambda *i: (0,) * n, **kw)


def project(halo, first, x, xh, gains, cos, sin, wq, wk, wv):
    r, d = x.shape
    dp, nz, _, cols = wq.shape
    rt = (halo + 1) * r

    def kern(x_ref, xh_ref, gn_ref, cos_ref, sin_ref, wq_ref, wk_ref, wv_ref, n_ref, q_ref, k_ref, v_ref, w_s):
        @pl.when(pl.program_id(0) == 0)
        def _():
            g = gain_row(gn_ref, 0)
            t = lax.axis_index("tensor")
            for j in range(halo):
                v = xh_ref[j].astype(F32)
                n = (v * inv_rms(v) * g).astype(BF16)
                n_ref[pl.ds((halo - 1 - j) * r, r), :] = jnp.where(t >= j + 1, n, jnp.zeros_like(n))
            v = x_ref[...].astype(F32)
            n_ref[pl.ds(halo * r, r), :] = (v * inv_rms(v) * g).astype(BF16)

        w_s[:, 0:cols] = rows(wq_ref)
        w_s[:, cols : 2 * cols] = rows(wk_ref)
        w_s[:, 2 * cols :] = rows(wv_ref)

        tile = 256

        @pl.loop(0, rt // tile)
        def _(i):
            at = pl.ds(pl.multiple_of(i * tile, tile), tile)
            n = n_ref[at, :]
            y = dot_nn(n, w_s[:, cols:])
            cs, sn = cos_ref[at, :], sin_ref[at, :]
            for h in range(cols // HD):
                k_ref[at, h * HD : (h + 1) * HD] = turn(y[:, h * HD : (h + 1) * HD], cs, sn).astype(BF16)
            v_ref[at, :] = y[:, cols:].astype(BF16)

            @pl.when(i >= halo * r // tile)
            def _():
                z = dot_nn(n, w_s[:, 0:cols])
                to = pl.ds(pl.multiple_of(i * tile - halo * r, tile), tile)
                for h in range(cols // HD):
                    q_ref[to, h * HD : (h + 1) * HD] = turn(z[:, h * HD : (h + 1) * HD], cs, sn).astype(BF16)

    wspec = pl.BlockSpec((dp, 1, wq.shape[2], cols), lambda t: (0, t, 0, 0))
    col = lambda n: pl.BlockSpec((n, cols), lambda t: (0, t))
    return pl.pallas_call(
        kern,
        grid=(nz,),
        in_specs=[full((r, d)), full((halo, r, d)), full(gains.shape), full((rt, HD)), full((rt, HD))] + [wspec] * 3,
        out_specs=[full((rt, d)), col(r), col(rt), col(rt)],
        out_shape=[
            jax.ShapeDtypeStruct((rt, d), BF16),
            jax.ShapeDtypeStruct((r, d), BF16),
            jax.ShapeDtypeStruct((rt, d), BF16),
            jax.ShapeDtypeStruct((rt, d), BF16),
        ],
        scratch_shapes=[pltpu.VMEM((d, 3 * cols), BF16)],
        compiler_params=pltpu.CompilerParams(vmem_limit_bytes=VL, dimension_semantics=("arbitrary",)),
        name="project",
    )(x, xh, gains, cos, sin, wq, wk, wv)


def allowed_of(seg_q, seg_k, q0, k0):
    n, m = seg_q.shape[0], seg_k.shape[1]
    qp = lax.broadcasted_iota(jnp.int32, (n, m), 0) + q0
    kp = lax.broadcasted_iota(jnp.int32, (n, m), 1) + k0
    return (seg_q == seg_k) & (kp <= qp)


QT = 256
C2 = HD**-0.5 * math.log2(math.e)


def attend(halo, window, q, k, v, mk, mv, seg_q, seg_k):
    r, d = q.shape
    rt = k.shape[0]
    nz, ksel, blk, cols = mk.shape
    per = cols // HD
    nm = ksel * blk

    def kern(q_ref, k_ref, v_ref, mk_ref, mv_ref, sq_ref, sk_ref, o_ref, l_ref):
        km = mk_ref[0].reshape(nm, HD)
        vm = mv_ref[0].reshape(nm, HD)
        for i in range(r // QT):
            at = slice(i * QT, (i + 1) * QT)
            k0 = halo * r - window + i * QT
            ks = slice(k0, k0 + window + QT)
            qq = q_ref[at, :]
            ok = allowed_of(sq_ref[at, :], sk_ref[:, ks], halo * r + i * QT, k0)
            sl = jnp.where(ok, dot_nt(qq, k_ref[ks, :]), MASKED)
            sm = dot_nt(qq, km)
            m = jnp.maximum(jnp.max(sl, axis=1, keepdims=True), jnp.max(sm, axis=1, keepdims=True))
            mc = m * C2
            el = jnp.exp2(sl * C2 - mc)
            em = jnp.exp2(sm * C2 - mc)
            tot = jnp.sum(el, axis=1, keepdims=True) + jnp.sum(em, axis=1, keepdims=True)
            acc = dot_nn(el.astype(BF16), v_ref[ks, :]) + dot_nn(em.astype(BF16), vm)
            o_ref[at, :] = (acc / tot).astype(BF16)
            l_ref[0, at, :] = mc + jnp.log2(tot)

    head = lambda n: pl.BlockSpec((n, HD), lambda h: (0, h))
    mem = pl.BlockSpec((1, ksel, blk, HD), lambda h: (h // per, 0, 0, h % per))
    return pl.pallas_call(
        kern,
        grid=(d // HD,),
        in_specs=[head(r), head(rt), head(rt), mem, mem, full((r, 1)), full((1, rt))],
        out_specs=[head(r), pl.BlockSpec((1, r, 1), lambda h: (h, 0, 0))],
        out_shape=[jax.ShapeDtypeStruct((r, d), BF16), jax.ShapeDtypeStruct((d // HD, r, 1), F32)],
        compiler_params=pltpu.CompilerParams(vmem_limit_bytes=VL, dimension_semantics=("arbitrary",)),
        name="attend",
    )(q, k, v, mk, mv, seg_q, seg_k)


def attend_back(halo, window, q, k, v, mk, mv, seg_q, seg_k, o, lse, do, cos, sin):
    r, d = q.shape
    rt = k.shape[0]
    nz, ksel, blk, cols = mk.shape
    per = cols // HD
    nm = ksel * blk
    scale = HD**-0.5

    def kern(q_ref, k_ref, v_ref, mk_ref, mv_ref, sq_ref, sk_ref, o_ref, l_ref, do_ref, cos_ref, sin_ref,
             dq_ref, dk_ref, dv_ref, sdk, sdv):
        km = mk_ref[0].reshape(nm, HD)
        vm = mv_ref[0].reshape(nm, HD)
        sdk[...] = jnp.zeros_like(sdk)
        sdv[...] = jnp.zeros_like(sdv)
        for i in range(r // QT):
            at = slice(i * QT, (i + 1) * QT)
            k0 = halo * r - window + i * QT
            ks = slice(k0, k0 + window + QT)
            own = slice(halo * r + i * QT, halo * r + (i + 1) * QT)
            qq, dd = q_ref[at, :], do_ref[at, :]
            lse_c = l_ref[0, at, :]
            delta = jnp.sum(dd.astype(F32) * o_ref[at, :].astype(F32), axis=1, keepdims=True)
            ok = allowed_of(sq_ref[at, :], sk_ref[:, ks], halo * r + i * QT, k0)
            pm = jnp.exp2(dot_nt(qq, km) * C2 - lse_c)
            dsm = (pm * (dot_nt(dd, vm) - delta)).astype(BF16)
            plo = jnp.where(ok, jnp.exp2(dot_nt(qq, k_ref[ks, :]) * C2 - lse_c), 0.0)
            dsl = (plo * (dot_nt(dd, v_ref[ks, :]) - delta)).astype(BF16)
            dq = (dot_nn(dsm, km) + dot_nn(dsl, k_ref[ks, :])) * scale
            dq_ref[at, :] = turn(dq, cos_ref[own, :], -sin_ref[own, :]).astype(BF16)
            sdk[ks, :] += dot_tn(dsl, qq)
            sdv[ks, :] += dot_tn(plo.astype(BF16), dd)
        dk_ref[...] = turn(sdk[...] * scale, cos_ref[...], -sin_ref[...]).astype(BF16)
        dv_ref[...] = sdv[...].astype(BF16)

    head = lambda n: pl.BlockSpec((n, HD), lambda h: (0, h))
    mem = pl.BlockSpec((1, ksel, blk, HD), lambda h: (h // per, 0, 0, h % per))
    return pl.pallas_call(
        kern,
        grid=(d // HD,),
        in_specs=[head(r), head(rt), head(rt), mem, mem, full((r, 1)), full((1, rt)), head(r),
                  pl.BlockSpec((1, r, 1), lambda h: (h, 0, 0)), head(r), full((rt, HD)), full((rt, HD))],
        out_specs=[head(r), head(rt), head(rt)],
        out_shape=[jax.ShapeDtypeStruct((n, d), BF16) for n in (r, rt, rt)],
        scratch_shapes=[pltpu.VMEM((rt, HD), F32)] * 2,
        compiler_params=pltpu.CompilerParams(vmem_limit_bytes=VL, dimension_semantics=("arbitrary",)),
        name="attend_back",
    )(q, k, v, mk, mv, seg_q, seg_k, o, lse, do, cos, sin)


def out_norm(x, o, wo, gains):
    r, d = x.shape
    dp, nz, kk, _ = wo.shape

    def kern(x_ref, o_ref, w_ref, gn_ref, h_ref, n_ref):
        t = pl.program_id(0)

        @pl.when(t == 0)
        def _():
            h_ref[...] = x_ref[...].astype(F32)

        w = lanes(w_ref)
        tile = 256

        @pl.loop(0, r // tile)
        def _(i):
            at = pl.ds(pl.multiple_of(i * tile, tile), tile)
            h_ref[at, :] += dot_nn(o_ref[at, :], w)

        @pl.when(t == pl.num_programs(0) - 1)
        def _():
            h = h_ref[...]
            n_ref[...] = (h * inv_rms(h) * gain_row(gn_ref, 1)).astype(BF16)

    return pl.pallas_call(
        kern,
        grid=(nz,),
        in_specs=[full((r, d)), pl.BlockSpec((r, kk), lambda t: (0, t)),
                  pl.BlockSpec((dp, 1, kk, wo.shape[3]), lambda t: (0, t, 0, 0)), full(gains.shape)],
        out_specs=[full((r, d)), full((r, d))],
        out_shape=[jax.ShapeDtypeStruct((r, d), F32), jax.ShapeDtypeStruct((r, d), BF16)],
        compiler_params=pltpu.CompilerParams(vmem_limit_bytes=VL, dimension_semantics=("arbitrary",)),
        name="out_norm",
    )(x, o, wo, gains)


def feed(h, n2, c, gains, wg, wu, wd, wo):
    r, d = h.shape
    dp, nz, ff, _ = wg.shape
    kk = wo.shape[2]

    def kern(h_ref, n_ref, c_ref, gn_ref, wg_ref, wu_ref, wd_ref, wo_ref,
             hid_ref, dg_ref, du_ref, out_ref, dh_ref, dhb_ref, do_ref, gg_ref, sg, su, sd, acc):
        t = pl.program_id(0)
        last = pl.num_programs(0) - 1
        sg[...] = lanes(wg_ref)
        su[...] = lanes(wu_ref)
        sd[...] = lanes(wd_ref)

        @pl.when(t == 0)
        def _():
            out_ref[...] = h_ref[...]
            acc[...] = jnp.zeros_like(acc)

        tile = 128

        @pl.loop(0, r // tile)
        def _(i):
            at = pl.ds(pl.multiple_of(i * tile, tile), tile)
            n = n_ref[at, :]
            gate = dot_nt(n, sg[...])
            up = dot_nt(n, su[...])
            dhid = dot_nt(c_ref[at, :], sd[...])
            sig = 1.0 / (1.0 + jnp.exp(-gate))
            act = gate * sig
            hid = (act * up).astype(BF16)
            hid_ref[0, at, :] = hid
            dg = (dhid * up * (sig * (1.0 + gate * (1.0 - sig)))).astype(BF16)
            du = (dhid * act).astype(BF16)
            dg_ref[0, at, :] = dg
            du_ref[0, at, :] = du
            out_ref[at, :] += dot_nn(hid, sd[...])
            acc[at, :] += dot_nn(dg, sg[...]) + dot_nn(du, su[...])

        @pl.when(t == last)
        def _():
            g = gain_row(gn_ref, 1)
            h = h_ref[...]
            dn = acc[...]
            iv = inv_rms(h)
            gg_ref[...] = jnp.sum(dn * h * iv, axis=0, keepdims=True)
            gd = dn * g
            dh = c_ref[...].astype(F32) + iv * gd - h * (iv * iv * iv * jnp.mean(h * gd, axis=1, keepdims=True))
            dh_ref[...] = dh
            dhb_ref[...] = dh.astype(BF16)

            @pl.loop(0, nz)
            def _(u):
                w = jnp.concatenate([wo_ref[e, u] for e in range(dp)], axis=1)
                do_ref[u] = dot_nt(dhb_ref[...], w).astype(BF16)

    wspec = pl.BlockSpec((dp, 1, ff, wg.shape[3]), lambda t: (0, t, 0, 0))
    piece = pl.BlockSpec((1, r, ff), lambda t: (t, 0, 0))
    one = lambda s: full(s, 1)
    return pl.pallas_call(
        kern,
        grid=(nz,),
        in_specs=[one((r, d)), one((r, d)), one((r, d)), one(gains.shape), wspec, wspec, wspec, one(wo.shape)],
        out_specs=[piece, piece, piece, full((r, d)), full((r, d)), full((r, d)), full((nz, r, kk)), full((1, d))],
        out_shape=[jax.ShapeDtypeStruct((nz, r, ff), BF16)] * 3
        + [jax.ShapeDtypeStruct((r, d), F32), jax.ShapeDtypeStruct((r, d), F32), jax.ShapeDtypeStruct((r, d), BF16),
           jax.ShapeDtypeStruct((nz, r, kk), BF16), jax.ShapeDtypeStruct((1, d), F32)],
        scratch_shapes=[pltpu.VMEM((ff, d), BF16)] * 3 + [pltpu.VMEM((r, d), F32)],
        compiler_params=pltpu.CompilerParams(vmem_limit_bytes=VL, dimension_semantics=("arbitrary",)),
        name="feed",
    )(h, n2, c, gains, wg, wu, wd, wo)


def project_back(halo, x, xh, dq, dk, dv, wq, wk, wv):
    r, d = x.shape
    dp, nz, _, cols = wq.shape
    rt = (halo + 1) * r

    def kern(x_ref, xh_ref, dq_ref, dk_ref, dv_ref, wq_ref, wk_ref, wv_ref, own_ref, hb_ref, gg_ref, acc, w_s):
        t = pl.program_id(0)
        w_s[:, 0:cols] = rows(wk_ref)
        w_s[:, cols : 2 * cols] = rows(wv_ref)
        w_s[:, 2 * cols :] = rows(wq_ref)

        @pl.when(t == 0)
        def _():
            acc[...] = jnp.zeros_like(acc)

        tile = 256

        @pl.loop(0, rt // tile)
        def _(i):
            at = pl.ds(pl.multiple_of(i * tile, tile), tile)
            acc[at, :] += dot_nt(jnp.concatenate([dk_ref[at, :], dv_ref[at, :]], axis=1), w_s[:, 0 : 2 * cols])

        @pl.loop(0, r // tile)
        def _(i):
            at = pl.ds(pl.multiple_of(i * tile, tile), tile)
            to = pl.ds(pl.multiple_of(i * tile + halo * r, tile), tile)
            acc[to, :] += dot_nt(dq_ref[at, :], w_s[:, 2 * cols :])

        @pl.when(t == pl.num_programs(0) - 1)
        def _():
            me = lax.axis_index("tensor")
            own_ref[...] = acc[halo * r :, :]
            hb_ref[...] = acc[: halo * r, :].astype(BF16)
            v = x_ref[...].astype(F32)
            g = jnp.sum(acc[halo * r :, :] * v * inv_rms(v), axis=0, keepdims=True)
            for j in range(halo):
                v = xh_ref[j].astype(F32)
                lo = (halo - 1 - j) * r
                more = jnp.sum(acc[lo : lo + r, :] * v * inv_rms(v), axis=0, keepdims=True)
                g = g + jnp.where(me >= j + 1, more, jnp.zeros_like(more))
            gg_ref[...] = g

    wspec = pl.BlockSpec((dp, 1, wq.shape[2], cols), lambda t: (0, t, 0, 0))
    col = lambda n: pl.BlockSpec((n, cols), lambda t: (0, t))
    return pl.pallas_call(
        kern,
        grid=(nz,),
        in_specs=[full((r, d)), full((halo, r, d)), col(r), col(rt), col(rt)] + [wspec] * 3,
        out_specs=[full((r, d)), full((halo * r, d)), full((1, d))],
        out_shape=[jax.ShapeDtypeStruct((r, d), F32), jax.ShapeDtypeStruct((halo * r, d), BF16),
                   jax.ShapeDtypeStruct((1, d), F32)],
        scratch_shapes=[pltpu.VMEM((rt, d), F32), pltpu.VMEM((d, 3 * cols), BF16)],
        compiler_params=pltpu.CompilerParams(vmem_limit_bytes=VL, dimension_semantics=("arbitrary",)),
        name="project_back",
    )(x, xh, dq, dk, dv, wq, wk, wv)


def feed_grads(hid, dg, du, n2, c):
    nz, r, ff = hid[0].shape
    half = n2[0].shape[1]
    nb = half // 128

    def kern(h0, h1, g0, g1, u0, u1, n0, n1, c0, c1, gg, gu, gd):
        def put(out, a0, a1, b0, b1):
            y = (dot_tn(a0[0], b0[...]) + dot_tn(a1[0], b1[...])).astype(BF16)
            for e in range(nb):
                out[e, 0] = y[:, e * 128 : (e + 1) * 128]

        put(gg, g0, g1, n0, n1)
        put(gu, u0, u1, n0, n1)
        put(gd, h0, h1, c0, c1)

    piece = pl.BlockSpec((1, r, ff), lambda t: (t, 0, 0))
    out = pl.BlockSpec((nb, 1, ff, 128), lambda t: (0, t, 0, 0))
    return pl.pallas_call(
        kern,
        grid=(nz,),
        in_specs=[piece] * 6 + [full((r, half))] * 4,
        out_specs=[out] * 3,
        out_shape=[jax.ShapeDtypeStruct((nb, nz, ff, 128), BF16)] * 3,
        compiler_params=pltpu.CompilerParams(vmem_limit_bytes=VL, dimension_semantics=("arbitrary",)),
        name="feed_grads",
    )(*hid, *dg, *du, *n2, *c)


def attn_grads(halo, nz, o, dhb, n1, dq, dk, dv):
    r, d = o[0].shape
    half = dhb[0].shape[1]
    rt = (halo + 1) * r
    nb, cols = half // 128, d // nz

    def kern(o0, o1, b0, b1, n0, m1, q0, q1, k0, k1, v0, v1, go, gq, gk, gv):
        y = (dot_tn(o0[...], b0[...]) + dot_tn(o1[...], b1[...])).astype(BF16)
        for e in range(nb):
            go[e, 0] = y[:, e * 128 : (e + 1) * 128]
        own = pl.ds(halo * r, r)
        for out, p0, p1, a0, a1 in (
            (gq, q0, q1, n0.at[own], m1.at[own]),
            (gk, k0, k1, n0, m1),
            (gv, v0, v1, n0, m1),
        ):
            y = (dot_tn(a0[...], p0[...]) + dot_tn(a1[...], p1[...])).astype(BF16)
            for e in range(nb):
                out[e, 0] = y[e * 128 : (e + 1) * 128, :]

    col = lambda n: pl.BlockSpec((n, cols), lambda t: (0, t))
    out1 = pl.BlockSpec((nb, 1, cols, 128), lambda t: (0, t, 0, 0))
    out2 = pl.BlockSpec((nb, 1, 128, cols), lambda t: (0, t, 0, 0))
    return pl.pallas_call(
        kern,
        grid=(nz,),
        in_specs=[col(r)] * 2 + [full((r, half))] * 2 + [full((rt, half))] * 2 + [col(r)] * 2 + [col(rt)] * 4,
        out_specs=[out1, out2, out2, out2],
        out_shape=[jax.ShapeDtypeStruct((nb, nz, cols, 128), BF16)]
        + [jax.ShapeDtypeStruct((nb, nz, 128, cols), BF16)] * 3,
        compiler_params=pltpu.CompilerParams(vmem_limit_bytes=VL, dimension_semantics=("arbitrary",)),
        name="attn_grads",
    )(*o, *dhb, *n1, *dq, *dk, *dv)


def input_grad(halo, x, gains, dn1, more, dh):
    r, d = x.shape
    tile = 256

    def kern(x_ref, gn_ref, dn_ref, m_ref, dh_ref, out_ref):
        t = lax.axis_index("tensor")
        nz = lax.axis_size("tensor")
        dn = dn_ref[...]
        for j in range(halo):
            v = m_ref[j].astype(F32)
            dn = dn + jnp.where(t + j + 1 < nz, v, jnp.zeros_like(v))
        v = x_ref[...].astype(F32)
        iv = inv_rms(v)
        gd = dn * gain_row(gn_ref, 0)
        out_ref[...] = dh_ref[...] + iv * gd - v * (iv * iv * iv * jnp.mean(v * gd, axis=1, keepdims=True))

    row = pl.BlockSpec((tile, d), lambda i: (i, 0))
    return pl.pallas_call(
        kern,
        grid=(r // tile,),
        in_specs=[row, full(gains.shape), row, pl.BlockSpec((halo, tile, d), lambda i: (0, i, 0)), row],
        out_specs=row,
        out_shape=jax.ShapeDtypeStruct((r, d), F32),
        compiler_params=pltpu.CompilerParams(vmem_limit_bytes=VL, dimension_semantics=("arbitrary",)),
        name="input_grad",
    )(x, gains, dn1, more, dh)


def fwd_kernel(g, cap, nq, ksel, halo, window, units, n_w, *refs):
    refs = list(refs)
    take = lambda n: [refs.pop(0) for _ in range(n)]
    requests, sel, seg_q, seg_k = take(4)
    x, gains, mem_k, mem_v, cos, sin = take(6)
    shards = take(n_w)
    bufs = take(n_w)
    xh, gains_all, mk, mv = take(4)
    n1_o, q_o, k_o, v_o, o_o, l_o, h_o, n2_o = take(8)
    loc, stage_k, stage_v, rec_k, rec_v = take(5)
    req_in, req_s = take(2)
    x_v, xh_v, n_v, n2_v, h_v, cos_v, sin_v, gn_v, wqkv = take(9)
    ss, rs, msl, mss, mrs, zss, zrs, xss, xrs, qss, qrs, gss, grs, cs = take(14)
    a, b, c, t, me = coords(g)
    r, d = x_v.shape
    greet(g, me, t)
    rq, gn = [], []
    for k in range(1, g.dp):
        to = (me + k) % g.dp
        m = send(requests.at[to], req_in.at[me], qss.at[k], qrs.at[k], to, t)
        m.start()
        rq.append(m)
    for k in range(1, g.dp):
        to = (me + k) % g.dp
        m = send(gains, gains_all.at[me], gss.at[k], grs.at[k], to, t)
        m.start()
        gn.append(m)
    own_r = pltpu.make_async_copy(requests.at[me], req_in.at[me], qss.at[0])
    own_r.start()
    own_g = pltpu.make_async_copy(gains, gains_all.at[me], gss.at[0])
    own_g.start()
    load_k = pltpu.make_async_copy(mem_k, loc, msl.at[0])
    load_v = pltpu.make_async_copy(mem_v, loc, msl.at[1])
    load_k.start()
    per = gather_sems(g)
    gs = [Gather(g, shards[w], bufs[w], rows_, bf, (ss, rs), i * per) for i, (w, rows_, bf) in enumerate(units)]
    proj, out_, gate_up, down = gs[:4], gs[4:6], gs[6:8], gs[8:]
    for u in proj + out_:
        u.start_z()
    xs = []
    for k in range(1, halo + 1):
        m = send(x, xh.at[k - 1], xss.at[k - 1], xrs.at[k - 1], me, (t + k) % g.nz)
        xs.append(m)

        @pl.when(t + k < g.nz)
        def _():
            m.start()

    lx = [
        pltpu.make_async_copy(x, x_v, cs.at[0]),
        pltpu.make_async_copy(cos, cos_v, cs.at[1]),
        pltpu.make_async_copy(sin, sin_v, cs.at[2]),
    ]
    for m in lx:
        m.start()
    own_r.wait()
    own_g.wait()
    for m in rq:
        m.wait()
    cp = pltpu.make_async_copy(req_in, req_s, qrs.at[0])
    cp.start()
    cp.wait()

    def exchange(stage, rec, i, load):
        load.wait()

        @pl.loop(0, g.dp)
        def _(s):
            for k in range(cap):
                stage[s, k] = loc[req_s[s, 0, k]]

        out = []
        for k in range(1, g.dp):
            to = (me + k) % g.dp
            m = send(stage.at[to], rec.at[me], mss.at[i, k], mrs.at[i, k], to, t)
            m.start()
            out.append(m)
        own = pltpu.make_async_copy(stage.at[me], rec.at[me], mss.at[i, 0])
        own.start()
        return out + [own]

    ek = exchange(stage_k, rec_k, 0, load_k)
    load_v.start()
    for u in proj + out_:
        u.start_first()
    for u in gate_up + down:
        u.start_z()
    ev = exchange(stage_v, rec_v, 1, load_v)
    for u in proj + out_:
        u.start_second()

    def spread(moves, rec, zst, out, i):
        for m in moves:
            m.wait()

        @pl.loop(0, nq)
        def _(q):
            for j in range(ksel):
                zst[q, j] = rec[sel[q * ksel + j] // cap, sel[q * ksel + j] % cap]

        res = []
        for k in range(1, g.nz):
            to = (t + k) % g.nz
            m = send(zst.at[to], out.at[t], zss.at[i, k], zrs.at[i, k], me, to)
            m.start()
            res.append(m)
        own = pltpu.make_async_copy(zst.at[t], out.at[t], zss.at[i, 0])
        own.start()
        return res + [own]

    zk = spread(ek, rec_k, stage_k, mk, 0)
    for u in gate_up + down:
        u.start_first()
    for m in gn:
        m.wait()
    cg = pltpu.make_async_copy(gains_all, gn_v, cs.at[3])
    cg.start()
    cg.wait()
    for m in lx:
        m.wait()
    gain1, gain2 = gain_row(gn_v, 0), gain_row(gn_v, 1)
    v = x_v[...].astype(F32)
    n_v[halo * r :, :] = (v * inv_rms(v) * gain1).astype(BF16)
    for k, m in enumerate(xs):

        @pl.when(t >= k + 1)
        def _():
            m.wait_recv()

        lo = (halo - 1 - k) * r

        @pl.when(t >= k + 1)
        def _():
            ch = pltpu.make_async_copy(xh.at[k], xh_v, cs.at[4])
            ch.start()
            ch.wait()
            v = xh_v[...].astype(F32)
            n_v[lo : lo + r, :] = (v * inv_rms(v) * gain1).astype(BF16)

        @pl.when(t < k + 1)
        def _():
            n_v[lo : lo + r, :] = jnp.zeros((r, d), BF16)

    cn = pltpu.make_async_copy(n_v, n1_o, cs.at[5])
    cn.start()
    for u in proj + out_:
        u.start_core()
    zv = spread(ev, rec_v, stage_v, mv, 1)
    for u in proj:
        u.finish()

    dp, nz, kd, cols = bufs[0].shape
    rt = (halo + 1) * r
    tile = 512
    wq, wk, wv, wo = bufs[:4]

    def project(wq_ref, wk_ref, wv_ref, q_ref, k_ref, v_ref):
        for e in range(dp):
            wqkv[e * kd : (e + 1) * kd, 0:cols] = wq_ref[e, 0]
            wqkv[e * kd : (e + 1) * kd, cols : 2 * cols] = wk_ref[e, 0]
            wqkv[e * kd : (e + 1) * kd, 2 * cols :] = wv_ref[e, 0]

        def turned(y, cs_, sn_):
            return jnp.concatenate(
                [turn(y[:, h * HD : (h + 1) * HD], cs_, sn_).astype(BF16) for h in range(cols // HD)], axis=1
            )

        @pl.loop(0, rt // tile)
        def _(i):
            at = pl.ds(pl.multiple_of(i * tile, tile), tile)
            n = n_v[at, :]
            cs_, sn_ = cos_v[at, :], sin_v[at, :]
            k_ref[at, :] = turned(dot_nn(n, wqkv[:, cols : 2 * cols]), cs_, sn_)
            v_ref[at, :] = dot_nn(n, wqkv[:, 2 * cols :]).astype(BF16)

            @pl.when(i >= halo * r // tile)
            def _():
                to = pl.ds(pl.multiple_of(i * tile - halo * r, tile), tile)
                q_ref[to, :] = turned(dot_nn(n, wqkv[:, 0:cols]), cs_, sn_)

    wspec = pl.BlockSpec((dp, 1, kd, cols), lambda u: (0, u, 0, 0))
    col = lambda n: pl.BlockSpec((n, cols), lambda u: (0, u))
    pltpu.emit_pipeline(project, grid=(nz,), in_specs=[wspec] * 3, out_specs=[col(r), col(rt), col(rt)])(
        wq, wk, wv, q_o, k_o, v_o
    )
    for u in gate_up:
        u.start_second()
    for m in zk + zv:
        m.wait()

    blk = mk.shape[2]
    nm, per_t = ksel * blk, cols // HD

    def attend(q_ref, k_ref, v_ref, mk_ref, mv_ref, o_ref, l_ref):
        km = mk_ref[0].reshape(nm, HD)
        vm = mv_ref[0].reshape(nm, HD)
        for i in range(r // QT):
            at = slice(i * QT, (i + 1) * QT)
            k0 = halo * r - window + i * QT
            ks = slice(k0, k0 + window + QT)
            qq = q_ref[at, :]
            ok = allowed_of(seg_q[at, :], seg_k[:, ks], halo * r + i * QT, k0)
            sl = jnp.where(ok, dot_nt(qq, k_ref[ks, :]), MASKED)
            sm = dot_nt(qq, km)
            mx = jnp.maximum(jnp.max(sl, axis=1, keepdims=True), jnp.max(sm, axis=1, keepdims=True))
            mc = mx * C2
            el = jnp.exp2(sl * C2 - mc)
            em = jnp.exp2(sm * C2 - mc)
            tot = jnp.sum(el, axis=1, keepdims=True) + jnp.sum(em, axis=1, keepdims=True)
            acc = dot_nn(el.astype(BF16), v_ref[ks, :]) + dot_nn(em.astype(BF16), vm)
            o_ref[at, :] = (acc / tot).astype(BF16)
            l_ref[0, at, :] = mc + jnp.log2(tot)

    head = lambda n: pl.BlockSpec((n, HD), lambda h: (0, h))
    mem = pl.BlockSpec((1, ksel, blk, HD), lambda h: (h // per_t, 0, 0, h % per_t))
    pltpu.emit_pipeline(
        attend,
        grid=(d // HD,),
        in_specs=[head(r), head(rt), head(rt), mem, mem],
        out_specs=[head(r), pl.BlockSpec((1, r, 1), lambda h: (h, 0, 0))],
    )(q_o, k_o, v_o, mk, mv, o_o, l_o)
    for u in down:
        u.start_second()
    for u in gate_up:
        u.start_core()
    for u in out_:
        u.finish()

    h_v[...] = x_v[...].astype(F32)
    kk = wo.shape[2]

    def out_proj(o_ref, w_ref):
        h_v[...] += dot_nn(o_ref[...], jnp.concatenate([w_ref[e, 0] for e in range(dp)], axis=1))

    pltpu.emit_pipeline(
        out_proj,
        grid=(nz,),
        in_specs=[pl.BlockSpec((r, kk), lambda u: (0, u)), pl.BlockSpec((dp, 1, kk, wo.shape[3]), lambda u: (0, u, 0, 0))],
    )(o_o, wo)
    h = h_v[...]
    n2_v[...] = (h * inv_rms(h) * gain2).astype(BF16)
    ch = pltpu.make_async_copy(h_v, h_o, cs.at[6])
    ch.start()
    c2 = pltpu.make_async_copy(n2_v, n2_o, cs.at[7])
    c2.start()
    for u in down:
        u.start_core()
    for u in gate_up + down:
        u.finish()
    for m in (cn, ch, c2):
        m.wait()
    for k, m in enumerate(xs):

        @pl.when(t + k + 1 < g.nz)
        def _():
            m.wait_send()


def fwd(g, cap, halo, window, requests, sel, seg_q, seg_k, x, gains, mem_k, mem_v, cos, sin, shards, nq, ksel):
    blk = mem_k.shape[1:]
    r, d = x.shape
    rt = (halo + 1) * r
    units = []
    for w, s in enumerate(shards):
        n = s.shape[0]
        if w in (0, 4):
            units.append((w, (0, n), True))
        elif w in (1, 5):
            units.append((w, (0, n), False))
        else:
            units.append((w, (0, n // 2), True))
            units.append((w, (n // 2, n - n // 2), False))
    n_w = len(shards)
    any_ = pl.BlockSpec(memory_space=pl.ANY)
    vm = pl.BlockSpec(memory_space=pltpu.VMEM)
    nsem = len(units) * gather_sems(g)
    dma = lambda *n: pltpu.SemaphoreType.DMA(n)
    st = lambda s, dt=BF16: jax.ShapeDtypeStruct(s, dt)
    out_shape = (
        [st((g.dp, g.nz) + s.shape) for s in shards]
        + [st((halo,) + x.shape), st((g.dp,) + gains.shape, F32)]
        + [st((g.nz, ksel) + blk)] * 2
        + [st((rt, d)), st((r, d)), st((rt, d)), st((rt, d)), st((r, d)), st((d // HD, r, 1), F32), st((r, d), F32), st((r, d))]
    )
    scratch = (
        [pltpu.VMEM(mem_k.shape, BF16)]
        + [pltpu.VMEM((g.dp, cap) + blk, BF16)] * 4
        + [pltpu.VMEM((g.dp, 8, 128), jnp.int32), pltpu.SMEM((g.dp, 8, 128), jnp.int32)]
        + [pltpu.VMEM((r, d), BF16), pltpu.VMEM((r, d), BF16), pltpu.VMEM((rt, d), BF16), pltpu.VMEM((r, d), BF16)]
        + [pltpu.VMEM((r, d), F32), pltpu.VMEM((rt, HD), F32), pltpu.VMEM((rt, HD), F32)]
        + [pltpu.VMEM((g.dp,) + gains.shape, F32), pltpu.VMEM((d, 3 * shards[0].shape[1]), BF16)]
        + [dma(nsem), dma(nsem), dma(2), dma(2, g.dp), dma(2, g.dp), dma(2, g.nz), dma(2, g.nz)]
        + [dma(halo), dma(halo), dma(g.dp), dma(g.dp), dma(g.dp), dma(g.dp), dma(8)]
    )
    return pl.pallas_call(
        functools.partial(fwd_kernel, g, cap, nq, ksel, halo, window, units, n_w),
        out_shape=out_shape,
        in_specs=[vm, pl.BlockSpec(memory_space=pltpu.SMEM), vm, vm] + [any_] * (6 + n_w),
        out_specs=[any_] * len(out_shape),
        scratch_shapes=scratch,
        compiler_params=pltpu.CompilerParams(collective_id=0, has_side_effects=True, vmem_limit_bytes=63 * 2**20),
        name="forward",
    )(requests, sel, seg_q, seg_k, x, gains, mem_k, mem_v, cos, sin, *shards)


class Scatter:
    def __init__(self, g, src, rows, b_first, bufs, sems, out):
        self.g, self.src, self.rows, self.b_first, self.out = g, src, rows, b_first, out
        self.acc, self.r1, self.r2, self.r3 = bufs
        self.sems, self.next = sems, 0
        self.sent = []

    def _sem(self):
        i = self.next
        self.next += 1
        return self.sems[0].at[i], self.sems[1].at[i]

    def _e(self, f, s):
        return s * self.g.nb + f if self.b_first else f * self.g.nb + s

    def _dp(self, f, s, c):
        return self._e(f, s) * 2 + c

    def _mine(self):
        a, b, c, t, me = coords(self.g)
        f, s = (b, a) if self.b_first else (a, b)
        n1, n2 = (self.g.nb, self.g.na) if self.b_first else (self.g.na, self.g.nb)
        return f, s, c, t, me, n1, n2

    def start_first(self):
        f, s, c, t, me, n1, n2 = self._mine()
        lo, n = self.rows
        self.own, self.first = [], []
        for k in range(1, n1):
            to = (f + k) % n1
            for j in range(n2):
                x, y = self._sem()
                d = send(self.src.at[self._e(to, j), :, pl.ds(lo, n), :], self.r1.at[k - 1, j], x, y, self._dp(to, s, c), t)
                d.start()
                self.first.append(d)
        for j in range(n2):
            x, _ = self._sem()
            d = pltpu.make_async_copy(self.src.at[self._e(f, j), :, pl.ds(lo, n), :], self.acc.at[j], x)
            d.start()
            self.own.append(d)
        self.sent += self.first

    def start_second(self):
        f, s, c, t, me, n1, n2 = self._mine()
        for d in self.own:
            d.wait()
        for d in self.first:
            d.wait_recv()
        for j in range(n2):

            @pl.loop(0, self.g.nz)
            def _(u):
                v = self.acc[j, u].astype(F32)
                for k in range(n1 - 1):
                    v = v + self.r1[k, j, u].astype(F32)
                self.acc[j, u] = v.astype(BF16)

        self.second = []
        for k in range(1, n2):
            to = (s + k) % n2
            x, y = self._sem()
            d = send(self.acc.at[to], self.r2.at[k - 1], x, y, self._dp(f, to, c), t)
            d.start()
            self.second.append(d)
        self.sent += self.second

    def start_z(self):
        f, s, c, t, me, n1, n2 = self._mine()
        for d in self.second:
            d.wait_recv()

        @pl.loop(0, self.g.nz)
        def _(u):
            v = self.acc[s, u].astype(F32)
            for k in range(n2 - 1):
                v = v + self.r2[k, u].astype(F32)
            self.acc[s, u] = v.astype(BF16)

        self.third = []
        for k in range(1, self.g.nz):
            to = (t + k) % self.g.nz
            x, y = self._sem()
            d = send(self.acc.at[s, to], self.r3.at[k - 1], x, y, me, to)
            d.start()
            self.third.append(d)
        self.sent += self.third

    def finish(self):
        f, s, c, t, me, n1, n2 = self._mine()
        lo, n = self.rows
        for d in self.third:
            d.wait_recv()
        v = self.acc[s, t].astype(F32)
        for k in range(self.g.nz - 1):
            v = v + self.r3[k].astype(F32)
        self.out[pl.ds(lo, n), :] = v
        for d in self.sent:
            d.wait_send()


def scatter_sems(g):
    return (g.na - 1) * g.na + g.na + (g.na - 1) + (g.nz - 1)


def k2_kernel(g, halo, units, n_w, *refs):
    refs = list(refs)
    take = lambda n: [refs.pop(0) for _ in range(n)]
    gains, hb = take(2)
    srcs = take(n_w)
    gout, more = take(2)
    outs = take(n_w)
    bufs = [take(4) for _ in units]
    sems = [take(2) for _ in units]
    gz, gs, gd = take(3)
    zss, zrs, dss, drs, hss, hrs = take(6)
    a, b, c, t, me = coords(g)
    greet(g, me, t)
    us = [
        Scatter(g, srcs[w], rows, bf, bufs[i], sems[i], outs[w]) for i, (w, rows, bf) in enumerate(units)
    ]
    pairs = [us[i : i + 2] for i in range(0, len(us), 2)]
    np_ = len(pairs)
    r = more.shape[1]
    hd = []
    for j in range(halo):
        d = send(hb.at[pl.ds((halo - 1 - j) * r, r), :], more.at[j], hss.at[j], hrs.at[j], me, (t + g.nz - 1 - j) % g.nz)
        hd.append(d)

        @pl.when(t >= j + 1)
        def _():
            d.start()

    zg = []
    for k in range(1, g.nz):
        d = send(gains, gz.at[k - 1], zss.at[k - 1], zrs.at[k - 1], me, (t + k) % g.nz)
        d.start()
        zg.append(d)
    for p in range(min(2, np_)):
        for u in pairs[p]:
            u.start_first()
    for d in zg:
        d.wait()
    tot = gains[...]
    for k in range(g.nz - 1):
        tot = tot + gz[k]
    for e in range(g.dp):
        gs[e] = tot[:, e * 128 : (e + 1) * 128]
    dg = []
    for k in range(1, g.dp):
        to = (me + k) % g.dp
        d = send(gs.at[to], gd.at[me], dss.at[k], drs.at[k], to, t)
        d.start()
        dg.append(d)
    own = pltpu.make_async_copy(gs.at[me], gd.at[me], dss.at[0])
    own.start()
    for p in range(np_):
        for u in pairs[p]:
            u.start_second()
        if p + 2 < np_:
            for u in pairs[p + 2]:
                u.start_first()
        if p >= 1:
            for u in pairs[p - 1]:
                u.start_z()
    for u in pairs[-1]:
        u.start_z()
    own.wait()
    for d in dg:
        d.wait()
    v = gd[0]
    for e in range(1, g.dp):
        v = v + gd[e]
    gout[...] = v
    for u in us:
        u.finish()
    for j, d in enumerate(hd):

        @pl.when(t >= j + 1)
        def _():
            d.wait_send()

        @pl.when(t + j + 1 < g.nz)
        def _():
            d.wait_recv()


def halves(srcs_rows):
    units = []
    for item in srcs_rows:
        if len(item) == 2:
            (w0, n0), (w1, n1) = item
            units += [(w0, (0, n0), True), (w1, (0, n1), False)]
        else:
            ((w, n),) = item
            units += [(w, (0, n // 2), True), (w, (n // 2, n - n // 2), False)]
    return units


def k2(g, halo, gains, hb, srcs, units, r):
    any_ = pl.BlockSpec(memory_space=pl.ANY)
    vm = pl.BlockSpec(memory_space=pltpu.VMEM)
    dma = lambda *n: pltpu.SemaphoreType.DMA(n)
    d = hb.shape[1]
    n_w = len(srcs)
    scratch = []
    for w, (lo, n), bf in units:
        cols = srcs[w].shape[3]
        n1, n2 = (g.nb, g.na) if bf else (g.na, g.nb)
        scratch += [
            pltpu.VMEM((n2, g.nz, n, cols), BF16),
            pltpu.VMEM((n1 - 1, n2, g.nz, n, cols), BF16),
            pltpu.VMEM((n2 - 1, g.nz, n, cols), BF16),
            pltpu.VMEM((g.nz - 1, n, cols), BF16),
        ]
    scratch += [dma(scatter_sems(g))] * (2 * len(units))
    scratch += [pltpu.VMEM((g.nz - 1,) + gains.shape, F32), pltpu.VMEM((g.dp, 2, 128), F32), pltpu.VMEM((g.dp, 2, 128), F32)]
    scratch += [dma(g.nz), dma(g.nz), dma(g.dp), dma(g.dp), dma(halo), dma(halo)]
    out_shape = [jax.ShapeDtypeStruct((2, 128), F32), jax.ShapeDtypeStruct((halo, r, d), BF16)] + [
        jax.ShapeDtypeStruct(s.shape[2:], F32) for s in srcs
    ]
    return pl.pallas_call(
        functools.partial(k2_kernel, g, halo, units, n_w),
        out_shape=out_shape,
        in_specs=[vm, any_] + [any_] * n_w,
        out_specs=[vm, any_] + [vm] * n_w,
        scratch_shapes=scratch,
        compiler_params=pltpu.CompilerParams(collective_id=1, has_side_effects=True, vmem_limit_bytes=60 * 2**20),
        name="bwd_exchange",
    )(gains, hb, *srcs)


HEADS = 8
QB = 512


def normalize(field, gain_vec):
    return field * lax.rsqrt(jnp.mean(field * field, axis=-1, keepdims=True) + EPSILON) * gain_vec


def rotate(field, heads_here):
    row_total = field.shape[0]
    head_size = field.shape[1] // heads_here
    half_width = head_size // 2
    frequencies = 10000.0 ** (-jnp.arange(half_width, dtype=jnp.float32) * 2.0 / head_size)
    angles = jnp.arange(row_total, dtype=jnp.float32)[:, None] * frequencies[None, :]
    cosine = jnp.cos(angles)[:, None, :]
    sine_table = jnp.sin(angles)[:, None, :]
    split_heads = field.reshape(row_total, heads_here, head_size)
    first_half = split_heads[..., :half_width]
    second_half = split_heads[..., half_width:]
    turned = jnp.concatenate(
        [
            first_half * cosine - second_half * sine_table,
            second_half * cosine + first_half * sine_table,
        ],
        axis=-1,
    )
    return turned.reshape(row_total, heads_here * head_size)


def contract_rows(left, right):
    return lax.dot_general(
        left, right, (((0,), (0,)), ((), ())), preferred_element_type=jnp.float32
    )


def against(left, right):
    return lax.dot_general(
        left, right, (((1,), (1,)), ((), ())), preferred_element_type=jnp.float32
    )


def spread_rows(local_rows, matrices):
    piece_rows = lax.all_gather(local_rows, "tensor", axis=0, tiled=True)
    return jnp.concatenate(
        [jnp.dot(piece_rows, matrix, preferred_element_type=jnp.float32) for matrix in matrices],
        axis=1,
    )


def reduce_rows(left, right):
    return lax.psum_scatter(
        jnp.dot(left, right, preferred_element_type=jnp.float32).astype(jnp.bfloat16),
        "tensor",
        scatter_dimension=0,
        tiled=True,
    ).astype(jnp.float32)


def return_rows(pairs):
    summed = against(pairs[0][0], pairs[0][1])
    for grad_block, matrix in pairs[1:]:
        summed = summed + against(grad_block, matrix)
    return lax.psum_scatter(
        summed.astype(jnp.bfloat16), "tensor", scatter_dimension=0, tiled=True
    ).astype(jnp.float32)


def weight_grads(local_rows, grads_list):
    piece_rows = lax.all_gather(local_rows, "tensor", axis=0, tiled=True)
    return tuple((contract_rows(piece_rows, grad_one) for grad_one in grads_list))


def all_rows(local_grad):
    return lax.all_gather(local_grad, "tensor", axis=0, tiled=True)


def on_device_any(
    block_in,
    segments,
    retrieved,
    partner,
    memory_keys,
    memory_values,
    gain_attn,
    w_query,
    w_key,
    w_value,
    w_out,
    gain_ffn,
    w_gate,
    w_up,
    w_down,
    cotangent,
):
    tensor_size = lax.axis_size("tensor")
    dp_size = lax.axis_size("dp")
    heads_here = HEADS // tensor_size
    head_width = heads_here * HD
    score_scale = HD ** (-0.5)
    seq_len = segments.shape[1]
    query_blocks = seq_len // QB
    stream_in = block_in[0].astype(jnp.float32)
    seg_row = segments[0]
    positions = jnp.arange(seq_len)
    gathered = (
        lax.all_gather(gain_attn, "dp", axis=0, tiled=True),
        lax.all_gather(w_query, "dp", axis=0, tiled=True),
        lax.all_gather(w_key, "dp", axis=0, tiled=True),
        lax.all_gather(w_value, "dp", axis=0, tiled=True),
        lax.all_gather(w_out, "dp", axis=1, tiled=True),
        lax.all_gather(gain_ffn, "dp", axis=0, tiled=True),
        lax.all_gather(w_gate, "dp", axis=0, tiled=True),
        lax.all_gather(w_up, "dp", axis=0, tiled=True),
        lax.all_gather(w_down, "dp", axis=1, tiled=True),
    )
    gain_one, query_w, key_w, value_w, out_w, gain_two, gate_w, up_w, down_w = gathered
    wanted = retrieved[0].reshape(-1)
    request_total = wanted.shape[0]
    capacity = max(2, (2 * request_total + dp_size - 1) // dp_size)
    blocks_dev = memory_keys.shape[1]
    from_partner = wanted // MEMB
    block_index = wanted % MEMB
    owner_dev = block_index // blocks_dev
    local_block = block_index % blocks_dev
    seq_id = jnp.where(from_partner == 0, lax.axis_index("dp"), partner[0])
    owner_hits = (owner_dev[:, None] == jnp.arange(dp_size)[None, :]).astype(jnp.int32)
    slot_index = jnp.sum((jnp.cumsum(owner_hits, axis=0) - 1) * owner_hits, axis=1)
    requests = (
        jnp.zeros((dp_size, capacity, 2), jnp.int32)
        .at[owner_dev, slot_index]
        .set(jnp.stack([seq_id, local_block], axis=-1))
    )
    received = lax.all_to_all(requests, "dp", split_axis=0, concat_axis=0, tiled=True)
    picked_keys = memory_keys[received[..., 0], received[..., 1]]
    picked_values = memory_values[received[..., 0], received[..., 1]]
    fetched_keys = lax.all_to_all(picked_keys, "dp", split_axis=0, concat_axis=0, tiled=True)
    fetched_values = lax.all_to_all(picked_values, "dp", split_axis=0, concat_axis=0, tiled=True)
    memory_k = fetched_keys[owner_dev, slot_index].reshape(query_blocks, -1, heads_here, HD)
    memory_v = fetched_values[owner_dev, slot_index].reshape(query_blocks, -1, heads_here, HD)
    normed = normalize(stream_in, gain_one.astype(jnp.float32)).astype(jnp.bfloat16)
    qkv_rows = spread_rows(normed, [query_w, key_w, value_w])
    query_raw = qkv_rows[:, :head_width]
    key_raw = qkv_rows[:, head_width : 2 * head_width]
    queries = rotate(query_raw, heads_here).astype(jnp.bfloat16)
    keys_all = rotate(key_raw, heads_here).astype(jnp.bfloat16).reshape(seq_len, heads_here, HD)
    values_all = qkv_rows[:, 2 * head_width :].astype(jnp.bfloat16).reshape(seq_len, heads_here, HD)
    query_tiles = queries.reshape(query_blocks, QB, heads_here, HD)
    seg_tiles = seg_row.reshape(query_blocks, QB)
    pos_tiles = positions.reshape(query_blocks, QB)

    def scores_of(query_blk, seg_blk, pos_blk, key_mem):
        local_scores = jnp.einsum(
            "qhd,khd->hqk", query_blk, keys_all, preferred_element_type=jnp.float32
        )
        memory_scores = jnp.einsum(
            "qhd,khd->hqk", query_blk, key_mem, preferred_element_type=jnp.float32
        )
        raw_scores = jnp.concatenate([local_scores, memory_scores], axis=-1) * score_scale
        allowed = (seg_blk[:, None] == seg_row[None, :]) & (positions[None, :] <= pos_blk[:, None])
        allowed = jnp.concatenate(
            [allowed, jnp.ones((query_blk.shape[0], key_mem.shape[0]), dtype=jnp.bool_)], axis=1
        )
        return (raw_scores, allowed)

    def forward_block(pieces):
        query_blk, seg_blk, pos_blk, key_mem, value_mem = pieces
        raw_scores, allowed = scores_of(query_blk, seg_blk, pos_blk, key_mem)
        masked = jnp.where(allowed[None], raw_scores, MASKED)
        row_max = jnp.max(masked, axis=-1, keepdims=True)
        expo = jnp.exp(masked - row_max)
        row_total = jnp.sum(expo, axis=-1, keepdims=True)
        weights_soft = (expo / row_total).astype(jnp.bfloat16)
        values_both = jnp.concatenate([values_all, value_mem], axis=0)
        result = jnp.einsum(
            "hqk,khd->qhd", weights_soft, values_both, preferred_element_type=jnp.float32
        )
        return (result, (row_max + jnp.log(row_total))[..., 0])

    attended, log_totals = lax.map(
        forward_block, (query_tiles, seg_tiles, pos_tiles, memory_k, memory_v)
    )
    mixed = attended.reshape(seq_len, head_width).astype(jnp.bfloat16)
    stream = stream_in + reduce_rows(mixed, out_w)
    normed_ffn = normalize(stream, gain_two.astype(jnp.float32)).astype(jnp.bfloat16)
    gate_up = spread_rows(normed_ffn, [gate_w, up_w])
    hidden_width = gate_w.shape[1]
    gate_pre = gate_up[:, :hidden_width]
    up_pre = gate_up[:, hidden_width:]
    hidden = (jax.nn.silu(gate_pre) * up_pre).astype(jnp.bfloat16)
    block_out = stream + reduce_rows(hidden, down_w)
    gathered_back = (
        lax.all_gather(gain_attn, "dp", axis=0, tiled=True),
        lax.all_gather(w_query, "dp", axis=0, tiled=True),
        lax.all_gather(w_key, "dp", axis=0, tiled=True),
        lax.all_gather(w_value, "dp", axis=0, tiled=True),
        lax.all_gather(w_out, "dp", axis=1, tiled=True),
        lax.all_gather(gain_ffn, "dp", axis=0, tiled=True),
        lax.all_gather(w_gate, "dp", axis=0, tiled=True),
        lax.all_gather(w_up, "dp", axis=0, tiled=True),
        lax.all_gather(w_down, "dp", axis=1, tiled=True),
    )
    gain_one, query_w, key_w, value_w, out_w, gain_two, gate_w, up_w, down_w = gathered_back
    dout_rows = cotangent[0]

    def gated(gate_in, up_in):
        return jax.nn.silu(gate_in) * up_in

    dout_full = all_rows(dout_rows)
    grad_down = contract_rows(hidden, dout_full)
    d_hidden = against(dout_full, down_w)
    gated_value, pull_gated = jax.vjp(gated, gate_pre, up_pre)
    d_gate, d_up = pull_gated(d_hidden)
    d_gate = d_gate.astype(jnp.bfloat16)
    d_up = d_up.astype(jnp.bfloat16)
    d_norm_ffn = return_rows([(d_gate, gate_w), (d_up, up_w)])
    grad_gate, grad_up = weight_grads(normed_ffn, [d_gate, d_up])
    norm_value, pull_norm_ffn = jax.vjp(normalize, stream, gain_two.astype(jnp.float32))
    d_stream_norm, grad_gain_ffn = pull_norm_ffn(d_norm_ffn)
    d_stream = dout_rows.astype(jnp.float32) + d_stream_norm
    d_stream_full = all_rows(d_stream.astype(jnp.bfloat16))
    grad_out = contract_rows(mixed, d_stream_full)
    d_mixed = against(d_stream_full, out_w).astype(jnp.bfloat16)
    d_mixed_tiles = d_mixed.reshape(query_blocks, QB, heads_here, HD)

    def backward_block(carry_sums, pieces):
        key_sum, value_sum = carry_sums
        query_blk, seg_blk, pos_blk, key_mem, value_mem, log_blk, grad_blk = pieces
        raw_scores, allowed = scores_of(query_blk, seg_blk, pos_blk, key_mem)
        probs = jnp.where(allowed[None], jnp.exp(raw_scores - log_blk[..., None]), 0.0)
        values_both = jnp.concatenate([values_all, value_mem], axis=0)
        d_probs = jnp.einsum(
            "qhd,khd->hqk", grad_blk, values_both, preferred_element_type=jnp.float32
        )
        shared = jnp.sum(probs * d_probs, axis=-1, keepdims=True)
        d_scores = (probs * (d_probs - shared)).astype(jnp.bfloat16)
        probs_low = probs.astype(jnp.bfloat16)
        keys_both = jnp.concatenate([keys_all, key_mem], axis=0)
        d_query = (
            jnp.einsum("hqk,khd->qhd", d_scores, keys_both, preferred_element_type=jnp.float32)
            * score_scale
        )
        key_sum = (
            key_sum
            + jnp.einsum(
                "hqk,qhd->khd",
                d_scores[..., :seq_len],
                query_blk,
                preferred_element_type=jnp.float32,
            )
            * score_scale
        )
        value_sum = value_sum + jnp.einsum(
            "hqk,qhd->khd", probs_low[..., :seq_len], grad_blk, preferred_element_type=jnp.float32
        )
        return ((key_sum, value_sum), d_query)

    zero_grads = jnp.zeros((seq_len, heads_here, HD), jnp.float32)
    (d_keys, d_values), d_queries = lax.scan(
        backward_block,
        (zero_grads, zero_grads),
        (query_tiles, seg_tiles, pos_tiles, memory_k, memory_v, log_totals, d_mixed_tiles),
    )

    def turn(field):
        return rotate(field, heads_here)

    turned_value, pull_turn = jax.vjp(turn, query_raw)
    d_query_raw = pull_turn(d_queries.reshape(seq_len, head_width))[0].astype(jnp.bfloat16)
    d_key_raw = pull_turn(d_keys.reshape(seq_len, head_width))[0].astype(jnp.bfloat16)
    d_value_raw = d_values.reshape(seq_len, head_width).astype(jnp.bfloat16)
    d_norm_attn = return_rows([(d_query_raw, query_w), (d_key_raw, key_w), (d_value_raw, value_w)])
    grad_query, grad_key, grad_value = weight_grads(normed, [d_query_raw, d_key_raw, d_value_raw])
    norm_first, pull_norm_attn = jax.vjp(normalize, stream_in, gain_one.astype(jnp.float32))
    d_input_norm, grad_gain_attn = pull_norm_attn(d_norm_attn)
    grad_in = d_stream + d_input_norm
    grad_gain_attn, grad_gain_ffn = lax.psum((grad_gain_attn, grad_gain_ffn), "tensor")
    results = (
        lax.psum_scatter(
            grad_gain_attn.astype(jnp.bfloat16), "dp", scatter_dimension=0, tiled=True
        ).astype(jnp.float32),
        lax.psum_scatter(
            grad_query.astype(jnp.bfloat16), "dp", scatter_dimension=0, tiled=True
        ).astype(jnp.float32),
        lax.psum_scatter(
            grad_key.astype(jnp.bfloat16), "dp", scatter_dimension=0, tiled=True
        ).astype(jnp.float32),
        lax.psum_scatter(
            grad_value.astype(jnp.bfloat16), "dp", scatter_dimension=0, tiled=True
        ).astype(jnp.float32),
        lax.psum_scatter(
            grad_out.astype(jnp.bfloat16), "dp", scatter_dimension=1, tiled=True
        ).astype(jnp.float32),
        lax.psum_scatter(
            grad_gain_ffn.astype(jnp.bfloat16), "dp", scatter_dimension=0, tiled=True
        ).astype(jnp.float32),
        lax.psum_scatter(
            grad_gate.astype(jnp.bfloat16), "dp", scatter_dimension=0, tiled=True
        ).astype(jnp.float32),
        lax.psum_scatter(
            grad_up.astype(jnp.bfloat16), "dp", scatter_dimension=0, tiled=True
        ).astype(jnp.float32),
        lax.psum_scatter(
            grad_down.astype(jnp.bfloat16), "dp", scatter_dimension=1, tiled=True
        ).astype(jnp.float32),
    )
    return (block_out[None], grad_in[None]) + results


def cover(halo, r, t):
    half = HD // 2
    freq = 10000.0 ** (-jnp.arange(half, dtype=F32) * 2.0 / HD)
    pos = (t * r - halo * r + jnp.arange((halo + 1) * r)).astype(F32)
    ang = pos[:, None] * freq[None, :]
    cos, sin = jnp.cos(ang), jnp.sin(ang)
    return jnp.concatenate([cos, cos], axis=1), jnp.concatenate([-sin, sin], axis=1)


def on_device(*args):
    x, dp = args[0], lax.axis_size("dp")
    side = math.isqrt(dp // 2)
    if 2 * side * side == dp and x.shape[2] % (128 * dp) == 0:
        return on_device_rows(*args)
    return on_device_any(*args)


def on_device_rows(
    block_in, segments, retrieved, partner, memory_keys, memory_values,
    gain_attn, w_query, w_key, w_value, w_out, gain_ffn, w_gate, w_up, w_down, cotangent,
):
    g = Grid(lax.axis_size("dp"), lax.axis_size("tensor"))
    t, me = lax.axis_index("tensor"), lax.axis_index("dp")
    x, c = block_in[0], cotangent[0]
    r, d = x.shape
    seq_len = segments.shape[1]
    window = seq_len // 4
    halo = -(-window // r)
    nq, ksel = retrieved.shape[1:]
    cap = max(2, -(-2 * nq * ksel // g.dp))
    req, sel = plan_requests(retrieved[0], partner[0], g.dp, memory_keys.shape[1], cap)
    gains = jnp.stack([gain_attn, gain_ffn]).astype(F32)
    flat = lambda m: m.reshape((-1,) + m.shape[2:])
    shards = [w_query, w_key, w_value, w_out, w_gate.T, w_up.T, w_down]
    cos, sin = cover(halo, r, t)
    padded = jnp.concatenate([jnp.full((halo * r,), -1, jnp.int32), segments[0]])
    seg = lax.dynamic_slice(padded, (t * r,), ((halo + 1) * r,))
    seg_k, seg_q = seg[None, :], seg[halo * r :, None]
    (wq, wk, wv, wo, wg, wu, wd, xh, gn, mk, mv, n1, q, k, v, o, lse, h, n2) = fwd(
        g, cap, halo, window, req, sel, seg_q, seg_k, x, gains, flat(memory_keys), flat(memory_values), cos, sin,
        shards, nq, ksel,
    )
    hid, dg, du, block_out, dh, dhb, do, gg_ffn = feed(h, n2, c, gn, wg, wu, wd, wo)
    do = jnp.transpose(do, (1, 0, 2)).reshape(r, d)
    dq, dk, dv = attend_back(halo, window, q, k, v, mk, mv, seg_q, seg_k, o, lse, do, cos, sin)
    dn1, hb, gg_attn = project_back(halo, x, xh, dq, dk, dv, wq, wk, wv)

    core = me % 2
    pairs = [(i, i ^ 1) for i in range(g.dp)]
    other = lambda y: lax.ppermute(y, "dp", pairs)

    def cut(y):
        z = y.reshape(y.shape[0], d // 256, 2, 128)
        mine = lax.dynamic_index_in_dim(z, core, 2, False).reshape(y.shape[0], d // 2)
        theirs = lax.dynamic_index_in_dim(z, 1 - core, 2, False).reshape(y.shape[0], d // 2)
        return mine, other(theirs)

    both = lambda y: (y, other(y))
    ggt, gut, gdn = feed_grads(both(hid), both(dg), both(du), cut(n2), cut(c))
    go, gq, gk, gv = attn_grads(halo, g.nz, both(o), cut(dhb), cut(n1), both(dq), both(dk), both(dv))
    srcs = [ggt, gut, gdn, go, gq, gk, gv]
    n = lambda w: (w, srcs[w].shape[2])
    units = halves([(n(0), n(1)), (n(2),), (n(3),), (n(4), n(5)), (n(6),)])
    gains_part = jnp.concatenate([gg_attn, gg_ffn], axis=0)
    gout, more, o_gate, o_up, o_down, o_out, o_q, o_k, o_v = k2(g, halo, gains_part, hb, srcs, units, r)
    grad_in = input_grad(halo, x, gn, dn1, more, dh)
    return (
        block_out[None], grad_in[None], gout[0], o_q, o_k, o_v, o_out, gout[1], o_gate.T, o_up.T, o_down,
    )


def solution(mesh):
    return jax.shard_map(
        on_device,
        mesh=mesh,
        in_specs=(
            P("dp", "tensor", None), P("dp", None), P("dp", None, None), P("dp"),
            P(None, "dp", None, "tensor"), P(None, "dp", None, "tensor"),
            P("dp"), P("dp", "tensor"), P("dp", "tensor"), P("dp", "tensor"), P("tensor", "dp"),
            P("dp"), P("dp", "tensor"), P("dp", "tensor"), P("tensor", "dp"), P("dp", "tensor", None),
        ),
        out_specs=(
            P("dp", "tensor", None), P("dp", "tensor", None),
            P("dp"), P("dp", "tensor"), P("dp", "tensor"), P("dp", "tensor"), P("tensor", "dp"),
            P("dp"), P("dp", "tensor"), P("dp", "tensor"), P("tensor", "dp"),
        ),
        check_vma=False,
    )
```

```python
import functools
import math

import jax
import jax.numpy as jnp
from jax import lax
from jax.experimental import pallas as pl
from jax.experimental.pallas import tpu as pltpu
from jax.sharding import PartitionSpec as P
MESH = pl.DeviceIdType.MESH
MEMB = 128


class Grid:
    def __init__(self, dp, tensor):
        side = math.isqrt(dp // 2)
        assert side * side * 2 == dp
        self.na, self.nb, self.nc, self.nz, self.dp = side, side, 2, tensor, dp


def coords(g):
    me = lax.axis_index("dp")
    t = lax.axis_index("tensor")
    return me // (2 * g.nb), (me // 2) % g.nb, me % 2, t, me


def send(src, dst, ssem, rsem, dp, t):
    return pltpu.make_async_remote_copy(
        src_ref=src, dst_ref=dst, send_sem=ssem, recv_sem=rsem, device_id=(dp, t), device_id_type=MESH
    )


def greet(g, me, t):
    bar = pltpu.get_barrier_semaphore()
    for k in range(1, g.dp):
        pl.semaphore_signal(bar, inc=1, device_id=((me + k) % g.dp, t), device_id_type=MESH)
    for k in range(1, g.nz):
        pl.semaphore_signal(bar, inc=1, device_id=(me, (t + k) % g.nz), device_id_type=MESH)
    pl.semaphore_wait(bar, g.dp - 1 + g.nz - 1)


class Gather:
    def __init__(self, g, shard, buf, rows, b_first, sems, base):
        self.g, self.shard, self.buf, self.rows, self.b_first = g, shard, buf, rows, b_first
        self.sems, self.next = sems, base
        self.sent = []

    def _sem(self):
        i = self.next
        self.next += 1
        return self.sems[0].at[i], self.sems[1].at[i]

    def at(self, dp, t=None):
        lo, n = self.rows
        if t is None:
            return self.buf.at[dp, :, pl.ds(lo, n), :]
        return self.buf.at[dp, t, pl.ds(lo, n), :]

    def start_z(self):
        g = self.g
        a, b, c, t, me = coords(g)
        lo, n = self.rows
        src = self.shard.at[pl.ds(lo, n), :]
        self.z = []
        for k in range(1, g.nz):
            s, r = self._sem()
            d = send(src, self.at(me, t), s, r, me, (t + k) % g.nz)
            d.start()
            self.z.append(d)
        s, _ = self._sem()
        self.own = pltpu.make_async_copy(src, self.at(me, t), s)
        self.own.start()
        self.sent += self.z

    def _dp(self, a, b, c):
        return (a * self.g.nb + b) * 2 + c

    def _core(self, dp, c):
        s, r = self._sem()
        d = send(self.at(dp), self.at(dp), s, r, coords(self.g)[4] + 1 - 2 * c, coords(self.g)[3])
        d.start()
        self.core.append(d)
        self.sent.append(d)

    def start_first(self):
        g = self.g
        a, b, c, t, me = coords(g)
        self.own.wait()
        for d in self.z:
            d.wait_recv()
        self.first, self.core = [], []
        n1 = g.nb if self.b_first else g.na
        for k in range(1, n1):
            to = self._dp(a, (b + k) % n1, c) if self.b_first else self._dp((a + k) % n1, b, c)
            s, r = self._sem()
            d = send(self.at(me), self.at(me), s, r, to, t)
            d.start()
            self.first.append(d)
        self.sent += self.first
        self._core(me, c)

    def start_second(self):
        g = self.g
        a, b, c, t, me = coords(g)
        n1, n2 = (g.nb, g.na) if self.b_first else (g.na, g.nb)
        for d in self.first:
            d.wait_recv()
        held = [self._dp(a, (b - k) % n1, c) if self.b_first else self._dp((a - k) % n1, b, c) for k in range(n1)]
        self.second = []
        for slot in held:
            for k in range(1, n2):
                to = self._dp((a + k) % n2, b, c) if self.b_first else self._dp(a, (b + k) % n2, c)
                s, r = self._sem()
                d = send(self.at(slot), self.at(slot), s, r, to, t)
                d.start()
                self.second.append(d)
        for slot in held[1:]:
            self._core(slot, c)
        self.sent += self.second

    def start_core(self):
        g = self.g
        a, b, c, t, me = coords(g)
        n1, n2 = (g.nb, g.na) if self.b_first else (g.na, g.nb)
        for d in self.second:
            d.wait_recv()
        for k1 in range(n1):
            for k in range(1, n2):
                slot = (
                    self._dp((a - k) % n2, (b - k1) % n1, c)
                    if self.b_first
                    else self._dp((a - k1) % n1, (b - k) % n2, c)
                )
                self._core(slot, c)

    def finish(self):
        for d in self.core:
            d.wait_recv()
        for d in self.sent:
            d.wait_send()


def gather_sems(g):
    return g.nz + (g.na - 1) + g.na * (g.na - 1) + g.na * g.nb


def plan_requests(retrieved, partner, dp_size, blocks_dev, cap):
    wanted = retrieved.reshape(-1)
    n = wanted.shape[0]
    from_partner = wanted // MEMB
    block_index = wanted % MEMB
    owner = block_index // blocks_dev
    local = block_index % blocks_dev
    seq = jnp.where(from_partner == 0, lax.axis_index("dp"), partner)
    flat = seq * blocks_dev + local
    i = jnp.arange(n)
    slot = jnp.sum(((owner[:, None] == owner[None, :]) & (i[None, :] < i[:, None])).astype(jnp.int32), axis=1)
    hit = (owner[None, None, :] == jnp.arange(dp_size)[:, None, None]) & (
        slot[None, None, :] == jnp.arange(128)[None, :, None]
    )
    req = jnp.sum(jnp.where(hit, flat[None, None, :], 0), axis=2)
    return jnp.broadcast_to(req[:, None, :], (dp_size, 8, 128)).astype(jnp.int32), (owner * cap + slot).astype(jnp.int32)


HD = 128
EPSILON = 1e-05
MASKED = -1e30
F32, BF16 = jnp.float32, jnp.bfloat16


def dot_nn(x, y):
    return lax.dot_general(x, y, (((1,), (0,)), ((), ())), preferred_element_type=F32)


def dot_nt(x, y):
    return lax.dot_general(x, y, (((1,), (1,)), ((), ())), preferred_element_type=F32)


def dot_tn(x, y):
    return lax.dot_general(x, y, (((0,), (0,)), ((), ())), preferred_element_type=F32)


def inv_rms(v):
    return lax.rsqrt(jnp.mean(v * v, axis=-1, keepdims=True) + EPSILON)


def gain_row(gains_ref, which):
    n = gains_ref.shape[0]
    return jnp.concatenate([gains_ref[d, which : which + 1, :] for d in range(n)], axis=1)


def turn(v, cos, sin):
    return v * cos + pltpu.roll(v, HD // 2, axis=1) * sin


def lanes(ref):
    return jnp.concatenate([ref[d, 0] for d in range(ref.shape[0])], axis=1)


def rows(ref):
    return jnp.concatenate([ref[d, 0] for d in range(ref.shape[0])], axis=0)


VL = 60 * 2**20


def full(shape, buffers=None):
    n = len(shape)
    kw = {} if buffers is None else dict(pipeline_mode=pl.Buffered(buffers))
    return pl.BlockSpec(shape, lambda *i: (0,) * n, **kw)


def allowed_of(seg_q, seg_k, q0, k0):
    n, m = seg_q.shape[0], seg_k.shape[1]
    qp = lax.broadcasted_iota(jnp.int32, (n, m), 0) + q0
    kp = lax.broadcasted_iota(jnp.int32, (n, m), 1) + k0
    return (seg_q == seg_k) & (kp <= qp)


QT = 256
C2 = HD**-0.5 * math.log2(math.e)


def fwd_kernel(g, cap, nq, ksel, halo, window, units, n_w, *refs):
    refs = list(refs)
    take = lambda n: [refs.pop(0) for _ in range(n)]
    requests, sel, seg_q, seg_k = take(4)
    x, gains, mem_k, mem_v, cos, sin = take(6)
    shards = take(n_w)
    bufs = take(n_w)
    xh, gains_all, mk, mv = take(4)
    n1_o, q_o, k_o, v_o, o_o, l_o, h_o, n2_o = take(8)
    loc, stage_k, stage_v, rec_k, rec_v = take(5)
    req_in, req_s = take(2)
    x_v, xh_v, n_v, n2_v, h_v, cos_v, sin_v, gn_v, wqkv = take(9)
    ss, rs, msl, mss, mrs, zss, zrs, xss, xrs, qss, qrs, gss, grs, cs = take(14)
    a, b, c, t, me = coords(g)
    r, d = x_v.shape
    greet(g, me, t)
    rq, gn = [], []
    for k in range(1, g.dp):
        to = (me + k) % g.dp
        m = send(requests.at[to], req_in.at[me], qss.at[k], qrs.at[k], to, t)
        m.start()
        rq.append(m)
    for k in range(1, g.dp):
        to = (me + k) % g.dp
        m = send(gains, gains_all.at[me], gss.at[k], grs.at[k], to, t)
        m.start()
        gn.append(m)
    own_r = pltpu.make_async_copy(requests.at[me], req_in.at[me], qss.at[0])
    own_r.start()
    own_g = pltpu.make_async_copy(gains, gains_all.at[me], gss.at[0])
    own_g.start()
    load_k = pltpu.make_async_copy(mem_k, loc, msl.at[0])
    load_v = pltpu.make_async_copy(mem_v, loc, msl.at[1])
    load_k.start()
    per = gather_sems(g)
    gs = [Gather(g, shards[w], bufs[w], rows_, bf, (ss, rs), i * per) for i, (w, rows_, bf) in enumerate(units)]
    proj, out_, gate_up, down = gs[:4], gs[4:6], gs[6:8], gs[8:]
    for u in proj + out_:
        u.start_z()
    xs = []
    for k in range(1, halo + 1):
        m = send(x, xh.at[k - 1], xss.at[k - 1], xrs.at[k - 1], me, (t + k) % g.nz)
        xs.append(m)

        @pl.when(t + k < g.nz)
        def _():
            m.start()

    lx = [
        pltpu.make_async_copy(x, x_v, cs.at[0]),
        pltpu.make_async_copy(cos, cos_v, cs.at[1]),
        pltpu.make_async_copy(sin, sin_v, cs.at[2]),
    ]
    for m in lx:
        m.start()
    own_r.wait()
    own_g.wait()
    for m in rq:
        m.wait()
    cp = pltpu.make_async_copy(req_in, req_s, qrs.at[0])
    cp.start()
    cp.wait()

    def exchange(stage, rec, i, load):
        load.wait()

        @pl.loop(0, g.dp)
        def _(s):
            for k in range(cap):
                stage[s, k] = loc[req_s[s, 0, k]]

        out = []
        for k in range(1, g.dp):
            to = (me + k) % g.dp
            m = send(stage.at[to], rec.at[me], mss.at[i, k], mrs.at[i, k], to, t)
            m.start()
            out.append(m)
        own = pltpu.make_async_copy(stage.at[me], rec.at[me], mss.at[i, 0])
        own.start()
        return out + [own]

    ek = exchange(stage_k, rec_k, 0, load_k)
    load_v.start()
    for u in proj + out_:
        u.start_first()
    for u in gate_up + down:
        u.start_z()
    ev = exchange(stage_v, rec_v, 1, load_v)
    for u in proj + out_:
        u.start_second()

    def spread(moves, rec, zst, out, i):
        for m in moves:
            m.wait()

        @pl.loop(0, nq)
        def _(q):
            for j in range(ksel):
                zst[q, j] = rec[sel[q * ksel + j] // cap, sel[q * ksel + j] % cap]

        res = []
        for k in range(1, g.nz):
            to = (t + k) % g.nz
            m = send(zst.at[to], out.at[t], zss.at[i, k], zrs.at[i, k], me, to)
            m.start()
            res.append(m)
        own = pltpu.make_async_copy(zst.at[t], out.at[t], zss.at[i, 0])
        own.start()
        return res + [own]

    zk = spread(ek, rec_k, stage_k, mk, 0)
    for u in gate_up + down:
        u.start_first()
    for m in gn:
        m.wait()
    cg = pltpu.make_async_copy(gains_all, gn_v, cs.at[3])
    cg.start()
    cg.wait()
    for m in lx:
        m.wait()
    gain1, gain2 = gain_row(gn_v, 0), gain_row(gn_v, 1)
    v = x_v[...].astype(F32)
    n_v[halo * r :, :] = (v * inv_rms(v) * gain1).astype(BF16)
    for k, m in enumerate(xs):

        @pl.when(t >= k + 1)
        def _():
            m.wait_recv()

        lo = (halo - 1 - k) * r

        @pl.when(t >= k + 1)
        def _():
            ch = pltpu.make_async_copy(xh.at[k], xh_v, cs.at[4])
            ch.start()
            ch.wait()
            v = xh_v[...].astype(F32)
            n_v[lo : lo + r, :] = (v * inv_rms(v) * gain1).astype(BF16)

        @pl.when(t < k + 1)
        def _():
            n_v[lo : lo + r, :] = jnp.zeros((r, d), BF16)

    cn = pltpu.make_async_copy(n_v, n1_o, cs.at[5])
    cn.start()
    for u in proj + out_:
        u.start_core()
    zv = spread(ev, rec_v, stage_v, mv, 1)
    for u in proj:
        u.finish()

    dp, nz, kd, cols = bufs[0].shape
    rt = (halo + 1) * r
    tile = 512
    wq, wk, wv, wo = bufs[:4]

    def project(wq_ref, wk_ref, wv_ref, q_ref, k_ref, v_ref):
        for e in range(dp):
            wqkv[e * kd : (e + 1) * kd, 0:cols] = wq_ref[e, 0]
            wqkv[e * kd : (e + 1) * kd, cols : 2 * cols] = wk_ref[e, 0]
            wqkv[e * kd : (e + 1) * kd, 2 * cols :] = wv_ref[e, 0]

        def turned(y, cs_, sn_):
            return jnp.concatenate(
                [turn(y[:, h * HD : (h + 1) * HD], cs_, sn_).astype(BF16) for h in range(cols // HD)], axis=1
            )

        @pl.loop(0, rt // tile)
        def _(i):
            at = pl.ds(pl.multiple_of(i * tile, tile), tile)
            n = n_v[at, :]
            cs_, sn_ = cos_v[at, :], sin_v[at, :]
            k_ref[at, :] = turned(dot_nn(n, wqkv[:, cols : 2 * cols]), cs_, sn_)
            v_ref[at, :] = dot_nn(n, wqkv[:, 2 * cols :]).astype(BF16)

            @pl.when(i >= halo * r // tile)
            def _():
                to = pl.ds(pl.multiple_of(i * tile - halo * r, tile), tile)
                q_ref[to, :] = turned(dot_nn(n, wqkv[:, 0:cols]), cs_, sn_)

    wspec = pl.BlockSpec((dp, 1, kd, cols), lambda u: (0, u, 0, 0))
    col = lambda n: pl.BlockSpec((n, cols), lambda u: (0, u))
    pltpu.emit_pipeline(project, grid=(nz,), in_specs=[wspec] * 3, out_specs=[col(r), col(rt), col(rt)])(
        wq, wk, wv, q_o, k_o, v_o
    )
    for u in gate_up:
        u.start_second()
    for m in zk + zv:
        m.wait()

    blk = mk.shape[2]
    nm, per_t = ksel * blk, cols // HD

    def attend(q_ref, k_ref, v_ref, mk_ref, mv_ref, o_ref, l_ref):
        km = mk_ref[0].reshape(nm, HD)
        vm = mv_ref[0].reshape(nm, HD)
        for i in range(r // QT):
            at = slice(i * QT, (i + 1) * QT)
            k0 = halo * r - window + i * QT
            ks = slice(k0, k0 + window + QT)
            qq = q_ref[at, :]
            ok = allowed_of(seg_q[at, :], seg_k[:, ks], halo * r + i * QT, k0)
            sl = jnp.where(ok, dot_nt(qq, k_ref[ks, :]), MASKED)
            sm = dot_nt(qq, km)
            mx = jnp.maximum(jnp.max(sl, axis=1, keepdims=True), jnp.max(sm, axis=1, keepdims=True))
            mc = mx * C2
            el = jnp.exp2(sl * C2 - mc)
            em = jnp.exp2(sm * C2 - mc)
            tot = jnp.sum(el, axis=1, keepdims=True) + jnp.sum(em, axis=1, keepdims=True)
            acc = dot_nn(el.astype(BF16), v_ref[ks, :]) + dot_nn(em.astype(BF16), vm)
            o_ref[at, :] = (acc / tot).astype(BF16)
            l_ref[0, at, :] = mc + jnp.log2(tot)

    head = lambda n: pl.BlockSpec((n, HD), lambda h: (0, h))
    mem = pl.BlockSpec((1, ksel, blk, HD), lambda h: (h // per_t, 0, 0, h % per_t))
    pltpu.emit_pipeline(
        attend,
        grid=(d // HD,),
        in_specs=[head(r), head(rt), head(rt), mem, mem],
        out_specs=[head(r), pl.BlockSpec((1, r, 1), lambda h: (h, 0, 0))],
    )(q_o, k_o, v_o, mk, mv, o_o, l_o)
    for u in down:
        u.start_second()
    for u in gate_up:
        u.start_core()
    for u in out_:
        u.finish()

    h_v[...] = x_v[...].astype(F32)
    kk = wo.shape[2]

    def out_proj(o_ref, w_ref):
        h_v[...] += dot_nn(o_ref[...], jnp.concatenate([w_ref[e, 0] for e in range(dp)], axis=1))

    pltpu.emit_pipeline(
        out_proj,
        grid=(nz,),
        in_specs=[pl.BlockSpec((r, kk), lambda u: (0, u)), pl.BlockSpec((dp, 1, kk, wo.shape[3]), lambda u: (0, u, 0, 0))],
    )(o_o, wo)
    h = h_v[...]
    n2_v[...] = (h * inv_rms(h) * gain2).astype(BF16)
    ch = pltpu.make_async_copy(h_v, h_o, cs.at[6])
    ch.start()
    c2 = pltpu.make_async_copy(n2_v, n2_o, cs.at[7])
    c2.start()
    for u in down:
        u.start_core()
    for u in gate_up + down:
        u.finish()
    for m in (cn, ch, c2):
        m.wait()
    for k, m in enumerate(xs):

        @pl.when(t + k + 1 < g.nz)
        def _():
            m.wait_send()


def fwd(g, cap, halo, window, requests, sel, seg_q, seg_k, x, gains, mem_k, mem_v, cos, sin, shards, nq, ksel):
    blk = mem_k.shape[1:]
    r, d = x.shape
    rt = (halo + 1) * r
    units = []
    for w, s in enumerate(shards):
        n = s.shape[0]
        if w in (0, 4):
            units.append((w, (0, n), True))
        elif w in (1, 5):
            units.append((w, (0, n), False))
        else:
            units.append((w, (0, n // 2), True))
            units.append((w, (n // 2, n - n // 2), False))
    n_w = len(shards)
    any_ = pl.BlockSpec(memory_space=pl.ANY)
    vm = pl.BlockSpec(memory_space=pltpu.VMEM)
    nsem = len(units) * gather_sems(g)
    dma = lambda *n: pltpu.SemaphoreType.DMA(n)
    st = lambda s, dt=BF16: jax.ShapeDtypeStruct(s, dt)
    out_shape = (
        [st((g.dp, g.nz) + s.shape) for s in shards]
        + [st((halo,) + x.shape), st((g.dp,) + gains.shape, F32)]
        + [st((g.nz, ksel) + blk)] * 2
        + [st((rt, d)), st((r, d)), st((rt, d)), st((rt, d)), st((r, d)), st((d // HD, r, 1), F32), st((r, d), F32), st((r, d))]
    )
    scratch = (
        [pltpu.VMEM(mem_k.shape, BF16)]
        + [pltpu.VMEM((g.dp, cap) + blk, BF16)] * 4
        + [pltpu.VMEM((g.dp, 8, 128), jnp.int32), pltpu.SMEM((g.dp, 8, 128), jnp.int32)]
        + [pltpu.VMEM((r, d), BF16), pltpu.VMEM((r, d), BF16), pltpu.VMEM((rt, d), BF16), pltpu.VMEM((r, d), BF16)]
        + [pltpu.VMEM((r, d), F32), pltpu.VMEM((rt, HD), F32), pltpu.VMEM((rt, HD), F32)]
        + [pltpu.VMEM((g.dp,) + gains.shape, F32), pltpu.VMEM((d, 3 * shards[0].shape[1]), BF16)]
        + [dma(nsem), dma(nsem), dma(2), dma(2, g.dp), dma(2, g.dp), dma(2, g.nz), dma(2, g.nz)]
        + [dma(halo), dma(halo), dma(g.dp), dma(g.dp), dma(g.dp), dma(g.dp), dma(8)]
    )
    return pl.pallas_call(
        functools.partial(fwd_kernel, g, cap, nq, ksel, halo, window, units, n_w),
        out_shape=out_shape,
        in_specs=[vm, pl.BlockSpec(memory_space=pltpu.SMEM), vm, vm] + [any_] * (6 + n_w),
        out_specs=[any_] * len(out_shape),
        scratch_shapes=scratch,
        compiler_params=pltpu.CompilerParams(collective_id=0, has_side_effects=True, vmem_limit_bytes=63 * 2**20),
        name="forward",
    )(requests, sel, seg_q, seg_k, x, gains, mem_k, mem_v, cos, sin, *shards)


def feed(g, h, n2, c, gains, wg, wu, wd, wo):
    r, d = h.shape
    dp, nz, ff, _ = wg.shape
    kk = wo.shape[2]
    half = d // 2

    def kern(h_ref, n_ref, c_ref, gn_ref, wg_ref, wu_ref, wd_ref, wo_ref,
             hid_ref, dg_ref, du_ref, out_ref, dh_ref, dhb_ref, do_ref, gg_ref, phid, pdg, pdu, pn, pc,
             sg, su, sd, acc, ss, rs, hs, hr):
        t = pl.program_id(0)
        last = pl.num_programs(0) - 1
        _, _, core, tz, me = coords(g)
        peer = me + 1 - 2 * core

        def half_copies():
            res = []
            for i, (src, dst) in enumerate(((n_ref, pn), (c_ref, pc))):
                for e in range(dp // 2):
                    col = pl.multiple_of((2 * e + 1 - core) * 128, 128)
                    res.append(send(src.at[:, pl.ds(col, 128)], dst.at[:, pl.ds(e * 128, 128)],
                                    hs.at[i, e], hr.at[i, e], peer, tz))
            return res

        def hidden_copies(u):
            return [send(src.at[0], dst.at[u], ss.at[i, u], rs.at[i, u], peer, tz)
                    for i, (src, dst) in enumerate(((hid_ref, phid), (dg_ref, pdg), (du_ref, pdu)))]

        @pl.when(t == 0)
        def _():
            bar = pltpu.get_barrier_semaphore()
            pl.semaphore_signal(bar, inc=1, device_id=(peer, tz), device_id_type=MESH)
            pl.semaphore_wait(bar, 1)
            for m in half_copies():
                m.start()
            out_ref[...] = h_ref[...]
            acc[...] = jnp.zeros_like(acc)

        for e in range(dp):
            at = slice(e * 128, (e + 1) * 128)
            sg[:, at] = wg_ref[e, 0]
            su[:, at] = wu_ref[e, 0]
            sd[:, at] = wd_ref[e, 0]
        tile = ff // 2

        @pl.loop(0, 2)
        def _(i):
            at = pl.ds(pl.multiple_of(i * tile, 16), tile)
            gate = dot_nt(sg[at, :], n_ref[...])
            up = dot_nt(su[at, :], n_ref[...])
            dhid = dot_nt(sd[at, :], c_ref[...])
            sig = 1.0 / (1.0 + jnp.exp(-gate))
            act = gate * sig
            hid_ref[0, at, :] = (act * up).astype(BF16)
            dg_ref[0, at, :] = (dhid * up * (sig * (1.0 + gate * (1.0 - sig)))).astype(BF16)
            du_ref[0, at, :] = (dhid * act).astype(BF16)

        for m in hidden_copies(t):
            m.start()
        out_ref[...] += dot_tn(hid_ref[0], sd[...])
        acc[...] += dot_tn(dg_ref[0], sg[...]) + dot_tn(du_ref[0], su[...])
        for m in hidden_copies(t):
            m.wait_send()

        @pl.when(t == last)
        def _():
            gn = gain_row(gn_ref, 1)
            h = h_ref[...]
            dn = acc[...]
            iv = inv_rms(h)
            gg_ref[...] = jnp.sum(dn * h * iv, axis=0, keepdims=True)
            gd = dn * gn
            dh = c_ref[...].astype(F32) + iv * gd - h * (iv * iv * iv * jnp.mean(h * gd, axis=1, keepdims=True))
            dh_ref[...] = dh
            dhb_ref[...] = dh.astype(BF16)

            @pl.loop(0, nz)
            def _(u):
                w = jnp.concatenate([wo_ref[e, u] for e in range(dp)], axis=1)
                do_ref[u] = dot_nt(dhb_ref[...], w).astype(BF16)

            for m in half_copies():
                m.wait()
            for u in range(nz):
                for m in hidden_copies(u):
                    m.wait_recv()

    wspec = pl.BlockSpec((dp, 1, ff, wg.shape[3]), lambda t: (0, t, 0, 0))
    piece = pl.BlockSpec((1, ff, r), lambda t: (t, 0, 0))
    one = lambda s: full(s, 1)
    any_ = pl.BlockSpec(memory_space=pl.ANY)
    st = lambda s, dt=BF16: jax.ShapeDtypeStruct(s, dt)
    dma = lambda *n: pltpu.SemaphoreType.DMA(n)
    return pl.pallas_call(
        kern,
        grid=(nz,),
        in_specs=[one((r, d)), one((r, d)), one((r, d)), one(gains.shape), wspec, wspec, wspec, one(wo.shape)],
        out_specs=[piece, piece, piece, full((r, d)), full((r, d)), full((r, d)), full((nz, r, kk)), full((1, d))]
        + [any_] * 5,
        out_shape=[st((nz, ff, r))] * 3
        + [st((r, d), F32), st((r, d), F32), st((r, d)), st((nz, r, kk)), st((1, d), F32)]
        + [st((nz, ff, r))] * 3 + [st((r, half))] * 2,
        scratch_shapes=[pltpu.VMEM((ff, d), BF16)] * 3 + [pltpu.VMEM((r, d), F32)]
        + [dma(3, nz)] * 2 + [dma(2, dp // 2)] * 2,
        compiler_params=pltpu.CompilerParams(vmem_limit_bytes=VL, dimension_semantics=("arbitrary",),
                                             collective_id=2, has_side_effects=True),
        name="feed",
    )(h, n2, c, gains, wg, wu, wd, wo)


class Scatter:
    def __init__(self, g, src, rows_, b_first, bufs, sems, out):
        self.g, self.src, self.rows, self.b_first, self.out = g, src, rows_, b_first, out
        self.r1, self.r2, self.r3 = bufs
        self.sems, self.next = sems, 0
        self.sent = []

    def _sem(self):
        i = self.next
        self.next += 1
        return self.sems[0].at[i], self.sems[1].at[i]

    def _e(self, f, s):
        return s * self.g.nb + f if self.b_first else f * self.g.nb + s

    def _mine(self):
        a, b, c, t, me = coords(self.g)
        f, s = (b, a) if self.b_first else (a, b)
        n1, n2 = (self.g.nb, self.g.na) if self.b_first else (self.g.na, self.g.nb)
        return f, s, c, t, me, n1, n2

    def start_first(self):
        f, s, c, t, me, n1, n2 = self._mine()
        lo, n = self.rows
        self.first = []
        for k in range(1, n1):
            to = (f + k) % n1
            for j in range(n2):
                x, y = self._sem()
                m = send(self.src.at[self._e(to, j), :, pl.ds(lo, n), :], self.r1.at[k - 1, j], x, y,
                         self._e(to, s) * 2 + c, t)
                m.start()
                self.first.append(m)
        self.sent += self.first

    def start_second(self):
        f, s, c, t, me, n1, n2 = self._mine()
        lo, n = self.rows
        for m in self.first:
            m.wait_recv()
        for j in range(n2):
            e = self._e(f, j)

            @pl.loop(0, self.g.nz)
            def _(u):
                v = self.src[e, u, lo : lo + n, :].astype(F32)
                for k in range(n1 - 1):
                    v = v + self.r1[k, j, u].astype(F32)
                self.src[e, u, lo : lo + n, :] = v.astype(BF16)

        self.second = []
        for k in range(1, n2):
            to = (s + k) % n2
            x, y = self._sem()
            m = send(self.src.at[self._e(f, to), :, pl.ds(lo, n), :], self.r2.at[k - 1], x, y, self._e(f, to) * 2 + c, t)
            m.start()
            self.second.append(m)
        self.sent += self.second

    def start_z(self):
        f, s, c, t, me, n1, n2 = self._mine()
        lo, n = self.rows
        e = self._e(f, s)
        for m in self.second:
            m.wait_recv()

        @pl.loop(0, self.g.nz)
        def _(u):
            v = self.src[e, u, lo : lo + n, :].astype(F32)
            for k in range(n2 - 1):
                v = v + self.r2[k, u].astype(F32)
            self.src[e, u, lo : lo + n, :] = v.astype(BF16)

        self.third = []
        for k in range(1, self.g.nz):
            to = (t + k) % self.g.nz
            x, y = self._sem()
            m = send(self.src.at[e, to, pl.ds(lo, n), :], self.r3.at[k - 1], x, y, me, to)
            m.start()
            self.third.append(m)
        self.sent += self.third

    def finish(self):
        f, s, c, t, me, n1, n2 = self._mine()
        lo, n = self.rows
        for m in self.third:
            m.wait_recv()
        v = self.src[self._e(f, s), t, lo : lo + n, :].astype(F32)
        for k in range(self.g.nz - 1):
            v = v + self.r3[k].astype(F32)
        self.out[pl.ds(lo, n), :] = v
        for m in self.sent:
            m.wait_send()


def scatter_sems(g):
    return (g.na - 1) * g.na + (g.na - 1) + (g.nz - 1)


def back_kernel(g, halo, window, units, *refs):
    refs = list(refs)
    take = lambda n: [refs.pop(0) for _ in range(n)]
    seg_q, seg_k, gg_ffn, gn_ref = take(4)
    hid, dg, du, phid, pdg, pdu, n2, c_in, pn, pc = take(10)
    q, k, v, mk, mv, o, lse, do, dhb, n1 = take(10)
    x, xh, dh, wq, wk, wv, cos, sin = take(8)
    gout, grad_in = take(2)
    outs = take(7)
    dq, dk, dv, pdq, pdk, pdv, po = take(7)
    G = take(7)
    bufs = [take(3) for _ in units]
    sems = [take(2) for _ in units]
    n2_v, pn_v, c_v, pc_v, n1_v, pn1_v, dhb_v, pdhb_v = take(8)
    x_v, xh_v, dh_v, acc, hb_v, more, cos_v, sin_v, sdk, sdv, w_s = take(11)
    gz, gs, gd, gp = take(4)
    zss, zrs, dss, drs, hss, hrs, ls, css, crs = take(9)
    a, b, core, t, me = coords(g)
    peer = me + 1 - 2 * core
    r, d = x_v.shape
    rt = (halo + 1) * r
    nz, ff, _ = hid.shape
    dp, _, kd, cols = wq.shape
    nb = dp // 2
    half = d // 2
    ksel, blk = mk.shape[1:3]
    nm, per_t = ksel * blk, cols // HD
    greet(g, me, t)
    us = [Scatter(g, G[w], rows_, bf, bufs[i], sems[i], outs[w]) for i, (w, rows_, bf) in enumerate(units)]
    of = lambda *ws: [u for u, (w, _, _) in zip(us, units) if w in ws]

    loads = []

    def load(src, dst):
        m = pltpu.make_async_copy(src, dst, ls.at[len(loads)])
        m.start()
        loads.append(m)
        return m

    def mine(src, dst):
        return [load(src.at[:, pl.ds(pl.multiple_of((2 * e + core) * 128, 128), 128)], dst.at[:, pl.ds(e * 128, 128)])
                for e in range(nb)]

    l_ffn = mine(n2, n2_v) + mine(c_in, c_v) + [load(pn, pn_v), load(pc, pc_v)]
    l_rest = mine(n1, n1_v) + mine(dhb, dhb_v)
    l_x = [load(x, x_v), load(dh, dh_v), load(cos, cos_v), load(sin, sin_v)]
    cores = []

    def to_peer(src, dst):
        i = len(cores)
        m = send(src, dst, css.at[i], crs.at[i], peer, t)
        m.start()
        cores.append(m)
        return m

    def theirs(src, dst):
        return [to_peer(src.at[:, pl.ds(pl.multiple_of((2 * e + 1 - core) * 128, 128), 128)], dst.at[:, pl.ds(e * 128, 128)])
                for e in range(nb)]

    p_rest = theirs(n1, pn1_v) + theirs(dhb, pdhb_v) + [to_peer(o, po)]
    for m in l_ffn:
        m.wait()

    def ffn_grads(A, B, mine_v, peer_v, out):
        def body(a_ref, b_ref):
            u = pl.program_id(0)
            y = (dot_nn(a_ref[0], mine_v[...]) + dot_nn(b_ref[0], peer_v[...])).astype(BF16)
            for e in range(nb):
                out[e, u] = y[:, e * 128 : (e + 1) * 128]

        piece = pl.BlockSpec((1, ff, r), lambda u: (u, 0, 0))
        pltpu.emit_pipeline(body, grid=(nz,), in_specs=[piece] * 2)(A, B)

    ffn_grads(hid, phid, c_v, pc_v, G[2])
    for u in of(2):
        u.start_first()
    ffn_grads(dg, pdg, n2_v, pn_v, G[0])
    for u in of(0):
        u.start_first()
    ffn_grads(du, pdu, n2_v, pn_v, G[1])
    for u in of(1):
        u.start_first()
    for m in l_rest + p_rest + l_x:
        m.wait()

    col = lambda n: pl.BlockSpec((n, cols), lambda u: (0, u))

    def out_grads(a_ref, b_ref):
        u = pl.program_id(0)
        y = (dot_tn(a_ref[...], dhb_v[...]) + dot_tn(b_ref[...], pdhb_v[...])).astype(BF16)
        for e in range(nb):
            G[3][e, u] = y[:, e * 128 : (e + 1) * 128]

    pltpu.emit_pipeline(out_grads, grid=(nz,), in_specs=[col(r)] * 2)(o, po)
    for u in of(2):
        u.start_second()

    scale = HD**-0.5

    def attend_back(q_ref, k_ref, v_ref, mk_ref, mv_ref, o_ref, l_ref, do_ref, dq_ref, dk_ref, dv_ref):
        km = mk_ref[0].reshape(nm, HD)
        vm = mv_ref[0].reshape(nm, HD)
        sdk[...] = jnp.zeros_like(sdk)
        sdv[...] = jnp.zeros_like(sdv)
        for i in range(r // QT):
            at = slice(i * QT, (i + 1) * QT)
            k0 = halo * r - window + i * QT
            ks = slice(k0, k0 + window + QT)
            own = slice(halo * r + i * QT, halo * r + (i + 1) * QT)
            qq, dd = q_ref[at, :], do_ref[0, at, :]
            lse_c = l_ref[0, at, :]
            delta = jnp.sum(dd.astype(F32) * o_ref[at, :].astype(F32), axis=1, keepdims=True)
            ok = allowed_of(seg_q[at, :], seg_k[:, ks], halo * r + i * QT, k0)
            pm = jnp.exp2(dot_nt(qq, km) * C2 - lse_c)
            dsm = (pm * (dot_nt(dd, vm) - delta)).astype(BF16)
            plo = jnp.where(ok, jnp.exp2(dot_nt(qq, k_ref[ks, :]) * C2 - lse_c), 0.0)
            dsl = (plo * (dot_nt(dd, v_ref[ks, :]) - delta)).astype(BF16)
            dqv = (dot_nn(dsm, km) + dot_nn(dsl, k_ref[ks, :])) * scale
            dq_ref[at, :] = turn(dqv, cos_v[own, :], -sin_v[own, :]).astype(BF16)
            sdk[ks, :] += dot_tn(dsl, qq)
            sdv[ks, :] += dot_tn(plo.astype(BF16), dd)
        dk_ref[...] = turn(sdk[...] * scale, cos_v[...], -sin_v[...]).astype(BF16)
        dv_ref[...] = sdv[...].astype(BF16)

    head = lambda n: pl.BlockSpec((n, HD), lambda h: (0, h))
    mem = pl.BlockSpec((1, ksel, blk, HD), lambda h: (h // per_t, 0, 0, h % per_t))
    pltpu.emit_pipeline(
        attend_back,
        grid=(d // HD,),
        in_specs=[head(r), head(rt), head(rt), mem, mem, head(r), pl.BlockSpec((1, r, 1), lambda h: (h, 0, 0)),
                  pl.BlockSpec((1, r, HD), lambda h: (h // per_t, 0, h % per_t))],
        out_specs=[head(r), head(rt), head(rt)],
    )(q, k, v, mk, mv, o, lse, do, dq, dk, dv)
    p_att = [to_peer(dq, pdq), to_peer(dk, pdk), to_peer(dv, pdv)]
    for u in of(0):
        u.start_second()
    for u in of(3):
        u.start_first()
    for u in of(2):
        u.start_z()

    acc[...] = jnp.zeros_like(acc)

    def project_back(dq_ref, dk_ref, dv_ref, wq_ref, wk_ref, wv_ref):
        for e in range(dp):
            at = slice(e * kd, (e + 1) * kd)
            w_s[at, 0:cols] = wk_ref[e, 0]
            w_s[at, cols : 2 * cols] = wv_ref[e, 0]
            w_s[at, 2 * cols :] = wq_ref[e, 0]
        tile = 512

        @pl.loop(0, rt // tile)
        def _(i):
            at = pl.ds(pl.multiple_of(i * tile, tile), tile)
            acc[at, :] += dot_nt(jnp.concatenate([dk_ref[at, :], dv_ref[at, :]], axis=1), w_s[:, 0 : 2 * cols])

        acc[halo * r :, :] += dot_nt(dq_ref[...], w_s[:, 2 * cols :])

    wspec = pl.BlockSpec((dp, 1, kd, cols), lambda u: (0, u, 0, 0))
    pltpu.emit_pipeline(project_back, grid=(nz,), in_specs=[col(r), col(rt), col(rt)] + [wspec] * 3)(
        dq, dk, dv, wq, wk, wv
    )
    hb_v[...] = acc[: halo * r, :].astype(BF16)
    hd = []
    for j in range(halo):
        m = send(hb_v.at[pl.ds((halo - 1 - j) * r, r), :], more.at[j], hss.at[j], hrs.at[j], me, (t + g.nz - 1 - j) % g.nz)
        hd.append(m)

        @pl.when(t >= j + 1)
        def _():
            m.start()

    vx = x_v[...].astype(F32)
    gp[0:1, :] = jnp.sum(acc[halo * r :, :] * vx * inv_rms(vx), axis=0, keepdims=True)
    gp[1:2, :] = gg_ffn[...]
    for j in range(halo):

        @pl.when(t >= j + 1)
        def _():
            cx = pltpu.make_async_copy(xh.at[j], xh_v, zss.at[g.nz - 1])
            cx.start()
            cx.wait()
            vh = xh_v[...].astype(F32)
            lo = (halo - 1 - j) * r
            gp[0:1, :] = gp[0:1, :] + jnp.sum(acc[lo : lo + r, :] * vh * inv_rms(vh), axis=0, keepdims=True)

    zg = []
    for i in range(1, g.nz):
        m = send(gp, gz.at[i - 1], zss.at[i - 1], zrs.at[i - 1], me, (t + i) % g.nz)
        m.start()
        zg.append(m)
    for u in of(1):
        u.start_second()
    for u in of(0):
        u.start_z()
    for m in p_att:
        m.wait()

    own = pl.ds(halo * r, r)

    def proj_grads(q0, q1, k0, k1, v0, v1):
        u = pl.program_id(0)
        for out, p0, p1, a0, a1 in (
            (G[4], q0, q1, n1_v.at[own], pn1_v.at[own]),
            (G[5], k0, k1, n1_v, pn1_v),
            (G[6], v0, v1, n1_v, pn1_v),
        ):
            y = (dot_tn(a0[...], p0[...]) + dot_tn(a1[...], p1[...])).astype(BF16)
            for e in range(nb):
                out[e, u] = y[e * 128 : (e + 1) * 128, :]

    pltpu.emit_pipeline(proj_grads, grid=(nz,), in_specs=[col(r)] * 2 + [col(rt)] * 4)(dq, pdq, dk, pdk, dv, pdv)
    for u in of(4, 5, 6):
        u.start_first()
    for m in zg:
        m.wait()
    tot = gp[...]
    for i in range(g.nz - 1):
        tot = tot + gz[i]
    for e in range(g.dp):
        gs[e] = tot[:, e * 128 : (e + 1) * 128]
    ds_ = []
    for i in range(1, g.dp):
        to = (me + i) % g.dp
        m = send(gs.at[to], gd.at[me], dss.at[i], drs.at[i], to, t)
        m.start()
        ds_.append(m)
    og = pltpu.make_async_copy(gs.at[me], gd.at[me], dss.at[0])
    og.start()
    for u in of(3):
        u.start_second()
    for u in of(1):
        u.start_z()
    for u in of(4, 5, 6):
        u.start_second()
    for u in of(3):
        u.start_z()

    for j, m in enumerate(hd):

        @pl.when(t + j + 1 < g.nz)
        def _():
            m.wait_recv()
            acc[halo * r :, :] = acc[halo * r :, :] + more[j].astype(F32)

        @pl.when(t >= j + 1)
        def _():
            m.wait_send()

    vx = x_v[...].astype(F32)
    iv = inv_rms(vx)
    gd_ = acc[halo * r :, :] * gain_row(gn_ref, 0)
    grad_in[...] = dh_v[...] + iv * gd_ - vx * (iv * iv * iv * jnp.mean(vx * gd_, axis=1, keepdims=True))
    for u in of(4, 5, 6):
        u.start_z()
    og.wait()
    for m in ds_:
        m.wait()
    s = gd[0]
    for e in range(1, g.dp):
        s = s + gd[e]
    gout[...] = s
    for u in us:
        u.finish()


def back(g, halo, window, seg_q, seg_k, gg_ffn, gains, hid, dg, du, phid, pdg, pdu, n2, c, pn, pc,
         q, k, v, mk, mv, o, lse, do, dhb, n1, x, xh, dh, wq, wk, wv, cos, sin):
    r, d = x.shape
    rt = (halo + 1) * r
    nz, ff, _ = hid.shape
    dp, _, kd, cols = wq.shape
    nb, half = dp // 2, d // 2
    any_ = pl.BlockSpec(memory_space=pl.ANY)
    vm = pl.BlockSpec(memory_space=pltpu.VMEM)
    dma = lambda *n: pltpu.SemaphoreType.DMA(n)
    st = lambda s, dt=BF16: jax.ShapeDtypeStruct(s, dt)
    pieces = [(ff, 128)] * 3 + [(cols, 128)] + [(kd, cols)] * 3
    units = []
    for w in (2, 0, 1, 3):
        n = pieces[w][0]
        units += [(w, (0, n // 2), True), (w, (n // 2, n - n // 2), False)]
    units += [(4, (0, kd), True), (5, (0, kd), False), (6, (0, kd // 2), True), (6, (kd // 2, kd - kd // 2), False)]
    scratch = [pltpu.VMEM((nb, nz) + p, BF16) for p in pieces]
    for w, (lo, n), bf in units:
        cc = pieces[w][1]
        n1_, n2_ = (g.nb, g.na) if bf else (g.na, g.nb)
        scratch += [
            pltpu.VMEM((n1_ - 1, n2_, nz, n, cc), BF16),
            pltpu.VMEM((n2_ - 1, nz, n, cc), BF16),
            pltpu.VMEM((nz - 1, n, cc), BF16),
        ]
    scratch += [dma(scatter_sems(g))] * (2 * len(units))
    scratch += [pltpu.VMEM((r, half), BF16)] * 4 + [pltpu.VMEM((rt, half), BF16)] * 2 + [pltpu.VMEM((r, half), BF16)] * 2
    scratch += [pltpu.VMEM((r, d), BF16)] * 2 + [pltpu.VMEM((r, d), F32), pltpu.VMEM((rt, d), F32)]
    scratch += [pltpu.VMEM((halo * r, d), BF16), pltpu.VMEM((halo, r, d), BF16)]
    scratch += [pltpu.VMEM((rt, HD), F32)] * 4 + [pltpu.VMEM((d, 3 * cols), BF16)]
    scratch += [pltpu.VMEM((nz - 1, 2, d), F32), pltpu.VMEM((dp, 2, 128), F32), pltpu.VMEM((dp, 2, 128), F32), pltpu.VMEM((2, d), F32)]
    scratch += [dma(nz), dma(nz), dma(dp), dma(dp), dma(halo), dma(halo), dma(4 * nb + 6), dma(2 * nb + 4), dma(2 * nb + 4)]
    out_shape = (
        [st((2, 128), F32), st((r, d), F32)]
        + [st(p, F32) for p in pieces]
        + [st((r, d)), st((rt, d)), st((rt, d)), st((r, d)), st((rt, d)), st((rt, d)), st((r, d))]
    )
    return pl.pallas_call(
        functools.partial(back_kernel, g, halo, window, units),
        out_shape=out_shape,
        in_specs=[vm] * 4 + [any_] * 28,
        out_specs=[vm] * 9 + [any_] * 7,
        scratch_shapes=scratch,
        compiler_params=pltpu.CompilerParams(collective_id=1, has_side_effects=True, vmem_limit_bytes=63 * 2**20),
        name="backward",
    )(seg_q, seg_k, gg_ffn, gains, hid, dg, du, phid, pdg, pdu, n2, c, pn, pc, q, k, v, mk, mv, o, lse, do, dhb, n1,
      x, xh, dh, wq, wk, wv, cos, sin)


HEADS = 8
QB = 512


def normalize(field, gain_vec):
    return field * lax.rsqrt(jnp.mean(field * field, axis=-1, keepdims=True) + EPSILON) * gain_vec


def rotate(field, heads_here):
    row_total = field.shape[0]
    head_size = field.shape[1] // heads_here
    half_width = head_size // 2
    frequencies = 10000.0 ** (-jnp.arange(half_width, dtype=jnp.float32) * 2.0 / head_size)
    angles = jnp.arange(row_total, dtype=jnp.float32)[:, None] * frequencies[None, :]
    cosine = jnp.cos(angles)[:, None, :]
    sine_table = jnp.sin(angles)[:, None, :]
    split_heads = field.reshape(row_total, heads_here, head_size)
    first_half = split_heads[..., :half_width]
    second_half = split_heads[..., half_width:]
    turned = jnp.concatenate(
        [
            first_half * cosine - second_half * sine_table,
            second_half * cosine + first_half * sine_table,
        ],
        axis=-1,
    )
    return turned.reshape(row_total, heads_here * head_size)


def contract_rows(left, right):
    return lax.dot_general(
        left, right, (((0,), (0,)), ((), ())), preferred_element_type=jnp.float32
    )


def against(left, right):
    return lax.dot_general(
        left, right, (((1,), (1,)), ((), ())), preferred_element_type=jnp.float32
    )


def spread_rows(local_rows, matrices):
    piece_rows = lax.all_gather(local_rows, "tensor", axis=0, tiled=True)
    return jnp.concatenate(
        [jnp.dot(piece_rows, matrix, preferred_element_type=jnp.float32) for matrix in matrices],
        axis=1,
    )


def reduce_rows(left, right):
    return lax.psum_scatter(
        jnp.dot(left, right, preferred_element_type=jnp.float32).astype(jnp.bfloat16),
        "tensor",
        scatter_dimension=0,
        tiled=True,
    ).astype(jnp.float32)


def return_rows(pairs):
    summed = against(pairs[0][0], pairs[0][1])
    for grad_block, matrix in pairs[1:]:
        summed = summed + against(grad_block, matrix)
    return lax.psum_scatter(
        summed.astype(jnp.bfloat16), "tensor", scatter_dimension=0, tiled=True
    ).astype(jnp.float32)


def weight_grads(local_rows, grads_list):
    piece_rows = lax.all_gather(local_rows, "tensor", axis=0, tiled=True)
    return tuple((contract_rows(piece_rows, grad_one) for grad_one in grads_list))


def all_rows(local_grad):
    return lax.all_gather(local_grad, "tensor", axis=0, tiled=True)


def on_device_any(
    block_in,
    segments,
    retrieved,
    partner,
    memory_keys,
    memory_values,
    gain_attn,
    w_query,
    w_key,
    w_value,
    w_out,
    gain_ffn,
    w_gate,
    w_up,
    w_down,
    cotangent,
):
    tensor_size = lax.axis_size("tensor")
    dp_size = lax.axis_size("dp")
    heads_here = HEADS // tensor_size
    head_width = heads_here * HD
    score_scale = HD ** (-0.5)
    seq_len = segments.shape[1]
    query_blocks = seq_len // QB
    stream_in = block_in[0].astype(jnp.float32)
    seg_row = segments[0]
    positions = jnp.arange(seq_len)
    gathered = (
        lax.all_gather(gain_attn, "dp", axis=0, tiled=True),
        lax.all_gather(w_query, "dp", axis=0, tiled=True),
        lax.all_gather(w_key, "dp", axis=0, tiled=True),
        lax.all_gather(w_value, "dp", axis=0, tiled=True),
        lax.all_gather(w_out, "dp", axis=1, tiled=True),
        lax.all_gather(gain_ffn, "dp", axis=0, tiled=True),
        lax.all_gather(w_gate, "dp", axis=0, tiled=True),
        lax.all_gather(w_up, "dp", axis=0, tiled=True),
        lax.all_gather(w_down, "dp", axis=1, tiled=True),
    )
    gain_one, query_w, key_w, value_w, out_w, gain_two, gate_w, up_w, down_w = gathered
    wanted = retrieved[0].reshape(-1)
    request_total = wanted.shape[0]
    capacity = max(2, (2 * request_total + dp_size - 1) // dp_size)
    blocks_dev = memory_keys.shape[1]
    from_partner = wanted // MEMB
    block_index = wanted % MEMB
    owner_dev = block_index // blocks_dev
    local_block = block_index % blocks_dev
    seq_id = jnp.where(from_partner == 0, lax.axis_index("dp"), partner[0])
    owner_hits = (owner_dev[:, None] == jnp.arange(dp_size)[None, :]).astype(jnp.int32)
    slot_index = jnp.sum((jnp.cumsum(owner_hits, axis=0) - 1) * owner_hits, axis=1)
    requests = (
        jnp.zeros((dp_size, capacity, 2), jnp.int32)
        .at[owner_dev, slot_index]
        .set(jnp.stack([seq_id, local_block], axis=-1))
    )
    received = lax.all_to_all(requests, "dp", split_axis=0, concat_axis=0, tiled=True)
    picked_keys = memory_keys[received[..., 0], received[..., 1]]
    picked_values = memory_values[received[..., 0], received[..., 1]]
    fetched_keys = lax.all_to_all(picked_keys, "dp", split_axis=0, concat_axis=0, tiled=True)
    fetched_values = lax.all_to_all(picked_values, "dp", split_axis=0, concat_axis=0, tiled=True)
    memory_k = fetched_keys[owner_dev, slot_index].reshape(query_blocks, -1, heads_here, HD)
    memory_v = fetched_values[owner_dev, slot_index].reshape(query_blocks, -1, heads_here, HD)
    normed = normalize(stream_in, gain_one.astype(jnp.float32)).astype(jnp.bfloat16)
    qkv_rows = spread_rows(normed, [query_w, key_w, value_w])
    query_raw = qkv_rows[:, :head_width]
    key_raw = qkv_rows[:, head_width : 2 * head_width]
    queries = rotate(query_raw, heads_here).astype(jnp.bfloat16)
    keys_all = rotate(key_raw, heads_here).astype(jnp.bfloat16).reshape(seq_len, heads_here, HD)
    values_all = qkv_rows[:, 2 * head_width :].astype(jnp.bfloat16).reshape(seq_len, heads_here, HD)
    query_tiles = queries.reshape(query_blocks, QB, heads_here, HD)
    seg_tiles = seg_row.reshape(query_blocks, QB)
    pos_tiles = positions.reshape(query_blocks, QB)

    def scores_of(query_blk, seg_blk, pos_blk, key_mem):
        local_scores = jnp.einsum(
            "qhd,khd->hqk", query_blk, keys_all, preferred_element_type=jnp.float32
        )
        memory_scores = jnp.einsum(
            "qhd,khd->hqk", query_blk, key_mem, preferred_element_type=jnp.float32
        )
        raw_scores = jnp.concatenate([local_scores, memory_scores], axis=-1) * score_scale
        allowed = (seg_blk[:, None] == seg_row[None, :]) & (positions[None, :] <= pos_blk[:, None])
        allowed = jnp.concatenate(
            [allowed, jnp.ones((query_blk.shape[0], key_mem.shape[0]), dtype=jnp.bool_)], axis=1
        )
        return (raw_scores, allowed)

    def forward_block(pieces):
        query_blk, seg_blk, pos_blk, key_mem, value_mem = pieces
        raw_scores, allowed = scores_of(query_blk, seg_blk, pos_blk, key_mem)
        masked = jnp.where(allowed[None], raw_scores, MASKED)
        row_max = jnp.max(masked, axis=-1, keepdims=True)
        expo = jnp.exp(masked - row_max)
        row_total = jnp.sum(expo, axis=-1, keepdims=True)
        weights_soft = (expo / row_total).astype(jnp.bfloat16)
        values_both = jnp.concatenate([values_all, value_mem], axis=0)
        result = jnp.einsum(
            "hqk,khd->qhd", weights_soft, values_both, preferred_element_type=jnp.float32
        )
        return (result, (row_max + jnp.log(row_total))[..., 0])

    attended, log_totals = lax.map(
        forward_block, (query_tiles, seg_tiles, pos_tiles, memory_k, memory_v)
    )
    mixed = attended.reshape(seq_len, head_width).astype(jnp.bfloat16)
    stream = stream_in + reduce_rows(mixed, out_w)
    normed_ffn = normalize(stream, gain_two.astype(jnp.float32)).astype(jnp.bfloat16)
    gate_up = spread_rows(normed_ffn, [gate_w, up_w])
    hidden_width = gate_w.shape[1]
    gate_pre = gate_up[:, :hidden_width]
    up_pre = gate_up[:, hidden_width:]
    hidden = (jax.nn.silu(gate_pre) * up_pre).astype(jnp.bfloat16)
    block_out = stream + reduce_rows(hidden, down_w)
    gathered_back = (
        lax.all_gather(gain_attn, "dp", axis=0, tiled=True),
        lax.all_gather(w_query, "dp", axis=0, tiled=True),
        lax.all_gather(w_key, "dp", axis=0, tiled=True),
        lax.all_gather(w_value, "dp", axis=0, tiled=True),
        lax.all_gather(w_out, "dp", axis=1, tiled=True),
        lax.all_gather(gain_ffn, "dp", axis=0, tiled=True),
        lax.all_gather(w_gate, "dp", axis=0, tiled=True),
        lax.all_gather(w_up, "dp", axis=0, tiled=True),
        lax.all_gather(w_down, "dp", axis=1, tiled=True),
    )
    gain_one, query_w, key_w, value_w, out_w, gain_two, gate_w, up_w, down_w = gathered_back
    dout_rows = cotangent[0]

    def gated(gate_in, up_in):
        return jax.nn.silu(gate_in) * up_in

    dout_full = all_rows(dout_rows)
    grad_down = contract_rows(hidden, dout_full)
    d_hidden = against(dout_full, down_w)
    gated_value, pull_gated = jax.vjp(gated, gate_pre, up_pre)
    d_gate, d_up = pull_gated(d_hidden)
    d_gate = d_gate.astype(jnp.bfloat16)
    d_up = d_up.astype(jnp.bfloat16)
    d_norm_ffn = return_rows([(d_gate, gate_w), (d_up, up_w)])
    grad_gate, grad_up = weight_grads(normed_ffn, [d_gate, d_up])
    norm_value, pull_norm_ffn = jax.vjp(normalize, stream, gain_two.astype(jnp.float32))
    d_stream_norm, grad_gain_ffn = pull_norm_ffn(d_norm_ffn)
    d_stream = dout_rows.astype(jnp.float32) + d_stream_norm
    d_stream_full = all_rows(d_stream.astype(jnp.bfloat16))
    grad_out = contract_rows(mixed, d_stream_full)
    d_mixed = against(d_stream_full, out_w).astype(jnp.bfloat16)
    d_mixed_tiles = d_mixed.reshape(query_blocks, QB, heads_here, HD)

    def backward_block(carry_sums, pieces):
        key_sum, value_sum = carry_sums
        query_blk, seg_blk, pos_blk, key_mem, value_mem, log_blk, grad_blk = pieces
        raw_scores, allowed = scores_of(query_blk, seg_blk, pos_blk, key_mem)
        probs = jnp.where(allowed[None], jnp.exp(raw_scores - log_blk[..., None]), 0.0)
        values_both = jnp.concatenate([values_all, value_mem], axis=0)
        d_probs = jnp.einsum(
            "qhd,khd->hqk", grad_blk, values_both, preferred_element_type=jnp.float32
        )
        shared = jnp.sum(probs * d_probs, axis=-1, keepdims=True)
        d_scores = (probs * (d_probs - shared)).astype(jnp.bfloat16)
        probs_low = probs.astype(jnp.bfloat16)
        keys_both = jnp.concatenate([keys_all, key_mem], axis=0)
        d_query = (
            jnp.einsum("hqk,khd->qhd", d_scores, keys_both, preferred_element_type=jnp.float32)
            * score_scale
        )
        key_sum = (
            key_sum
            + jnp.einsum(
                "hqk,qhd->khd",
                d_scores[..., :seq_len],
                query_blk,
                preferred_element_type=jnp.float32,
            )
            * score_scale
        )
        value_sum = value_sum + jnp.einsum(
            "hqk,qhd->khd", probs_low[..., :seq_len], grad_blk, preferred_element_type=jnp.float32
        )
        return ((key_sum, value_sum), d_query)

    zero_grads = jnp.zeros((seq_len, heads_here, HD), jnp.float32)
    (d_keys, d_values), d_queries = lax.scan(
        backward_block,
        (zero_grads, zero_grads),
        (query_tiles, seg_tiles, pos_tiles, memory_k, memory_v, log_totals, d_mixed_tiles),
    )

    def turn(field):
        return rotate(field, heads_here)

    turned_value, pull_turn = jax.vjp(turn, query_raw)
    d_query_raw = pull_turn(d_queries.reshape(seq_len, head_width))[0].astype(jnp.bfloat16)
    d_key_raw = pull_turn(d_keys.reshape(seq_len, head_width))[0].astype(jnp.bfloat16)
    d_value_raw = d_values.reshape(seq_len, head_width).astype(jnp.bfloat16)
    d_norm_attn = return_rows([(d_query_raw, query_w), (d_key_raw, key_w), (d_value_raw, value_w)])
    grad_query, grad_key, grad_value = weight_grads(normed, [d_query_raw, d_key_raw, d_value_raw])
    norm_first, pull_norm_attn = jax.vjp(normalize, stream_in, gain_one.astype(jnp.float32))
    d_input_norm, grad_gain_attn = pull_norm_attn(d_norm_attn)
    grad_in = d_stream + d_input_norm
    grad_gain_attn, grad_gain_ffn = lax.psum((grad_gain_attn, grad_gain_ffn), "tensor")
    results = (
        lax.psum_scatter(
            grad_gain_attn.astype(jnp.bfloat16), "dp", scatter_dimension=0, tiled=True
        ).astype(jnp.float32),
        lax.psum_scatter(
            grad_query.astype(jnp.bfloat16), "dp", scatter_dimension=0, tiled=True
        ).astype(jnp.float32),
        lax.psum_scatter(
            grad_key.astype(jnp.bfloat16), "dp", scatter_dimension=0, tiled=True
        ).astype(jnp.float32),
        lax.psum_scatter(
            grad_value.astype(jnp.bfloat16), "dp", scatter_dimension=0, tiled=True
        ).astype(jnp.float32),
        lax.psum_scatter(
            grad_out.astype(jnp.bfloat16), "dp", scatter_dimension=1, tiled=True
        ).astype(jnp.float32),
        lax.psum_scatter(
            grad_gain_ffn.astype(jnp.bfloat16), "dp", scatter_dimension=0, tiled=True
        ).astype(jnp.float32),
        lax.psum_scatter(
            grad_gate.astype(jnp.bfloat16), "dp", scatter_dimension=0, tiled=True
        ).astype(jnp.float32),
        lax.psum_scatter(
            grad_up.astype(jnp.bfloat16), "dp", scatter_dimension=0, tiled=True
        ).astype(jnp.float32),
        lax.psum_scatter(
            grad_down.astype(jnp.bfloat16), "dp", scatter_dimension=1, tiled=True
        ).astype(jnp.float32),
    )
    return (block_out[None], grad_in[None]) + results


def cover(halo, r, t):
    half = HD // 2
    freq = 10000.0 ** (-jnp.arange(half, dtype=F32) * 2.0 / HD)
    pos = (t * r - halo * r + jnp.arange((halo + 1) * r)).astype(F32)
    ang = pos[:, None] * freq[None, :]
    cos, sin = jnp.cos(ang), jnp.sin(ang)
    return jnp.concatenate([cos, cos], axis=1), jnp.concatenate([-sin, sin], axis=1)


def on_device(*args):
    x, dp = args[0], lax.axis_size("dp")
    side = math.isqrt(dp // 2)
    if 2 * side * side == dp and x.shape[2] % (128 * dp) == 0:
        return on_device_rows(*args)
    return on_device_any(*args)


def on_device_rows(
    block_in, segments, retrieved, partner, memory_keys, memory_values,
    gain_attn, w_query, w_key, w_value, w_out, gain_ffn, w_gate, w_up, w_down, cotangent,
):
    g = Grid(lax.axis_size("dp"), lax.axis_size("tensor"))
    t, me = lax.axis_index("tensor"), lax.axis_index("dp")
    x, c = block_in[0], cotangent[0]
    r, d = x.shape
    seq_len = segments.shape[1]
    window = seq_len // 4
    halo = -(-window // r)
    nq, ksel = retrieved.shape[1:]
    cap = max(2, -(-2 * nq * ksel // g.dp))
    req, sel = plan_requests(retrieved[0], partner[0], g.dp, memory_keys.shape[1], cap)
    gains = jnp.stack([gain_attn, gain_ffn]).astype(F32)
    flat = lambda m: m.reshape((-1,) + m.shape[2:])
    shards = [w_query, w_key, w_value, w_out, w_gate.T, w_up.T, w_down]
    cos, sin = cover(halo, r, t)
    padded = jnp.concatenate([jnp.full((halo * r,), -1, jnp.int32), segments[0]])
    seg = lax.dynamic_slice(padded, (t * r,), ((halo + 1) * r,))
    seg_k, seg_q = seg[None, :], seg[halo * r :, None]
    (wq, wk, wv, wo, wg, wu, wd, xh, gn, mk, mv, n1, q, k, v, o, lse, h, n2) = fwd(
        g, cap, halo, window, req, sel, seg_q, seg_k, x, gains, flat(memory_keys), flat(memory_values), cos, sin,
        shards, nq, ksel,
    )
    (hid, dg, du, block_out, dh, dhb, do, gg_ffn, phid, pdg, pdu, pn, pc) = feed(g, h, n2, c, gn, wg, wu, wd, wo)
    gout, grad_in, o_gate, o_up, o_down, o_out, o_q, o_k, o_v = back(
        g, halo, window, seg_q, seg_k, gg_ffn, gn, hid, dg, du, phid, pdg, pdu, n2, c, pn, pc,
        q, k, v, mk, mv, o, lse, do, dhb, n1, x, xh, dh, wq, wk, wv, cos, sin,
    )[:9]
    return (
        block_out[None], grad_in[None], gout[0], o_q, o_k, o_v, o_out, gout[1], o_gate.T, o_up.T, o_down,
    )


def solution(mesh):
    return jax.shard_map(
        on_device,
        mesh=mesh,
        in_specs=(
            P("dp", "tensor", None), P("dp", None), P("dp", None, None), P("dp"),
            P(None, "dp", None, "tensor"), P(None, "dp", None, "tensor"),
            P("dp"), P("dp", "tensor"), P("dp", "tensor"), P("dp", "tensor"), P("tensor", "dp"),
            P("dp"), P("dp", "tensor"), P("dp", "tensor"), P("tensor", "dp"), P("dp", "tensor", None),
        ),
        out_specs=(
            P("dp", "tensor", None), P("dp", "tensor", None),
            P("dp"), P("dp", "tensor"), P("dp", "tensor"), P("dp", "tensor"), P("tensor", "dp"),
            P("dp"), P("dp", "tensor"), P("dp", "tensor"), P("tensor", "dp"),
        ),
        check_vma=False,
    )
```

```python
import functools
import math

import jax
import jax.numpy as jnp
import numpy as np
from jax import lax
from jax.experimental import pallas as pl
from jax.experimental.pallas import tpu as pltpu
from jax.sharding import PartitionSpec as P
MESH = pl.DeviceIdType.MESH
MEMB = 128


class Grid:
    def __init__(self, dp, tensor):
        side = math.isqrt(dp // 2)
        assert side * side * 2 == dp
        self.na, self.nb, self.nc, self.nz, self.dp = side, side, 2, tensor, dp


def coords(g):
    me = lax.axis_index("dp")
    t = lax.axis_index("tensor")
    return me // (2 * g.nb), (me // 2) % g.nb, me % 2, t, me


def send(src, dst, ssem, rsem, dp, t):
    return pltpu.make_async_remote_copy(
        src_ref=src, dst_ref=dst, send_sem=ssem, recv_sem=rsem, device_id=(dp, t), device_id_type=MESH
    )


class Copy:
    def __init__(self, make):
        self.make = make

    def start(self):
        self.make().start()

    def wait(self):
        self.make().wait()

    def wait_send(self):
        self.make().wait_send()

    def wait_recv(self):
        self.make().wait_recv()


def greet(g, me, t):
    bar = pltpu.get_barrier_semaphore()
    for k in range(1, g.dp):
        pl.semaphore_signal(bar, inc=1, device_id=((me + k) % g.dp, t), device_id_type=MESH)
    for k in range(1, g.nz):
        pl.semaphore_signal(bar, inc=1, device_id=(me, (t + k) % g.nz), device_id_type=MESH)
    pl.semaphore_wait(bar, g.dp - 1 + g.nz - 1)


class Gather:
    def __init__(self, g, shard, buf, rows, b_first, lanes, sems, base):
        self.g, self.shard, self.buf, self.rows, self.b_first, self.lanes = g, shard, buf, rows, b_first, lanes
        self.sems, self.next = sems, base
        self.sent = []

    def at(self, dp, t=None):
        lo, n = self.rows
        if self.lanes:
            width = self.shard.shape[1]
            col = pl.ds(pl.multiple_of(dp * width, 128), width)
            return self.buf.at[slice(None) if t is None else t, pl.ds(lo, n), col]
        depth, width = self.shard.shape
        row = pl.ds(pl.multiple_of(dp * depth + lo, 16), n)
        return self.buf.at[row, slice(None) if t is None else pl.ds(pl.multiple_of(t * width, 128), width)]

    def _sem(self):
        i = self.next
        self.next += 1
        return i

    def _push(self, src, dst, to):
        i = self._sem()
        m = Copy(lambda: send(src(), dst(), self.sems[0].at[i], self.sems[1].at[i], *to()))
        m.start()
        self.sent.append(m)
        return m

    def _slot(self, k1, k2):
        g = self.g
        a, b, c, t, me = coords(g)
        if self.b_first:
            return (((a + g.na - k2) % g.na) * g.nb + (b + g.nb - k1) % g.nb) * 2 + c
        return (((a + g.na - k1) % g.na) * g.nb + (b + g.nb - k2) % g.nb) * 2 + c

    def _sizes(self):
        return (self.g.nb, self.g.na) if self.b_first else (self.g.na, self.g.nb)

    def start_z(self):
        g = self.g
        lo, n = self.rows
        src = lambda: self.shard.at[pl.ds(lo, n), :]

        def here():
            a, b, c, t, me = coords(g)
            return self.at(me, t)

        def to(k):
            a, b, c, t, me = coords(g)
            return me, (t + k) % g.nz

        self.z = [self._push(src, here, functools.partial(to, k)) for k in range(1, g.nz)]
        i = self._sem()
        self.own = Copy(lambda: pltpu.make_async_copy(src(), here(), self.sems[0].at[i]))
        self.own.start()

    def _slab(self, k1, k2):
        return lambda: self.at(self._slot(k1, k2))

    def _core(self, k1, k2):
        def to():
            a, b, c, t, me = coords(self.g)
            return me + 1 - 2 * c, t

        self.core.append(self._push(self._slab(k1, k2), self._slab(k1, k2), to))

    def start_first(self):
        n1, n2 = self._sizes()
        self.own.wait()
        for m in self.z:
            m.wait_recv()
        self.core = []
        to = lambda k: (self._slot(n1 - k, 0), lax.axis_index("tensor"))
        self.first = [
            self._push(self._slab(0, 0), self._slab(0, 0), functools.partial(to, k)) for k in range(1, n1)
        ]
        self._core(0, 0)

    def start_second(self):
        n1, n2 = self._sizes()
        for m in self.first:
            m.wait_recv()
        to = lambda k: (self._slot(0, n2 - k), lax.axis_index("tensor"))
        self.second = [
            self._push(self._slab(k1, 0), self._slab(k1, 0), functools.partial(to, k))
            for k1 in range(n1)
            for k in range(1, n2)
        ]
        for k1 in range(1, n1):
            self._core(k1, 0)

    def start_core(self):
        n1, n2 = self._sizes()
        for m in self.second:
            m.wait_recv()
        for k1 in range(n1):
            for k2 in range(1, n2):
                self._core(k1, k2)

    def finish(self):
        for m in self.core:
            m.wait_recv()
        for m in self.sent:
            m.wait_send()


def gather_sems(g):
    return g.nz + (g.na - 1) + g.na * (g.na - 1) + g.na * g.nb


def plan_requests(retrieved, partner, dp_size, blocks_dev, cap):
    wanted = retrieved.reshape(-1)
    n = wanted.shape[0]
    from_partner = wanted // MEMB
    block_index = wanted % MEMB
    owner = block_index // blocks_dev
    local = block_index % blocks_dev
    seq = jnp.where(from_partner == 0, lax.axis_index("dp"), partner)
    flat = seq * blocks_dev + local
    i = jnp.arange(n)
    slot = jnp.sum(((owner[:, None] == owner[None, :]) & (i[None, :] < i[:, None])).astype(jnp.int32), axis=1)
    hit = (owner[None, None, :] == jnp.arange(dp_size)[:, None, None]) & (
        slot[None, None, :] == jnp.arange(128)[None, :, None]
    )
    req = jnp.sum(jnp.where(hit, flat[None, None, :], 0), axis=2)
    return jnp.broadcast_to(req[:, None, :], (dp_size, 8, 128)).astype(jnp.int32), (owner * cap + slot).astype(jnp.int32)


HD = 128
EPSILON = 1e-05
MASKED = -1e30
F32, BF16 = jnp.float32, jnp.bfloat16


def dot_nn(x, y):
    return lax.dot_general(x, y, (((1,), (0,)), ((), ())), preferred_element_type=F32)


def dot_nt(x, y):
    return lax.dot_general(x, y, (((1,), (1,)), ((), ())), preferred_element_type=F32)


def dot_tn(x, y):
    return lax.dot_general(x, y, (((0,), (0,)), ((), ())), preferred_element_type=F32)


def inv_rms(v):
    return lax.rsqrt(jnp.mean(v * v, axis=-1, keepdims=True) + EPSILON)


def gain_row(gains_ref, which):
    n = gains_ref.shape[0]
    return jnp.concatenate([gains_ref[d, which : which + 1, :] for d in range(n)], axis=1)


def turn(v, cos, sin):
    return v * cos + pltpu.roll(v, HD // 2, axis=1) * sin


def lanes(ref):
    return jnp.concatenate([ref[d, 0] for d in range(ref.shape[0])], axis=1)


def rows(ref):
    return jnp.concatenate([ref[d, 0] for d in range(ref.shape[0])], axis=0)


VL = 60 * 2**20


def full(shape, buffers=None):
    n = len(shape)
    kw = {} if buffers is None else dict(pipeline_mode=pl.Buffered(buffers))
    return pl.BlockSpec(shape, lambda *i: (0,) * n, **kw)


def allowed_of(seg_q, seg_k, q0, k0):
    n, m = seg_q.shape[0], seg_k.shape[1]
    qp = lax.broadcasted_iota(jnp.int32, (n, m), 0) + q0
    kp = lax.broadcasted_iota(jnp.int32, (n, m), 1) + k0
    return (seg_q == seg_k) & (kp <= qp)


QT = 256
C2 = HD**-0.5 * math.log2(math.e)


class Scatter:
    def __init__(self, g, src, rows, b_first, bufs, sems, out):
        self.g, self.src, self.rows, self.b_first, self.out = g, src, rows, b_first, out
        self.r1, self.r2, self.r3 = bufs
        self.sems, self.next = sems, 0
        self.sent = []

    def _push(self, src, dst, to):
        i = self.next
        self.next += 1
        m = Copy(lambda: send(src(), dst(), self.sems[0].at[i], self.sems[1].at[i], *to()))
        m.start()
        self.sent.append(m)
        return m

    def _e(self, f, s):
        return s * self.g.nb + f if self.b_first else f * self.g.nb + s

    def _mine(self):
        a, b, c, t, me = coords(self.g)
        f, s = (b, a) if self.b_first else (a, b)
        n1, n2 = (self.g.nb, self.g.na) if self.b_first else (self.g.na, self.g.nb)
        return f, s, c, t, me, n1, n2

    def start_first(self):
        n1, n2 = self._mine()[5:]
        lo, n = self.rows

        def src(k, j):
            f = self._mine()[0]
            return self.src.at[self._e((f + k) % n1, j), :, pl.ds(lo, n), :]

        def dst(k, j):
            return self.r1.at[k - 1, j]

        def to(k):
            f, s, c, t = self._mine()[:4]
            return self._e((f + k) % n1, s) * 2 + c, t

        bind = functools.partial
        self.first = [
            self._push(bind(src, k, j), bind(dst, k, j), bind(to, k)) for k in range(1, n1) for j in range(n2)
        ]

    def start_second(self):
        f, s, c, t, me, n1, n2 = self._mine()
        lo, n = self.rows
        for m in self.first:
            m.wait_recv()
        for j in range(n2):
            e = self._e(f, j)

            @pl.loop(0, self.g.nz)
            def _(u):
                v = self.src[e, u, lo : lo + n, :].astype(F32)
                for k in range(n1 - 1):
                    v = v + self.r1[k, j, u].astype(F32)
                self.src[e, u, lo : lo + n, :] = v.astype(BF16)

        def src(k):
            f, s = self._mine()[:2]
            return self.src.at[self._e(f, (s + k) % n2), :, pl.ds(lo, n), :]

        def dst(k):
            return self.r2.at[k - 1]

        def to(k):
            f, s, c, t = self._mine()[:4]
            return self._e(f, (s + k) % n2) * 2 + c, t

        bind = functools.partial
        self.second = [self._push(bind(src, k), bind(dst, k), bind(to, k)) for k in range(1, n2)]

    def start_z(self):
        f, s, c, t, me, n1, n2 = self._mine()
        lo, n = self.rows
        nz = self.g.nz
        e = self._e(f, s)
        for m in self.second:
            m.wait_recv()

        @pl.loop(0, nz)
        def _(u):
            v = self.src[e, u, lo : lo + n, :].astype(F32)
            for k in range(n2 - 1):
                v = v + self.r2[k, u].astype(F32)
            self.src[e, u, lo : lo + n, :] = v.astype(BF16)

        def src(k):
            f, s, c, t = self._mine()[:4]
            return self.src.at[self._e(f, s), (t + k) % nz, pl.ds(lo, n), :]

        def dst(k):
            return self.r3.at[k - 1]

        def to(k):
            t, me = self._mine()[3:5]
            return me, (t + k) % nz

        bind = functools.partial
        self.third = [self._push(bind(src, k), bind(dst, k), bind(to, k)) for k in range(1, nz)]

    def finish(self):
        f, s, c, t, me, n1, n2 = self._mine()
        lo, n = self.rows
        for m in self.third:
            m.wait_recv()
        v = self.src[self._e(f, s), t, lo : lo + n, :].astype(F32)
        for k in range(self.g.nz - 1):
            v = v + self.r3[k].astype(F32)
        self.out[pl.ds(lo, n), :] = v
        for m in self.sent:
            m.wait_send()


def scatter_sems(g):
    return (g.na - 1) * g.na + (g.na - 1) + (g.nz - 1)


def rope_tables(halo, nz, r):
    half = HD // 2
    freq = 10000.0 ** (-np.arange(half, dtype=np.float64) * 2.0 / HD)
    both = lambda p: np.concatenate([np.cos(p[:, None] * freq), np.sin(p[:, None] * freq)], axis=1).astype(np.float32)
    n = nz + halo
    starts = (np.arange(-(-n // 8) * 8) - halo) * float(r)
    return both(np.arange(r, dtype=np.float64)), both(starts)


def layer_kernel(g, cfg, *refs):
    cap, nq, ksel, halo, window, gunits, sunits = cfg
    refs = list(refs)
    take = lambda n: [refs.pop(0) for _ in range(n)]
    requests, sel, seg_q, seg_k, tab1, tab2 = take(6)
    x, gains, mem_k, mem_v, cot = take(5)
    shards = take(7)
    gout = take(1)[0]
    outs = take(7)
    block_out, grad_in = take(2)
    bufs = take(7)
    wq, wk, wv, wo, wg, wu, wd = bufs
    xh, mk, mv, rec_k, rec_v, n1, q, k, v, o, lse = take(11)
    hid, sa, sb, dg, du, phid, pdg, pdu, do, dq, dk, dv, pdq, pdk, pdv, po, dh_o = take(17)
    req_in, req_s, gn_v, cos_v, sin_v = take(5)
    rbufs = [take(3) for _ in sunits]
    rsems = [take(2) for _ in sunits]
    pn_v, pc_v, pn1_v, pdhb_v, more = take(5)
    gz, gs, gd, gp = take(4)
    ss, rs, ms, qss, qrs, gss, grs, mss, mrs, zss, zrs, xss, xrs = take(13)
    css, crs, hss, hrs, ass, ars, dss, drs = take(8)
    a, b, core, t, me = coords(g)
    peer = me + 1 - 2 * core
    r, d = block_out.shape
    rt = (halo + 1) * r
    nz, ff, _ = hid.shape
    dp = g.dp
    nb, half = dp // 2, d // 2
    kd, cols = shards[0].shape
    blk = mk.shape[2]
    nm, per_t = ksel * blk, cols // HD
    heads = d // HD
    any_ = pl.BlockSpec(memory_space=pl.ANY)

    def local(src, dst, i):
        m = pltpu.make_async_copy(src, dst, ms.at[i])
        m.start()
        return m

    ncore = [0]

    def to_peer(src, dst):
        i = ncore[0]
        ncore[0] += 1
        m = send(src, dst, css.at[i], crs.at[i], peer, t)
        m.start()
        return m

    def lane_block(ref, e, c_):
        return ref.at[:, pl.ds(pl.multiple_of((2 * e + c_) * 128, 128), 128)]

    def theirs(src, dst):
        return [to_peer(lane_block(src, e, 1 - core), dst.at[:, pl.ds(e * 128, 128)]) for e in range(nb)]

    def keep_half(src, dst):
        for e in range(nb):
            dst[:, e * 128 : (e + 1) * 128] = src[:, pl.ds(pl.multiple_of((2 * e + core) * 128, 128), 128)]

    per = gather_sems(g)
    gat = [Gather(g, shards[w], bufs[w], rows_, bf, lanes_, (ss, rs), i * per)
           for i, (w, rows_, bf, lanes_) in enumerate(gunits)]
    gof = lambda *ws: [u for u, s in zip(gat, gunits) if s[0] in ws]
    proj, out_, gate_up, down = gof(0, 1, 2), gof(3), gof(4, 5), gof(6)

    head = lambda n, lo: pl.BlockSpec((n, HD), lambda h: (0, h + lo))
    mem = lambda lo: pl.BlockSpec((1, ksel, blk, HD), lambda h: ((h + lo) // per_t, 0, 0, (h + lo) % per_t))
    col = lambda n: pl.BlockSpec((n, cols), lambda u: (0, u))
    piece = pl.BlockSpec((1, ff, r), lambda u: (u, 0, 0))
    wcol = pl.BlockSpec((d, cols), lambda u: (0, u))
    wrow = lambda n: pl.BlockSpec((1, n, d), lambda u: (u, 0, 0))

    greet(g, me, t)
    def forward(loc, stage_k, stage_v, x_v, xh_v, n_v):
        rq, gn = [], []
        for i in range(1, dp):
            to = (me + i) % dp
            m = send(requests.at[to], req_in.at[me], qss.at[i], qrs.at[i], to, t)
            m.start()
            rq.append(m)
        for i in range(1, dp):
            to = (me + i) % dp
            m = send(gains, gn_v.at[me], gss.at[i], grs.at[i], to, t)
            m.start()
            gn.append(m)
        own_r = pltpu.make_async_copy(requests.at[me], req_in.at[me], qss.at[0])
        own_r.start()
        own_g = pltpu.make_async_copy(gains, gn_v.at[me], gss.at[0])
        own_g.start()
        load_k = local(mem_k, loc, 0)
        for u in proj + out_:
            u.start_z()
        xs = []
        for i in range(1, halo + 1):
            m = send(x, xh.at[i - 1], xss.at[i - 1], xrs.at[i - 1], me, (t + i) % nz)
            xs.append(m)

            @pl.when(t + i < nz)
            def _():
                m.start()

        lx = local(x, x_v, 1)
        own_r.wait()
        for m in rq:
            m.wait()
        cp = local(req_in, req_s, 2)
        cp.wait()

        def exchange(stage, rec, i, load):
            load.wait()

            @pl.loop(0, dp)
            def _(s):
                for j in range(cap):
                    stage[s, j] = loc[req_s[s, 0, j]]

            out = []
            for j in range(1, dp):
                to = (me + j) % dp
                m = send(stage.at[to], rec.at[pl.ds(me * cap, cap)], mss.at[i, j], mrs.at[i, j], to, t)
                m.start()
                out.append(m)
            own = pltpu.make_async_copy(stage.at[me], rec.at[pl.ds(me * cap, cap)], mss.at[i, 0])
            own.start()
            return out + [own]

        ek = exchange(stage_k, rec_k, 0, load_k)
        load_v = local(mem_v, loc, 3)
        for u in gate_up:
            u.start_z()
        ev = exchange(stage_v, rec_v, 1, load_v)
        for u in proj + out_:
            u.start_first()

        left = lax.broadcasted_iota(jnp.int32, (r, HD), 1) < HD // 2
        c1 = tab1[...]
        s1 = pltpu.roll(c1, HD // 2, axis=1)
        cc, sc = jnp.where(left, c1, s1), jnp.where(left, s1, c1)
        for j in range(halo + 1):
            c2 = jnp.broadcast_to(tab2[pl.ds(t + j, 1), :], (r, HD))
            s2 = pltpu.roll(c2, HD // 2, axis=1)
            ce, se = jnp.where(left, c2, s2), jnp.where(left, s2, c2)
            cos_v[j * r : (j + 1) * r, :] = cc * ce - sc * se
            sin_ = sc * ce + cc * se
            sin_v[j * r : (j + 1) * r, :] = jnp.where(left, -sin_, sin_)

        own_g.wait()
        for m in gn:
            m.wait()
        lx.wait()
        gain1 = gain_row(gn_v, 0)
        vx = x_v[...].astype(F32)
        n_v[halo * r :, :] = (vx * inv_rms(vx) * gain1).astype(BF16)
        for i, m in enumerate(xs):
            lo = (halo - 1 - i) * r

            @pl.when(t >= i + 1)
            def _():
                m.wait_recv()
                ch = local(xh.at[i], xh_v, 4)
                ch.wait()
                vh = xh_v[...].astype(F32)
                n_v[lo : lo + r, :] = (vh * inv_rms(vh) * gain1).astype(BF16)

            @pl.when(t < i + 1)
            def _():
                n_v[lo : lo + r, :] = jnp.zeros((r, d), BF16)

        cn = local(n_v, n1, 5)

        def spread(moves, rec, zst, out, i):
            for m in moves:
                m.wait()
            lr = local(rec, loc.at[pl.ds(0, dp * cap)], 6)
            lr.wait()

            @pl.loop(0, nq)
            def _(s):
                for j in range(ksel):
                    zst[s, j] = loc[sel[s * ksel + j]]

            res = []
            for j in range(1, nz):
                to = (t + j) % nz
                m = send(zst.at[to], out.at[t], zss.at[i, j], zrs.at[i, j], me, to)
                m.start()
                res.append(m)
            own = pltpu.make_async_copy(zst.at[t], out.at[t], zss.at[i, 0])
            own.start()
            return res + [own]

        zk = spread(ek, rec_k, stage_k, mk, 0)
        zv = spread(ev, rec_v, stage_v, mv, 1)
        for u in down:
            u.start_z()
        for u in proj:
            u.start_second()
        for u in gate_up:
            u.start_first()
        for u in out_:
            u.start_second()
        for u in proj:
            u.start_core()
        for u in proj:
            u.finish()

        def turned(y, cs_, sn_):
            return jnp.concatenate(
                [turn(y[:, h * HD : (h + 1) * HD], cs_, sn_).astype(BF16) for h in range(cols // HD)], axis=1
            )

        def project(wq_ref, wk_ref, wv_ref, q_ref, k_ref, v_ref):
            @pl.loop(0, halo + 1)
            def _(i):
                at = pl.ds(pl.multiple_of(i * r, r), r)
                n = n_v[at, :]
                k_ref[at, :] = turned(dot_nn(n, wk_ref[...]), cos_v[at, :], sin_v[at, :])
                v_ref[at, :] = dot_nn(n, wv_ref[...]).astype(BF16)

            q_ref[...] = turned(dot_nn(n_v[halo * r :, :], wq_ref[...]), cos_v[halo * r :, :], sin_v[halo * r :, :])

        pltpu.emit_pipeline(project, grid=(nz,), in_specs=[wcol] * 3, out_specs=[col(r), col(rt), col(rt)])(
            wq, wk, wv, q, k, v
        )
        for m in zk + zv:
            m.wait()
        cn.wait()
        for i, m in enumerate(xs):

            @pl.when(t + i + 1 < nz)
            def _():
                m.wait_send()

    nblk = mem_k.shape[0]
    pl.run_scoped(
        forward,
        pltpu.VMEM((nblk, blk, cols), BF16),
        pltpu.VMEM((max(dp, nq), cap, blk, cols), BF16),
        pltpu.VMEM((max(dp, nq), cap, blk, cols), BF16),
        pltpu.VMEM((r, d), BF16),
        pltpu.VMEM((r, d), BF16),
        pltpu.VMEM((rt, d), BF16),
    )

    def attend(q_ref, k_ref, v_ref, mk_ref, mv_ref, o_ref, l_ref):
        km = mk_ref[0].reshape(nm, HD)
        vm = mv_ref[0].reshape(nm, HD)
        for i in range(r // QT):
            at = slice(i * QT, (i + 1) * QT)
            k0 = halo * r - window + i * QT
            ks = slice(k0, k0 + window + QT)
            qq = q_ref[at, :]
            ok = allowed_of(seg_q[at, :], seg_k[:, ks], halo * r + i * QT, k0)
            sl = jnp.where(ok, dot_nt(qq, k_ref[ks, :]), MASKED)
            sm = dot_nt(qq, km)
            mx = jnp.maximum(jnp.max(sl, axis=1, keepdims=True), jnp.max(sm, axis=1, keepdims=True))
            mc = mx * C2
            el = jnp.exp2(sl * C2 - mc)
            em = jnp.exp2(sm * C2 - mc)
            tot = jnp.sum(el, axis=1, keepdims=True) + jnp.sum(em, axis=1, keepdims=True)
            acc = dot_nn(el.astype(BF16), v_ref[ks, :]) + dot_nn(em.astype(BF16), vm)
            o_ref[at, :] = (acc / tot).astype(BF16)
            l_ref[0, at, :] = mc + jnp.log2(tot)

    def run_attend(lo, n):
        pltpu.emit_pipeline(
            attend,
            grid=(n,),
            in_specs=[head(r, lo), head(rt, lo), head(rt, lo), mem(lo), mem(lo)],
            out_specs=[head(r, lo), pl.BlockSpec((1, r, 1), lambda h: (h + lo, 0, 0))],
        )(q, k, v, mk, mv, o, lse)

    run_attend(0, heads // 2)
    for u in gate_up:
        u.start_second()
    for u in down:
        u.start_first()
    run_attend(heads // 2, heads - heads // 2)
    for u in out_:
        u.start_core()
    for u in out_:
        u.finish()

    us = [None] * len(sunits)

    def rest(h_v, n2_v, c_v, n2h, ch, acc, *G):
        for i, (w, rows_, bf) in enumerate(sunits):
            us[i] = Scatter(g, G[w], rows_, bf, rbufs[i], rsems[i], outs[w])
        of = lambda *ws: [u for u, s in zip(us, sunits) if s[0] in ws]
        lc = local(cot, c_v, 0)
        lx = local(x, n2_v, 1)
        to_o = to_peer(o, po)
        lx.wait()
        h_v[...] = n2_v[...].astype(F32)

        def out_proj(o_ref, w_ref):
            h_v[...] += dot_nn(o_ref[...], w_ref[0])

        pltpu.emit_pipeline(out_proj, grid=(nz,), in_specs=[col(r), wrow(cols)])(o, wo)
        gain2 = gain_row(gn_v, 1)
        hv = h_v[...]
        n2_v[...] = (hv * inv_rms(hv) * gain2).astype(BF16)
        lc.wait()
        p_n = theirs(n2_v, pn_v) + theirs(c_v, pc_v)
        keep_half(n2_v, n2h)
        keep_half(c_v, ch)
        for u in gate_up:
            u.start_core()
        for u in gate_up:
            u.finish()

        tile = ff // 2

        def hidden(wg_ref, wu_ref, hid_ref, a_ref, b_ref):
            @pl.loop(0, 2)
            def _(i):
                at = pl.ds(pl.multiple_of(i * tile, 16), tile)
                gate = dot_nt(wg_ref[0, at, :], n2_v[...])
                up = dot_nt(wu_ref[0, at, :], n2_v[...])
                sig = 1.0 / (1.0 + jnp.exp(-gate))
                act = gate * sig
                hid_ref[0, at, :] = (act * up).astype(BF16)
                a_ref[0, at, :] = (up * (sig * (1.0 + gate * (1.0 - sig)))).astype(BF16)
                b_ref[0, at, :] = act.astype(BF16)

        pltpu.emit_pipeline(hidden, grid=(nz,), in_specs=[wrow(ff)] * 2, out_specs=[piece] * 3)(wg, wu, hid, sa, sb)
        p_h = to_peer(hid, phid)
        for u in down:
            u.start_second()
        for m in p_n + [p_h, to_o]:
            m.wait()

        def ffn_grads(A, B, mine_v, peer_v, out):
            def body(a_ref, b_ref):
                u = pl.program_id(0)
                y = (dot_nn(a_ref[0], mine_v[...]) + dot_nn(b_ref[0], peer_v[...])).astype(BF16)
                for e in range(nb):
                    out[e, u] = y[:, e * 128 : (e + 1) * 128]

            pltpu.emit_pipeline(body, grid=(nz,), in_specs=[piece] * 2)(A, B)

        ffn_grads(hid, phid, ch, pc_v, G[2])
        for u in of(2):
            u.start_first()
        for u in down:
            u.start_core()
        for u in down:
            u.finish()

        def hidden_back(wd_ref, a_ref, b_ref, dg_ref, du_ref):
            @pl.loop(0, 2)
            def _(i):
                at = pl.ds(pl.multiple_of(i * tile, 16), tile)
                dhid = dot_nt(wd_ref[0, at, :], c_v[...])
                dg_ref[0, at, :] = (dhid * a_ref[0, at, :].astype(F32)).astype(BF16)
                du_ref[0, at, :] = (dhid * b_ref[0, at, :].astype(F32)).astype(BF16)

        pltpu.emit_pipeline(hidden_back, grid=(nz,), in_specs=[wrow(ff), piece, piece], out_specs=[piece] * 2)(
            wd, sa, sb, dg, du
        )
        p_g, p_u = to_peer(dg, pdg), to_peer(du, pdu)
        acc[0:r, :] = jnp.zeros((r, d), F32)

        def norm_grad(dg_ref, du_ref, wg_ref, wu_ref):
            acc[0:r, :] += dot_tn(dg_ref[0], wg_ref[0]) + dot_tn(du_ref[0], wu_ref[0])

        pltpu.emit_pipeline(norm_grad, grid=(nz,), in_specs=[piece, piece, wrow(ff), wrow(ff)])(dg, du, wg, wu)
        for u in of(2):
            u.start_second()
        p_g.wait()
        ffn_grads(dg, pdg, n2h, pn_v, G[0])
        for u in of(0):
            u.start_first()
        p_u.wait()
        ffn_grads(du, pdu, n2h, pn_v, G[1])
        for u in of(1):
            u.start_first()

        def attention_back(dhb_v, dhbh, n1h, sdk, sdv, hb_v):
            dn = acc[0:r, :]
            hv = h_v[...]
            iv = inv_rms(hv)
            gp[1:2, :] = jnp.sum(dn * hv * iv, axis=0, keepdims=True)
            gdn = dn * gain2
            dh = c_v[...].astype(F32) + iv * gdn - hv * (iv * iv * iv * jnp.mean(hv * gdn, axis=1, keepdims=True))
            acc[0:r, :] = dh
            dhb_v[...] = dh.astype(BF16)
            ld = local(acc.at[pl.ds(0, r)], dh_o, 2)
            p_r = theirs(dhb_v, pdhb_v) + theirs(n1, pn1_v)
            keep_half(dhb_v, dhbh)
            ln = [local(lane_block(n1, e, core), n1h.at[:, pl.ds(e * 128, 128)], 8 + e) for e in range(nb)]

            def mixed_grad(w_ref, do_ref):
                do_ref[...] = dot_nt(dhb_v[...], w_ref[0]).astype(BF16)

            pltpu.emit_pipeline(mixed_grad, grid=(nz,), in_specs=[wrow(cols)], out_specs=[col(r)])(wo, do)
            for u in of(2):
                u.start_z()

            scale = HD**-0.5

            def attend_back(q_ref, k_ref, v_ref, mk_ref, mv_ref, o_ref, l_ref, do_ref, dq_ref, dk_ref, dv_ref):
                km = mk_ref[0].reshape(nm, HD)
                vm = mv_ref[0].reshape(nm, HD)
                sdk[...] = jnp.zeros_like(sdk)
                sdv[...] = jnp.zeros_like(sdv)
                for i in range(r // QT):
                    at = slice(i * QT, (i + 1) * QT)
                    k0 = halo * r - window + i * QT
                    ks = slice(k0, k0 + window + QT)
                    own = slice(halo * r + i * QT, halo * r + (i + 1) * QT)
                    qq, dd = q_ref[at, :], do_ref[at, :]
                    lse_c = l_ref[0, at, :]
                    delta = jnp.sum(dd.astype(F32) * o_ref[at, :].astype(F32), axis=1, keepdims=True)
                    ok = allowed_of(seg_q[at, :], seg_k[:, ks], halo * r + i * QT, k0)
                    pm = jnp.exp2(dot_nt(qq, km) * C2 - lse_c)
                    dsm = (pm * (dot_nt(dd, vm) - delta)).astype(BF16)
                    plo = jnp.where(ok, jnp.exp2(dot_nt(qq, k_ref[ks, :]) * C2 - lse_c), 0.0)
                    dsl = (plo * (dot_nt(dd, v_ref[ks, :]) - delta)).astype(BF16)
                    dqv = (dot_nn(dsm, km) + dot_nn(dsl, k_ref[ks, :])) * scale
                    dq_ref[at, :] = turn(dqv, cos_v[own, :], -sin_v[own, :]).astype(BF16)
                    sdk[ks, :] += dot_tn(dsl, qq)
                    sdv[ks, :] += dot_tn(plo.astype(BF16), dd)
                dk_ref[...] = turn(sdk[...] * scale, cos_v[...], -sin_v[...]).astype(BF16)
                dv_ref[...] = sdv[...].astype(BF16)

            def run_back(lo, n):
                pltpu.emit_pipeline(
                    attend_back,
                    grid=(n,),
                    in_specs=[head(r, lo), head(rt, lo), head(rt, lo), mem(lo), mem(lo), head(r, lo),
                              pl.BlockSpec((1, r, 1), lambda h: (h + lo, 0, 0)), head(r, lo)],
                    out_specs=[head(r, lo), head(rt, lo), head(rt, lo)],
                )(q, k, v, mk, mv, o, lse, do, dq, dk, dv)

            run_back(0, heads // 2)
            for m in p_r + ln:
                m.wait()

            def out_grads(a_ref, b_ref):
                u = pl.program_id(0)
                y = (dot_tn(a_ref[...], dhbh[...]) + dot_tn(b_ref[...], pdhb_v[...])).astype(BF16)
                for e in range(nb):
                    G[3][e, u] = y[:, e * 128 : (e + 1) * 128]

            pltpu.emit_pipeline(out_grads, grid=(nz,), in_specs=[col(r)] * 2)(o, po)
            for u in of(3):
                u.start_first()
            run_back(heads // 2, heads - heads // 2)
            p_att = [to_peer(dq, pdq), to_peer(dk, pdk), to_peer(dv, pdv)]
            for u in of(0):
                u.start_second()
            ld.wait()

            acc[...] = jnp.zeros_like(acc)

            def project_back(dq_ref, dk_ref, dv_ref, wq_ref, wk_ref, wv_ref):
                @pl.loop(0, halo + 1)
                def _(i):
                    at = pl.ds(pl.multiple_of(i * r, r), r)
                    acc[at, :] += dot_nt(dk_ref[at, :], wk_ref[...]) + dot_nt(dv_ref[at, :], wv_ref[...])

                acc[halo * r :, :] += dot_nt(dq_ref[...], wq_ref[...])

            pltpu.emit_pipeline(project_back, grid=(nz,), in_specs=[col(r), col(rt), col(rt)] + [wcol] * 3)(
                dq, dk, dv, wq, wk, wv
            )
            hb_v[...] = acc[: halo * r, :].astype(BF16)
            hd = []
            for j in range(halo):
                m = send(hb_v.at[pl.ds((halo - 1 - j) * r, r), :], more.at[j], hss.at[j], hrs.at[j], me,
                         (t + nz - 1 - j) % nz)
                hd.append(m)

                @pl.when(t >= j + 1)
                def _():
                    m.start()

            for u in of(1):
                u.start_second()
            for u in of(0):
                u.start_z()
            for u in of(3):
                u.start_second()
            for m in p_att:
                m.wait()

            own = pl.ds(halo * r, r)

            def grads_of(out, p0, p1, a0, a1):
                def body(x_ref, y_ref):
                    u = pl.program_id(0)
                    y = (dot_tn(a0[...], x_ref[...]) + dot_tn(a1[...], y_ref[...])).astype(BF16)
                    for e in range(nb):
                        out[e, u] = y[e * 128 : (e + 1) * 128, :]

                n = p0.shape[0]
                pltpu.emit_pipeline(body, grid=(nz,), in_specs=[col(n)] * 2)(p0, p1)

            grads_of(G[4], dq, pdq, n1h.at[own], pn1_v.at[own])
            grads_of(G[5], dk, pdk, n1h, pn1_v)
            for u in of(4, 5):
                u.start_first()
            grads_of(G[6], dv, pdv, n1h, pn1_v)
            for u in of(6):
                u.start_first()

            lx2 = local(x, c_v, 3)
            lx2.wait()
            vx = c_v[...].astype(F32)
            gp[0:1, :] = jnp.sum(acc[halo * r :, :] * vx * inv_rms(vx), axis=0, keepdims=True)
            for j in range(halo):

                @pl.when(t >= j + 1)
                def _():
                    cx = local(xh.at[j], n2_v, 4)
                    cx.wait()
                    vh = n2_v[...].astype(F32)
                    lo = (halo - 1 - j) * r
                    gp[0:1, :] = gp[0:1, :] + jnp.sum(acc[lo : lo + r, :] * vh * inv_rms(vh), axis=0, keepdims=True)

            zg = []
            for i in range(1, nz):
                m = send(gp, gz.at[i - 1], ass.at[i - 1], ars.at[i - 1], me, (t + i) % nz)
                m.start()
                zg.append(m)
            for u in of(1):
                u.start_z()
            for u in of(4, 5):
                u.start_second()

            def feed_out(hid_ref, wd_ref):
                h_v[...] += dot_tn(hid_ref[0], wd_ref[0])

            pltpu.emit_pipeline(feed_out, grid=(nz,), in_specs=[piece, wrow(ff)])(hid, wd)
            lo_ = local(h_v, block_out, 5)
            for u in of(6):
                u.start_second()
            for u in of(3):
                u.start_z()
            for m in zg:
                m.wait()
            tot = gp[...]
            for i in range(nz - 1):
                tot = tot + gz[i]
            for e in range(dp):
                gs[e] = tot[:, e * 128 : (e + 1) * 128]
            ds_ = []
            for i in range(1, dp):
                to = (me + i) % dp
                m = send(gs.at[to], gd.at[me], dss.at[i], drs.at[i], to, t)
                m.start()
                ds_.append(m)
            og = pltpu.make_async_copy(gs.at[me], gd.at[me], dss.at[0])
            og.start()
            for u in of(4, 5):
                u.start_z()

            lo_.wait()
            ld2 = local(dh_o, h_v, 6)
            for j, m in enumerate(hd):

                @pl.when(t + j + 1 < nz)
                def _():
                    m.wait_recv()
                    acc[halo * r :, :] = acc[halo * r :, :] + more[j].astype(F32)

                @pl.when(t >= j + 1)
                def _():
                    m.wait_send()

            ld2.wait()
            vx = c_v[...].astype(F32)
            iv = inv_rms(vx)
            gdx = acc[halo * r :, :] * gain_row(gn_v, 0)
            acc[halo * r :, :] = h_v[...] + iv * gdx - vx * (iv * iv * iv * jnp.mean(vx * gdx, axis=1, keepdims=True))
            lg = local(acc.at[pl.ds(halo * r, r)], grad_in, 7)
            for u in of(6):
                u.start_z()
            og.wait()
            for m in ds_:
                m.wait()
            tot = gd[0]
            for e in range(1, dp):
                tot = tot + gd[e]
            gout[...] = tot
            for u in us:
                u.finish()
            lg.wait()

        pl.run_scoped(
            attention_back,
            pltpu.VMEM((r, d), BF16),
            pltpu.VMEM((r, half), BF16),
            pltpu.VMEM((rt, half), BF16),
            pltpu.VMEM((rt, HD), F32),
            pltpu.VMEM((rt, HD), F32),
            pltpu.VMEM((halo * r, d), BF16),
        )

    pieces = [o_.shape for o_ in outs]
    pl.run_scoped(
        rest,
        pltpu.VMEM((r, d), F32),
        pltpu.VMEM((r, d), BF16),
        pltpu.VMEM((r, d), BF16),
        pltpu.VMEM((r, half), BF16),
        pltpu.VMEM((r, half), BF16),
        pltpu.VMEM((rt, d), F32),
        *[pltpu.VMEM((nb, nz) + tuple(p), BF16) for p in pieces],
    )


def run_layer(g, cap, halo, window, requests, sel, seg_q, seg_k, x, gains, mem_k, mem_v, cot, shards, nq, ksel):
    blk, cols = mem_k.shape[1:]
    r, d = x.shape
    rt = (halo + 1) * r
    nz, dp = g.nz, g.dp
    half = d // 2
    kd, ff = shards[0].shape[0], shards[4].shape[0]
    heads = d // HD
    tab1, tab2 = (jnp.asarray(v) for v in rope_tables(halo, nz, r))
    gunits = []
    for w, s in enumerate(shards):
        n, lanes_ = s.shape[0], w >= 3
        if w in (0, 4):
            gunits.append((w, (0, n), True, lanes_))
        elif w in (1, 5):
            gunits.append((w, (0, n), False, lanes_))
        else:
            gunits.append((w, (0, n // 2), True, lanes_))
            gunits.append((w, (n // 2, n - n // 2), False, lanes_))
    pieces = [(ff, 128)] * 3 + [(cols, 128)] + [(kd, cols)] * 3
    sunits = []
    for w in (2, 0, 1, 3):
        n = pieces[w][0]
        sunits += [(w, (0, n // 2), True), (w, (n // 2, n - n // 2), False)]
    sunits += [(4, (0, kd), True), (5, (0, kd), False), (6, (0, kd // 2), True), (6, (kd // 2, kd - kd // 2), False)]
    any_ = pl.BlockSpec(memory_space=pl.ANY)
    vm = pl.BlockSpec(memory_space=pltpu.VMEM)
    dma = lambda *n: pltpu.SemaphoreType.DMA(n)
    st = lambda s, dt=BF16: jax.ShapeDtypeStruct(s, dt)
    nsem = len(gunits) * gather_sems(g)
    hbm = (
        [st((d, d))] * 3 + [st((nz, cols, d))] + [st((nz, ff, d))] * 3
        + [st((halo, r, d))] + [st((nz, ksel, blk, cols))] * 2 + [st((dp * cap, blk, cols))] * 2
        + [st((rt, d)), st((r, d)), st((rt, d)), st((rt, d)), st((r, d)), st((heads, r, 1), F32)]
        + [st((nz, ff, r))] * 8 + [st((r, d)), st((r, d)), st((rt, d)), st((rt, d))]
        + [st((r, d)), st((rt, d)), st((rt, d)), st((r, d)), st((r, d), F32)]
    )
    out_shape = [st((2, 128), F32)] + [st(p, F32) for p in pieces] + [st((r, d), F32)] * 2 + hbm
    scratch = [pltpu.VMEM((dp, 8, 128), jnp.int32), pltpu.SMEM((dp, 8, 128), jnp.int32), pltpu.VMEM((dp, 2, 128), F32)]
    scratch += [pltpu.VMEM((rt, HD), F32)] * 2
    for w, (lo, n), bf in sunits:
        cc = pieces[w][1]
        n1_, n2_ = (g.nb, g.na) if bf else (g.na, g.nb)
        scratch += [
            pltpu.VMEM((n1_ - 1, n2_, nz, n, cc), BF16),
            pltpu.VMEM((n2_ - 1, nz, n, cc), BF16),
            pltpu.VMEM((nz - 1, n, cc), BF16),
        ]
    scratch += [dma(scatter_sems(g))] * (2 * len(sunits))
    scratch += [pltpu.VMEM((r, half), BF16)] * 2 + [pltpu.VMEM((rt, half), BF16), pltpu.VMEM((r, half), BF16)]
    scratch += [pltpu.VMEM((halo, r, d), BF16)]
    scratch += [pltpu.VMEM((nz - 1, 2, d), F32), pltpu.VMEM((dp, 2, 128), F32), pltpu.VMEM((dp, 2, 128), F32), pltpu.VMEM((2, d), F32)]
    ncore = 7 + 4 * (dp // 2)
    scratch += [dma(nsem), dma(nsem), dma(8 + dp // 2), dma(dp), dma(dp), dma(dp), dma(dp), dma(2, dp), dma(2, dp)]
    scratch += [dma(2, nz), dma(2, nz), dma(halo), dma(halo)]
    scratch += [dma(ncore), dma(ncore), dma(halo), dma(halo), dma(nz), dma(nz), dma(dp), dma(dp)]
    cfg = (cap, nq, ksel, halo, window, gunits, sunits)
    return pl.pallas_call(
        functools.partial(layer_kernel, g, cfg),
        out_shape=out_shape,
        in_specs=[vm, pl.BlockSpec(memory_space=pltpu.SMEM), vm, vm, vm, vm] + [any_] * (5 + len(shards)),
        out_specs=[vm] * 8 + [any_] * (2 + len(hbm)),
        scratch_shapes=scratch,
        compiler_params=pltpu.CompilerParams(collective_id=0, has_side_effects=True, vmem_limit_bytes=67043328),
        name="layer",
    )(requests, sel, seg_q, seg_k, tab1, tab2, x, gains, mem_k, mem_v, cot, *shards)


HEADS = 8
QB = 512


def normalize(field, gain_vec):
    return field * lax.rsqrt(jnp.mean(field * field, axis=-1, keepdims=True) + EPSILON) * gain_vec


def rotate(field, heads_here):
    row_total = field.shape[0]
    head_size = field.shape[1] // heads_here
    half_width = head_size // 2
    frequencies = 10000.0 ** (-jnp.arange(half_width, dtype=jnp.float32) * 2.0 / head_size)
    angles = jnp.arange(row_total, dtype=jnp.float32)[:, None] * frequencies[None, :]
    cosine = jnp.cos(angles)[:, None, :]
    sine_table = jnp.sin(angles)[:, None, :]
    split_heads = field.reshape(row_total, heads_here, head_size)
    first_half = split_heads[..., :half_width]
    second_half = split_heads[..., half_width:]
    turned = jnp.concatenate(
        [
            first_half * cosine - second_half * sine_table,
            second_half * cosine + first_half * sine_table,
        ],
        axis=-1,
    )
    return turned.reshape(row_total, heads_here * head_size)


def contract_rows(left, right):
    return lax.dot_general(
        left, right, (((0,), (0,)), ((), ())), preferred_element_type=jnp.float32
    )


def against(left, right):
    return lax.dot_general(
        left, right, (((1,), (1,)), ((), ())), preferred_element_type=jnp.float32
    )


def spread_rows(local_rows, matrices):
    piece_rows = lax.all_gather(local_rows, "tensor", axis=0, tiled=True)
    return jnp.concatenate(
        [jnp.dot(piece_rows, matrix, preferred_element_type=jnp.float32) for matrix in matrices],
        axis=1,
    )


def reduce_rows(left, right):
    return lax.psum_scatter(
        jnp.dot(left, right, preferred_element_type=jnp.float32).astype(jnp.bfloat16),
        "tensor",
        scatter_dimension=0,
        tiled=True,
    ).astype(jnp.float32)


def return_rows(pairs):
    summed = against(pairs[0][0], pairs[0][1])
    for grad_block, matrix in pairs[1:]:
        summed = summed + against(grad_block, matrix)
    return lax.psum_scatter(
        summed.astype(jnp.bfloat16), "tensor", scatter_dimension=0, tiled=True
    ).astype(jnp.float32)


def weight_grads(local_rows, grads_list):
    piece_rows = lax.all_gather(local_rows, "tensor", axis=0, tiled=True)
    return tuple((contract_rows(piece_rows, grad_one) for grad_one in grads_list))


def all_rows(local_grad):
    return lax.all_gather(local_grad, "tensor", axis=0, tiled=True)


def on_device_any(
    block_in,
    segments,
    retrieved,
    partner,
    memory_keys,
    memory_values,
    gain_attn,
    w_query,
    w_key,
    w_value,
    w_out,
    gain_ffn,
    w_gate,
    w_up,
    w_down,
    cotangent,
):
    tensor_size = lax.axis_size("tensor")
    dp_size = lax.axis_size("dp")
    heads_here = HEADS // tensor_size
    head_width = heads_here * HD
    score_scale = HD ** (-0.5)
    seq_len = segments.shape[1]
    query_blocks = seq_len // QB
    stream_in = block_in[0].astype(jnp.float32)
    seg_row = segments[0]
    positions = jnp.arange(seq_len)
    gathered = (
        lax.all_gather(gain_attn, "dp", axis=0, tiled=True),
        lax.all_gather(w_query, "dp", axis=0, tiled=True),
        lax.all_gather(w_key, "dp", axis=0, tiled=True),
        lax.all_gather(w_value, "dp", axis=0, tiled=True),
        lax.all_gather(w_out, "dp", axis=1, tiled=True),
        lax.all_gather(gain_ffn, "dp", axis=0, tiled=True),
        lax.all_gather(w_gate, "dp", axis=0, tiled=True),
        lax.all_gather(w_up, "dp", axis=0, tiled=True),
        lax.all_gather(w_down, "dp", axis=1, tiled=True),
    )
    gain_one, query_w, key_w, value_w, out_w, gain_two, gate_w, up_w, down_w = gathered
    wanted = retrieved[0].reshape(-1)
    request_total = wanted.shape[0]
    capacity = max(2, (2 * request_total + dp_size - 1) // dp_size)
    blocks_dev = memory_keys.shape[1]
    from_partner = wanted // MEMB
    block_index = wanted % MEMB
    owner_dev = block_index // blocks_dev
    local_block = block_index % blocks_dev
    seq_id = jnp.where(from_partner == 0, lax.axis_index("dp"), partner[0])
    owner_hits = (owner_dev[:, None] == jnp.arange(dp_size)[None, :]).astype(jnp.int32)
    slot_index = jnp.sum((jnp.cumsum(owner_hits, axis=0) - 1) * owner_hits, axis=1)
    requests = (
        jnp.zeros((dp_size, capacity, 2), jnp.int32)
        .at[owner_dev, slot_index]
        .set(jnp.stack([seq_id, local_block], axis=-1))
    )
    received = lax.all_to_all(requests, "dp", split_axis=0, concat_axis=0, tiled=True)
    picked_keys = memory_keys[received[..., 0], received[..., 1]]
    picked_values = memory_values[received[..., 0], received[..., 1]]
    fetched_keys = lax.all_to_all(picked_keys, "dp", split_axis=0, concat_axis=0, tiled=True)
    fetched_values = lax.all_to_all(picked_values, "dp", split_axis=0, concat_axis=0, tiled=True)
    memory_k = fetched_keys[owner_dev, slot_index].reshape(query_blocks, -1, heads_here, HD)
    memory_v = fetched_values[owner_dev, slot_index].reshape(query_blocks, -1, heads_here, HD)
    normed = normalize(stream_in, gain_one.astype(jnp.float32)).astype(jnp.bfloat16)
    qkv_rows = spread_rows(normed, [query_w, key_w, value_w])
    query_raw = qkv_rows[:, :head_width]
    key_raw = qkv_rows[:, head_width : 2 * head_width]
    queries = rotate(query_raw, heads_here).astype(jnp.bfloat16)
    keys_all = rotate(key_raw, heads_here).astype(jnp.bfloat16).reshape(seq_len, heads_here, HD)
    values_all = qkv_rows[:, 2 * head_width :].astype(jnp.bfloat16).reshape(seq_len, heads_here, HD)
    query_tiles = queries.reshape(query_blocks, QB, heads_here, HD)
    seg_tiles = seg_row.reshape(query_blocks, QB)
    pos_tiles = positions.reshape(query_blocks, QB)

    def scores_of(query_blk, seg_blk, pos_blk, key_mem):
        local_scores = jnp.einsum(
            "qhd,khd->hqk", query_blk, keys_all, preferred_element_type=jnp.float32
        )
        memory_scores = jnp.einsum(
            "qhd,khd->hqk", query_blk, key_mem, preferred_element_type=jnp.float32
        )
        raw_scores = jnp.concatenate([local_scores, memory_scores], axis=-1) * score_scale
        allowed = (seg_blk[:, None] == seg_row[None, :]) & (positions[None, :] <= pos_blk[:, None])
        allowed = jnp.concatenate(
            [allowed, jnp.ones((query_blk.shape[0], key_mem.shape[0]), dtype=jnp.bool_)], axis=1
        )
        return (raw_scores, allowed)

    def forward_block(pieces):
        query_blk, seg_blk, pos_blk, key_mem, value_mem = pieces
        raw_scores, allowed = scores_of(query_blk, seg_blk, pos_blk, key_mem)
        masked = jnp.where(allowed[None], raw_scores, MASKED)
        row_max = jnp.max(masked, axis=-1, keepdims=True)
        expo = jnp.exp(masked - row_max)
        row_total = jnp.sum(expo, axis=-1, keepdims=True)
        weights_soft = (expo / row_total).astype(jnp.bfloat16)
        values_both = jnp.concatenate([values_all, value_mem], axis=0)
        result = jnp.einsum(
            "hqk,khd->qhd", weights_soft, values_both, preferred_element_type=jnp.float32
        )
        return (result, (row_max + jnp.log(row_total))[..., 0])

    attended, log_totals = lax.map(
        forward_block, (query_tiles, seg_tiles, pos_tiles, memory_k, memory_v)
    )
    mixed = attended.reshape(seq_len, head_width).astype(jnp.bfloat16)
    stream = stream_in + reduce_rows(mixed, out_w)
    normed_ffn = normalize(stream, gain_two.astype(jnp.float32)).astype(jnp.bfloat16)
    gate_up = spread_rows(normed_ffn, [gate_w, up_w])
    hidden_width = gate_w.shape[1]
    gate_pre = gate_up[:, :hidden_width]
    up_pre = gate_up[:, hidden_width:]
    hidden = (jax.nn.silu(gate_pre) * up_pre).astype(jnp.bfloat16)
    block_out = stream + reduce_rows(hidden, down_w)
    gathered_back = (
        lax.all_gather(gain_attn, "dp", axis=0, tiled=True),
        lax.all_gather(w_query, "dp", axis=0, tiled=True),
        lax.all_gather(w_key, "dp", axis=0, tiled=True),
        lax.all_gather(w_value, "dp", axis=0, tiled=True),
        lax.all_gather(w_out, "dp", axis=1, tiled=True),
        lax.all_gather(gain_ffn, "dp", axis=0, tiled=True),
        lax.all_gather(w_gate, "dp", axis=0, tiled=True),
        lax.all_gather(w_up, "dp", axis=0, tiled=True),
        lax.all_gather(w_down, "dp", axis=1, tiled=True),
    )
    gain_one, query_w, key_w, value_w, out_w, gain_two, gate_w, up_w, down_w = gathered_back
    dout_rows = cotangent[0]

    def gated(gate_in, up_in):
        return jax.nn.silu(gate_in) * up_in

    dout_full = all_rows(dout_rows)
    grad_down = contract_rows(hidden, dout_full)
    d_hidden = against(dout_full, down_w)
    gated_value, pull_gated = jax.vjp(gated, gate_pre, up_pre)
    d_gate, d_up = pull_gated(d_hidden)
    d_gate = d_gate.astype(jnp.bfloat16)
    d_up = d_up.astype(jnp.bfloat16)
    d_norm_ffn = return_rows([(d_gate, gate_w), (d_up, up_w)])
    grad_gate, grad_up = weight_grads(normed_ffn, [d_gate, d_up])
    norm_value, pull_norm_ffn = jax.vjp(normalize, stream, gain_two.astype(jnp.float32))
    d_stream_norm, grad_gain_ffn = pull_norm_ffn(d_norm_ffn)
    d_stream = dout_rows.astype(jnp.float32) + d_stream_norm
    d_stream_full = all_rows(d_stream.astype(jnp.bfloat16))
    grad_out = contract_rows(mixed, d_stream_full)
    d_mixed = against(d_stream_full, out_w).astype(jnp.bfloat16)
    d_mixed_tiles = d_mixed.reshape(query_blocks, QB, heads_here, HD)

    def backward_block(carry_sums, pieces):
        key_sum, value_sum = carry_sums
        query_blk, seg_blk, pos_blk, key_mem, value_mem, log_blk, grad_blk = pieces
        raw_scores, allowed = scores_of(query_blk, seg_blk, pos_blk, key_mem)
        probs = jnp.where(allowed[None], jnp.exp(raw_scores - log_blk[..., None]), 0.0)
        values_both = jnp.concatenate([values_all, value_mem], axis=0)
        d_probs = jnp.einsum(
            "qhd,khd->hqk", grad_blk, values_both, preferred_element_type=jnp.float32
        )
        shared = jnp.sum(probs * d_probs, axis=-1, keepdims=True)
        d_scores = (probs * (d_probs - shared)).astype(jnp.bfloat16)
        probs_low = probs.astype(jnp.bfloat16)
        keys_both = jnp.concatenate([keys_all, key_mem], axis=0)
        d_query = (
            jnp.einsum("hqk,khd->qhd", d_scores, keys_both, preferred_element_type=jnp.float32)
            * score_scale
        )
        key_sum = (
            key_sum
            + jnp.einsum(
                "hqk,qhd->khd",
                d_scores[..., :seq_len],
                query_blk,
                preferred_element_type=jnp.float32,
            )
            * score_scale
        )
        value_sum = value_sum + jnp.einsum(
            "hqk,qhd->khd", probs_low[..., :seq_len], grad_blk, preferred_element_type=jnp.float32
        )
        return ((key_sum, value_sum), d_query)

    zero_grads = jnp.zeros((seq_len, heads_here, HD), jnp.float32)
    (d_keys, d_values), d_queries = lax.scan(
        backward_block,
        (zero_grads, zero_grads),
        (query_tiles, seg_tiles, pos_tiles, memory_k, memory_v, log_totals, d_mixed_tiles),
    )

    def turn(field):
        return rotate(field, heads_here)

    turned_value, pull_turn = jax.vjp(turn, query_raw)
    d_query_raw = pull_turn(d_queries.reshape(seq_len, head_width))[0].astype(jnp.bfloat16)
    d_key_raw = pull_turn(d_keys.reshape(seq_len, head_width))[0].astype(jnp.bfloat16)
    d_value_raw = d_values.reshape(seq_len, head_width).astype(jnp.bfloat16)
    d_norm_attn = return_rows([(d_query_raw, query_w), (d_key_raw, key_w), (d_value_raw, value_w)])
    grad_query, grad_key, grad_value = weight_grads(normed, [d_query_raw, d_key_raw, d_value_raw])
    norm_first, pull_norm_attn = jax.vjp(normalize, stream_in, gain_one.astype(jnp.float32))
    d_input_norm, grad_gain_attn = pull_norm_attn(d_norm_attn)
    grad_in = d_stream + d_input_norm
    grad_gain_attn, grad_gain_ffn = lax.psum((grad_gain_attn, grad_gain_ffn), "tensor")
    results = (
        lax.psum_scatter(
            grad_gain_attn.astype(jnp.bfloat16), "dp", scatter_dimension=0, tiled=True
        ).astype(jnp.float32),
        lax.psum_scatter(
            grad_query.astype(jnp.bfloat16), "dp", scatter_dimension=0, tiled=True
        ).astype(jnp.float32),
        lax.psum_scatter(
            grad_key.astype(jnp.bfloat16), "dp", scatter_dimension=0, tiled=True
        ).astype(jnp.float32),
        lax.psum_scatter(
            grad_value.astype(jnp.bfloat16), "dp", scatter_dimension=0, tiled=True
        ).astype(jnp.float32),
        lax.psum_scatter(
            grad_out.astype(jnp.bfloat16), "dp", scatter_dimension=1, tiled=True
        ).astype(jnp.float32),
        lax.psum_scatter(
            grad_gain_ffn.astype(jnp.bfloat16), "dp", scatter_dimension=0, tiled=True
        ).astype(jnp.float32),
        lax.psum_scatter(
            grad_gate.astype(jnp.bfloat16), "dp", scatter_dimension=0, tiled=True
        ).astype(jnp.float32),
        lax.psum_scatter(
            grad_up.astype(jnp.bfloat16), "dp", scatter_dimension=0, tiled=True
        ).astype(jnp.float32),
        lax.psum_scatter(
            grad_down.astype(jnp.bfloat16), "dp", scatter_dimension=1, tiled=True
        ).astype(jnp.float32),
    )
    return (block_out[None], grad_in[None]) + results


def on_device(*args):
    x, dp = args[0], lax.axis_size("dp")
    side = math.isqrt(dp // 2)
    if 2 * side * side == dp and x.shape[2] % (128 * dp) == 0:
        return on_device_rows(*args)
    return on_device_any(*args)


def on_device_rows(
    block_in, segments, retrieved, partner, memory_keys, memory_values,
    gain_attn, w_query, w_key, w_value, w_out, gain_ffn, w_gate, w_up, w_down, cotangent,
):
    g = Grid(lax.axis_size("dp"), lax.axis_size("tensor"))
    t, me = lax.axis_index("tensor"), lax.axis_index("dp")
    x, c = block_in[0], cotangent[0]
    r, d = x.shape
    seq_len = segments.shape[1]
    window = seq_len // 4
    halo = -(-window // r)
    nq, ksel = retrieved.shape[1:]
    cap = max(2, -(-2 * nq * ksel // g.dp))
    req, sel = plan_requests(retrieved[0], partner[0], g.dp, memory_keys.shape[1], cap)
    gains = jnp.stack([gain_attn, gain_ffn]).astype(F32)
    flat = lambda m: m.reshape((-1,) + m.shape[2:])
    shards = [w_query, w_key, w_value, w_out, w_gate.T, w_up.T, w_down]
    padded = jnp.concatenate([jnp.full((halo * r,), -1, jnp.int32), segments[0]])
    seg = lax.dynamic_slice(padded, (t * r,), ((halo + 1) * r,))
    seg_k, seg_q = seg[None, :], seg[halo * r :, None]
    gout, o_gate, o_up, o_down, o_out, o_q, o_k, o_v, block_out, grad_in = run_layer(
        g, cap, halo, window, req, sel, seg_q, seg_k, x, gains, flat(memory_keys), flat(memory_values), c, shards, nq, ksel
    )[:10]
    return (
        block_out[None], grad_in[None], gout[0], o_q, o_k, o_v, o_out, gout[1], o_gate.T, o_up.T, o_down,
    )


def solution(mesh):
    return jax.shard_map(
        on_device,
        mesh=mesh,
        in_specs=(
            P("dp", "tensor", None), P("dp", None), P("dp", None, None), P("dp"),
            P(None, "dp", None, "tensor"), P(None, "dp", None, "tensor"),
            P("dp"), P("dp", "tensor"), P("dp", "tensor"), P("dp", "tensor"), P("tensor", "dp"),
            P("dp"), P("dp", "tensor"), P("dp", "tensor"), P("tensor", "dp"), P("dp", "tensor", None),
        ),
        out_specs=(
            P("dp", "tensor", None), P("dp", "tensor", None),
            P("dp"), P("dp", "tensor"), P("dp", "tensor"), P("dp", "tensor"), P("tensor", "dp"),
            P("dp"), P("dp", "tensor"), P("dp", "tensor"), P("tensor", "dp"),
        ),
        check_vma=False,
    )
```

```python
import functools
import math

import jax
import jax.numpy as jnp
import numpy as np
from jax import lax
from jax.experimental import pallas as pl
from jax.experimental.pallas import tpu as pltpu
from jax.sharding import PartitionSpec as P
MESH = pl.DeviceIdType.MESH
MEMB = 128


class Grid:
    def __init__(self, dp, tensor):
        side = math.isqrt(dp // 2)
        assert side * side * 2 == dp
        self.na, self.nb, self.nc, self.nz, self.dp = side, side, 2, tensor, dp


def coords(g):
    me = lax.axis_index("dp")
    t = lax.axis_index("tensor")
    return me // (2 * g.nb), (me // 2) % g.nb, me % 2, t, me


def send(src, dst, ssem, rsem, dp, t):
    return pltpu.make_async_remote_copy(
        src_ref=src, dst_ref=dst, send_sem=ssem, recv_sem=rsem, device_id=(dp, t), device_id_type=MESH
    )


class Copy:
    def __init__(self, make):
        self.make = make

    def start(self):
        self.make().start()

    def wait(self):
        self.make().wait()

    def wait_send(self):
        self.make().wait_send()

    def wait_recv(self):
        self.make().wait_recv()


def greet(g, me, t):
    bar = pltpu.get_barrier_semaphore()
    for k in range(1, g.dp):
        pl.semaphore_signal(bar, inc=1, device_id=((me + k) % g.dp, t), device_id_type=MESH)
    for k in range(1, g.nz):
        pl.semaphore_signal(bar, inc=1, device_id=(me, (t + k) % g.nz), device_id_type=MESH)
    pl.semaphore_wait(bar, g.dp - 1 + g.nz - 1)


class Gather:
    def __init__(self, g, shard, buf, rows, b_first, lanes, sems, base):
        self.g, self.shard, self.buf, self.rows, self.b_first, self.lanes = g, shard, buf, rows, b_first, lanes
        self.sems, self.count, self.base = sems, 0, base
        lo, n = rows
        nz = g.nz
        n1, n2 = (g.nb, g.na) if b_first else (g.na, g.nb)
        bind = functools.partial
        shard_rows = lambda: shard.at[pl.ds(lo, n), :]
        tensor = lambda: lax.axis_index("tensor")

        def here():
            a, b, c, t, me = coords(g)
            return self.at(me, t)

        def passed(k):
            a, b, c, t, me = coords(g)
            return self.at(me, (t + nz - 2 * k) % nz)

        def far(k):
            a, b, c, t, me = coords(g)
            return me, (t + 2 * k) % nz

        def pair():
            a, b, c, t, me = coords(g)
            return me, t + 1 - 2 * (t % 2)

        def other_core():
            a, b, c, t, me = coords(g)
            return me + 1 - 2 * c, t

        slab = lambda k1, k2: bind(lambda k1, k2: self.at(self._slot(k1, k2)), k1, k2)
        to1 = lambda k: (self._slot(n1 - k, 0), tensor())
        to2 = lambda k: (self._slot(0, n2 - k), tensor())
        self.far = [self._copy(shard_rows, here, bind(far, k)) for k in range(1, nz // 2)]
        self.near = [self._copy(shard_rows, here, pair)]
        self.relayed = [self._copy(bind(passed, k), bind(passed, k), pair) for k in range(1, nz // 2)]
        i = self._sem()
        self.own = Copy(lambda: pltpu.make_async_copy(shard_rows(), here(), sems[0].at[i]))
        self.first = [self._copy(slab(0, 0), slab(0, 0), bind(to1, k)) for k in range(1, n1)]
        self.second = [
            self._copy(slab(k1, 0), slab(k1, 0), bind(to2, k)) for k1 in range(n1) for k in range(1, n2)
        ]
        core = lambda k1, k2: self._copy(slab(k1, k2), slab(k1, k2), other_core)
        self.core0 = [core(0, 0)]
        self.core1 = [core(k1, 0) for k1 in range(1, n1)]
        self.core2 = [core(k1, k2) for k1 in range(n1) for k2 in range(1, n2)]

    def at(self, dp, t=None):
        lo, n = self.rows
        if self.lanes:
            width = self.shard.shape[1]
            col = pl.ds(pl.multiple_of(dp * width, 128), width)
            return self.buf.at[slice(None) if t is None else t, pl.ds(lo, n), col]
        depth, width = self.shard.shape
        row = pl.ds(pl.multiple_of(dp * depth + lo, 16), n)
        return self.buf.at[row, slice(None) if t is None else pl.ds(pl.multiple_of(t * width, 128), width)]

    def _sem(self):
        i = self.base + self.count
        self.count += 1
        return i

    def _copy(self, src, dst, to):
        i = self._sem()
        return Copy(lambda: send(src(), dst(), self.sems[0].at[i], self.sems[1].at[i], *to()))

    def _slot(self, k1, k2):
        g = self.g
        a, b, c, t, me = coords(g)
        if self.b_first:
            return (((a + g.na - k2) % g.na) * g.nb + (b + g.nb - k1) % g.nb) * 2 + c
        return (((a + g.na - k1) % g.na) * g.nb + (b + g.nb - k2) % g.nb) * 2 + c

    def start_z(self):
        for m in self.far + self.near + [self.own]:
            m.start()

    def relay_z(self):
        for m, n in zip(self.far, self.relayed):
            m.wait_recv()
            n.start()

    def start_first(self):
        self.own.wait()
        for m in self.near + self.relayed:
            m.wait_recv()
        for m in self.first + self.core0:
            m.start()

    def start_second(self):
        for m in self.first:
            m.wait_recv()
        for m in self.second + self.core1:
            m.start()

    def start_core(self):
        for m in self.second:
            m.wait_recv()
        for m in self.core2:
            m.start()

    def finish(self):
        core = self.core0 + self.core1 + self.core2
        for m in core:
            m.wait_recv()
        for m in self.far + self.near + self.relayed + self.first + self.second + core:
            m.wait_send()


def gather_sems(g):
    return g.nz + (g.na - 1) + g.na * (g.na - 1) + g.na * g.nb


def plan_requests(retrieved, partner, dp_size, blocks_dev, cap):
    wanted = retrieved.reshape(-1)
    n = wanted.shape[0]
    from_partner = wanted // MEMB
    block_index = wanted % MEMB
    owner = block_index // blocks_dev
    local = block_index % blocks_dev
    seq = jnp.where(from_partner == 0, lax.axis_index("dp"), partner)
    flat = seq * blocks_dev + local
    i = jnp.arange(n)
    slot = jnp.sum(((owner[:, None] == owner[None, :]) & (i[None, :] < i[:, None])).astype(jnp.int32), axis=1)
    hit = (owner[None, None, :] == jnp.arange(dp_size)[:, None, None]) & (
        slot[None, None, :] == jnp.arange(128)[None, :, None]
    )
    req = jnp.sum(jnp.where(hit, flat[None, None, :], 0), axis=2)
    return jnp.broadcast_to(req[:, None, :], (dp_size, 8, 128)).astype(jnp.int32), (owner * cap + slot).astype(jnp.int32)


HD = 128
EPSILON = 1e-05
MASKED = -1e30
F32, BF16 = jnp.float32, jnp.bfloat16


def dot_nn(x, y):
    return lax.dot_general(x, y, (((1,), (0,)), ((), ())), preferred_element_type=F32)


def dot_nt(x, y):
    return lax.dot_general(x, y, (((1,), (1,)), ((), ())), preferred_element_type=F32)


def dot_tn(x, y):
    return lax.dot_general(x, y, (((0,), (0,)), ((), ())), preferred_element_type=F32)


def inv_rms(v):
    return lax.rsqrt(jnp.mean(v * v, axis=-1, keepdims=True) + EPSILON)


def gain_row(gains_ref, which):
    n = gains_ref.shape[0]
    return jnp.concatenate([gains_ref[d, which : which + 1, :] for d in range(n)], axis=1)


def turn(v, cos, sin):
    return v * cos + pltpu.roll(v, HD // 2, axis=1) * sin


def lanes(ref):
    return jnp.concatenate([ref[d, 0] for d in range(ref.shape[0])], axis=1)


def rows(ref):
    return jnp.concatenate([ref[d, 0] for d in range(ref.shape[0])], axis=0)


VL = 60 * 2**20


def full(shape, buffers=None):
    n = len(shape)
    kw = {} if buffers is None else dict(pipeline_mode=pl.Buffered(buffers))
    return pl.BlockSpec(shape, lambda *i: (0,) * n, **kw)


def allowed_of(seg_q, seg_k, q0, k0):
    n, m = seg_q.shape[0], seg_k.shape[1]
    qp = lax.broadcasted_iota(jnp.int32, (n, m), 0) + q0
    kp = lax.broadcasted_iota(jnp.int32, (n, m), 1) + k0
    return (seg_q == seg_k) & (kp <= qp)


QT = 256
C2 = HD**-0.5 * math.log2(math.e)


class Scatter:
    def __init__(self, g, src, rows, b_first, bufs, sems, out):
        self.g, self.src, self.rows, self.b_first, self.out = g, src, rows, b_first, out
        self.r1, self.r2, self.r3 = bufs
        self.sems, self.count = sems, 0
        n1, n2 = self._mine()[5:]
        nz = g.nz
        lo, n = rows
        bind = functools.partial
        at = lambda e, t: src.at[e, t, pl.ds(lo, n), :]

        def src1(k, j):
            f = self._mine()[0]
            return at(self._e((f + k) % n1, j), slice(None))

        def to1(k):
            f, s, c, t = self._mine()[:4]
            return self._e((f + k) % n1, s) * 2 + c, t

        def src2(k):
            f, s = self._mine()[:2]
            return at(self._e(f, (s + k) % n2), slice(None))

        def to2(k):
            f, s, c, t = self._mine()[:4]
            return self._e(f, (s + k) % n2) * 2 + c, t

        def src_near(k):
            f, s, c, t = self._mine()[:4]
            return at(self._e(f, s), (t + 1 - 2 * (t % 2) + 2 * k) % nz)

        def to_near():
            t, me = self._mine()[3:5]
            return me, t + 1 - 2 * (t % 2)

        def src_far(k):
            f, s, c, t = self._mine()[:4]
            return at(self._e(f, s), (t + 2 * k) % nz)

        def to_far(k):
            t, me = self._mine()[3:5]
            return me, (t + 2 * k) % nz

        land = lambda ref, *i: bind(lambda ref, i: ref.at[i], ref, i)
        self.first = [
            self._copy(bind(src1, k, j), land(self.r1, k - 1, j), bind(to1, k)) for k in range(1, n1) for j in range(n2)
        ]
        self.second = [self._copy(bind(src2, k), land(self.r2, k - 1), bind(to2, k)) for k in range(1, n2)]
        self.near = [self._copy(bind(src_near, k), land(self.r3, k), to_near) for k in range(nz // 2)]
        self.far = [
            self._copy(bind(src_far, k), land(self.r3, nz // 2 + k - 1), bind(to_far, k)) for k in range(1, nz // 2)
        ]

    def _copy(self, src, dst, to):
        i = self.count
        self.count += 1
        return Copy(lambda: send(src(), dst(), self.sems[0].at[i], self.sems[1].at[i], *to()))

    def _e(self, f, s):
        return s * self.g.nb + f if self.b_first else f * self.g.nb + s

    def _mine(self):
        a, b, c, t, me = coords(self.g)
        f, s = (b, a) if self.b_first else (a, b)
        n1, n2 = (self.g.nb, self.g.na) if self.b_first else (self.g.na, self.g.nb)
        return f, s, c, t, me, n1, n2

    def _add(self, e, u, more):
        lo, n = self.rows
        v = self.src[e, u, lo : lo + n, :].astype(F32)
        for m in more:
            v = v + m.astype(F32)
        self.src[e, u, lo : lo + n, :] = v.astype(BF16)

    def start_first(self):
        for m in self.first:
            m.start()

    def start_second(self):
        f, s, c, t, me, n1, n2 = self._mine()
        for m in self.first:
            m.wait_recv()
        for j in range(n2):

            @pl.loop(0, self.g.nz)
            def _(u):
                self._add(self._e(f, j), u, [self.r1[k, j, u] for k in range(n1 - 1)])

        for m in self.second:
            m.start()

    def start_z(self):
        f, s, c, t, me, n1, n2 = self._mine()
        for m in self.second:
            m.wait_recv()

        @pl.loop(0, self.g.nz)
        def _(u):
            self._add(self._e(f, s), u, [self.r2[k, u] for k in range(n2 - 1)])

        for m in self.near:
            m.start()

    def relay_z(self):
        f, s, c, t, me, n1, n2 = self._mine()
        for k, m in enumerate(self.near):
            m.wait_recv()
            self._add(self._e(f, s), (t + 2 * k) % self.g.nz, [self.r3[k]])
        for m in self.far:
            m.start()

    def finish(self):
        f, s, c, t, me, n1, n2 = self._mine()
        lo, n = self.rows
        half = self.g.nz // 2
        for m in self.far:
            m.wait_recv()
        v = self.src[self._e(f, s), t, lo : lo + n, :].astype(F32)
        for k in range(half - 1):
            v = v + self.r3[half + k].astype(F32)
        self.out[pl.ds(lo, n), :] = v
        for m in self.first + self.second + self.near + self.far:
            m.wait_send()


def scatter_sems(g):
    return (g.na - 1) * g.na + (g.na - 1) + (g.nz - 1)


POLL = dict(attend=6, back_down=2, back_gate=5)


def rope_tables(halo, nz, r):
    half = HD // 2
    freq = 10000.0 ** (-np.arange(half, dtype=np.float64) * 2.0 / HD)
    both = lambda p: np.concatenate([np.cos(p[:, None] * freq), np.sin(p[:, None] * freq)], axis=1).astype(np.float32)
    n = nz + halo
    starts = (np.arange(-(-n // 8) * 8) - halo) * float(r)
    return both(np.arange(r, dtype=np.float64)), both(starts)


def layer_kernel(g, cfg, *refs):
    cap, nq, ksel, halo, window, gunits, sunits = cfg
    refs = list(refs)
    take = lambda n: [refs.pop(0) for _ in range(n)]
    requests, sel, seg_q, seg_k, tab1, tab2 = take(6)
    x, gains, mem_k, mem_v, cot = take(5)
    shards = take(7)
    gout = take(1)[0]
    outs = take(7)
    block_out, grad_in = take(2)
    bufs = take(7)
    wq, wk, wv, wo, wg, wu, wd = bufs
    xh, mk, mv, rec_k, rec_v, n1, q, k, v, o, lse = take(11)
    hid, phid, pdg, pdu, do, dq, dk, dv, pdq, pdk, pdv, po, dh_o = take(13)
    req_in, req_s, gn_v, cos_v, sin_v = take(5)
    rbufs = [take(3) for _ in sunits]
    rsems = [take(2) for _ in sunits]
    pn_v, pc_v, pn1_v, pdhb_v, more = take(5)
    gz, gs, gd, gp = take(4)
    ss, rs, ms, qss, qrs, gss, grs, mss, mrs, zss, zrs, xss, xrs = take(13)
    css, crs, hss, hrs, ass, ars, dss, drs, fss, frs, fls = take(11)
    a, b, core, t, me = coords(g)
    peer = me + 1 - 2 * core
    r, d = block_out.shape
    rt = (halo + 1) * r
    nz, ff, _ = hid.shape
    dp = g.dp
    nb, half = dp // 2, d // 2
    kd, cols = shards[0].shape
    blk = mk.shape[2]
    nm, per_t = ksel * blk, cols // HD
    heads = d // HD
    any_ = pl.BlockSpec(memory_space=pl.ANY)

    def local(src, dst, i):
        m = pltpu.make_async_copy(src, dst, ms.at[i])
        m.start()
        return m

    ncore = [0]

    def to_peer(src, dst):
        i = ncore[0]
        ncore[0] += 1
        m = send(src, dst, css.at[i], crs.at[i], peer, t)
        m.start()
        return m

    def lane_block(ref, e, c_):
        return ref.at[:, pl.ds(pl.multiple_of((2 * e + c_) * 128, 128), 128)]

    def theirs(src, dst):
        return [to_peer(lane_block(src, e, 1 - core), dst.at[:, pl.ds(e * 128, 128)]) for e in range(nb)]

    def keep_half(src, dst):
        for e in range(nb):
            dst[:, e * 128 : (e + 1) * 128] = src[:, pl.ds(pl.multiple_of((2 * e + core) * 128, 128), 128)]

    per = gather_sems(g)
    gat = [Gather(g, shards[w], bufs[w], rows_, bf, lanes_, (ss, rs), i * per)
           for i, (w, rows_, bf, lanes_) in enumerate(gunits)]
    gof = lambda *ws: [u for u, s in zip(gat, gunits) if s[0] in ws]
    proj, out_, gate_up, down = gof(0, 1, 2), gof(3), gof(4, 5), gof(6)

    def piped(body, n, in_specs, out_specs=(), polls=()):
        def step(*blocks):
            body(*blocks)
            for at, fns in polls:

                @pl.when(pl.program_id(0) == at)
                def _():
                    for fn in fns:
                        fn()

        return pltpu.emit_pipeline(step, grid=(n,), in_specs=in_specs, out_specs=out_specs)

    every = lambda units, *names: [getattr(u, name) for name in names for u in units]

    head = lambda n: pl.BlockSpec((n, HD), lambda h: (0, h))
    mem = pl.BlockSpec((1, ksel, blk, HD), lambda h: (h // per_t, 0, 0, h % per_t))
    row_stat = pl.BlockSpec((1, r, 1), lambda h: (h, 0, 0))
    col = lambda n: pl.BlockSpec((n, cols), lambda u: (0, u))
    piece = pl.BlockSpec((1, ff, r), lambda u: (u, 0, 0))
    wcol = pl.BlockSpec((d, cols), lambda u: (0, u))
    wrow = lambda n: pl.BlockSpec((1, n, d), lambda u: (u, 0, 0))

    def forward(loc, stage_k, stage_v, x_v, xh_v, n_v):
        load_k = local(mem_k, loc, 0)
        lx = local(x, x_v, 1)
        greet(g, me, t)
        rq, gn = [], []
        for i in range(1, dp):
            to = (me + i) % dp
            m = send(requests.at[to], req_in.at[me], qss.at[i], qrs.at[i], to, t)
            m.start()
            rq.append(m)
        own_r = pltpu.make_async_copy(requests.at[me], req_in.at[me], qss.at[0])
        own_r.start()
        for u in proj + out_:
            u.start_z()
        for i in range(1, dp):
            to = (me + i) % dp
            m = send(gains, gn_v.at[me], gss.at[i], grs.at[i], to, t)
            m.start()
            gn.append(m)
        own_g = pltpu.make_async_copy(gains, gn_v.at[me], gss.at[0])
        own_g.start()
        xs = []
        for i in range(1, halo + 1):
            m = send(x, xh.at[i - 1], xss.at[i - 1], xrs.at[i - 1], me, (t + i) % nz)
            xs.append(m)

            @pl.when(t + i < nz)
            def _():
                m.start()

        own_r.wait()
        for m in rq:
            m.wait()
        cp = local(req_in, req_s, 2)
        cp.wait()
        parts = cols // 128
        lane = lambda p: pl.ds(p * 128, 128)

        def pick(stage, to):
            for j in range(cap):
                stage[to, j] = loc[req_s[to, 0, j]]

        def exchange(stage, rec, i, load):
            load.wait()
            out = [[] for _ in range(parts)]
            mine = pl.ds(me * cap, cap)

            def go(p, j):
                to = (me + j) % dp
                m = send(stage.at[to, :, :, lane(p)], rec.at[mine, :, lane(p)], mss.at[i, p, j], mrs.at[i, p, j], to, t)
                m.start()
                out[p].append(m)

            for j in range(1, dp):
                pick(stage, (me + j) % dp)
                go(0, j)
            for p in range(1, parts):
                for j in range(1, dp):
                    go(p, j)
            pick(stage, me)
            for p in range(parts):
                own = pltpu.make_async_copy(stage.at[me, :, :, lane(p)], rec.at[mine, :, lane(p)], mss.at[i, p, 0])
                own.start()
                out[p].append(own)
            return out

        ek = exchange(stage_k, rec_k, 0, load_k)
        load_v = local(mem_v, loc, 3)
        for u in gate_up:
            u.start_z()
        for u in proj + out_:
            u.relay_z()
        ev = exchange(stage_v, rec_v, 1, load_v)
        for u in proj + out_:
            u.start_first()
        for u in gate_up:
            u.relay_z()

        left = lax.broadcasted_iota(jnp.int32, (r, HD), 1) < HD // 2
        c1 = tab1[...]
        s1 = pltpu.roll(c1, HD // 2, axis=1)
        cc, sc = jnp.where(left, c1, s1), jnp.where(left, s1, c1)
        for j in range(halo + 1):
            c2 = jnp.broadcast_to(tab2[pl.ds(t + j, 1), :], (r, HD))
            s2 = pltpu.roll(c2, HD // 2, axis=1)
            ce, se = jnp.where(left, c2, s2), jnp.where(left, s2, c2)
            cos_v[j * r : (j + 1) * r, :] = cc * ce - sc * se
            sin_ = sc * ce + cc * se
            sin_v[j * r : (j + 1) * r, :] = jnp.where(left, -sin_, sin_)

        own_g.wait()
        for m in gn:
            m.wait()
        lx.wait()
        gain1 = gain_row(gn_v, 0)
        vx = x_v[...].astype(F32)
        n_v[halo * r :, :] = (vx * inv_rms(vx) * gain1).astype(BF16)
        for i, m in enumerate(xs):
            lo = (halo - 1 - i) * r

            @pl.when(t >= i + 1)
            def _():
                m.wait_recv()
                ch = local(xh.at[i], xh_v, 4)
                ch.wait()
                vh = xh_v[...].astype(F32)
                n_v[lo : lo + r, :] = (vh * inv_rms(vh) * gain1).astype(BF16)

            @pl.when(t < i + 1)
            def _():
                n_v[lo : lo + r, :] = jnp.zeros((r, d), BF16)

        cn = local(n_v, n1, 5)

        def spread(moves, rec, zst, out, i, p):
            for m in moves[p]:
                m.wait()
            lr = local(rec.at[:, :, lane(p)], loc.at[pl.ds(0, dp * cap), :, lane(p)], 6)
            lr.wait()

            @pl.loop(0, nq)
            def _(s):
                for j in range(ksel):
                    zst[s, j, :, lane(p)] = loc[sel[s * ksel + j], :, lane(p)]

            res = []
            for j in range(1, nz):
                to = (t + j) % nz
                m = send(zst.at[to, :, :, lane(p)], out.at[t, :, :, lane(p)], zss.at[i, p, j], zrs.at[i, p, j], me, to)
                m.start()
                res.append(m)
            own = pltpu.make_async_copy(zst.at[t, :, :, lane(p)], out.at[t, :, :, lane(p)], zss.at[i, p, 0])
            own.start()
            return res + [own]

        zk, zv = [], []
        for p in range(parts):
            zk += spread(ek, rec_k, stage_k, mk, 0, p)
        for p in range(parts):
            zv += spread(ev, rec_v, stage_v, mv, 1, p)
        for u in down:
            u.start_z()
        for u in proj:
            u.start_second()
        for u in out_:
            u.start_second()
        for u in gate_up:
            u.start_first()
        for u in proj:
            u.start_core()
        for u in proj:
            u.finish()

        def turned(y, cs_, sn_):
            return jnp.concatenate(
                [turn(y[:, h * HD : (h + 1) * HD], cs_, sn_).astype(BF16) for h in range(cols // HD)], axis=1
            )

        def project(wq_ref, wk_ref, wv_ref, q_ref, k_ref, v_ref):
            @pl.loop(0, halo + 1)
            def _(i):
                at = pl.ds(pl.multiple_of(i * r, r), r)
                n = n_v[at, :]
                k_ref[at, :] = turned(dot_nn(n, wk_ref[...]), cos_v[at, :], sin_v[at, :])
                v_ref[at, :] = dot_nn(n, wv_ref[...]).astype(BF16)

            q_ref[...] = turned(dot_nn(n_v[halo * r :, :], wq_ref[...]), cos_v[halo * r :, :], sin_v[halo * r :, :])

        piped(project, nz, [wcol] * 3, [col(r), col(rt), col(rt)])(wq, wk, wv, q, k, v)
        for u in out_:
            u.start_core()
        for u in down:
            u.relay_z()
        for m in zk + zv:
            m.wait()
        cn.wait()
        for i, m in enumerate(xs):

            @pl.when(t + i + 1 < nz)
            def _():
                m.wait_send()

    nblk = mem_k.shape[0]
    pl.run_scoped(
        forward,
        pltpu.VMEM((nblk, blk, cols), BF16),
        pltpu.VMEM((max(dp, nq), cap, blk, cols), BF16),
        pltpu.VMEM((max(dp, nq), cap, blk, cols), BF16),
        pltpu.VMEM((r, d), BF16),
        pltpu.VMEM((r, d), BF16),
        pltpu.VMEM((rt, d), BF16),
    )

    def attend(q_ref, k_ref, v_ref, mk_ref, mv_ref, o_ref, l_ref):
        km = mk_ref[0].reshape(nm, HD)
        vm = mv_ref[0].reshape(nm, HD)
        for i in range(r // QT):
            at = slice(i * QT, (i + 1) * QT)
            k0 = halo * r - window + i * QT
            ks = slice(k0, k0 + window + QT)
            qq = q_ref[at, :]
            ok = allowed_of(seg_q[at, :], seg_k[:, ks], halo * r + i * QT, k0)
            sl = jnp.where(ok, dot_nt(qq, k_ref[ks, :]), MASKED)
            sm = dot_nt(qq, km)
            mx = jnp.maximum(jnp.max(sl, axis=1, keepdims=True), jnp.max(sm, axis=1, keepdims=True))
            mc = mx * C2
            el = jnp.exp2(sl * C2 - mc)
            em = jnp.exp2(sm * C2 - mc)
            tot = jnp.sum(el, axis=1, keepdims=True) + jnp.sum(em, axis=1, keepdims=True)
            acc = dot_nn(el.astype(BF16), v_ref[ks, :]) + dot_nn(em.astype(BF16), vm)
            o_ref[at, :] = (acc / tot).astype(BF16)
            l_ref[0, at, :] = mc + jnp.log2(tot)

    piped(
        attend,
        heads,
        [head(r), head(rt), head(rt), mem, mem],
        [head(r), row_stat],
        [(POLL["attend"], every(gate_up, "start_second") + every(down, "start_first"))],
    )(q, k, v, mk, mv, o, lse)
    for u in out_:
        u.finish()

    sof = lambda us, *ws: [u for u in us if u.which in ws]

    def units(G):
        res = []
        for i, (w, rows_, bf) in enumerate(sunits):
            if w in G:
                u = Scatter(g, G[w], rows_, bf, rbufs[i], rsems[i], outs[w])
                u.which = w
                res.append(u)
        return res

    def rest(h_v, n2_v, c_v, n2h, ch, acc, *gf):
        fu = units(dict(enumerate(gf)))
        lc = local(cot, c_v, 0)
        lx = local(x, n2_v, 1)
        to_o = to_peer(o, po)
        lx.wait()
        h_v[...] = n2_v[...].astype(F32)

        def out_proj(o_ref, w_ref):
            h_v[...] += dot_nn(o_ref[...], w_ref[0])

        piped(out_proj, nz, [col(r), wrow(cols)])(o, wo)
        gain2 = gain_row(gn_v, 1)
        hv = h_v[...]
        n2_v[...] = (hv * inv_rms(hv) * gain2).astype(BF16)
        lc.wait()
        p_n = theirs(n2_v, pn_v) + theirs(c_v, pc_v)
        keep_half(n2_v, n2h)
        keep_half(c_v, ch)
        for u in gate_up:
            u.start_core()
        for u in gate_up:
            u.finish()

        def feed_forward(hid_v, a_v, b_v):
            tile = ff // 2
            give = lambda src, dst, i, u: send(src.at[u], dst.at[u], fss.at[i, u], frs.at[i, u], peer, t)
            keep = lambda u: pltpu.make_async_copy(hid_v.at[u], hid.at[u], fls.at[u])

            def hidden(wg_ref, wu_ref):
                u = pl.program_id(0)

                @pl.loop(0, 2)
                def _(i):
                    at = pl.ds(pl.multiple_of(i * tile, 16), tile)
                    gate = dot_nt(wg_ref[0, at, :], n2_v[...])
                    up = dot_nt(wu_ref[0, at, :], n2_v[...])
                    sig = 1.0 / (1.0 + jnp.exp(-gate))
                    act = gate * sig
                    hid_v[u, at, :] = (act * up).astype(BF16)
                    a_v[u, at, :] = (up * (sig * (1.0 + gate * (1.0 - sig)))).astype(BF16)
                    b_v[u, at, :] = act.astype(BF16)

                give(hid_v, phid, 0, u).start()
                keep(u).start()

            piped(hidden, nz, [wrow(ff)] * 2)(wg, wu)
            for u in down:
                u.start_second()
            for m in p_n:
                m.wait()

            def ffn_grads(mine_t, B, i, mine_v, peer_v, out):
                for u in range(nz):
                    give(mine_t, B, i, u).wait()

                def body(b_ref):
                    u = pl.program_id(0)
                    y = (dot_nn(mine_t[u], mine_v[...]) + dot_nn(b_ref[0], peer_v[...])).astype(BF16)
                    for e in range(nb):
                        out[e, u] = y[:, e * 128 : (e + 1) * 128]

                piped(body, nz, [piece])(B)

            ffn_grads(hid_v, phid, 0, ch, pc_v, gf[2])
            for u in sof(fu, 2):
                u.start_first()
            for u in down:
                u.start_core()
            for u in down:
                u.finish()
            acc[0:r, :] = jnp.zeros((r, d), F32)

            def hidden_back(wd_ref, wg_ref, wu_ref):
                u = pl.program_id(0)

                @pl.loop(0, 2)
                def _(i):
                    at = pl.ds(pl.multiple_of(i * tile, 16), tile)
                    dhid = dot_nt(wd_ref[0, at, :], c_v[...])
                    a_v[u, at, :] = (dhid * a_v[u, at, :].astype(F32)).astype(BF16)
                    b_v[u, at, :] = (dhid * b_v[u, at, :].astype(F32)).astype(BF16)

                give(a_v, pdg, 1, u).start()
                give(b_v, pdu, 2, u).start()
                acc[0:r, :] += dot_tn(a_v[u], wg_ref[0]) + dot_tn(b_v[u], wu_ref[0])

            piped(hidden_back, nz, [wrow(ff)] * 3)(wd, wg, wu)
            ffn_grads(a_v, pdg, 1, n2h, pn_v, gf[0])
            for u in sof(fu, 2):
                u.start_second()
            for u in sof(fu, 0):
                u.start_first()
            ffn_grads(b_v, pdu, 2, n2h, pn_v, gf[1])
            for u in sof(fu, 1):
                u.start_first()
            for u in range(nz):
                keep(u).wait()

        pl.run_scoped(feed_forward, *[pltpu.VMEM((nz, ff, r), BF16)] * 3)
        to_o.wait()

        def attention_back(dhb_v, dhbh, n1h, sdk, sdv, hb_v, *ga):
            G = dict(zip((3, 4, 5, 6), ga))
            us = fu + units(G)
            of = lambda *ws: sof(us, *ws)
            dn = acc[0:r, :]
            hv = h_v[...]
            iv = inv_rms(hv)
            gp[1:2, :] = jnp.sum(dn * hv * iv, axis=0, keepdims=True)
            gdn = dn * gain2
            dh = c_v[...].astype(F32) + iv * gdn - hv * (iv * iv * iv * jnp.mean(hv * gdn, axis=1, keepdims=True))
            acc[0:r, :] = dh
            dhb_v[...] = dh.astype(BF16)
            ld = local(acc.at[pl.ds(0, r)], dh_o, 2)
            p_r = theirs(dhb_v, pdhb_v) + theirs(n1, pn1_v)
            keep_half(dhb_v, dhbh)
            ln = [local(lane_block(n1, e, core), n1h.at[:, pl.ds(e * 128, 128)], 8 + e) for e in range(nb)]

            def mixed_grad(w_ref, do_ref):
                do_ref[...] = dot_nt(dhb_v[...], w_ref[0]).astype(BF16)

            piped(mixed_grad, nz, [wrow(cols)], [col(r)])(wo, do)
            for u in of(2):
                u.start_z()

            scale = HD**-0.5

            def attend_back(q_ref, k_ref, v_ref, mk_ref, mv_ref, o_ref, l_ref, do_ref, dq_ref, dk_ref, dv_ref):
                km = mk_ref[0].reshape(nm, HD)
                vm = mv_ref[0].reshape(nm, HD)
                sdk[...] = jnp.zeros_like(sdk)
                sdv[...] = jnp.zeros_like(sdv)
                for i in range(r // QT):
                    at = slice(i * QT, (i + 1) * QT)
                    k0 = halo * r - window + i * QT
                    ks = slice(k0, k0 + window + QT)
                    own = slice(halo * r + i * QT, halo * r + (i + 1) * QT)
                    qq, dd = q_ref[at, :], do_ref[at, :]
                    lse_c = l_ref[0, at, :]
                    delta = jnp.sum(dd.astype(F32) * o_ref[at, :].astype(F32), axis=1, keepdims=True)
                    ok = allowed_of(seg_q[at, :], seg_k[:, ks], halo * r + i * QT, k0)
                    pm = jnp.exp2(dot_nt(qq, km) * C2 - lse_c)
                    dsm = (pm * (dot_nt(dd, vm) - delta)).astype(BF16)
                    plo = jnp.where(ok, jnp.exp2(dot_nt(qq, k_ref[ks, :]) * C2 - lse_c), 0.0)
                    dsl = (plo * (dot_nt(dd, v_ref[ks, :]) - delta)).astype(BF16)
                    dqv = (dot_nn(dsm, km) + dot_nn(dsl, k_ref[ks, :])) * scale
                    dq_ref[at, :] = turn(dqv, cos_v[own, :], -sin_v[own, :]).astype(BF16)
                    sdk[ks, :] += dot_tn(dsl, qq)
                    sdv[ks, :] += dot_tn(plo.astype(BF16), dd)
                dk_ref[...] = turn(sdk[...] * scale, cos_v[...], -sin_v[...]).astype(BF16)
                dv_ref[...] = sdv[...].astype(BF16)

            piped(
                attend_back,
                heads,
                [head(r), head(rt), head(rt), mem, mem, head(r), row_stat, head(r)],
                [head(r), head(rt), head(rt)],
                [(POLL["back_down"], every(of(2), "relay_z")), (POLL["back_gate"], every(of(0), "start_second"))],
            )(q, k, v, mk, mv, o, lse, do, dq, dk, dv)
            p_att = [to_peer(dq, pdq), to_peer(dk, pdk), to_peer(dv, pdv)]
            ld.wait()

            acc[...] = jnp.zeros_like(acc)

            def halo_back(dk_ref, dv_ref, wk_ref, wv_ref):
                acc[: halo * r, :] += dot_nt(dk_ref[...], wk_ref[...]) + dot_nt(dv_ref[...], wv_ref[...])

            piped(halo_back, nz, [col(halo * r)] * 2 + [wcol] * 2)(dk, dv, wk, wv)
            hb_v[...] = acc[: halo * r, :].astype(BF16)
            hd = []
            for j in range(halo):
                m = send(hb_v.at[pl.ds((halo - 1 - j) * r, r), :], more.at[j], hss.at[j], hrs.at[j], me,
                         (t + nz - 1 - j) % nz)
                hd.append(m)

                @pl.when(t >= j + 1)
                def _():
                    m.start()

            for u in of(1):
                u.start_second()

            def own_back(dq_ref, dk_ref, dv_ref, wq_ref, wk_ref, wv_ref):
                acc[halo * r :, :] += (
                    dot_nt(dq_ref[...], wq_ref[...]) + dot_nt(dk_ref[...], wk_ref[...]) + dot_nt(dv_ref[...], wv_ref[...])
                )

            own_rows = pl.BlockSpec((r, cols), lambda u: (halo, u))
            piped(own_back, nz, [col(r), own_rows, own_rows] + [wcol] * 3)(dq, dk, dv, wq, wk, wv)
            for u in of(0):
                u.start_z()
            for m in p_r + ln:
                m.wait()

            def out_grads(a_ref, b_ref):
                u = pl.program_id(0)
                y = (dot_tn(a_ref[...], dhbh[...]) + dot_tn(b_ref[...], pdhb_v[...])).astype(BF16)
                for e in range(nb):
                    G[3][e, u] = y[:, e * 128 : (e + 1) * 128]

            piped(out_grads, nz, [col(r)] * 2)(o, po)
            for u in of(3):
                u.start_first()
            for m in p_att:
                m.wait()

            own = pl.ds(halo * r, r)

            def grads_of(out, p0, p1, a0, a1):
                def body(x_ref, y_ref):
                    u = pl.program_id(0)
                    y = (dot_tn(a0[...], x_ref[...]) + dot_tn(a1[...], y_ref[...])).astype(BF16)
                    for e in range(nb):
                        out[e, u] = y[e * 128 : (e + 1) * 128, :]

                n = p0.shape[0]
                piped(body, nz, [col(n)] * 2)(p0, p1)

            grads_of(G[4], dq, pdq, n1h.at[own], pn1_v.at[own])
            for u in of(4):
                u.start_first()
            for u in of(1):
                u.start_z()
            grads_of(G[5], dk, pdk, n1h, pn1_v)
            for u in of(5):
                u.start_first()
            for u in of(0):
                u.relay_z()
            for u in of(3):
                u.start_second()
            grads_of(G[6], dv, pdv, n1h, pn1_v)
            for u in of(6):
                u.start_first()
            for u in of(1):
                u.relay_z()

            lx2 = local(x, c_v, 3)
            lx2.wait()
            vx = c_v[...].astype(F32)
            gp[0:1, :] = jnp.sum(acc[halo * r :, :] * vx * inv_rms(vx), axis=0, keepdims=True)
            for j in range(halo):

                @pl.when(t >= j + 1)
                def _():
                    cx = local(xh.at[j], n2_v, 4)
                    cx.wait()
                    vh = n2_v[...].astype(F32)
                    lo = (halo - 1 - j) * r
                    gp[0:1, :] = gp[0:1, :] + jnp.sum(acc[lo : lo + r, :] * vh * inv_rms(vh), axis=0, keepdims=True)

            zg = []
            for i in range(1, nz):
                m = send(gp, gz.at[i - 1], ass.at[i - 1], ars.at[i - 1], me, (t + i) % nz)
                m.start()
                zg.append(m)
            def feed_out(hid_ref, wd_ref):
                h_v[...] += dot_tn(hid_ref[0], wd_ref[0])

            piped(feed_out, nz, [piece, wrow(ff)])(hid, wd)
            lo_ = local(h_v, block_out, 5)
            for u in of(3):
                u.start_z()
            for u in of(4, 5):
                u.start_second()
            for m in zg:
                m.wait()
            tot = gp[...]
            for i in range(nz - 1):
                tot = tot + gz[i]
            for e in range(dp):
                gs[e] = tot[:, e * 128 : (e + 1) * 128]
            ds_ = []
            for i in range(1, dp):
                to = (me + i) % dp
                m = send(gs.at[to], gd.at[me], dss.at[i], drs.at[i], to, t)
                m.start()
                ds_.append(m)
            og = pltpu.make_async_copy(gs.at[me], gd.at[me], dss.at[0])
            og.start()
            lo_.wait()
            ld2 = local(dh_o, h_v, 6)
            for u in of(6):
                u.start_second()
            for j, m in enumerate(hd):

                @pl.when(t + j + 1 < nz)
                def _():
                    m.wait_recv()
                    acc[halo * r :, :] = acc[halo * r :, :] + more[j].astype(F32)

                @pl.when(t >= j + 1)
                def _():
                    m.wait_send()

            ld2.wait()
            vx = c_v[...].astype(F32)
            iv = inv_rms(vx)
            gdx = acc[halo * r :, :] * gain_row(gn_v, 0)
            acc[halo * r :, :] = h_v[...] + iv * gdx - vx * (iv * iv * iv * jnp.mean(vx * gdx, axis=1, keepdims=True))
            lg = local(acc.at[pl.ds(halo * r, r)], grad_in, 7)
            for u in of(3):
                u.relay_z()
            for u in of(4, 5, 6):
                u.start_z()
            for u in of(4, 5, 6):
                u.relay_z()
            og.wait()
            for m in ds_:
                m.wait()
            tot = gd[0]
            for e in range(1, dp):
                tot = tot + gd[e]
            gout[...] = tot
            for u in us:
                u.finish()
            lg.wait()

        pl.run_scoped(
            attention_back,
            pltpu.VMEM((r, d), BF16),
            pltpu.VMEM((r, half), BF16),
            pltpu.VMEM((rt, half), BF16),
            pltpu.VMEM((rt, HD), F32),
            pltpu.VMEM((rt, HD), F32),
            pltpu.VMEM((halo * r, d), BF16),
            *[pltpu.VMEM((nb, nz) + tuple(o_.shape), BF16) for o_ in outs[3:]],
        )

    pl.run_scoped(
        rest,
        pltpu.VMEM((r, d), F32),
        pltpu.VMEM((r, d), BF16),
        pltpu.VMEM((r, d), BF16),
        pltpu.VMEM((r, half), BF16),
        pltpu.VMEM((r, half), BF16),
        pltpu.VMEM((rt, d), F32),
        *[pltpu.VMEM((nb, nz) + tuple(o_.shape), BF16) for o_ in outs[:3]],
    )


def run_layer(g, cap, halo, window, requests, sel, seg_q, seg_k, x, gains, mem_k, mem_v, cot, shards, nq, ksel):
    blk, cols = mem_k.shape[1:]
    r, d = x.shape
    rt = (halo + 1) * r
    nz, dp = g.nz, g.dp
    half = d // 2
    kd, ff = shards[0].shape[0], shards[4].shape[0]
    heads = d // HD
    tab1, tab2 = (jnp.asarray(v) for v in rope_tables(halo, nz, r))
    gunits = []
    for w, s in enumerate(shards):
        n, lanes_ = s.shape[0], w >= 3
        if w in (0, 4):
            gunits.append((w, (0, n), True, lanes_))
        elif w in (1, 5):
            gunits.append((w, (0, n), False, lanes_))
        else:
            gunits.append((w, (0, n // 2), True, lanes_))
            gunits.append((w, (n // 2, n - n // 2), False, lanes_))
    pieces = [(ff, 128)] * 3 + [(cols, 128)] + [(kd, cols)] * 3
    sunits = []
    for w in (2, 0, 1, 3):
        n = pieces[w][0]
        sunits += [(w, (0, n // 2), True), (w, (n // 2, n - n // 2), False)]
    sunits += [(4, (0, kd), True), (5, (0, kd), False), (6, (0, kd // 2), True), (6, (kd // 2, kd - kd // 2), False)]
    any_ = pl.BlockSpec(memory_space=pl.ANY)
    vm = pl.BlockSpec(memory_space=pltpu.VMEM)
    dma = lambda *n: pltpu.SemaphoreType.DMA(n)
    st = lambda s, dt=BF16: jax.ShapeDtypeStruct(s, dt)
    nsem = len(gunits) * gather_sems(g)
    hbm = (
        [st((d, d))] * 3 + [st((nz, cols, d))] + [st((nz, ff, d))] * 3
        + [st((halo, r, d))] + [st((nz, ksel, blk, cols))] * 2 + [st((dp * cap, blk, cols))] * 2
        + [st((rt, d)), st((r, d)), st((rt, d)), st((rt, d)), st((r, d)), st((heads, r, 1), F32)]
        + [st((nz, ff, r))] * 4 + [st((r, d)), st((r, d)), st((rt, d)), st((rt, d))]
        + [st((r, d)), st((rt, d)), st((rt, d)), st((r, d)), st((r, d), F32)]
    )
    out_shape = [st((2, 128), F32)] + [st(p, F32) for p in pieces] + [st((r, d), F32)] * 2 + hbm
    scratch = [pltpu.VMEM((dp, 8, 128), jnp.int32), pltpu.SMEM((dp, 8, 128), jnp.int32), pltpu.VMEM((dp, 2, 128), F32)]
    scratch += [pltpu.VMEM((rt, HD), F32)] * 2
    for w, (lo, n), bf in sunits:
        cc = pieces[w][1]
        n1_, n2_ = (g.nb, g.na) if bf else (g.na, g.nb)
        scratch += [
            pltpu.VMEM((n1_ - 1, n2_, nz, n, cc), BF16),
            pltpu.VMEM((n2_ - 1, nz, n, cc), BF16),
            pltpu.VMEM((nz - 1, n, cc), BF16),
        ]
    scratch += [dma(scatter_sems(g))] * (2 * len(sunits))
    scratch += [pltpu.VMEM((r, half), BF16)] * 2 + [pltpu.VMEM((rt, half), BF16), pltpu.VMEM((r, half), BF16)]
    scratch += [pltpu.VMEM((halo, r, d), BF16)]
    scratch += [pltpu.VMEM((nz - 1, 2, d), F32), pltpu.VMEM((dp, 2, 128), F32), pltpu.VMEM((dp, 2, 128), F32), pltpu.VMEM((2, d), F32)]
    ncore = 4 + 4 * (dp // 2)
    parts = cols // 128
    scratch += [dma(nsem), dma(nsem), dma(8 + dp // 2), dma(dp), dma(dp), dma(dp), dma(dp), dma(2, parts, dp), dma(2, parts, dp)]
    scratch += [dma(2, parts, nz), dma(2, parts, nz), dma(halo), dma(halo)]
    scratch += [dma(ncore), dma(ncore), dma(halo), dma(halo), dma(nz), dma(nz), dma(dp), dma(dp)]
    scratch += [dma(3, nz), dma(3, nz), dma(nz)]
    cfg = (cap, nq, ksel, halo, window, gunits, sunits)
    return pl.pallas_call(
        functools.partial(layer_kernel, g, cfg),
        out_shape=out_shape,
        in_specs=[vm, pl.BlockSpec(memory_space=pltpu.SMEM), vm, vm, vm, vm] + [any_] * (5 + len(shards)),
        out_specs=[vm] * 8 + [any_] * (2 + len(hbm)),
        scratch_shapes=scratch,
        compiler_params=pltpu.CompilerParams(collective_id=0, has_side_effects=True, vmem_limit_bytes=67043328),
        name="layer",
    )(requests, sel, seg_q, seg_k, tab1, tab2, x, gains, mem_k, mem_v, cot, *shards)


HEADS = 8
QB = 512


def normalize(field, gain_vec):
    return field * lax.rsqrt(jnp.mean(field * field, axis=-1, keepdims=True) + EPSILON) * gain_vec


def rotate(field, heads_here):
    row_total = field.shape[0]
    head_size = field.shape[1] // heads_here
    half_width = head_size // 2
    frequencies = 10000.0 ** (-jnp.arange(half_width, dtype=jnp.float32) * 2.0 / head_size)
    angles = jnp.arange(row_total, dtype=jnp.float32)[:, None] * frequencies[None, :]
    cosine = jnp.cos(angles)[:, None, :]
    sine_table = jnp.sin(angles)[:, None, :]
    split_heads = field.reshape(row_total, heads_here, head_size)
    first_half = split_heads[..., :half_width]
    second_half = split_heads[..., half_width:]
    turned = jnp.concatenate(
        [
            first_half * cosine - second_half * sine_table,
            second_half * cosine + first_half * sine_table,
        ],
        axis=-1,
    )
    return turned.reshape(row_total, heads_here * head_size)


def contract_rows(left, right):
    return lax.dot_general(
        left, right, (((0,), (0,)), ((), ())), preferred_element_type=jnp.float32
    )


def against(left, right):
    return lax.dot_general(
        left, right, (((1,), (1,)), ((), ())), preferred_element_type=jnp.float32
    )


def spread_rows(local_rows, matrices):
    piece_rows = lax.all_gather(local_rows, "tensor", axis=0, tiled=True)
    return jnp.concatenate(
        [jnp.dot(piece_rows, matrix, preferred_element_type=jnp.float32) for matrix in matrices],
        axis=1,
    )


def reduce_rows(left, right):
    return lax.psum_scatter(
        jnp.dot(left, right, preferred_element_type=jnp.float32).astype(jnp.bfloat16),
        "tensor",
        scatter_dimension=0,
        tiled=True,
    ).astype(jnp.float32)


def return_rows(pairs):
    summed = against(pairs[0][0], pairs[0][1])
    for grad_block, matrix in pairs[1:]:
        summed = summed + against(grad_block, matrix)
    return lax.psum_scatter(
        summed.astype(jnp.bfloat16), "tensor", scatter_dimension=0, tiled=True
    ).astype(jnp.float32)


def weight_grads(local_rows, grads_list):
    piece_rows = lax.all_gather(local_rows, "tensor", axis=0, tiled=True)
    return tuple((contract_rows(piece_rows, grad_one) for grad_one in grads_list))


def all_rows(local_grad):
    return lax.all_gather(local_grad, "tensor", axis=0, tiled=True)


def on_device_any(
    block_in,
    segments,
    retrieved,
    partner,
    memory_keys,
    memory_values,
    gain_attn,
    w_query,
    w_key,
    w_value,
    w_out,
    gain_ffn,
    w_gate,
    w_up,
    w_down,
    cotangent,
):
    tensor_size = lax.axis_size("tensor")
    dp_size = lax.axis_size("dp")
    heads_here = HEADS // tensor_size
    head_width = heads_here * HD
    score_scale = HD ** (-0.5)
    seq_len = segments.shape[1]
    query_blocks = seq_len // QB
    stream_in = block_in[0].astype(jnp.float32)
    seg_row = segments[0]
    positions = jnp.arange(seq_len)
    gathered = (
        lax.all_gather(gain_attn, "dp", axis=0, tiled=True),
        lax.all_gather(w_query, "dp", axis=0, tiled=True),
        lax.all_gather(w_key, "dp", axis=0, tiled=True),
        lax.all_gather(w_value, "dp", axis=0, tiled=True),
        lax.all_gather(w_out, "dp", axis=1, tiled=True),
        lax.all_gather(gain_ffn, "dp", axis=0, tiled=True),
        lax.all_gather(w_gate, "dp", axis=0, tiled=True),
        lax.all_gather(w_up, "dp", axis=0, tiled=True),
        lax.all_gather(w_down, "dp", axis=1, tiled=True),
    )
    gain_one, query_w, key_w, value_w, out_w, gain_two, gate_w, up_w, down_w = gathered
    wanted = retrieved[0].reshape(-1)
    request_total = wanted.shape[0]
    capacity = max(2, (2 * request_total + dp_size - 1) // dp_size)
    blocks_dev = memory_keys.shape[1]
    from_partner = wanted // MEMB
    block_index = wanted % MEMB
    owner_dev = block_index // blocks_dev
    local_block = block_index % blocks_dev
    seq_id = jnp.where(from_partner == 0, lax.axis_index("dp"), partner[0])
    owner_hits = (owner_dev[:, None] == jnp.arange(dp_size)[None, :]).astype(jnp.int32)
    slot_index = jnp.sum((jnp.cumsum(owner_hits, axis=0) - 1) * owner_hits, axis=1)
    requests = (
        jnp.zeros((dp_size, capacity, 2), jnp.int32)
        .at[owner_dev, slot_index]
        .set(jnp.stack([seq_id, local_block], axis=-1))
    )
    received = lax.all_to_all(requests, "dp", split_axis=0, concat_axis=0, tiled=True)
    picked_keys = memory_keys[received[..., 0], received[..., 1]]
    picked_values = memory_values[received[..., 0], received[..., 1]]
    fetched_keys = lax.all_to_all(picked_keys, "dp", split_axis=0, concat_axis=0, tiled=True)
    fetched_values = lax.all_to_all(picked_values, "dp", split_axis=0, concat_axis=0, tiled=True)
    memory_k = fetched_keys[owner_dev, slot_index].reshape(query_blocks, -1, heads_here, HD)
    memory_v = fetched_values[owner_dev, slot_index].reshape(query_blocks, -1, heads_here, HD)
    normed = normalize(stream_in, gain_one.astype(jnp.float32)).astype(jnp.bfloat16)
    qkv_rows = spread_rows(normed, [query_w, key_w, value_w])
    query_raw = qkv_rows[:, :head_width]
    key_raw = qkv_rows[:, head_width : 2 * head_width]
    queries = rotate(query_raw, heads_here).astype(jnp.bfloat16)
    keys_all = rotate(key_raw, heads_here).astype(jnp.bfloat16).reshape(seq_len, heads_here, HD)
    values_all = qkv_rows[:, 2 * head_width :].astype(jnp.bfloat16).reshape(seq_len, heads_here, HD)
    query_tiles = queries.reshape(query_blocks, QB, heads_here, HD)
    seg_tiles = seg_row.reshape(query_blocks, QB)
    pos_tiles = positions.reshape(query_blocks, QB)

    def scores_of(query_blk, seg_blk, pos_blk, key_mem):
        local_scores = jnp.einsum(
            "qhd,khd->hqk", query_blk, keys_all, preferred_element_type=jnp.float32
        )
        memory_scores = jnp.einsum(
            "qhd,khd->hqk", query_blk, key_mem, preferred_element_type=jnp.float32
        )
        raw_scores = jnp.concatenate([local_scores, memory_scores], axis=-1) * score_scale
        allowed = (seg_blk[:, None] == seg_row[None, :]) & (positions[None, :] <= pos_blk[:, None])
        allowed = jnp.concatenate(
            [allowed, jnp.ones((query_blk.shape[0], key_mem.shape[0]), dtype=jnp.bool_)], axis=1
        )
        return (raw_scores, allowed)

    def forward_block(pieces):
        query_blk, seg_blk, pos_blk, key_mem, value_mem = pieces
        raw_scores, allowed = scores_of(query_blk, seg_blk, pos_blk, key_mem)
        masked = jnp.where(allowed[None], raw_scores, MASKED)
        row_max = jnp.max(masked, axis=-1, keepdims=True)
        expo = jnp.exp(masked - row_max)
        row_total = jnp.sum(expo, axis=-1, keepdims=True)
        weights_soft = (expo / row_total).astype(jnp.bfloat16)
        values_both = jnp.concatenate([values_all, value_mem], axis=0)
        result = jnp.einsum(
            "hqk,khd->qhd", weights_soft, values_both, preferred_element_type=jnp.float32
        )
        return (result, (row_max + jnp.log(row_total))[..., 0])

    attended, log_totals = lax.map(
        forward_block, (query_tiles, seg_tiles, pos_tiles, memory_k, memory_v)
    )
    mixed = attended.reshape(seq_len, head_width).astype(jnp.bfloat16)
    stream = stream_in + reduce_rows(mixed, out_w)
    normed_ffn = normalize(stream, gain_two.astype(jnp.float32)).astype(jnp.bfloat16)
    gate_up = spread_rows(normed_ffn, [gate_w, up_w])
    hidden_width = gate_w.shape[1]
    gate_pre = gate_up[:, :hidden_width]
    up_pre = gate_up[:, hidden_width:]
    hidden = (jax.nn.silu(gate_pre) * up_pre).astype(jnp.bfloat16)
    block_out = stream + reduce_rows(hidden, down_w)
    gathered_back = (
        lax.all_gather(gain_attn, "dp", axis=0, tiled=True),
        lax.all_gather(w_query, "dp", axis=0, tiled=True),
        lax.all_gather(w_key, "dp", axis=0, tiled=True),
        lax.all_gather(w_value, "dp", axis=0, tiled=True),
        lax.all_gather(w_out, "dp", axis=1, tiled=True),
        lax.all_gather(gain_ffn, "dp", axis=0, tiled=True),
        lax.all_gather(w_gate, "dp", axis=0, tiled=True),
        lax.all_gather(w_up, "dp", axis=0, tiled=True),
        lax.all_gather(w_down, "dp", axis=1, tiled=True),
    )
    gain_one, query_w, key_w, value_w, out_w, gain_two, gate_w, up_w, down_w = gathered_back
    dout_rows = cotangent[0]

    def gated(gate_in, up_in):
        return jax.nn.silu(gate_in) * up_in

    dout_full = all_rows(dout_rows)
    grad_down = contract_rows(hidden, dout_full)
    d_hidden = against(dout_full, down_w)
    gated_value, pull_gated = jax.vjp(gated, gate_pre, up_pre)
    d_gate, d_up = pull_gated(d_hidden)
    d_gate = d_gate.astype(jnp.bfloat16)
    d_up = d_up.astype(jnp.bfloat16)
    d_norm_ffn = return_rows([(d_gate, gate_w), (d_up, up_w)])
    grad_gate, grad_up = weight_grads(normed_ffn, [d_gate, d_up])
    norm_value, pull_norm_ffn = jax.vjp(normalize, stream, gain_two.astype(jnp.float32))
    d_stream_norm, grad_gain_ffn = pull_norm_ffn(d_norm_ffn)
    d_stream = dout_rows.astype(jnp.float32) + d_stream_norm
    d_stream_full = all_rows(d_stream.astype(jnp.bfloat16))
    grad_out = contract_rows(mixed, d_stream_full)
    d_mixed = against(d_stream_full, out_w).astype(jnp.bfloat16)
    d_mixed_tiles = d_mixed.reshape(query_blocks, QB, heads_here, HD)

    def backward_block(carry_sums, pieces):
        key_sum, value_sum = carry_sums
        query_blk, seg_blk, pos_blk, key_mem, value_mem, log_blk, grad_blk = pieces
        raw_scores, allowed = scores_of(query_blk, seg_blk, pos_blk, key_mem)
        probs = jnp.where(allowed[None], jnp.exp(raw_scores - log_blk[..., None]), 0.0)
        values_both = jnp.concatenate([values_all, value_mem], axis=0)
        d_probs = jnp.einsum(
            "qhd,khd->hqk", grad_blk, values_both, preferred_element_type=jnp.float32
        )
        shared = jnp.sum(probs * d_probs, axis=-1, keepdims=True)
        d_scores = (probs * (d_probs - shared)).astype(jnp.bfloat16)
        probs_low = probs.astype(jnp.bfloat16)
        keys_both = jnp.concatenate([keys_all, key_mem], axis=0)
        d_query = (
            jnp.einsum("hqk,khd->qhd", d_scores, keys_both, preferred_element_type=jnp.float32)
            * score_scale
        )
        key_sum = (
            key_sum
            + jnp.einsum(
                "hqk,qhd->khd",
                d_scores[..., :seq_len],
                query_blk,
                preferred_element_type=jnp.float32,
            )
            * score_scale
        )
        value_sum = value_sum + jnp.einsum(
            "hqk,qhd->khd", probs_low[..., :seq_len], grad_blk, preferred_element_type=jnp.float32
        )
        return ((key_sum, value_sum), d_query)

    zero_grads = jnp.zeros((seq_len, heads_here, HD), jnp.float32)
    (d_keys, d_values), d_queries = lax.scan(
        backward_block,
        (zero_grads, zero_grads),
        (query_tiles, seg_tiles, pos_tiles, memory_k, memory_v, log_totals, d_mixed_tiles),
    )

    def turn(field):
        return rotate(field, heads_here)

    turned_value, pull_turn = jax.vjp(turn, query_raw)
    d_query_raw = pull_turn(d_queries.reshape(seq_len, head_width))[0].astype(jnp.bfloat16)
    d_key_raw = pull_turn(d_keys.reshape(seq_len, head_width))[0].astype(jnp.bfloat16)
    d_value_raw = d_values.reshape(seq_len, head_width).astype(jnp.bfloat16)
    d_norm_attn = return_rows([(d_query_raw, query_w), (d_key_raw, key_w), (d_value_raw, value_w)])
    grad_query, grad_key, grad_value = weight_grads(normed, [d_query_raw, d_key_raw, d_value_raw])
    norm_first, pull_norm_attn = jax.vjp(normalize, stream_in, gain_one.astype(jnp.float32))
    d_input_norm, grad_gain_attn = pull_norm_attn(d_norm_attn)
    grad_in = d_stream + d_input_norm
    grad_gain_attn, grad_gain_ffn = lax.psum((grad_gain_attn, grad_gain_ffn), "tensor")
    results = (
        lax.psum_scatter(
            grad_gain_attn.astype(jnp.bfloat16), "dp", scatter_dimension=0, tiled=True
        ).astype(jnp.float32),
        lax.psum_scatter(
            grad_query.astype(jnp.bfloat16), "dp", scatter_dimension=0, tiled=True
        ).astype(jnp.float32),
        lax.psum_scatter(
            grad_key.astype(jnp.bfloat16), "dp", scatter_dimension=0, tiled=True
        ).astype(jnp.float32),
        lax.psum_scatter(
            grad_value.astype(jnp.bfloat16), "dp", scatter_dimension=0, tiled=True
        ).astype(jnp.float32),
        lax.psum_scatter(
            grad_out.astype(jnp.bfloat16), "dp", scatter_dimension=1, tiled=True
        ).astype(jnp.float32),
        lax.psum_scatter(
            grad_gain_ffn.astype(jnp.bfloat16), "dp", scatter_dimension=0, tiled=True
        ).astype(jnp.float32),
        lax.psum_scatter(
            grad_gate.astype(jnp.bfloat16), "dp", scatter_dimension=0, tiled=True
        ).astype(jnp.float32),
        lax.psum_scatter(
            grad_up.astype(jnp.bfloat16), "dp", scatter_dimension=0, tiled=True
        ).astype(jnp.float32),
        lax.psum_scatter(
            grad_down.astype(jnp.bfloat16), "dp", scatter_dimension=1, tiled=True
        ).astype(jnp.float32),
    )
    return (block_out[None], grad_in[None]) + results


def on_device(*args):
    x, dp = args[0], lax.axis_size("dp")
    side = math.isqrt(dp // 2)
    if 2 * side * side == dp and x.shape[2] % (128 * dp) == 0:
        return on_device_rows(*args)
    return on_device_any(*args)


def on_device_rows(
    block_in, segments, retrieved, partner, memory_keys, memory_values,
    gain_attn, w_query, w_key, w_value, w_out, gain_ffn, w_gate, w_up, w_down, cotangent,
):
    g = Grid(lax.axis_size("dp"), lax.axis_size("tensor"))
    t, me = lax.axis_index("tensor"), lax.axis_index("dp")
    x, c = block_in[0], cotangent[0]
    r, d = x.shape
    seq_len = segments.shape[1]
    window = seq_len // 4
    halo = -(-window // r)
    nq, ksel = retrieved.shape[1:]
    cap = max(2, -(-2 * nq * ksel // g.dp))
    req, sel = plan_requests(retrieved[0], partner[0], g.dp, memory_keys.shape[1], cap)
    gains = jnp.stack([gain_attn, gain_ffn]).astype(F32)
    flat = lambda m: m.reshape((-1,) + m.shape[2:])
    shards = [w_query, w_key, w_value, w_out, w_gate.T, w_up.T, w_down]
    padded = jnp.concatenate([jnp.full((halo * r,), -1, jnp.int32), segments[0]])
    seg = lax.dynamic_slice(padded, (t * r,), ((halo + 1) * r,))
    seg_k, seg_q = seg[None, :], seg[halo * r :, None]
    gout, o_gate, o_up, o_down, o_out, o_q, o_k, o_v, block_out, grad_in = run_layer(
        g, cap, halo, window, req, sel, seg_q, seg_k, x, gains, flat(memory_keys), flat(memory_values), c, shards, nq, ksel
    )[:10]
    return (
        block_out[None], grad_in[None], gout[0], o_q, o_k, o_v, o_out, gout[1], o_gate.T, o_up.T, o_down,
    )


def solution(mesh):
    return jax.shard_map(
        on_device,
        mesh=mesh,
        in_specs=(
            P("dp", "tensor", None), P("dp", None), P("dp", None, None), P("dp"),
            P(None, "dp", None, "tensor"), P(None, "dp", None, "tensor"),
            P("dp"), P("dp", "tensor"), P("dp", "tensor"), P("dp", "tensor"), P("tensor", "dp"),
            P("dp"), P("dp", "tensor"), P("dp", "tensor"), P("tensor", "dp"), P("dp", "tensor", None),
        ),
        out_specs=(
            P("dp", "tensor", None), P("dp", "tensor", None),
            P("dp"), P("dp", "tensor"), P("dp", "tensor"), P("dp", "tensor"), P("tensor", "dp"),
            P("dp"), P("dp", "tensor"), P("dp", "tensor"), P("tensor", "dp"),
        ),
        check_vma=False,
    )
```

```python
import functools
import math

import jax
import jax.numpy as jnp
import numpy as np
from jax import lax
from jax.experimental import pallas as pl
from jax.experimental.pallas import tpu as pltpu
from jax.sharding import PartitionSpec as P
MESH = pl.DeviceIdType.MESH
MEMB = 128


class Grid:
    def __init__(self, dp, tensor):
        side = math.isqrt(dp // 2)
        assert side * side * 2 == dp
        self.na, self.nb, self.nc, self.nz, self.dp = side, side, 2, tensor, dp


def coords(g):
    me = lax.axis_index("dp")
    t = lax.axis_index("tensor")
    return me // (2 * g.nb), (me // 2) % g.nb, me % 2, t, me


def send(src, dst, ssem, rsem, dp, t):
    return pltpu.make_async_remote_copy(
        src_ref=src, dst_ref=dst, send_sem=ssem, recv_sem=rsem, device_id=(dp, t), device_id_type=MESH
    )


class Copy:
    def __init__(self, make):
        self.make = make

    def start(self):
        self.make().start()

    def wait(self):
        self.make().wait()

    def wait_send(self):
        self.make().wait_send()

    def wait_recv(self):
        self.make().wait_recv()


def greet(g, me, t):
    bar = pltpu.get_barrier_semaphore()
    for k in range(1, g.dp):
        pl.semaphore_signal(bar, inc=1, device_id=((me + k) % g.dp, t), device_id_type=MESH)
    for k in range(1, g.nz):
        pl.semaphore_signal(bar, inc=1, device_id=(me, (t + k) % g.nz), device_id_type=MESH)
    pl.semaphore_wait(bar, g.dp - 1 + g.nz - 1)


class Gather:
    def __init__(self, g, shard, buf, rows, b_first, lanes, sems, base):
        self.g, self.shard, self.buf, self.rows, self.b_first, self.lanes = g, shard, buf, rows, b_first, lanes
        self.sems, self.count, self.base = sems, 0, base
        lo, n = rows
        nz = g.nz
        n1, n2 = (g.nb, g.na) if b_first else (g.na, g.nb)
        bind = functools.partial
        shard_rows = lambda: shard.at[pl.ds(lo, n), :]
        tensor = lambda: lax.axis_index("tensor")

        def here():
            a, b, c, t, me = coords(g)
            return self.at(me, t)

        def passed(k):
            a, b, c, t, me = coords(g)
            return self.at(me, (t + nz - 2 * k) % nz)

        def far(k):
            a, b, c, t, me = coords(g)
            return me, (t + 2 * k) % nz

        def pair():
            a, b, c, t, me = coords(g)
            return me, t + 1 - 2 * (t % 2)

        def other_core():
            a, b, c, t, me = coords(g)
            return me + 1 - 2 * c, t

        slab = lambda k1, k2: bind(lambda k1, k2: self.at(self._slot(k1, k2)), k1, k2)
        to1 = lambda k: (self._slot(n1 - k, 0), tensor())
        to2 = lambda k: (self._slot(0, n2 - k), tensor())
        self.far = [self._copy(shard_rows, here, bind(far, k)) for k in range(1, nz // 2)]
        self.near = [self._copy(shard_rows, here, pair)]
        self.relayed = [self._copy(bind(passed, k), bind(passed, k), pair) for k in range(1, nz // 2)]
        i = self._sem()
        self.own = Copy(lambda: pltpu.make_async_copy(shard_rows(), here(), sems[0].at[i]))
        self.first = [self._copy(slab(0, 0), slab(0, 0), bind(to1, k)) for k in range(1, n1)]
        self.second = [
            self._copy(slab(k1, 0), slab(k1, 0), bind(to2, k)) for k1 in range(n1) for k in range(1, n2)
        ]
        core = lambda k1, k2: self._copy(slab(k1, k2), slab(k1, k2), other_core)
        self.core0 = [core(0, 0)]
        self.core1 = [core(k1, 0) for k1 in range(1, n1)]
        self.core2 = [core(k1, k2) for k1 in range(n1) for k2 in range(1, n2)]

    def at(self, dp, t=None):
        lo, n = self.rows
        if self.lanes:
            width = self.shard.shape[1]
            col = pl.ds(pl.multiple_of(dp * width, 128), width)
            return self.buf.at[slice(None) if t is None else t, pl.ds(lo, n), col]
        depth, width = self.shard.shape
        row = pl.ds(pl.multiple_of(dp * depth + lo, 16), n)
        return self.buf.at[row, slice(None) if t is None else pl.ds(pl.multiple_of(t * width, 128), width)]

    def _sem(self):
        i = self.base + self.count
        self.count += 1
        return i

    def _copy(self, src, dst, to):
        i = self._sem()
        return Copy(lambda: send(src(), dst(), self.sems[0].at[i], self.sems[1].at[i], *to()))

    def _slot(self, k1, k2):
        g = self.g
        a, b, c, t, me = coords(g)
        if self.b_first:
            return (((a + g.na - k2) % g.na) * g.nb + (b + g.nb - k1) % g.nb) * 2 + c
        return (((a + g.na - k1) % g.na) * g.nb + (b + g.nb - k2) % g.nb) * 2 + c

    def start_z(self):
        for m in self.far + self.near + [self.own]:
            m.start()

    def relay_z(self):
        for m, n in zip(self.far, self.relayed):
            m.wait_recv()
            n.start()

    def start_first(self):
        self.own.wait()
        for m in self.near + self.relayed:
            m.wait_recv()
        for m in self.first + self.core0:
            m.start()

    def start_second(self):
        for m in self.first:
            m.wait_recv()
        for m in self.second + self.core1:
            m.start()

    def start_core(self):
        for m in self.second:
            m.wait_recv()
        for m in self.core2:
            m.start()

    def finish(self):
        core = self.core0 + self.core1 + self.core2
        for m in core:
            m.wait_recv()
        for m in self.far + self.near + self.relayed + self.first + self.second + core:
            m.wait_send()


def gather_sems(g):
    return g.nz + (g.na - 1) + g.na * (g.na - 1) + g.na * g.nb


def plan_requests(retrieved, partner, dp_size, blocks_dev, cap):
    wanted = retrieved.reshape(-1)
    n = wanted.shape[0]
    from_partner = wanted // MEMB
    block_index = wanted % MEMB
    owner = block_index // blocks_dev
    local = block_index % blocks_dev
    seq = jnp.where(from_partner == 0, lax.axis_index("dp"), partner)
    flat = seq * blocks_dev + local
    i = jnp.arange(n)
    slot = jnp.sum(((owner[:, None] == owner[None, :]) & (i[None, :] < i[:, None])).astype(jnp.int32), axis=1)
    hit = (owner[None, None, :] == jnp.arange(dp_size)[:, None, None]) & (
        slot[None, None, :] == jnp.arange(128)[None, :, None]
    )
    req = jnp.sum(jnp.where(hit, flat[None, None, :], 0), axis=2)
    return jnp.broadcast_to(req[:, None, :], (dp_size, 8, 128)).astype(jnp.int32), (owner * cap + slot).astype(jnp.int32)


HD = 128
EPSILON = 1e-05
MASKED = -1e30
F32, BF16 = jnp.float32, jnp.bfloat16


def dot_nn(x, y):
    return lax.dot_general(x, y, (((1,), (0,)), ((), ())), preferred_element_type=F32)


def dot_nt(x, y):
    return lax.dot_general(x, y, (((1,), (1,)), ((), ())), preferred_element_type=F32)


def dot_tn(x, y):
    return lax.dot_general(x, y, (((0,), (0,)), ((), ())), preferred_element_type=F32)


def inv_rms(v):
    return lax.rsqrt(jnp.mean(v * v, axis=-1, keepdims=True) + EPSILON)


def gain_row(gains_ref, which):
    n = gains_ref.shape[0]
    return jnp.concatenate([gains_ref[d, which : which + 1, :] for d in range(n)], axis=1)


def turn(v, cos, sin):
    return v * cos + pltpu.roll(v, HD // 2, axis=1) * sin


def lanes(ref):
    return jnp.concatenate([ref[d, 0] for d in range(ref.shape[0])], axis=1)


def rows(ref):
    return jnp.concatenate([ref[d, 0] for d in range(ref.shape[0])], axis=0)


VL = 60 * 2**20


def full(shape, buffers=None):
    n = len(shape)
    kw = {} if buffers is None else dict(pipeline_mode=pl.Buffered(buffers))
    return pl.BlockSpec(shape, lambda *i: (0,) * n, **kw)


def allowed_of(seg_q, seg_k, q0, k0):
    n, m = seg_q.shape[0], seg_k.shape[1]
    qp = lax.broadcasted_iota(jnp.int32, (n, m), 0) + q0
    kp = lax.broadcasted_iota(jnp.int32, (n, m), 1) + k0
    return (seg_q == seg_k) & (kp <= qp)


QT = 256
C2 = HD**-0.5 * math.log2(math.e)


class Scatter:
    def __init__(self, g, src, rows, b_first, bufs, sems, out):
        self.g, self.src, self.rows, self.b_first, self.out = g, src, rows, b_first, out
        self.r1, self.r2, self.r3 = bufs
        self.sems, self.count = sems, 0
        n1, n2 = self._mine()[5:]
        nz = g.nz
        lo, n = rows
        bind = functools.partial
        at = lambda e, t: src.at[e, t, pl.ds(lo, n), :]

        def src1(k, j):
            f = self._mine()[0]
            return at(self._e((f + k) % n1, j), slice(None))

        def to1(k):
            f, s, c, t = self._mine()[:4]
            return self._e((f + k) % n1, s) * 2 + c, t

        def src2(k):
            f, s = self._mine()[:2]
            return at(self._e(f, (s + k) % n2), slice(None))

        def to2(k):
            f, s, c, t = self._mine()[:4]
            return self._e(f, (s + k) % n2) * 2 + c, t

        def src_near(k):
            f, s, c, t = self._mine()[:4]
            return at(self._e(f, s), (t + 1 - 2 * (t % 2) + 2 * k) % nz)

        def to_near():
            t, me = self._mine()[3:5]
            return me, t + 1 - 2 * (t % 2)

        def src_far(k):
            f, s, c, t = self._mine()[:4]
            return at(self._e(f, s), (t + 2 * k) % nz)

        def to_far(k):
            t, me = self._mine()[3:5]
            return me, (t + 2 * k) % nz

        land = lambda ref, *i: bind(lambda ref, i: ref.at[i], ref, i)
        self.first = [
            self._copy(bind(src1, k, j), land(self.r1, k - 1, j), bind(to1, k)) for k in range(1, n1) for j in range(n2)
        ]
        self.second = [self._copy(bind(src2, k), land(self.r2, k - 1), bind(to2, k)) for k in range(1, n2)]
        self.near = [self._copy(bind(src_near, k), land(self.r3, k), to_near) for k in range(nz // 2)]
        self.far = [
            self._copy(bind(src_far, k), land(self.r3, nz // 2 + k - 1), bind(to_far, k)) for k in range(1, nz // 2)
        ]

    def _copy(self, src, dst, to):
        i = self.count
        self.count += 1
        return Copy(lambda: send(src(), dst(), self.sems[0].at[i], self.sems[1].at[i], *to()))

    def _e(self, f, s):
        return s * self.g.nb + f if self.b_first else f * self.g.nb + s

    def _mine(self):
        a, b, c, t, me = coords(self.g)
        f, s = (b, a) if self.b_first else (a, b)
        n1, n2 = (self.g.nb, self.g.na) if self.b_first else (self.g.na, self.g.nb)
        return f, s, c, t, me, n1, n2

    def _add(self, e, u, more):
        lo, n = self.rows
        v = self.src[e, u, lo : lo + n, :].astype(F32)
        for m in more:
            v = v + m.astype(F32)
        self.src[e, u, lo : lo + n, :] = v.astype(BF16)

    def start_first(self):
        for m in self.first:
            m.start()

    def start_second(self):
        f, s, c, t, me, n1, n2 = self._mine()
        for m in self.first:
            m.wait_recv()
        for j in range(n2):

            @pl.loop(0, self.g.nz)
            def _(u):
                self._add(self._e(f, j), u, [self.r1[k, j, u] for k in range(n1 - 1)])

        for m in self.second:
            m.start()

    def start_z(self):
        f, s, c, t, me, n1, n2 = self._mine()
        for m in self.second:
            m.wait_recv()

        @pl.loop(0, self.g.nz)
        def _(u):
            self._add(self._e(f, s), u, [self.r2[k, u] for k in range(n2 - 1)])

        for m in self.near:
            m.start()

    def relay_z(self):
        f, s, c, t, me, n1, n2 = self._mine()
        for k, m in enumerate(self.near):
            m.wait_recv()
            self._add(self._e(f, s), (t + 2 * k) % self.g.nz, [self.r3[k]])
        for m in self.far:
            m.start()

    def finish(self):
        f, s, c, t, me, n1, n2 = self._mine()
        lo, n = self.rows
        half = self.g.nz // 2
        for m in self.far:
            m.wait_recv()
        v = self.src[self._e(f, s), t, lo : lo + n, :].astype(F32)
        for k in range(half - 1):
            v = v + self.r3[half + k].astype(F32)
        self.out[pl.ds(lo, n), :] = v
        for m in self.first + self.second + self.near + self.far:
            m.wait_send()


def scatter_sems(g):
    return (g.na - 1) * g.na + (g.na - 1) + (g.nz - 1)


POLL = dict(attend=0, attend_core=6, back_down=2, back_gate=5, own_out=1, own_up=3, out_z=0, out_q=3)


def rope_tables(halo, nz, r):
    half = HD // 2
    freq = 10000.0 ** (-np.arange(half, dtype=np.float64) * 2.0 / HD)
    both = lambda p: np.concatenate([np.cos(p[:, None] * freq), np.sin(p[:, None] * freq)], axis=1).astype(np.float32)
    n = nz + halo
    starts = (np.arange(-(-n // 8) * 8) - halo) * float(r)
    return both(np.arange(r, dtype=np.float64)), both(starts)


def layer_kernel(g, cfg, *refs):
    cap, nq, ksel, halo, window, gunits, sunits = cfg
    refs = list(refs)
    take = lambda n: [refs.pop(0) for _ in range(n)]
    requests, sel, segs, tab1, tab2 = take(5)
    x, gains, mem_k, mem_v, cot = take(5)
    shards = take(7)
    gout = take(1)[0]
    outs = take(7)
    block_out, grad_in = take(2)
    bufs = take(7)
    wq, wk, wv, wo, wg, wu, wd = bufs
    xh, mk, mv, rec_k, rec_v, n1, q, k, v, o, lse = take(11)
    hid, phid, pdg, pdu, do, dq, dk, dv, pdq, pdk, pdv, po, dh_o = take(13)
    req_in, req_s, gn_v, cos_v, sin_v = take(5)
    rbufs = [take(3) for _ in sunits]
    rsems = [take(2) for _ in sunits]
    pn_v, pc_v, pn1_v, pdhb_v, more = take(5)
    gz, gs, gd, gp = take(4)
    ss, rs, ms, qss, qrs, gss, grs, mss, mrs, zss, zrs, xss, xrs = take(13)
    css, crs, hss, hrs, ass, ars, dss, drs, fss, frs, fls = take(11)
    seg_q, seg_k = take(2)
    a, b, core, t, me = coords(g)
    peer = me + 1 - 2 * core
    r, d = block_out.shape
    rt = (halo + 1) * r
    nz, ff, _ = hid.shape
    dp = g.dp
    nb, half = dp // 2, d // 2
    kd, cols = shards[0].shape
    blk = mk.shape[2]
    nm, per_t = ksel * blk, cols // HD
    heads = d // HD
    any_ = pl.BlockSpec(memory_space=pl.ANY)

    def local(src, dst, i):
        m = pltpu.make_async_copy(src, dst, ms.at[i])
        m.start()
        return m

    ncore = [0]

    def to_peer(src, dst):
        i = ncore[0]
        ncore[0] += 1
        m = send(src, dst, css.at[i], crs.at[i], peer, t)
        m.start()
        return m

    def lane_block(ref, e, c_):
        return ref.at[:, pl.ds(pl.multiple_of((2 * e + c_) * 128, 128), 128)]

    def theirs(src, dst):
        return [to_peer(lane_block(src, e, 1 - core), dst.at[:, pl.ds(e * 128, 128)]) for e in range(nb)]

    def keep_half(src, dst):
        for e in range(nb):
            dst[:, e * 128 : (e + 1) * 128] = src[:, pl.ds(pl.multiple_of((2 * e + core) * 128, 128), 128)]

    per = gather_sems(g)
    gat = [Gather(g, shards[w], bufs[w], rows_, bf, lanes_, (ss, rs), i * per)
           for i, (w, rows_, bf, lanes_) in enumerate(gunits)]
    gof = lambda *ws: [u for u, s in zip(gat, gunits) if s[0] in ws]
    proj, out_, gate_up, down = gof(0, 1, 2), gof(3), gof(4, 5), gof(6)

    def piped(body, n, in_specs, out_specs=(), polls=()):
        def step(*blocks):
            body(*blocks)
            for at, fns in polls:

                @pl.when(pl.program_id(0) == at)
                def _():
                    for fn in fns:
                        fn()

        return pltpu.emit_pipeline(step, grid=(n,), in_specs=in_specs, out_specs=out_specs)

    every = lambda units, *names: [getattr(u, name) for name in names for u in units]

    head = lambda n: pl.BlockSpec((n, HD), lambda h: (0, h))
    mem = pl.BlockSpec((1, ksel, blk, HD), lambda h: (h // per_t, 0, 0, h % per_t))
    row_stat = pl.BlockSpec((1, r, 1), lambda h: (h, 0, 0))
    col = lambda n: pl.BlockSpec((n, cols), lambda u: (0, u))
    piece = pl.BlockSpec((1, ff, r), lambda u: (u, 0, 0))
    wcol = pl.BlockSpec((d, cols), lambda u: (0, u))
    wrow = lambda n: pl.BlockSpec((1, n, d), lambda u: (u, 0, 0))

    def forward(loc, stage_k, stage_v, x_v, xh_v, n_v):
        load_k = local(mem_k, loc, 0)
        lx = local(x, x_v, 1)
        greet(g, me, t)
        rq, gn = [], []
        for i in range(1, dp):
            to = (me + i) % dp
            m = send(requests.at[to], req_in.at[me], qss.at[i], qrs.at[i], to, t)
            m.start()
            rq.append(m)
        own_r = pltpu.make_async_copy(requests.at[me], req_in.at[me], qss.at[0])
        own_r.start()
        for u in proj + out_:
            u.start_z()
        for i in range(1, dp):
            to = (me + i) % dp
            m = send(gains, gn_v.at[me], gss.at[i], grs.at[i], to, t)
            m.start()
            gn.append(m)
        own_g = pltpu.make_async_copy(gains, gn_v.at[me], gss.at[0])
        own_g.start()
        xs = []
        for i in range(1, halo + 1):
            m = send(x, xh.at[i - 1], xss.at[i - 1], xrs.at[i - 1], me, (t + i) % nz)
            xs.append(m)

            @pl.when(t + i < nz)
            def _():
                m.start()

        own_r.wait()
        for m in rq:
            m.wait()
        cp = local(req_in, req_s, 2)
        cp.wait()
        parts = cols // 128
        lane = lambda p: pl.ds(p * 128, 128)

        def pick(stage, to):
            for j in range(cap):
                stage[to, j] = loc[req_s[to, 0, j]]

        def exchange(stage, rec, i, load):
            load.wait()
            out = [[] for _ in range(parts)]
            mine = pl.ds(me * cap, cap)

            def go(p, j):
                to = (me + j) % dp
                m = send(stage.at[to, :, :, lane(p)], rec.at[mine, :, lane(p)], mss.at[i, p, j], mrs.at[i, p, j], to, t)
                m.start()
                out[p].append(m)

            for j in range(1, dp):
                pick(stage, (me + j) % dp)
                go(0, j)
            for p in range(1, parts):
                for j in range(1, dp):
                    go(p, j)
            pick(stage, me)
            for p in range(parts):
                own = pltpu.make_async_copy(stage.at[me, :, :, lane(p)], rec.at[mine, :, lane(p)], mss.at[i, p, 0])
                own.start()
                out[p].append(own)
            return out

        ek = exchange(stage_k, rec_k, 0, load_k)
        load_v = local(mem_v, loc, 3)
        for u in gate_up:
            u.start_z()
        for u in proj + out_:
            u.relay_z()
        ev = exchange(stage_v, rec_v, 1, load_v)
        for u in proj + out_:
            u.start_first()
        for u in gate_up:
            u.relay_z()

        for j in range(halo + 1):
            lane_at = pl.multiple_of(jnp.maximum(t - halo + j, 0) * r, 128)
            part = segs[:, pl.ds(lane_at, r)]
            seg_k[:, j * r : (j + 1) * r] = jnp.where(t - halo + j >= 0, part, -jnp.ones_like(part))
        own_seg = segs[:, pl.ds(pl.multiple_of(t * r, 128), r)]
        seg_q[...] = jnp.transpose(jnp.broadcast_to(own_seg, (128, r)))

        left = lax.broadcasted_iota(jnp.int32, (r, HD), 1) < HD // 2
        c1 = tab1[...]
        s1 = pltpu.roll(c1, HD // 2, axis=1)
        cc, sc = jnp.where(left, c1, s1), jnp.where(left, s1, c1)
        for j in range(halo + 1):
            c2 = jnp.broadcast_to(tab2[pl.ds(t + j, 1), :], (r, HD))
            s2 = pltpu.roll(c2, HD // 2, axis=1)
            ce, se = jnp.where(left, c2, s2), jnp.where(left, s2, c2)
            cos_v[j * r : (j + 1) * r, :] = cc * ce - sc * se
            sin_ = sc * ce + cc * se
            sin_v[j * r : (j + 1) * r, :] = jnp.where(left, -sin_, sin_)

        own_g.wait()
        for m in gn:
            m.wait()
        lx.wait()
        gain1 = gain_row(gn_v, 0)
        vx = x_v[...].astype(F32)
        n_v[halo * r :, :] = (vx * inv_rms(vx) * gain1).astype(BF16)
        for i, m in enumerate(xs):
            lo = (halo - 1 - i) * r

            @pl.when(t >= i + 1)
            def _():
                m.wait_recv()
                ch = local(xh.at[i], xh_v, 4)
                ch.wait()
                vh = xh_v[...].astype(F32)
                n_v[lo : lo + r, :] = (vh * inv_rms(vh) * gain1).astype(BF16)

            @pl.when(t < i + 1)
            def _():
                n_v[lo : lo + r, :] = jnp.zeros((r, d), BF16)

        cn = local(n_v, n1, 5)

        def spread(moves, rec, zst, out, i, p):
            for m in moves[p]:
                m.wait()
            lr = local(rec.at[:, :, lane(p)], loc.at[pl.ds(0, dp * cap), :, lane(p)], 6)
            lr.wait()

            @pl.loop(0, nq)
            def _(s):
                for j in range(ksel):
                    zst[s, j, :, lane(p)] = loc[sel[s * ksel + j], :, lane(p)]

            res = []
            for j in range(1, nz):
                to = (t + j) % nz
                m = send(zst.at[to, :, :, lane(p)], out.at[t, :, :, lane(p)], zss.at[i, p, j], zrs.at[i, p, j], me, to)
                m.start()
                res.append(m)
            own = pltpu.make_async_copy(zst.at[t, :, :, lane(p)], out.at[t, :, :, lane(p)], zss.at[i, p, 0])
            own.start()
            return res + [own]

        zk, zv = [], []
        for p in range(parts):
            zk += spread(ek, rec_k, stage_k, mk, 0, p)
        for p in range(parts):
            zv += spread(ev, rec_v, stage_v, mv, 1, p)
        for u in down:
            u.start_z()
        for u in proj:
            u.start_second()
        for u in out_:
            u.start_second()
        for u in gate_up:
            u.start_first()
        for u in proj:
            u.start_core()
        for u in proj:
            u.finish()

        def turned(y, cs_, sn_):
            return jnp.concatenate(
                [turn(y[:, h * HD : (h + 1) * HD], cs_, sn_).astype(BF16) for h in range(cols // HD)], axis=1
            )

        def project(wq_ref, wk_ref, wv_ref, q_ref, k_ref, v_ref):
            @pl.loop(0, halo + 1)
            def _(i):
                at = pl.ds(pl.multiple_of(i * r, r), r)
                n = n_v[at, :]
                k_ref[at, :] = turned(dot_nn(n, wk_ref[...]), cos_v[at, :], sin_v[at, :])
                v_ref[at, :] = dot_nn(n, wv_ref[...]).astype(BF16)

            q_ref[...] = turned(dot_nn(n_v[halo * r :, :], wq_ref[...]), cos_v[halo * r :, :], sin_v[halo * r :, :])

        piped(project, nz, [wcol] * 3, [col(r), col(rt), col(rt)])(wq, wk, wv, q, k, v)
        for u in out_:
            u.start_core()
        for u in down:
            u.relay_z()
        for m in zk + zv:
            m.wait()
        cn.wait()
        for i, m in enumerate(xs):

            @pl.when(t + i + 1 < nz)
            def _():
                m.wait_send()

    nblk = mem_k.shape[0]
    pl.run_scoped(
        forward,
        pltpu.VMEM((nblk, blk, cols), BF16),
        pltpu.VMEM((max(dp, nq), cap, blk, cols), BF16),
        pltpu.VMEM((max(dp, nq), cap, blk, cols), BF16),
        pltpu.VMEM((r, d), BF16),
        pltpu.VMEM((r, d), BF16),
        pltpu.VMEM((rt, d), BF16),
    )

    def attend(q_ref, k_ref, v_ref, mk_ref, mv_ref, o_ref, l_ref):
        km = mk_ref[0].reshape(nm, HD)
        vm = mv_ref[0].reshape(nm, HD)
        for i in range(r // QT):
            at = slice(i * QT, (i + 1) * QT)
            k0 = halo * r - window + i * QT
            ks = slice(k0, k0 + window + QT)
            qq = q_ref[at, :]
            ok = allowed_of(seg_q[at, 0:1], seg_k[:, ks], halo * r + i * QT, k0)
            sl = jnp.where(ok, dot_nt(qq, k_ref[ks, :]), MASKED)
            sm = dot_nt(qq, km)
            mx = jnp.maximum(jnp.max(sl, axis=1, keepdims=True), jnp.max(sm, axis=1, keepdims=True))
            mc = mx * C2
            el = jnp.exp2(sl * C2 - mc)
            em = jnp.exp2(sm * C2 - mc)
            tot = jnp.sum(el, axis=1, keepdims=True) + jnp.sum(em, axis=1, keepdims=True)
            acc = dot_nn(el.astype(BF16), v_ref[ks, :]) + dot_nn(em.astype(BF16), vm)
            o_ref[at, :] = (acc / tot).astype(BF16)
            l_ref[0, at, :] = mc + jnp.log2(tot)

    piped(
        attend,
        heads,
        [head(r), head(rt), head(rt), mem, mem],
        [head(r), row_stat],
        [(POLL["attend"], every(gate_up, "start_second") + every(down, "start_first")),
         (POLL["attend_core"], every(gate_up, "start_core"))],
    )(q, k, v, mk, mv, o, lse)
    for u in out_:
        u.finish()

    sof = lambda us, *ws: [u for u in us if u.which in ws]

    def units(G):
        res = []
        for i, (w, rows_, bf) in enumerate(sunits):
            if w in G:
                u = Scatter(g, G[w], rows_, bf, rbufs[i], rsems[i], outs[w])
                u.which = w
                res.append(u)
        return res

    def rest(h_v, n2_v, c_v, n2h, ch, acc, *gf):
        fu = units(dict(enumerate(gf)))
        lc = local(cot, c_v, 0)
        lx = local(x, n2_v, 1)
        to_o = to_peer(o, po)
        lx.wait()
        h_v[...] = n2_v[...].astype(F32)

        def out_proj(o_ref, w_ref):
            h_v[...] += dot_nn(o_ref[...], w_ref[0])

        piped(out_proj, nz, [col(r), wrow(cols)])(o, wo)
        gain2 = gain_row(gn_v, 1)
        hv = h_v[...]
        n2_v[...] = (hv * inv_rms(hv) * gain2).astype(BF16)
        lc.wait()
        p_n = theirs(n2_v, pn_v) + theirs(c_v, pc_v)
        keep_half(n2_v, n2h)
        keep_half(c_v, ch)
        for u in gate_up:
            u.finish()

        def feed_forward(hid_v, a_v, b_v):
            tile = ff // 2
            give = lambda src, dst, i, u: send(src.at[u], dst.at[u], fss.at[i, u], frs.at[i, u], peer, t)
            keep = lambda u: pltpu.make_async_copy(hid_v.at[u], hid.at[u], fls.at[u])

            def hidden(wg_ref, wu_ref):
                u = pl.program_id(0)

                @pl.loop(0, 2)
                def _(i):
                    at = pl.ds(pl.multiple_of(i * tile, 16), tile)
                    gate = dot_nt(wg_ref[0, at, :], n2_v[...])
                    up = dot_nt(wu_ref[0, at, :], n2_v[...])
                    sig = 1.0 / (1.0 + jnp.exp(-gate))
                    act = gate * sig
                    hid_v[u, at, :] = (act * up).astype(BF16)
                    a_v[u, at, :] = (up * (sig * (1.0 + gate * (1.0 - sig)))).astype(BF16)
                    b_v[u, at, :] = act.astype(BF16)

                give(hid_v, phid, 0, u).start()
                keep(u).start()

            piped(hidden, nz, [wrow(ff)] * 2)(wg, wu)
            for u in down:
                u.start_second()
            for m in p_n:
                m.wait()

            def ffn_grads(mine_t, B, i, mine_v, peer_v, out):
                for u in range(nz):
                    give(mine_t, B, i, u).wait()

                def body(b_ref):
                    u = pl.program_id(0)
                    y = (dot_nn(mine_t[u], mine_v[...]) + dot_nn(b_ref[0], peer_v[...])).astype(BF16)
                    for e in range(nb):
                        out[e, u] = y[:, e * 128 : (e + 1) * 128]

                piped(body, nz, [piece])(B)

            ffn_grads(hid_v, phid, 0, ch, pc_v, gf[2])
            for u in sof(fu, 2):
                u.start_first()
            for u in down:
                u.start_core()
            for u in down:
                u.finish()
            acc[0:r, :] = jnp.zeros((r, d), F32)

            def hidden_back(wd_ref, wg_ref, wu_ref):
                u = pl.program_id(0)

                @pl.loop(0, 2)
                def _(i):
                    at = pl.ds(pl.multiple_of(i * tile, 16), tile)
                    dhid = dot_nt(wd_ref[0, at, :], c_v[...])
                    a_v[u, at, :] = (dhid * a_v[u, at, :].astype(F32)).astype(BF16)
                    b_v[u, at, :] = (dhid * b_v[u, at, :].astype(F32)).astype(BF16)

                give(a_v, pdg, 1, u).start()
                give(b_v, pdu, 2, u).start()
                acc[0:r, :] += dot_tn(a_v[u], wg_ref[0]) + dot_tn(b_v[u], wu_ref[0])

            piped(hidden_back, nz, [wrow(ff)] * 3)(wd, wg, wu)
            ffn_grads(a_v, pdg, 1, n2h, pn_v, gf[0])
            for u in sof(fu, 2):
                u.start_second()
            for u in sof(fu, 0):
                u.start_first()
            ffn_grads(b_v, pdu, 2, n2h, pn_v, gf[1])
            for u in sof(fu, 1):
                u.start_first()
            for u in range(nz):
                keep(u).wait()

        pl.run_scoped(feed_forward, *[pltpu.VMEM((nz, ff, r), BF16)] * 3)
        to_o.wait()

        def attention_back(dhb_v, dhbh, n1h, sdk, sdv, hb_v, *ga):
            G = dict(zip((3, 4, 5, 6), ga))
            us = fu + units(G)
            of = lambda *ws: sof(us, *ws)
            dn = acc[0:r, :]
            hv = h_v[...]
            iv = inv_rms(hv)
            gp[1:2, :] = jnp.sum(dn * hv * iv, axis=0, keepdims=True)
            gdn = dn * gain2
            dh = c_v[...].astype(F32) + iv * gdn - hv * (iv * iv * iv * jnp.mean(hv * gdn, axis=1, keepdims=True))
            acc[0:r, :] = dh
            dhb_v[...] = dh.astype(BF16)
            ld = local(acc.at[pl.ds(0, r)], dh_o, 2)
            p_r = theirs(dhb_v, pdhb_v) + theirs(n1, pn1_v)
            keep_half(dhb_v, dhbh)
            ln = [local(lane_block(n1, e, core), n1h.at[:, pl.ds(e * 128, 128)], 8 + e) for e in range(nb)]

            def mixed_grad(w_ref, do_ref):
                do_ref[...] = dot_nt(dhb_v[...], w_ref[0]).astype(BF16)

            piped(mixed_grad, nz, [wrow(cols)], [col(r)])(wo, do)
            for u in of(2):
                u.start_z()

            for m in p_r + ln:
                m.wait()

            def out_grads(a_ref, b_ref):
                u = pl.program_id(0)
                y = (dot_tn(a_ref[...], dhbh[...]) + dot_tn(b_ref[...], pdhb_v[...])).astype(BF16)
                for e in range(nb):
                    G[3][e, u] = y[:, e * 128 : (e + 1) * 128]

            piped(out_grads, nz, [col(r)] * 2)(o, po)
            for u in of(3):
                u.start_first()

            scale = HD**-0.5

            def attend_back(q_ref, k_ref, v_ref, mk_ref, mv_ref, o_ref, l_ref, do_ref, dq_ref, dk_ref, dv_ref):
                km = mk_ref[0].reshape(nm, HD)
                vm = mv_ref[0].reshape(nm, HD)
                sdk[...] = jnp.zeros_like(sdk)
                sdv[...] = jnp.zeros_like(sdv)
                for i in range(r // QT):
                    at = slice(i * QT, (i + 1) * QT)
                    k0 = halo * r - window + i * QT
                    ks = slice(k0, k0 + window + QT)
                    own = slice(halo * r + i * QT, halo * r + (i + 1) * QT)
                    qq, dd = q_ref[at, :], do_ref[at, :]
                    lse_c = l_ref[0, at, :]
                    delta = jnp.sum(dd.astype(F32) * o_ref[at, :].astype(F32), axis=1, keepdims=True)
                    ok = allowed_of(seg_q[at, 0:1], seg_k[:, ks], halo * r + i * QT, k0)
                    pm = jnp.exp2(dot_nt(qq, km) * C2 - lse_c)
                    dsm = (pm * (dot_nt(dd, vm) - delta)).astype(BF16)
                    plo = jnp.where(ok, jnp.exp2(dot_nt(qq, k_ref[ks, :]) * C2 - lse_c), 0.0)
                    dsl = (plo * (dot_nt(dd, v_ref[ks, :]) - delta)).astype(BF16)
                    dqv = (dot_nn(dsm, km) + dot_nn(dsl, k_ref[ks, :])) * scale
                    dq_ref[at, :] = turn(dqv, cos_v[own, :], -sin_v[own, :]).astype(BF16)
                    sdk[ks, :] += dot_tn(dsl, qq)
                    sdv[ks, :] += dot_tn(plo.astype(BF16), dd)
                dk_ref[...] = turn(sdk[...] * scale, cos_v[...], -sin_v[...]).astype(BF16)
                dv_ref[...] = sdv[...].astype(BF16)

            piped(
                attend_back,
                heads,
                [head(r), head(rt), head(rt), mem, mem, head(r), row_stat, head(r)],
                [head(r), head(rt), head(rt)],
                [(POLL["back_down"], every(of(2), "relay_z")), (POLL["back_gate"], every(of(0), "start_second"))],
            )(q, k, v, mk, mv, o, lse, do, dq, dk, dv)
            p_att = [to_peer(dq, pdq), to_peer(dk, pdk), to_peer(dv, pdv)]
            ld.wait()

            acc[...] = jnp.zeros_like(acc)

            def halo_back(dk_ref, dv_ref, wk_ref, wv_ref):
                acc[: halo * r, :] += dot_nt(dk_ref[...], wk_ref[...]) + dot_nt(dv_ref[...], wv_ref[...])

            piped(halo_back, nz, [col(halo * r)] * 2 + [wcol] * 2)(dk, dv, wk, wv)
            hb_v[...] = acc[: halo * r, :].astype(BF16)
            hd = []
            for j in range(halo):
                m = send(hb_v.at[pl.ds((halo - 1 - j) * r, r), :], more.at[j], hss.at[j], hrs.at[j], me,
                         (t + nz - 1 - j) % nz)
                hd.append(m)

                @pl.when(t >= j + 1)
                def _():
                    m.start()

            for u in of(1):
                u.start_second()

            for m in p_att:
                m.wait()

            own = pl.ds(halo * r, r)

            def grads_of(out, p0, p1, a0, a1):
                def body(x_ref, y_ref):
                    u = pl.program_id(0)
                    y = (dot_tn(a0[...], x_ref[...]) + dot_tn(a1[...], y_ref[...])).astype(BF16)
                    for e in range(nb):
                        out[e, u] = y[e * 128 : (e + 1) * 128, :]

                n = p0.shape[0]
                piped(body, nz, [col(n)] * 2)(p0, p1)

            grads_of(G[4], dq, pdq, n1h.at[own], pn1_v.at[own])
            for u in of(4):
                u.start_first()
            grads_of(G[5], dk, pdk, n1h, pn1_v)
            for u in of(5):
                u.start_first()
            grads_of(G[6], dv, pdv, n1h, pn1_v)
            for u in of(6):
                u.start_first()
            for u in of(0):
                u.start_z()

            def own_back(dq_ref, dk_ref, dv_ref, wq_ref, wk_ref, wv_ref):
                acc[halo * r :, :] += (
                    dot_nt(dq_ref[...], wq_ref[...]) + dot_nt(dk_ref[...], wk_ref[...]) + dot_nt(dv_ref[...], wv_ref[...])
                )

            own_rows = pl.BlockSpec((r, cols), lambda u: (halo, u))
            lx2 = local(x, c_v, 3)
            piped(
                own_back,
                nz,
                [col(r), own_rows, own_rows] + [wcol] * 3,
                (),
                [(POLL["own_out"], every(of(3), "start_second")), (POLL["own_up"], every(of(1), "start_z"))],
            )(dq, dk, dv, wq, wk, wv)
            for u in of(0):
                u.relay_z()
            for u in of(2):
                u.finish()

            lx2.wait()
            vx = c_v[...].astype(F32)
            gp[0:1, :] = jnp.sum(acc[halo * r :, :] * vx * inv_rms(vx), axis=0, keepdims=True)
            for j in range(halo):

                @pl.when(t >= j + 1)
                def _():
                    cx = local(xh.at[j], n2_v, 4)
                    cx.wait()
                    vh = n2_v[...].astype(F32)
                    lo = (halo - 1 - j) * r
                    gp[0:1, :] = gp[0:1, :] + jnp.sum(acc[lo : lo + r, :] * vh * inv_rms(vh), axis=0, keepdims=True)

            zg = []
            for i in range(1, nz):
                m = send(gp, gz.at[i - 1], ass.at[i - 1], ars.at[i - 1], me, (t + i) % nz)
                m.start()
                zg.append(m)

            def feed_out(hid_ref, wd_ref):
                h_v[...] += dot_tn(hid_ref[0], wd_ref[0])

            piped(
                feed_out,
                nz,
                [piece, wrow(ff)],
                (),
                [(POLL["out_z"], every(of(1), "relay_z") + every(of(3), "start_z")),
                 (POLL["out_q"], every(of(4, 5), "start_second"))],
            )(hid, wd)
            lo_ = local(h_v, block_out, 5)
            for u in of(0):
                u.finish()
            for m in zg:
                m.wait()
            tot = gp[...]
            for i in range(nz - 1):
                tot = tot + gz[i]
            for e in range(dp):
                gs[e] = tot[:, e * 128 : (e + 1) * 128]
            ds_ = []
            for i in range(1, dp):
                to = (me + i) % dp
                m = send(gs.at[to], gd.at[me], dss.at[i], drs.at[i], to, t)
                m.start()
                ds_.append(m)
            og = pltpu.make_async_copy(gs.at[me], gd.at[me], dss.at[0])
            og.start()
            lo_.wait()
            ld2 = local(dh_o, h_v, 6)
            for u in of(6):
                u.start_second()
            for u in of(3):
                u.relay_z()
            for u in of(4, 5):
                u.start_z()

            for j, m in enumerate(hd):

                @pl.when(t + j + 1 < nz)
                def _():
                    m.wait_recv()
                    acc[halo * r :, :] = acc[halo * r :, :] + more[j].astype(F32)

                @pl.when(t >= j + 1)
                def _():
                    m.wait_send()

            ld2.wait()
            for u in of(6):
                u.start_z()
            vx = c_v[...].astype(F32)
            iv = inv_rms(vx)
            gdx = acc[halo * r :, :] * gain_row(gn_v, 0)
            acc[halo * r :, :] = h_v[...] + iv * gdx - vx * (iv * iv * iv * jnp.mean(vx * gdx, axis=1, keepdims=True))
            lg = local(acc.at[pl.ds(halo * r, r)], grad_in, 7)
            for u in of(4, 5, 6):
                u.relay_z()
            for u in of(1, 3):
                u.finish()
            og.wait()
            for m in ds_:
                m.wait()
            tot = gd[0]
            for e in range(1, dp):
                tot = tot + gd[e]
            gout[...] = tot
            for u in of(4, 5, 6):
                u.finish()
            lg.wait()

        pl.run_scoped(
            attention_back,
            pltpu.VMEM((r, d), BF16),
            pltpu.VMEM((r, half), BF16),
            pltpu.VMEM((rt, half), BF16),
            pltpu.VMEM((rt, HD), F32),
            pltpu.VMEM((rt, HD), F32),
            pltpu.VMEM((halo * r, d), BF16),
            *[pltpu.VMEM((nb, nz) + tuple(o_.shape), BF16) for o_ in outs[3:]],
        )

    pl.run_scoped(
        rest,
        pltpu.VMEM((r, d), F32),
        pltpu.VMEM((r, d), BF16),
        pltpu.VMEM((r, d), BF16),
        pltpu.VMEM((r, half), BF16),
        pltpu.VMEM((r, half), BF16),
        pltpu.VMEM((rt, d), F32),
        *[pltpu.VMEM((nb, nz) + tuple(o_.shape), BF16) for o_ in outs[:3]],
    )


def run_layer(g, cap, halo, window, requests, sel, segs, x, gains, mem_k, mem_v, cot, shards, nq, ksel):
    blk, cols = mem_k.shape[1:]
    r, d = x.shape
    rt = (halo + 1) * r
    nz, dp = g.nz, g.dp
    half = d // 2
    kd, ff = shards[0].shape[0], shards[4].shape[0]
    heads = d // HD
    tab1, tab2 = (jnp.asarray(v) for v in rope_tables(halo, nz, r))
    gunits = []
    for w, s in enumerate(shards):
        n, lanes_ = s.shape[0], w >= 3
        if w in (0, 4):
            gunits.append((w, (0, n), True, lanes_))
        elif w in (1, 5):
            gunits.append((w, (0, n), False, lanes_))
        else:
            gunits.append((w, (0, n // 2), True, lanes_))
            gunits.append((w, (n // 2, n - n // 2), False, lanes_))
    pieces = [(ff, 128)] * 3 + [(cols, 128)] + [(kd, cols)] * 3
    sunits = []
    for w in (2, 0, 1, 3):
        n = pieces[w][0]
        sunits += [(w, (0, n // 2), True), (w, (n // 2, n - n // 2), False)]
    sunits += [(4, (0, kd), True), (5, (0, kd), False), (6, (0, kd // 2), True), (6, (kd // 2, kd - kd // 2), False)]
    any_ = pl.BlockSpec(memory_space=pl.ANY)
    vm = pl.BlockSpec(memory_space=pltpu.VMEM)
    dma = lambda *n: pltpu.SemaphoreType.DMA(n)
    st = lambda s, dt=BF16: jax.ShapeDtypeStruct(s, dt)
    nsem = len(gunits) * gather_sems(g)
    hbm = (
        [st((d, d))] * 3 + [st((nz, cols, d))] + [st((nz, ff, d))] * 3
        + [st((halo, r, d))] + [st((nz, ksel, blk, cols))] * 2 + [st((dp * cap, blk, cols))] * 2
        + [st((rt, d)), st((r, d)), st((rt, d)), st((rt, d)), st((r, d)), st((heads, r, 1), F32)]
        + [st((nz, ff, r))] * 4 + [st((r, d)), st((r, d)), st((rt, d)), st((rt, d))]
        + [st((r, d)), st((rt, d)), st((rt, d)), st((r, d)), st((r, d), F32)]
    )
    out_shape = [st((2, 128), F32)] + [st(p, F32) for p in pieces] + [st((r, d), F32)] * 2 + hbm
    scratch = [pltpu.VMEM((dp, 8, 128), jnp.int32), pltpu.SMEM((dp, 8, 128), jnp.int32), pltpu.VMEM((dp, 2, 128), F32)]
    scratch += [pltpu.VMEM((rt, HD), F32)] * 2
    for w, (lo, n), bf in sunits:
        cc = pieces[w][1]
        n1_, n2_ = (g.nb, g.na) if bf else (g.na, g.nb)
        scratch += [
            pltpu.VMEM((n1_ - 1, n2_, nz, n, cc), BF16),
            pltpu.VMEM((n2_ - 1, nz, n, cc), BF16),
            pltpu.VMEM((nz - 1, n, cc), BF16),
        ]
    scratch += [dma(scatter_sems(g))] * (2 * len(sunits))
    scratch += [pltpu.VMEM((r, half), BF16)] * 2 + [pltpu.VMEM((rt, half), BF16), pltpu.VMEM((r, half), BF16)]
    scratch += [pltpu.VMEM((halo, r, d), BF16)]
    scratch += [pltpu.VMEM((nz - 1, 2, d), F32), pltpu.VMEM((dp, 2, 128), F32), pltpu.VMEM((dp, 2, 128), F32), pltpu.VMEM((2, d), F32)]
    ncore = 4 + 4 * (dp // 2)
    parts = cols // 128
    scratch += [dma(nsem), dma(nsem), dma(8 + dp // 2), dma(dp), dma(dp), dma(dp), dma(dp), dma(2, parts, dp), dma(2, parts, dp)]
    scratch += [dma(2, parts, nz), dma(2, parts, nz), dma(halo), dma(halo)]
    scratch += [dma(ncore), dma(ncore), dma(halo), dma(halo), dma(nz), dma(nz), dma(dp), dma(dp)]
    scratch += [dma(3, nz), dma(3, nz), dma(nz)]
    scratch += [pltpu.VMEM((r, 128), jnp.int32), pltpu.VMEM((1, rt), jnp.int32)]
    cfg = (cap, nq, ksel, halo, window, gunits, sunits)
    return pl.pallas_call(
        functools.partial(layer_kernel, g, cfg),
        out_shape=out_shape,
        in_specs=[vm, pl.BlockSpec(memory_space=pltpu.SMEM), vm, vm, vm] + [any_] * (5 + len(shards)),
        out_specs=[vm] * 8 + [any_] * (2 + len(hbm)),
        scratch_shapes=scratch,
        compiler_params=pltpu.CompilerParams(collective_id=0, has_side_effects=True, vmem_limit_bytes=67043328),
        name="layer",
    )(requests, sel, segs, tab1, tab2, x, gains, mem_k, mem_v, cot, *shards)


def hand_out(gout, arrays):
    n = len(arrays)

    def kern(*refs):
        ins, outs, bufs, (ls, ss) = refs[: n + 1], refs[n + 1 : 2 * n + 3], refs[2 * n + 3 : 3 * n + 3], refs[3 * n + 3 :]
        loads = [pltpu.make_async_copy(ins[i + 1], bufs[i], ls.at[i]) for i in range(n)]
        stores = [pltpu.make_async_copy(bufs[i], outs[i + 2], ss.at[i]) for i in range(n)]
        for m in loads:
            m.start()
        outs[0][...] = ins[0][0:1, :]
        outs[1][...] = ins[0][1:2, :]
        for a, b in zip(loads, stores):
            a.wait()
            b.start()
        for m in stores:
            m.wait()

    any_ = pl.BlockSpec(memory_space=pl.ANY)
    vm = pl.BlockSpec(memory_space=pltpu.VMEM)
    gain = jax.ShapeDtypeStruct((1, 128), F32)
    return pl.pallas_call(
        kern,
        in_specs=[vm] + [any_] * n,
        out_specs=[vm] * 2 + [any_] * n,
        out_shape=[gain, gain] + [jax.ShapeDtypeStruct(a.shape, a.dtype) for a in arrays],
        scratch_shapes=[pltpu.VMEM(a.shape, a.dtype) for a in arrays] + [pltpu.SemaphoreType.DMA((n,))] * 2,
        compiler_params=pltpu.CompilerParams(vmem_limit_bytes=67043328),
        name="hand_out",
    )(gout, *arrays)


HEADS = 8
QB = 512


def normalize(field, gain_vec):
    return field * lax.rsqrt(jnp.mean(field * field, axis=-1, keepdims=True) + EPSILON) * gain_vec


def rotate(field, heads_here):
    row_total = field.shape[0]
    head_size = field.shape[1] // heads_here
    half_width = head_size // 2
    frequencies = 10000.0 ** (-jnp.arange(half_width, dtype=jnp.float32) * 2.0 / head_size)
    angles = jnp.arange(row_total, dtype=jnp.float32)[:, None] * frequencies[None, :]
    cosine = jnp.cos(angles)[:, None, :]
    sine_table = jnp.sin(angles)[:, None, :]
    split_heads = field.reshape(row_total, heads_here, head_size)
    first_half = split_heads[..., :half_width]
    second_half = split_heads[..., half_width:]
    turned = jnp.concatenate(
        [
            first_half * cosine - second_half * sine_table,
            second_half * cosine + first_half * sine_table,
        ],
        axis=-1,
    )
    return turned.reshape(row_total, heads_here * head_size)


def contract_rows(left, right):
    return lax.dot_general(
        left, right, (((0,), (0,)), ((), ())), preferred_element_type=jnp.float32
    )


def against(left, right):
    return lax.dot_general(
        left, right, (((1,), (1,)), ((), ())), preferred_element_type=jnp.float32
    )


def spread_rows(local_rows, matrices):
    piece_rows = lax.all_gather(local_rows, "tensor", axis=0, tiled=True)
    return jnp.concatenate(
        [jnp.dot(piece_rows, matrix, preferred_element_type=jnp.float32) for matrix in matrices],
        axis=1,
    )


def reduce_rows(left, right):
    return lax.psum_scatter(
        jnp.dot(left, right, preferred_element_type=jnp.float32).astype(jnp.bfloat16),
        "tensor",
        scatter_dimension=0,
        tiled=True,
    ).astype(jnp.float32)


def return_rows(pairs):
    summed = against(pairs[0][0], pairs[0][1])
    for grad_block, matrix in pairs[1:]:
        summed = summed + against(grad_block, matrix)
    return lax.psum_scatter(
        summed.astype(jnp.bfloat16), "tensor", scatter_dimension=0, tiled=True
    ).astype(jnp.float32)


def weight_grads(local_rows, grads_list):
    piece_rows = lax.all_gather(local_rows, "tensor", axis=0, tiled=True)
    return tuple((contract_rows(piece_rows, grad_one) for grad_one in grads_list))


def all_rows(local_grad):
    return lax.all_gather(local_grad, "tensor", axis=0, tiled=True)


def on_device_any(
    block_in,
    segments,
    retrieved,
    partner,
    memory_keys,
    memory_values,
    gain_attn,
    w_query,
    w_key,
    w_value,
    w_out,
    gain_ffn,
    w_gate,
    w_up,
    w_down,
    cotangent,
):
    tensor_size = lax.axis_size("tensor")
    dp_size = lax.axis_size("dp")
    heads_here = HEADS // tensor_size
    head_width = heads_here * HD
    score_scale = HD ** (-0.5)
    seq_len = segments.shape[1]
    query_blocks = seq_len // QB
    stream_in = block_in[0].astype(jnp.float32)
    seg_row = segments[0]
    positions = jnp.arange(seq_len)
    gathered = (
        lax.all_gather(gain_attn, "dp", axis=0, tiled=True),
        lax.all_gather(w_query, "dp", axis=0, tiled=True),
        lax.all_gather(w_key, "dp", axis=0, tiled=True),
        lax.all_gather(w_value, "dp", axis=0, tiled=True),
        lax.all_gather(w_out, "dp", axis=1, tiled=True),
        lax.all_gather(gain_ffn, "dp", axis=0, tiled=True),
        lax.all_gather(w_gate, "dp", axis=0, tiled=True),
        lax.all_gather(w_up, "dp", axis=0, tiled=True),
        lax.all_gather(w_down, "dp", axis=1, tiled=True),
    )
    gain_one, query_w, key_w, value_w, out_w, gain_two, gate_w, up_w, down_w = gathered
    wanted = retrieved[0].reshape(-1)
    request_total = wanted.shape[0]
    capacity = max(2, (2 * request_total + dp_size - 1) // dp_size)
    blocks_dev = memory_keys.shape[1]
    from_partner = wanted // MEMB
    block_index = wanted % MEMB
    owner_dev = block_index // blocks_dev
    local_block = block_index % blocks_dev
    seq_id = jnp.where(from_partner == 0, lax.axis_index("dp"), partner[0])
    owner_hits = (owner_dev[:, None] == jnp.arange(dp_size)[None, :]).astype(jnp.int32)
    slot_index = jnp.sum((jnp.cumsum(owner_hits, axis=0) - 1) * owner_hits, axis=1)
    requests = (
        jnp.zeros((dp_size, capacity, 2), jnp.int32)
        .at[owner_dev, slot_index]
        .set(jnp.stack([seq_id, local_block], axis=-1))
    )
    received = lax.all_to_all(requests, "dp", split_axis=0, concat_axis=0, tiled=True)
    picked_keys = memory_keys[received[..., 0], received[..., 1]]
    picked_values = memory_values[received[..., 0], received[..., 1]]
    fetched_keys = lax.all_to_all(picked_keys, "dp", split_axis=0, concat_axis=0, tiled=True)
    fetched_values = lax.all_to_all(picked_values, "dp", split_axis=0, concat_axis=0, tiled=True)
    memory_k = fetched_keys[owner_dev, slot_index].reshape(query_blocks, -1, heads_here, HD)
    memory_v = fetched_values[owner_dev, slot_index].reshape(query_blocks, -1, heads_here, HD)
    normed = normalize(stream_in, gain_one.astype(jnp.float32)).astype(jnp.bfloat16)
    qkv_rows = spread_rows(normed, [query_w, key_w, value_w])
    query_raw = qkv_rows[:, :head_width]
    key_raw = qkv_rows[:, head_width : 2 * head_width]
    queries = rotate(query_raw, heads_here).astype(jnp.bfloat16)
    keys_all = rotate(key_raw, heads_here).astype(jnp.bfloat16).reshape(seq_len, heads_here, HD)
    values_all = qkv_rows[:, 2 * head_width :].astype(jnp.bfloat16).reshape(seq_len, heads_here, HD)
    query_tiles = queries.reshape(query_blocks, QB, heads_here, HD)
    seg_tiles = seg_row.reshape(query_blocks, QB)
    pos_tiles = positions.reshape(query_blocks, QB)

    def scores_of(query_blk, seg_blk, pos_blk, key_mem):
        local_scores = jnp.einsum(
            "qhd,khd->hqk", query_blk, keys_all, preferred_element_type=jnp.float32
        )
        memory_scores = jnp.einsum(
            "qhd,khd->hqk", query_blk, key_mem, preferred_element_type=jnp.float32
        )
        raw_scores = jnp.concatenate([local_scores, memory_scores], axis=-1) * score_scale
        allowed = (seg_blk[:, None] == seg_row[None, :]) & (positions[None, :] <= pos_blk[:, None])
        allowed = jnp.concatenate(
            [allowed, jnp.ones((query_blk.shape[0], key_mem.shape[0]), dtype=jnp.bool_)], axis=1
        )
        return (raw_scores, allowed)

    def forward_block(pieces):
        query_blk, seg_blk, pos_blk, key_mem, value_mem = pieces
        raw_scores, allowed = scores_of(query_blk, seg_blk, pos_blk, key_mem)
        masked = jnp.where(allowed[None], raw_scores, MASKED)
        row_max = jnp.max(masked, axis=-1, keepdims=True)
        expo = jnp.exp(masked - row_max)
        row_total = jnp.sum(expo, axis=-1, keepdims=True)
        weights_soft = (expo / row_total).astype(jnp.bfloat16)
        values_both = jnp.concatenate([values_all, value_mem], axis=0)
        result = jnp.einsum(
            "hqk,khd->qhd", weights_soft, values_both, preferred_element_type=jnp.float32
        )
        return (result, (row_max + jnp.log(row_total))[..., 0])

    attended, log_totals = lax.map(
        forward_block, (query_tiles, seg_tiles, pos_tiles, memory_k, memory_v)
    )
    mixed = attended.reshape(seq_len, head_width).astype(jnp.bfloat16)
    stream = stream_in + reduce_rows(mixed, out_w)
    normed_ffn = normalize(stream, gain_two.astype(jnp.float32)).astype(jnp.bfloat16)
    gate_up = spread_rows(normed_ffn, [gate_w, up_w])
    hidden_width = gate_w.shape[1]
    gate_pre = gate_up[:, :hidden_width]
    up_pre = gate_up[:, hidden_width:]
    hidden = (jax.nn.silu(gate_pre) * up_pre).astype(jnp.bfloat16)
    block_out = stream + reduce_rows(hidden, down_w)
    gathered_back = (
        lax.all_gather(gain_attn, "dp", axis=0, tiled=True),
        lax.all_gather(w_query, "dp", axis=0, tiled=True),
        lax.all_gather(w_key, "dp", axis=0, tiled=True),
        lax.all_gather(w_value, "dp", axis=0, tiled=True),
        lax.all_gather(w_out, "dp", axis=1, tiled=True),
        lax.all_gather(gain_ffn, "dp", axis=0, tiled=True),
        lax.all_gather(w_gate, "dp", axis=0, tiled=True),
        lax.all_gather(w_up, "dp", axis=0, tiled=True),
        lax.all_gather(w_down, "dp", axis=1, tiled=True),
    )
    gain_one, query_w, key_w, value_w, out_w, gain_two, gate_w, up_w, down_w = gathered_back
    dout_rows = cotangent[0]

    def gated(gate_in, up_in):
        return jax.nn.silu(gate_in) * up_in

    dout_full = all_rows(dout_rows)
    grad_down = contract_rows(hidden, dout_full)
    d_hidden = against(dout_full, down_w)
    gated_value, pull_gated = jax.vjp(gated, gate_pre, up_pre)
    d_gate, d_up = pull_gated(d_hidden)
    d_gate = d_gate.astype(jnp.bfloat16)
    d_up = d_up.astype(jnp.bfloat16)
    d_norm_ffn = return_rows([(d_gate, gate_w), (d_up, up_w)])
    grad_gate, grad_up = weight_grads(normed_ffn, [d_gate, d_up])
    norm_value, pull_norm_ffn = jax.vjp(normalize, stream, gain_two.astype(jnp.float32))
    d_stream_norm, grad_gain_ffn = pull_norm_ffn(d_norm_ffn)
    d_stream = dout_rows.astype(jnp.float32) + d_stream_norm
    d_stream_full = all_rows(d_stream.astype(jnp.bfloat16))
    grad_out = contract_rows(mixed, d_stream_full)
    d_mixed = against(d_stream_full, out_w).astype(jnp.bfloat16)
    d_mixed_tiles = d_mixed.reshape(query_blocks, QB, heads_here, HD)

    def backward_block(carry_sums, pieces):
        key_sum, value_sum = carry_sums
        query_blk, seg_blk, pos_blk, key_mem, value_mem, log_blk, grad_blk = pieces
        raw_scores, allowed = scores_of(query_blk, seg_blk, pos_blk, key_mem)
        probs = jnp.where(allowed[None], jnp.exp(raw_scores - log_blk[..., None]), 0.0)
        values_both = jnp.concatenate([values_all, value_mem], axis=0)
        d_probs = jnp.einsum(
            "qhd,khd->hqk", grad_blk, values_both, preferred_element_type=jnp.float32
        )
        shared = jnp.sum(probs * d_probs, axis=-1, keepdims=True)
        d_scores = (probs * (d_probs - shared)).astype(jnp.bfloat16)
        probs_low = probs.astype(jnp.bfloat16)
        keys_both = jnp.concatenate([keys_all, key_mem], axis=0)
        d_query = (
            jnp.einsum("hqk,khd->qhd", d_scores, keys_both, preferred_element_type=jnp.float32)
            * score_scale
        )
        key_sum = (
            key_sum
            + jnp.einsum(
                "hqk,qhd->khd",
                d_scores[..., :seq_len],
                query_blk,
                preferred_element_type=jnp.float32,
            )
            * score_scale
        )
        value_sum = value_sum + jnp.einsum(
            "hqk,qhd->khd", probs_low[..., :seq_len], grad_blk, preferred_element_type=jnp.float32
        )
        return ((key_sum, value_sum), d_query)

    zero_grads = jnp.zeros((seq_len, heads_here, HD), jnp.float32)
    (d_keys, d_values), d_queries = lax.scan(
        backward_block,
        (zero_grads, zero_grads),
        (query_tiles, seg_tiles, pos_tiles, memory_k, memory_v, log_totals, d_mixed_tiles),
    )

    def turn(field):
        return rotate(field, heads_here)

    turned_value, pull_turn = jax.vjp(turn, query_raw)
    d_query_raw = pull_turn(d_queries.reshape(seq_len, head_width))[0].astype(jnp.bfloat16)
    d_key_raw = pull_turn(d_keys.reshape(seq_len, head_width))[0].astype(jnp.bfloat16)
    d_value_raw = d_values.reshape(seq_len, head_width).astype(jnp.bfloat16)
    d_norm_attn = return_rows([(d_query_raw, query_w), (d_key_raw, key_w), (d_value_raw, value_w)])
    grad_query, grad_key, grad_value = weight_grads(normed, [d_query_raw, d_key_raw, d_value_raw])
    norm_first, pull_norm_attn = jax.vjp(normalize, stream_in, gain_one.astype(jnp.float32))
    d_input_norm, grad_gain_attn = pull_norm_attn(d_norm_attn)
    grad_in = d_stream + d_input_norm
    grad_gain_attn, grad_gain_ffn = lax.psum((grad_gain_attn, grad_gain_ffn), "tensor")
    results = (
        lax.psum_scatter(
            grad_gain_attn.astype(jnp.bfloat16), "dp", scatter_dimension=0, tiled=True
        ).astype(jnp.float32),
        lax.psum_scatter(
            grad_query.astype(jnp.bfloat16), "dp", scatter_dimension=0, tiled=True
        ).astype(jnp.float32),
        lax.psum_scatter(
            grad_key.astype(jnp.bfloat16), "dp", scatter_dimension=0, tiled=True
        ).astype(jnp.float32),
        lax.psum_scatter(
            grad_value.astype(jnp.bfloat16), "dp", scatter_dimension=0, tiled=True
        ).astype(jnp.float32),
        lax.psum_scatter(
            grad_out.astype(jnp.bfloat16), "dp", scatter_dimension=1, tiled=True
        ).astype(jnp.float32),
        lax.psum_scatter(
            grad_gain_ffn.astype(jnp.bfloat16), "dp", scatter_dimension=0, tiled=True
        ).astype(jnp.float32),
        lax.psum_scatter(
            grad_gate.astype(jnp.bfloat16), "dp", scatter_dimension=0, tiled=True
        ).astype(jnp.float32),
        lax.psum_scatter(
            grad_up.astype(jnp.bfloat16), "dp", scatter_dimension=0, tiled=True
        ).astype(jnp.float32),
        lax.psum_scatter(
            grad_down.astype(jnp.bfloat16), "dp", scatter_dimension=1, tiled=True
        ).astype(jnp.float32),
    )
    return (block_out[None], grad_in[None]) + results


def on_device(*args):
    x, dp = args[0], lax.axis_size("dp")
    side = math.isqrt(dp // 2)
    if 2 * side * side == dp and x.shape[2] % (128 * dp) == 0:
        return on_device_rows(*args)
    return on_device_any(*args)


def on_device_rows(
    block_in, segments, retrieved, partner, memory_keys, memory_values,
    gain_attn, w_query, w_key, w_value, w_out, gain_ffn, w_gate, w_up, w_down, cotangent,
):
    g = Grid(lax.axis_size("dp"), lax.axis_size("tensor"))
    t, me = lax.axis_index("tensor"), lax.axis_index("dp")
    x, c = block_in[0], cotangent[0]
    r, d = x.shape
    seq_len = segments.shape[1]
    window = seq_len // 4
    halo = -(-window // r)
    nq, ksel = retrieved.shape[1:]
    cap = max(2, -(-2 * nq * ksel // g.dp))
    req, sel = plan_requests(retrieved[0], partner[0], g.dp, memory_keys.shape[1], cap)
    gains = jnp.stack([gain_attn, gain_ffn]).astype(F32)
    flat = lambda m: m.reshape((-1,) + m.shape[2:])
    shards = [w_query, w_key, w_value, w_out, w_gate.T, w_up.T, w_down]
    gout, o_gate, o_up, o_down, o_out, o_q, o_k, o_v, block_out, grad_in = run_layer(
        g, cap, halo, window, req, sel, segments, x, gains, flat(memory_keys), flat(memory_values), c, shards, nq, ksel
    )[:10]
    g_attn, g_ffn, block_out, grad_in, o_q, o_k, o_v, o_out, o_gate, o_up, o_down = hand_out(
        gout, (block_out, grad_in, o_q, o_k, o_v, o_out, o_gate, o_up, o_down)
    )
    return (
        block_out[None], grad_in[None], g_attn.reshape(-1), o_q, o_k, o_v, o_out, g_ffn.reshape(-1), o_gate.T, o_up.T, o_down,
    )


def solution(mesh):
    return jax.shard_map(
        on_device,
        mesh=mesh,
        in_specs=(
            P("dp", "tensor", None), P("dp", None), P("dp", None, None), P("dp"),
            P(None, "dp", None, "tensor"), P(None, "dp", None, "tensor"),
            P("dp"), P("dp", "tensor"), P("dp", "tensor"), P("dp", "tensor"), P("tensor", "dp"),
            P("dp"), P("dp", "tensor"), P("dp", "tensor"), P("tensor", "dp"), P("dp", "tensor", None),
        ),
        out_specs=(
            P("dp", "tensor", None), P("dp", "tensor", None),
            P("dp"), P("dp", "tensor"), P("dp", "tensor"), P("dp", "tensor"), P("tensor", "dp"),
            P("dp"), P("dp", "tensor"), P("dp", "tensor"), P("tensor", "dp"),
        ),
        check_vma=False,
    )
```

```python
import functools
import math

import jax
import jax.numpy as jnp
import numpy as np
from jax import lax
from jax.experimental import pallas as pl
from jax.experimental.pallas import tpu as pltpu
from jax.sharding import PartitionSpec as P
MESH = pl.DeviceIdType.MESH
MEMB = 128


class Grid:
    def __init__(self, dp, tensor):
        side = math.isqrt(dp // 2)
        assert side * side * 2 == dp
        self.na, self.nb, self.nc, self.nz, self.dp = side, side, 2, tensor, dp


def coords(g):
    me = lax.axis_index("dp")
    t = lax.axis_index("tensor")
    return me // (2 * g.nb), (me // 2) % g.nb, me % 2, t, me


def send(src, dst, ssem, rsem, dp, t):
    return pltpu.make_async_remote_copy(
        src_ref=src, dst_ref=dst, send_sem=ssem, recv_sem=rsem, device_id=(dp, t), device_id_type=MESH
    )


class Copy:
    def __init__(self, make):
        self.make = make

    def start(self):
        self.make().start()

    def wait(self):
        self.make().wait()

    def wait_send(self):
        self.make().wait_send()

    def wait_recv(self):
        self.make().wait_recv()


def greet(g, me, t):
    bar = pltpu.get_barrier_semaphore()
    for k in range(1, g.dp):
        pl.semaphore_signal(bar, inc=1, device_id=((me + k) % g.dp, t), device_id_type=MESH)
    for k in range(1, g.nz):
        pl.semaphore_signal(bar, inc=1, device_id=(me, (t + k) % g.nz), device_id_type=MESH)
    pl.semaphore_wait(bar, g.dp - 1 + g.nz - 1)


class Gather:
    def __init__(self, g, shard, buf, rows, b_first, lanes, sems, base):
        self.g, self.shard, self.buf, self.rows, self.b_first, self.lanes = g, shard, buf, rows, b_first, lanes
        self.sems, self.count, self.base = sems, 0, base
        lo, n = rows
        nz = g.nz
        n1, n2 = (g.nb, g.na) if b_first else (g.na, g.nb)
        bind = functools.partial
        shard_rows = lambda: shard.at[pl.ds(lo, n), :]
        tensor = lambda: lax.axis_index("tensor")

        def here():
            a, b, c, t, me = coords(g)
            return self.at(me, t)

        def passed(k):
            a, b, c, t, me = coords(g)
            return self.at(me, (t + nz - 2 * k) % nz)

        def far(k):
            a, b, c, t, me = coords(g)
            return me, (t + 2 * k) % nz

        def pair():
            a, b, c, t, me = coords(g)
            return me, t + 1 - 2 * (t % 2)

        def other_core():
            a, b, c, t, me = coords(g)
            return me + 1 - 2 * c, t

        slab = lambda k1, k2: bind(lambda k1, k2: self.at(self._slot(k1, k2)), k1, k2)
        to1 = lambda k: (self._slot(n1 - k, 0), tensor())
        to2 = lambda k: (self._slot(0, n2 - k), tensor())
        self.far = [self._copy(shard_rows, here, bind(far, k)) for k in range(1, nz // 2)]
        self.near = [self._copy(shard_rows, here, pair)]
        self.relayed = [self._copy(bind(passed, k), bind(passed, k), pair) for k in range(1, nz // 2)]
        i = self._sem()
        self.own = Copy(lambda: pltpu.make_async_copy(shard_rows(), here(), sems[0].at[i]))
        self.first = [self._copy(slab(0, 0), slab(0, 0), bind(to1, k)) for k in range(1, n1)]
        self.second = [
            self._copy(slab(k1, 0), slab(k1, 0), bind(to2, k)) for k1 in range(n1) for k in range(1, n2)
        ]
        core = lambda k1, k2: self._copy(slab(k1, k2), slab(k1, k2), other_core)
        self.core0 = [core(0, 0)]
        self.core1 = [core(k1, 0) for k1 in range(1, n1)]
        self.core2 = [core(k1, k2) for k1 in range(n1) for k2 in range(1, n2)]

    def at(self, dp, t=None):
        lo, n = self.rows
        if self.lanes:
            width = self.shard.shape[1]
            col = pl.ds(pl.multiple_of(dp * width, 128), width)
            return self.buf.at[slice(None) if t is None else t, pl.ds(lo, n), col]
        depth, width = self.shard.shape
        row = pl.ds(pl.multiple_of(dp * depth + lo, 16), n)
        return self.buf.at[row, slice(None) if t is None else pl.ds(pl.multiple_of(t * width, 128), width)]

    def _sem(self):
        i = self.base + self.count
        self.count += 1
        return i

    def _copy(self, src, dst, to):
        i = self._sem()
        return Copy(lambda: send(src(), dst(), self.sems[0].at[i], self.sems[1].at[i], *to()))

    def _slot(self, k1, k2):
        g = self.g
        a, b, c, t, me = coords(g)
        if self.b_first:
            return (((a + g.na - k2) % g.na) * g.nb + (b + g.nb - k1) % g.nb) * 2 + c
        return (((a + g.na - k1) % g.na) * g.nb + (b + g.nb - k2) % g.nb) * 2 + c

    def start_z(self):
        for m in self.far + self.near + [self.own]:
            m.start()

    def relay_z(self):
        for m, n in zip(self.far, self.relayed):
            m.wait_recv()
            n.start()

    def start_first(self):
        self.own.wait()
        for m in self.near + self.relayed:
            m.wait_recv()
        for m in self.first + self.core0:
            m.start()

    def start_second(self):
        for m in self.first:
            m.wait_recv()
        for m in self.second + self.core1:
            m.start()

    def start_core(self):
        for m in self.second:
            m.wait_recv()
        for m in self.core2:
            m.start()

    def finish(self):
        core = self.core0 + self.core1 + self.core2
        for m in core:
            m.wait_recv()
        for m in self.far + self.near + self.relayed + self.first + self.second + core:
            m.wait_send()


def gather_sems(g):
    return g.nz + (g.na - 1) + g.na * (g.na - 1) + g.na * g.nb


def plan_requests(retrieved, partner, dp_size, blocks_dev, cap):
    wanted = retrieved.reshape(-1)
    n = wanted.shape[0]
    from_partner = wanted // MEMB
    block_index = wanted % MEMB
    owner = block_index // blocks_dev
    local = block_index % blocks_dev
    seq = jnp.where(from_partner == 0, lax.axis_index("dp"), partner)
    flat = seq * blocks_dev + local
    i = jnp.arange(n)
    slot = jnp.sum(((owner[:, None] == owner[None, :]) & (i[None, :] < i[:, None])).astype(jnp.int32), axis=1)
    hit = (owner[None, None, :] == jnp.arange(dp_size)[:, None, None]) & (
        slot[None, None, :] == jnp.arange(128)[None, :, None]
    )
    req = jnp.sum(jnp.where(hit, flat[None, None, :], 0), axis=2)
    return jnp.broadcast_to(req[:, None, :], (dp_size, 8, 128)).astype(jnp.int32), (owner * cap + slot).astype(jnp.int32)


HD = 128
EPSILON = 1e-05
MASKED = -1e30
F32, BF16 = jnp.float32, jnp.bfloat16


def dot_nn(x, y):
    return lax.dot_general(x, y, (((1,), (0,)), ((), ())), preferred_element_type=F32)


def dot_nt(x, y):
    return lax.dot_general(x, y, (((1,), (1,)), ((), ())), preferred_element_type=F32)


def dot_tn(x, y):
    return lax.dot_general(x, y, (((0,), (0,)), ((), ())), preferred_element_type=F32)


def inv_rms(v):
    return lax.rsqrt(jnp.mean(v * v, axis=-1, keepdims=True) + EPSILON)


def gain_row(gains_ref, which):
    n = gains_ref.shape[0]
    return jnp.concatenate([gains_ref[d, which : which + 1, :] for d in range(n)], axis=1)


def turn(v, cos, sin):
    return v * cos + pltpu.roll(v, HD // 2, axis=1) * sin


def lanes(ref):
    return jnp.concatenate([ref[d, 0] for d in range(ref.shape[0])], axis=1)


def rows(ref):
    return jnp.concatenate([ref[d, 0] for d in range(ref.shape[0])], axis=0)


VL = 60 * 2**20


def full(shape, buffers=None):
    n = len(shape)
    kw = {} if buffers is None else dict(pipeline_mode=pl.Buffered(buffers))
    return pl.BlockSpec(shape, lambda *i: (0,) * n, **kw)


def allowed_of(seg_q, seg_k, q0, k0):
    n, m = seg_q.shape[0], seg_k.shape[1]
    qp = lax.broadcasted_iota(jnp.int32, (n, m), 0) + q0
    kp = lax.broadcasted_iota(jnp.int32, (n, m), 1) + k0
    return (seg_q == seg_k) & (kp <= qp)


QT = 256
C2 = HD**-0.5 * math.log2(math.e)


class Scatter:
    def __init__(self, g, src, rows, b_first, bufs, sems, out):
        self.g, self.src, self.rows, self.b_first, self.out = g, src, rows, b_first, out
        self.r1, self.r2, self.r3 = bufs
        self.sems, self.count = sems, 0
        n1, n2 = self._mine()[5:]
        nz = g.nz
        lo, n = rows
        bind = functools.partial
        at = lambda e, t: src.at[e, t, pl.ds(lo, n), :]

        def src1(k, j):
            f = self._mine()[0]
            return at(self._e((f + k) % n1, j), slice(None))

        def to1(k):
            f, s, c, t = self._mine()[:4]
            return self._e((f + k) % n1, s) * 2 + c, t

        def src2(k):
            f, s = self._mine()[:2]
            return at(self._e(f, (s + k) % n2), slice(None))

        def to2(k):
            f, s, c, t = self._mine()[:4]
            return self._e(f, (s + k) % n2) * 2 + c, t

        def src_near(k):
            f, s, c, t = self._mine()[:4]
            return at(self._e(f, s), (t + 1 - 2 * (t % 2) + 2 * k) % nz)

        def to_near():
            t, me = self._mine()[3:5]
            return me, t + 1 - 2 * (t % 2)

        def src_far(k):
            f, s, c, t = self._mine()[:4]
            return at(self._e(f, s), (t + 2 * k) % nz)

        def to_far(k):
            t, me = self._mine()[3:5]
            return me, (t + 2 * k) % nz

        land = lambda ref, *i: bind(lambda ref, i: ref.at[i], ref, i)
        self.first = [
            self._copy(bind(src1, k, j), land(self.r1, k - 1, j), bind(to1, k)) for k in range(1, n1) for j in range(n2)
        ]
        self.second = [self._copy(bind(src2, k), land(self.r2, k - 1), bind(to2, k)) for k in range(1, n2)]
        self.near = [self._copy(bind(src_near, k), land(self.r3, k), to_near) for k in range(nz // 2)]
        self.far = [
            self._copy(bind(src_far, k), land(self.r3, nz // 2 + k - 1), bind(to_far, k)) for k in range(1, nz // 2)
        ]

    def _copy(self, src, dst, to):
        i = self.count
        self.count += 1
        return Copy(lambda: send(src(), dst(), self.sems[0].at[i], self.sems[1].at[i], *to()))

    def _e(self, f, s):
        return s * self.g.nb + f if self.b_first else f * self.g.nb + s

    def _mine(self):
        a, b, c, t, me = coords(self.g)
        f, s = (b, a) if self.b_first else (a, b)
        n1, n2 = (self.g.nb, self.g.na) if self.b_first else (self.g.na, self.g.nb)
        return f, s, c, t, me, n1, n2

    def _add(self, e, u, more):
        lo, n = self.rows
        v = self.src[e, u, lo : lo + n, :].astype(F32)
        for m in more:
            v = v + m.astype(F32)
        self.src[e, u, lo : lo + n, :] = v.astype(BF16)

    def start_first(self):
        for m in self.first:
            m.start()

    def start_second(self):
        f, s, c, t, me, n1, n2 = self._mine()
        for m in self.first:
            m.wait_recv()
        for j in range(n2):

            @pl.loop(0, self.g.nz)
            def _(u):
                self._add(self._e(f, j), u, [self.r1[k, j, u] for k in range(n1 - 1)])

        for m in self.second:
            m.start()

    def start_z(self):
        f, s, c, t, me, n1, n2 = self._mine()
        for m in self.second:
            m.wait_recv()

        @pl.loop(0, self.g.nz)
        def _(u):
            self._add(self._e(f, s), u, [self.r2[k, u] for k in range(n2 - 1)])

        for m in self.near:
            m.start()

    def relay_z(self):
        f, s, c, t, me, n1, n2 = self._mine()
        for k, m in enumerate(self.near):
            m.wait_recv()
            self._add(self._e(f, s), (t + 2 * k) % self.g.nz, [self.r3[k]])
        for m in self.far:
            m.start()

    def finish(self):
        f, s, c, t, me, n1, n2 = self._mine()
        lo, n = self.rows
        half = self.g.nz // 2
        for m in self.far:
            m.wait_recv()
        v = self.src[self._e(f, s), t, lo : lo + n, :].astype(F32)
        for k in range(half - 1):
            v = v + self.r3[half + k].astype(F32)
        self.out[pl.ds(lo, n), :] = v
        for m in self.first + self.second + self.near + self.far:
            m.wait_send()


def scatter_sems(g):
    return (g.na - 1) * g.na + (g.na - 1) + (g.nz - 1)


POLL = dict(hidden_back=2, attend=0, attend_core=6, back_down=2, back_gate=5, own_up=3)


def rope_tables(halo, nz, r):
    half = HD // 2
    freq = 10000.0 ** (-np.arange(half, dtype=np.float64) * 2.0 / HD)
    both = lambda p: np.concatenate([np.cos(p[:, None] * freq), np.sin(p[:, None] * freq)], axis=1).astype(np.float32)
    n = nz + halo
    starts = (np.arange(-(-n // 8) * 8) - halo) * float(r)
    return both(np.arange(r, dtype=np.float64)), both(starts)


def layer_kernel(g, cfg, *refs):
    cap, nq, ksel, halo, window, gunits, sunits = cfg
    refs = list(refs)
    take = lambda n: [refs.pop(0) for _ in range(n)]
    requests, sel, segs, tab1, tab2 = take(5)
    x, gains, mem_k, mem_v, cot = take(5)
    shards = take(7)
    gout = take(1)[0]
    outs = take(7)
    block_out, grad_in = take(2)
    bufs = take(7)
    wq, wk, wv, wo, wg, wu, wd = bufs
    xh, mk, mv, rec_k, rec_v, n1, q, k, v, o, lse = take(11)
    hid, phid, pdg, pdu, do, dq, dk, dv, pdq, pdk, pdv, po, dh_o = take(13)
    req_in, req_s, gn_v, cos_v, sin_v = take(5)
    rbufs = [take(3) for _ in sunits]
    rsems = [take(2) for _ in sunits]
    pn_v, pc_v, pn1_v, pdhb_v, more = take(5)
    gz, gs, gd, gp = take(4)
    ss, rs, ms, qss, qrs, gss, grs, mss, mrs, zss, zrs, xss, xrs = take(13)
    css, crs, hss, hrs, ass, ars, dss, drs, fss, frs, fls = take(11)
    seg_q, seg_k = take(2)
    a, b, core, t, me = coords(g)
    peer = me + 1 - 2 * core
    r, d = block_out.shape
    rt = (halo + 1) * r
    nz, ff, _ = hid.shape
    dp = g.dp
    nb, half = dp // 2, d // 2
    kd, cols = shards[0].shape
    blk = mk.shape[2]
    nm, per_t = ksel * blk, cols // HD
    heads = d // HD
    any_ = pl.BlockSpec(memory_space=pl.ANY)

    def local(src, dst, i):
        m = pltpu.make_async_copy(src, dst, ms.at[i])
        m.start()
        return m

    ncore = [0]

    def to_peer(src, dst):
        i = ncore[0]
        ncore[0] += 1
        m = send(src, dst, css.at[i], crs.at[i], peer, t)
        m.start()
        return m

    def lane_block(ref, e, c_):
        return ref.at[:, pl.ds(pl.multiple_of((2 * e + c_) * 128, 128), 128)]

    def theirs(src, dst):
        return [to_peer(lane_block(src, e, 1 - core), dst.at[:, pl.ds(e * 128, 128)]) for e in range(nb)]

    def keep_half(src, dst):
        for e in range(nb):
            dst[:, e * 128 : (e + 1) * 128] = src[:, pl.ds(pl.multiple_of((2 * e + core) * 128, 128), 128)]

    per = gather_sems(g)
    gat = [Gather(g, shards[w], bufs[w], rows_, bf, lanes_, (ss, rs), i * per)
           for i, (w, rows_, bf, lanes_) in enumerate(gunits)]
    gof = lambda *ws: [u for u, s in zip(gat, gunits) if s[0] in ws]
    proj, out_, gate_up, down = gof(0, 1, 2), gof(3), gof(4, 5), gof(6)

    def piped(body, n, in_specs, out_specs=(), polls=()):
        def step(*blocks):
            body(*blocks)
            for at, fns in polls:

                @pl.when(pl.program_id(0) == at)
                def _():
                    for fn in fns:
                        fn()

        return pltpu.emit_pipeline(step, grid=(n,), in_specs=in_specs, out_specs=out_specs)

    every = lambda units, *names: [getattr(u, name) for name in names for u in units]

    head = lambda n: pl.BlockSpec((n, HD), lambda h: (0, h))
    mem = pl.BlockSpec((1, ksel, blk, HD), lambda h: (h // per_t, 0, 0, h % per_t))
    row_stat = pl.BlockSpec((1, r, 1), lambda h: (h, 0, 0))
    col = lambda n: pl.BlockSpec((n, cols), lambda u: (0, u))
    piece = pl.BlockSpec((1, ff, r), lambda u: (u, 0, 0))
    wcol = pl.BlockSpec((d, cols), lambda u: (0, u))
    wrow = lambda n: pl.BlockSpec((1, n, d), lambda u: (u, 0, 0))

    def forward(loc, stage_k, stage_v, x_v, xh_v, n_v):
        load_k = local(mem_k, loc, 0)
        lx = local(x, x_v, 1)
        greet(g, me, t)
        rq, gn = [], []
        for i in range(1, dp):
            to = (me + i) % dp
            m = send(requests.at[to], req_in.at[me], qss.at[i], qrs.at[i], to, t)
            m.start()
            rq.append(m)
        own_r = pltpu.make_async_copy(requests.at[me], req_in.at[me], qss.at[0])
        own_r.start()
        for u in proj + out_:
            u.start_z()
        for i in range(1, dp):
            to = (me + i) % dp
            m = send(gains, gn_v.at[me], gss.at[i], grs.at[i], to, t)
            m.start()
            gn.append(m)
        own_g = pltpu.make_async_copy(gains, gn_v.at[me], gss.at[0])
        own_g.start()
        xs = []
        for i in range(1, halo + 1):
            m = send(x, xh.at[i - 1], xss.at[i - 1], xrs.at[i - 1], me, (t + i) % nz)
            xs.append(m)

            @pl.when(t + i < nz)
            def _():
                m.start()

        own_r.wait()
        for m in rq:
            m.wait()
        cp = local(req_in, req_s, 2)
        cp.wait()
        parts = cols // 128
        lane = lambda p: pl.ds(p * 128, 128)

        def pick(stage, to):
            for j in range(cap):
                stage[to, j] = loc[req_s[to, 0, j]]

        def exchange(stage, rec, i, load):
            load.wait()
            out = [[] for _ in range(parts)]
            mine = pl.ds(me * cap, cap)

            def go(p, j):
                to = (me + j) % dp
                m = send(stage.at[to, :, :, lane(p)], rec.at[mine, :, lane(p)], mss.at[i, p, j], mrs.at[i, p, j], to, t)
                m.start()
                out[p].append(m)

            for j in range(1, dp):
                pick(stage, (me + j) % dp)
                go(0, j)
            for p in range(1, parts):
                for j in range(1, dp):
                    go(p, j)
            pick(stage, me)
            for p in range(parts):
                own = pltpu.make_async_copy(stage.at[me, :, :, lane(p)], rec.at[mine, :, lane(p)], mss.at[i, p, 0])
                own.start()
                out[p].append(own)
            return out

        ek = exchange(stage_k, rec_k, 0, load_k)
        load_v = local(mem_v, loc, 3)
        for u in gate_up:
            u.start_z()
        for u in proj + out_:
            u.relay_z()
        ev = exchange(stage_v, rec_v, 1, load_v)
        for u in proj + out_:
            u.start_first()
        for u in gate_up:
            u.relay_z()

        for j in range(halo + 1):
            lane_at = pl.multiple_of(jnp.maximum(t - halo + j, 0) * r, 128)
            part = segs[:, pl.ds(lane_at, r)]
            seg_k[:, j * r : (j + 1) * r] = jnp.where(t - halo + j >= 0, part, -jnp.ones_like(part))
        own_seg = segs[:, pl.ds(pl.multiple_of(t * r, 128), r)]
        seg_q[...] = jnp.transpose(jnp.broadcast_to(own_seg, (128, r)))

        left = lax.broadcasted_iota(jnp.int32, (r, HD), 1) < HD // 2
        c1 = tab1[...]
        s1 = pltpu.roll(c1, HD // 2, axis=1)
        cc, sc = jnp.where(left, c1, s1), jnp.where(left, s1, c1)
        for j in range(halo + 1):
            c2 = jnp.broadcast_to(tab2[pl.ds(t + j, 1), :], (r, HD))
            s2 = pltpu.roll(c2, HD // 2, axis=1)
            ce, se = jnp.where(left, c2, s2), jnp.where(left, s2, c2)
            cos_v[j * r : (j + 1) * r, :] = cc * ce - sc * se
            sin_ = sc * ce + cc * se
            sin_v[j * r : (j + 1) * r, :] = jnp.where(left, -sin_, sin_)

        own_g.wait()
        for m in gn:
            m.wait()
        lx.wait()
        gain1 = gain_row(gn_v, 0)
        vx = x_v[...].astype(F32)
        n_v[halo * r :, :] = (vx * inv_rms(vx) * gain1).astype(BF16)
        for i, m in enumerate(xs):
            lo = (halo - 1 - i) * r

            @pl.when(t >= i + 1)
            def _():
                m.wait_recv()
                ch = local(xh.at[i], xh_v, 4)
                ch.wait()
                vh = xh_v[...].astype(F32)
                n_v[lo : lo + r, :] = (vh * inv_rms(vh) * gain1).astype(BF16)

            @pl.when(t < i + 1)
            def _():
                n_v[lo : lo + r, :] = jnp.zeros((r, d), BF16)

        cn = local(n_v, n1, 5)

        def spread(moves, rec, zst, out, i, p):
            for m in moves[p]:
                m.wait()
            lr = local(rec.at[:, :, lane(p)], loc.at[pl.ds(0, dp * cap), :, lane(p)], 6)
            lr.wait()

            @pl.loop(0, nq)
            def _(s):
                for j in range(ksel):
                    zst[s, j, :, lane(p)] = loc[sel[s * ksel + j], :, lane(p)]

            res = []
            for j in range(1, nz):
                to = (t + j) % nz
                m = send(zst.at[to, :, :, lane(p)], out.at[t, :, :, lane(p)], zss.at[i, p, j], zrs.at[i, p, j], me, to)
                m.start()
                res.append(m)
            own = pltpu.make_async_copy(zst.at[t, :, :, lane(p)], out.at[t, :, :, lane(p)], zss.at[i, p, 0])
            own.start()
            return res + [own]

        zk, zv = [], []
        for p in range(parts):
            zk += spread(ek, rec_k, stage_k, mk, 0, p)
        for p in range(parts):
            zv += spread(ev, rec_v, stage_v, mv, 1, p)
        for u in down:
            u.start_z()
        for u in proj:
            u.start_second()
        for u in out_:
            u.start_second()
        for u in gate_up:
            u.start_first()
        for u in proj:
            u.start_core()
        for u in proj:
            u.finish()

        def turned(y, cs_, sn_):
            return jnp.concatenate(
                [turn(y[:, h * HD : (h + 1) * HD], cs_, sn_).astype(BF16) for h in range(cols // HD)], axis=1
            )

        def project(wq_ref, wk_ref, wv_ref, q_ref, k_ref, v_ref):
            @pl.loop(0, halo + 1)
            def _(i):
                at = pl.ds(pl.multiple_of(i * r, r), r)
                n = n_v[at, :]
                k_ref[at, :] = turned(dot_nn(n, wk_ref[...]), cos_v[at, :], sin_v[at, :])
                v_ref[at, :] = dot_nn(n, wv_ref[...]).astype(BF16)

            q_ref[...] = turned(dot_nn(n_v[halo * r :, :], wq_ref[...]), cos_v[halo * r :, :], sin_v[halo * r :, :])

        piped(project, nz, [wcol] * 3, [col(r), col(rt), col(rt)])(wq, wk, wv, q, k, v)
        for u in out_:
            u.start_core()
        for u in down:
            u.relay_z()
        for m in zk + zv:
            m.wait()
        cn.wait()
        for i, m in enumerate(xs):

            @pl.when(t + i + 1 < nz)
            def _():
                m.wait_send()

    nblk = mem_k.shape[0]
    pl.run_scoped(
        forward,
        pltpu.VMEM((nblk, blk, cols), BF16),
        pltpu.VMEM((max(dp, nq), cap, blk, cols), BF16),
        pltpu.VMEM((max(dp, nq), cap, blk, cols), BF16),
        pltpu.VMEM((r, d), BF16),
        pltpu.VMEM((r, d), BF16),
        pltpu.VMEM((rt, d), BF16),
    )

    def attend(q_ref, k_ref, v_ref, mk_ref, mv_ref, o_ref, l_ref):
        km = mk_ref[0].reshape(nm, HD)
        vm = mv_ref[0].reshape(nm, HD)
        for i in range(r // QT):
            at = slice(i * QT, (i + 1) * QT)
            k0 = halo * r - window + i * QT
            ks = slice(k0, k0 + window + QT)
            qq = q_ref[at, :]
            ok = allowed_of(seg_q[at, 0:1], seg_k[:, ks], halo * r + i * QT, k0)
            sl = jnp.where(ok, dot_nt(qq, k_ref[ks, :]), MASKED)
            sm = dot_nt(qq, km)
            mx = jnp.maximum(jnp.max(sl, axis=1, keepdims=True), jnp.max(sm, axis=1, keepdims=True))
            mc = mx * C2
            el = jnp.exp2(sl * C2 - mc)
            em = jnp.exp2(sm * C2 - mc)
            tot = jnp.sum(el, axis=1, keepdims=True) + jnp.sum(em, axis=1, keepdims=True)
            acc = dot_nn(el.astype(BF16), v_ref[ks, :]) + dot_nn(em.astype(BF16), vm)
            o_ref[at, :] = (acc / tot).astype(BF16)
            l_ref[0, at, :] = mc + jnp.log2(tot)

    piped(
        attend,
        heads,
        [head(r), head(rt), head(rt), mem, mem],
        [head(r), row_stat],
        [(POLL["attend"], every(gate_up, "start_second") + every(down, "start_first")),
         (POLL["attend_core"], every(gate_up, "start_core"))],
    )(q, k, v, mk, mv, o, lse)
    for u in out_:
        u.finish()

    sof = lambda us, *ws: [u for u in us if u.which in ws]

    def units(G):
        res = []
        for i, (w, rows_, bf) in enumerate(sunits):
            if w in G:
                u = Scatter(g, G[w], rows_, bf, rbufs[i], rsems[i], outs[w])
                u.which = w
                res.append(u)
        return res

    def rest(h_v, n2_v, c_v, n2h, ch, acc, *gf):
        fu = units(dict(enumerate(gf)))
        lc = local(cot, c_v, 0)
        lx = local(x, n2_v, 1)
        to_o = to_peer(o, po)
        lx.wait()
        h_v[...] = n2_v[...].astype(F32)

        def out_proj(o_ref, w_ref):
            h_v[...] += dot_nn(o_ref[...], w_ref[0])

        piped(out_proj, nz, [col(r), wrow(cols)])(o, wo)
        gain2 = gain_row(gn_v, 1)
        hv = h_v[...]
        n2_v[...] = (hv * inv_rms(hv) * gain2).astype(BF16)
        lc.wait()
        p_n = theirs(n2_v, pn_v) + theirs(c_v, pc_v)
        keep_half(n2_v, n2h)
        keep_half(c_v, ch)
        for u in gate_up:
            u.finish()

        def feed_forward(hid_v, a_v, b_v):
            tile = ff
            give = lambda src, dst, i, u: send(src.at[u], dst.at[u], fss.at[i, u], frs.at[i, u], peer, t)
            keep = lambda u: pltpu.make_async_copy(hid_v.at[u], hid.at[u], fls.at[u])

            def hidden(wg_ref, wu_ref):
                u = pl.program_id(0)

                @pl.loop(0, 1)
                def _(i):
                    at = pl.ds(pl.multiple_of(i * tile, 16), tile)
                    gate = dot_nt(wg_ref[0, at, :], n2_v[...])
                    up = dot_nt(wu_ref[0, at, :], n2_v[...])
                    sig = 1.0 / (1.0 + jnp.exp(-gate))
                    act = gate * sig
                    hid_v[u, at, :] = (act * up).astype(BF16)
                    a_v[u, at, :] = (up * (sig * (1.0 + gate * (1.0 - sig)))).astype(BF16)
                    b_v[u, at, :] = act.astype(BF16)

                give(hid_v, phid, 0, u).start()
                keep(u).start()

            piped(hidden, nz, [wrow(ff)] * 2)(wg, wu)
            for u in down:
                u.start_second()
            for m in p_n:
                m.wait()

            def ffn_grads(mine_t, B, i, mine_v, peer_v, out):
                for u in range(nz):
                    give(mine_t, B, i, u).wait()

                def body(b_ref):
                    u = pl.program_id(0)
                    y = (dot_nn(mine_t[u], mine_v[...]) + dot_nn(b_ref[0], peer_v[...])).astype(BF16)
                    for e in range(nb):
                        out[e, u] = y[:, e * 128 : (e + 1) * 128]

                piped(body, nz, [piece])(B)

            ffn_grads(hid_v, phid, 0, ch, pc_v, gf[2])
            for u in sof(fu, 2):
                u.start_first()
            for u in down:
                u.start_core()
            for u in down:
                u.finish()
            acc[0:r, :] = jnp.zeros((r, d), F32)

            def hidden_back(wd_ref, wg_ref, wu_ref):
                u = pl.program_id(0)

                @pl.loop(0, 1)
                def _(i):
                    at = pl.ds(pl.multiple_of(i * tile, 16), tile)
                    dhid = dot_nt(wd_ref[0, at, :], c_v[...])
                    a_v[u, at, :] = (dhid * a_v[u, at, :].astype(F32)).astype(BF16)
                    b_v[u, at, :] = (dhid * b_v[u, at, :].astype(F32)).astype(BF16)

                give(a_v, pdg, 1, u).start()
                give(b_v, pdu, 2, u).start()
                acc[0:r, :] += dot_tn(a_v[u], wg_ref[0]) + dot_tn(b_v[u], wu_ref[0])

            piped(hidden_back, nz, [wrow(ff)] * 3, (), [(POLL["hidden_back"], every(sof(fu, 2), "start_second"))])(wd, wg, wu)
            ffn_grads(a_v, pdg, 1, n2h, pn_v, gf[0])
            for u in sof(fu, 0):
                u.start_first()
            ffn_grads(b_v, pdu, 2, n2h, pn_v, gf[1])
            for u in sof(fu, 1):
                u.start_first()
            for u in range(nz):
                keep(u).wait()

        pl.run_scoped(feed_forward, *[pltpu.VMEM((nz, ff, r), BF16)] * 3)
        to_o.wait()

        def attention_back(dhb_v, dhbh, n1h, sdk, sdv, hb_v, *ga):
            G = dict(zip((3, 4, 5, 6), ga))
            us = fu + units(G)
            of = lambda *ws: sof(us, *ws)
            dn = acc[0:r, :]
            hv = h_v[...]
            iv = inv_rms(hv)
            gp[1:2, :] = jnp.sum(dn * hv * iv, axis=0, keepdims=True)
            gdn = dn * gain2
            dh = c_v[...].astype(F32) + iv * gdn - hv * (iv * iv * iv * jnp.mean(hv * gdn, axis=1, keepdims=True))
            acc[0:r, :] = dh
            dhb_v[...] = dh.astype(BF16)
            ld = local(acc.at[pl.ds(0, r)], dh_o, 2)
            p_r = theirs(dhb_v, pdhb_v) + theirs(n1, pn1_v)
            keep_half(dhb_v, dhbh)
            ln = [local(lane_block(n1, e, core), n1h.at[:, pl.ds(e * 128, 128)], 8 + e) for e in range(nb)]

            def mixed_grad(w_ref, do_ref):
                do_ref[...] = dot_nt(dhb_v[...], w_ref[0]).astype(BF16)

            piped(mixed_grad, nz, [wrow(cols)], [col(r)])(wo, do)
            for u in of(2):
                u.start_z()

            for m in p_r + ln:
                m.wait()

            def out_grads(a_ref, b_ref):
                u = pl.program_id(0)
                y = (dot_tn(a_ref[...], dhbh[...]) + dot_tn(b_ref[...], pdhb_v[...])).astype(BF16)
                for e in range(nb):
                    G[3][e, u] = y[:, e * 128 : (e + 1) * 128]

            piped(out_grads, nz, [col(r)] * 2)(o, po)
            for u in of(3):
                u.start_first()

            scale = HD**-0.5

            def attend_back(q_ref, k_ref, v_ref, mk_ref, mv_ref, o_ref, l_ref, do_ref, dq_ref, dk_ref, dv_ref):
                km = mk_ref[0].reshape(nm, HD)
                vm = mv_ref[0].reshape(nm, HD)
                sdk[...] = jnp.zeros_like(sdk)
                sdv[...] = jnp.zeros_like(sdv)
                for i in range(r // QT):
                    at = slice(i * QT, (i + 1) * QT)
                    k0 = halo * r - window + i * QT
                    ks = slice(k0, k0 + window + QT)
                    own = slice(halo * r + i * QT, halo * r + (i + 1) * QT)
                    qq, dd = q_ref[at, :], do_ref[at, :]
                    lse_c = l_ref[0, at, :]
                    delta = jnp.sum(dd.astype(F32) * o_ref[at, :].astype(F32), axis=1, keepdims=True)
                    ok = allowed_of(seg_q[at, 0:1], seg_k[:, ks], halo * r + i * QT, k0)
                    pm = jnp.exp2(dot_nt(qq, km) * C2 - lse_c)
                    dsm = (pm * (dot_nt(dd, vm) - delta)).astype(BF16)
                    plo = jnp.where(ok, jnp.exp2(dot_nt(qq, k_ref[ks, :]) * C2 - lse_c), 0.0)
                    dsl = (plo * (dot_nt(dd, v_ref[ks, :]) - delta)).astype(BF16)
                    dqv = (dot_nn(dsm, km) + dot_nn(dsl, k_ref[ks, :])) * scale
                    dq_ref[at, :] = turn(dqv, cos_v[own, :], -sin_v[own, :]).astype(BF16)
                    sdk[ks, :] += dot_tn(dsl, qq)
                    sdv[ks, :] += dot_tn(plo.astype(BF16), dd)
                dk_ref[...] = turn(sdk[...] * scale, cos_v[...], -sin_v[...]).astype(BF16)
                dv_ref[...] = sdv[...].astype(BF16)

            piped(
                attend_back,
                heads,
                [head(r), head(rt), head(rt), mem, mem, head(r), row_stat, head(r)],
                [head(r), head(rt), head(rt)],
                [(POLL["back_down"], every(of(2), "relay_z")), (POLL["back_gate"], every(of(0), "start_second"))],
            )(q, k, v, mk, mv, o, lse, do, dq, dk, dv)
            p_att = [to_peer(dq, pdq), to_peer(dk, pdk), to_peer(dv, pdv)]
            ld.wait()

            acc[...] = jnp.zeros_like(acc)

            def halo_back(dk_ref, dv_ref, wk_ref, wv_ref):
                acc[: halo * r, :] += dot_nt(dk_ref[...], wk_ref[...]) + dot_nt(dv_ref[...], wv_ref[...])

            piped(halo_back, nz, [col(halo * r)] * 2 + [wcol] * 2)(dk, dv, wk, wv)
            hb_v[...] = acc[: halo * r, :].astype(BF16)
            hd = []
            for j in range(halo):
                m = send(hb_v.at[pl.ds((halo - 1 - j) * r, r), :], more.at[j], hss.at[j], hrs.at[j], me,
                         (t + nz - 1 - j) % nz)
                hd.append(m)

                @pl.when(t >= j + 1)
                def _():
                    m.start()

            for u in of(1):
                u.start_second()

            def feed_out(hid_ref, wd_ref):
                h_v[...] += dot_tn(hid_ref[0], wd_ref[0])

            piped(feed_out, nz, [piece, wrow(ff)])(hid, wd)
            lo_ = local(h_v, block_out, 5)
            for m in p_att:
                m.wait()

            own = pl.ds(halo * r, r)

            def grads_of(out, p0, p1, a0, a1):
                def body(x_ref, y_ref):
                    u = pl.program_id(0)
                    y = (dot_tn(a0[...], x_ref[...]) + dot_tn(a1[...], y_ref[...])).astype(BF16)
                    for e in range(nb):
                        out[e, u] = y[e * 128 : (e + 1) * 128, :]

                n = p0.shape[0]
                piped(body, nz, [col(n)] * 2)(p0, p1)

            grads_of(G[4], dq, pdq, n1h.at[own], pn1_v.at[own])
            for u in of(4):
                u.start_first()
            grads_of(G[5], dk, pdk, n1h, pn1_v)
            for u in of(5):
                u.start_first()
            grads_of(G[6], dv, pdv, n1h, pn1_v)
            for u in of(6):
                u.start_first()
            for u in of(3):
                u.start_second()
            for u in of(0):
                u.start_z()
            lo_.wait()
            ld2 = local(dh_o, h_v, 6)

            def own_back(dq_ref, dk_ref, dv_ref, wq_ref, wk_ref, wv_ref):
                acc[halo * r :, :] += (
                    dot_nt(dq_ref[...], wq_ref[...]) + dot_nt(dk_ref[...], wk_ref[...]) + dot_nt(dv_ref[...], wv_ref[...])
                )

            own_rows = pl.BlockSpec((r, cols), lambda u: (halo, u))
            lx2 = local(x, c_v, 3)
            piped(
                own_back,
                nz,
                [col(r), own_rows, own_rows] + [wcol] * 3,
                (),
                [(POLL["own_up"], every(of(1), "start_z"))],
            )(dq, dk, dv, wq, wk, wv)
            for u in of(0):
                u.relay_z()
            for u in of(2):
                u.finish()

            lx2.wait()
            vx = c_v[...].astype(F32)
            gp[0:1, :] = jnp.sum(acc[halo * r :, :] * vx * inv_rms(vx), axis=0, keepdims=True)
            for j in range(halo):

                @pl.when(t >= j + 1)
                def _():
                    cx = local(xh.at[j], n2_v, 4)
                    cx.wait()
                    vh = n2_v[...].astype(F32)
                    lo = (halo - 1 - j) * r
                    gp[0:1, :] = gp[0:1, :] + jnp.sum(acc[lo : lo + r, :] * vh * inv_rms(vh), axis=0, keepdims=True)

            zg = []
            for i in range(1, nz):
                m = send(gp, gz.at[i - 1], ass.at[i - 1], ars.at[i - 1], me, (t + i) % nz)
                m.start()
                zg.append(m)
            for u in of(3):
                u.start_z()

            for j, m in enumerate(hd):

                @pl.when(t + j + 1 < nz)
                def _():
                    m.wait_recv()
                    acc[halo * r :, :] = acc[halo * r :, :] + more[j].astype(F32)

                @pl.when(t >= j + 1)
                def _():
                    m.wait_send()

            ld2.wait()
            vx = c_v[...].astype(F32)
            iv = inv_rms(vx)
            gdx = acc[halo * r :, :] * gain_row(gn_v, 0)
            acc[halo * r :, :] = h_v[...] + iv * gdx - vx * (iv * iv * iv * jnp.mean(vx * gdx, axis=1, keepdims=True))
            lg = local(acc.at[pl.ds(halo * r, r)], grad_in, 7)
            for u in of(4, 5):
                u.start_second()
            for u in of(1):
                u.relay_z()
            for m in zg:
                m.wait()
            tot = gp[...]
            for i in range(nz - 1):
                tot = tot + gz[i]
            for e in range(dp):
                gs[e] = tot[:, e * 128 : (e + 1) * 128]
            ds_ = []
            for i in range(1, dp):
                to = (me + i) % dp
                m = send(gs.at[to], gd.at[me], dss.at[i], drs.at[i], to, t)
                m.start()
                ds_.append(m)
            og = pltpu.make_async_copy(gs.at[me], gd.at[me], dss.at[0])
            og.start()
            for u in of(6):
                u.start_second()
            for u in of(3):
                u.relay_z()
            for u in of(0):
                u.finish()
            for u in of(4, 5):
                u.start_z()
            for u in of(1):
                u.finish()
            for u in of(6):
                u.start_z()
            for u in of(4, 5):
                u.relay_z()
            for u in of(3):
                u.finish()
            for u in of(6):
                u.relay_z()
            og.wait()
            for m in ds_:
                m.wait()
            tot = gd[0]
            for e in range(1, dp):
                tot = tot + gd[e]
            gout[...] = tot
            for u in of(4, 5, 6):
                u.finish()
            lg.wait()

        pl.run_scoped(
            attention_back,
            pltpu.VMEM((r, d), BF16),
            pltpu.VMEM((r, half), BF16),
            pltpu.VMEM((rt, half), BF16),
            pltpu.VMEM((rt, HD), F32),
            pltpu.VMEM((rt, HD), F32),
            pltpu.VMEM((halo * r, d), BF16),
            *[pltpu.VMEM((nb, nz) + tuple(o_.shape), BF16) for o_ in outs[3:]],
        )

    pl.run_scoped(
        rest,
        pltpu.VMEM((r, d), F32),
        pltpu.VMEM((r, d), BF16),
        pltpu.VMEM((r, d), BF16),
        pltpu.VMEM((r, half), BF16),
        pltpu.VMEM((r, half), BF16),
        pltpu.VMEM((rt, d), F32),
        *[pltpu.VMEM((nb, nz) + tuple(o_.shape), BF16) for o_ in outs[:3]],
    )


def run_layer(g, cap, halo, window, requests, sel, segs, x, gains, mem_k, mem_v, cot, shards, nq, ksel):
    blk, cols = mem_k.shape[1:]
    r, d = x.shape
    rt = (halo + 1) * r
    nz, dp = g.nz, g.dp
    half = d // 2
    kd, ff = shards[0].shape[0], shards[4].shape[0]
    heads = d // HD
    tab1, tab2 = (jnp.asarray(v) for v in rope_tables(halo, nz, r))
    gunits = []
    for w, s in enumerate(shards):
        n, lanes_ = s.shape[0], w >= 3
        if w in (0, 4):
            gunits.append((w, (0, n), True, lanes_))
        elif w in (1, 5):
            gunits.append((w, (0, n), False, lanes_))
        else:
            gunits.append((w, (0, n // 2), True, lanes_))
            gunits.append((w, (n // 2, n - n // 2), False, lanes_))
    pieces = [(ff, 128)] * 3 + [(cols, 128)] + [(kd, cols)] * 3
    sunits = []
    for w in (2, 0, 1, 3):
        n = pieces[w][0]
        sunits += [(w, (0, n // 2), True), (w, (n // 2, n - n // 2), False)]
    sunits += [(4, (0, kd), True), (5, (0, kd), False), (6, (0, kd // 2), True), (6, (kd // 2, kd - kd // 2), False)]
    any_ = pl.BlockSpec(memory_space=pl.ANY)
    vm = pl.BlockSpec(memory_space=pltpu.VMEM)
    dma = lambda *n: pltpu.SemaphoreType.DMA(n)
    st = lambda s, dt=BF16: jax.ShapeDtypeStruct(s, dt)
    nsem = len(gunits) * gather_sems(g)
    hbm = (
        [st((d, d))] * 3 + [st((nz, cols, d))] + [st((nz, ff, d))] * 3
        + [st((halo, r, d))] + [st((nz, ksel, blk, cols))] * 2 + [st((dp * cap, blk, cols))] * 2
        + [st((rt, d)), st((r, d)), st((rt, d)), st((rt, d)), st((r, d)), st((heads, r, 1), F32)]
        + [st((nz, ff, r))] * 4 + [st((r, d)), st((r, d)), st((rt, d)), st((rt, d))]
        + [st((r, d)), st((rt, d)), st((rt, d)), st((r, d)), st((r, d), F32)]
    )
    out_shape = [st((2, 128), F32)] + [st(p, F32) for p in pieces] + [st((r, d), F32)] * 2 + hbm
    scratch = [pltpu.VMEM((dp, 8, 128), jnp.int32), pltpu.SMEM((dp, 8, 128), jnp.int32), pltpu.VMEM((dp, 2, 128), F32)]
    scratch += [pltpu.VMEM((rt, HD), F32)] * 2
    for w, (lo, n), bf in sunits:
        cc = pieces[w][1]
        n1_, n2_ = (g.nb, g.na) if bf else (g.na, g.nb)
        scratch += [
            pltpu.VMEM((n1_ - 1, n2_, nz, n, cc), BF16),
            pltpu.VMEM((n2_ - 1, nz, n, cc), BF16),
            pltpu.VMEM((nz - 1, n, cc), BF16),
        ]
    scratch += [dma(scatter_sems(g))] * (2 * len(sunits))
    scratch += [pltpu.VMEM((r, half), BF16)] * 2 + [pltpu.VMEM((rt, half), BF16), pltpu.VMEM((r, half), BF16)]
    scratch += [pltpu.VMEM((halo, r, d), BF16)]
    scratch += [pltpu.VMEM((nz - 1, 2, d), F32), pltpu.VMEM((dp, 2, 128), F32), pltpu.VMEM((dp, 2, 128), F32), pltpu.VMEM((2, d), F32)]
    ncore = 4 + 4 * (dp // 2)
    parts = cols // 128
    scratch += [dma(nsem), dma(nsem), dma(8 + dp // 2), dma(dp), dma(dp), dma(dp), dma(dp), dma(2, parts, dp), dma(2, parts, dp)]
    scratch += [dma(2, parts, nz), dma(2, parts, nz), dma(halo), dma(halo)]
    scratch += [dma(ncore), dma(ncore), dma(halo), dma(halo), dma(nz), dma(nz), dma(dp), dma(dp)]
    scratch += [dma(3, nz), dma(3, nz), dma(nz)]
    scratch += [pltpu.VMEM((r, 128), jnp.int32), pltpu.VMEM((1, rt), jnp.int32)]
    cfg = (cap, nq, ksel, halo, window, gunits, sunits)
    return pl.pallas_call(
        functools.partial(layer_kernel, g, cfg),
        out_shape=out_shape,
        in_specs=[vm, pl.BlockSpec(memory_space=pltpu.SMEM), vm, vm, vm] + [any_] * (5 + len(shards)),
        out_specs=[vm] * 8 + [any_] * (2 + len(hbm)),
        scratch_shapes=scratch,
        compiler_params=pltpu.CompilerParams(collective_id=0, has_side_effects=True, vmem_limit_bytes=67043328),
        name="layer",
    )(requests, sel, segs, tab1, tab2, x, gains, mem_k, mem_v, cot, *shards)


def hand_out(gout, arrays):
    n = len(arrays)

    def kern(*refs):
        ins, outs, bufs, (ls, ss) = refs[: n + 1], refs[n + 1 : 2 * n + 3], refs[2 * n + 3 : 3 * n + 3], refs[3 * n + 3 :]
        loads = [pltpu.make_async_copy(ins[i + 1], bufs[i], ls.at[i]) for i in range(n)]
        stores = [pltpu.make_async_copy(bufs[i], outs[i + 2], ss.at[i]) for i in range(n)]
        for m in loads:
            m.start()
        outs[0][...] = ins[0][0:1, :]
        outs[1][...] = ins[0][1:2, :]
        for a, b in zip(loads, stores):
            a.wait()
            b.start()
        for m in stores:
            m.wait()

    any_ = pl.BlockSpec(memory_space=pl.ANY)
    vm = pl.BlockSpec(memory_space=pltpu.VMEM)
    gain = jax.ShapeDtypeStruct((1, 128), F32)
    return pl.pallas_call(
        kern,
        in_specs=[vm] + [any_] * n,
        out_specs=[vm] * 2 + [any_] * n,
        out_shape=[gain, gain] + [jax.ShapeDtypeStruct(a.shape, a.dtype) for a in arrays],
        scratch_shapes=[pltpu.VMEM(a.shape, a.dtype) for a in arrays] + [pltpu.SemaphoreType.DMA((n,))] * 2,
        compiler_params=pltpu.CompilerParams(vmem_limit_bytes=67043328),
        name="hand_out",
    )(gout, *arrays)


HEADS = 8
QB = 512


def normalize(field, gain_vec):
    return field * lax.rsqrt(jnp.mean(field * field, axis=-1, keepdims=True) + EPSILON) * gain_vec


def rotate(field, heads_here):
    row_total = field.shape[0]
    head_size = field.shape[1] // heads_here
    half_width = head_size // 2
    frequencies = 10000.0 ** (-jnp.arange(half_width, dtype=jnp.float32) * 2.0 / head_size)
    angles = jnp.arange(row_total, dtype=jnp.float32)[:, None] * frequencies[None, :]
    cosine = jnp.cos(angles)[:, None, :]
    sine_table = jnp.sin(angles)[:, None, :]
    split_heads = field.reshape(row_total, heads_here, head_size)
    first_half = split_heads[..., :half_width]
    second_half = split_heads[..., half_width:]
    turned = jnp.concatenate(
        [
            first_half * cosine - second_half * sine_table,
            second_half * cosine + first_half * sine_table,
        ],
        axis=-1,
    )
    return turned.reshape(row_total, heads_here * head_size)


def contract_rows(left, right):
    return lax.dot_general(
        left, right, (((0,), (0,)), ((), ())), preferred_element_type=jnp.float32
    )


def against(left, right):
    return lax.dot_general(
        left, right, (((1,), (1,)), ((), ())), preferred_element_type=jnp.float32
    )


def spread_rows(local_rows, matrices):
    piece_rows = lax.all_gather(local_rows, "tensor", axis=0, tiled=True)
    return jnp.concatenate(
        [jnp.dot(piece_rows, matrix, preferred_element_type=jnp.float32) for matrix in matrices],
        axis=1,
    )


def reduce_rows(left, right):
    return lax.psum_scatter(
        jnp.dot(left, right, preferred_element_type=jnp.float32).astype(jnp.bfloat16),
        "tensor",
        scatter_dimension=0,
        tiled=True,
    ).astype(jnp.float32)


def return_rows(pairs):
    summed = against(pairs[0][0], pairs[0][1])
    for grad_block, matrix in pairs[1:]:
        summed = summed + against(grad_block, matrix)
    return lax.psum_scatter(
        summed.astype(jnp.bfloat16), "tensor", scatter_dimension=0, tiled=True
    ).astype(jnp.float32)


def weight_grads(local_rows, grads_list):
    piece_rows = lax.all_gather(local_rows, "tensor", axis=0, tiled=True)
    return tuple((contract_rows(piece_rows, grad_one) for grad_one in grads_list))


def all_rows(local_grad):
    return lax.all_gather(local_grad, "tensor", axis=0, tiled=True)


def on_device_any(
    block_in,
    segments,
    retrieved,
    partner,
    memory_keys,
    memory_values,
    gain_attn,
    w_query,
    w_key,
    w_value,
    w_out,
    gain_ffn,
    w_gate,
    w_up,
    w_down,
    cotangent,
):
    tensor_size = lax.axis_size("tensor")
    dp_size = lax.axis_size("dp")
    heads_here = HEADS // tensor_size
    head_width = heads_here * HD
    score_scale = HD ** (-0.5)
    seq_len = segments.shape[1]
    query_blocks = seq_len // QB
    stream_in = block_in[0].astype(jnp.float32)
    seg_row = segments[0]
    positions = jnp.arange(seq_len)
    gathered = (
        lax.all_gather(gain_attn, "dp", axis=0, tiled=True),
        lax.all_gather(w_query, "dp", axis=0, tiled=True),
        lax.all_gather(w_key, "dp", axis=0, tiled=True),
        lax.all_gather(w_value, "dp", axis=0, tiled=True),
        lax.all_gather(w_out, "dp", axis=1, tiled=True),
        lax.all_gather(gain_ffn, "dp", axis=0, tiled=True),
        lax.all_gather(w_gate, "dp", axis=0, tiled=True),
        lax.all_gather(w_up, "dp", axis=0, tiled=True),
        lax.all_gather(w_down, "dp", axis=1, tiled=True),
    )
    gain_one, query_w, key_w, value_w, out_w, gain_two, gate_w, up_w, down_w = gathered
    wanted = retrieved[0].reshape(-1)
    request_total = wanted.shape[0]
    capacity = max(2, (2 * request_total + dp_size - 1) // dp_size)
    blocks_dev = memory_keys.shape[1]
    from_partner = wanted // MEMB
    block_index = wanted % MEMB
    owner_dev = block_index // blocks_dev
    local_block = block_index % blocks_dev
    seq_id = jnp.where(from_partner == 0, lax.axis_index("dp"), partner[0])
    owner_hits = (owner_dev[:, None] == jnp.arange(dp_size)[None, :]).astype(jnp.int32)
    slot_index = jnp.sum((jnp.cumsum(owner_hits, axis=0) - 1) * owner_hits, axis=1)
    requests = (
        jnp.zeros((dp_size, capacity, 2), jnp.int32)
        .at[owner_dev, slot_index]
        .set(jnp.stack([seq_id, local_block], axis=-1))
    )
    received = lax.all_to_all(requests, "dp", split_axis=0, concat_axis=0, tiled=True)
    picked_keys = memory_keys[received[..., 0], received[..., 1]]
    picked_values = memory_values[received[..., 0], received[..., 1]]
    fetched_keys = lax.all_to_all(picked_keys, "dp", split_axis=0, concat_axis=0, tiled=True)
    fetched_values = lax.all_to_all(picked_values, "dp", split_axis=0, concat_axis=0, tiled=True)
    memory_k = fetched_keys[owner_dev, slot_index].reshape(query_blocks, -1, heads_here, HD)
    memory_v = fetched_values[owner_dev, slot_index].reshape(query_blocks, -1, heads_here, HD)
    normed = normalize(stream_in, gain_one.astype(jnp.float32)).astype(jnp.bfloat16)
    qkv_rows = spread_rows(normed, [query_w, key_w, value_w])
    query_raw = qkv_rows[:, :head_width]
    key_raw = qkv_rows[:, head_width : 2 * head_width]
    queries = rotate(query_raw, heads_here).astype(jnp.bfloat16)
    keys_all = rotate(key_raw, heads_here).astype(jnp.bfloat16).reshape(seq_len, heads_here, HD)
    values_all = qkv_rows[:, 2 * head_width :].astype(jnp.bfloat16).reshape(seq_len, heads_here, HD)
    query_tiles = queries.reshape(query_blocks, QB, heads_here, HD)
    seg_tiles = seg_row.reshape(query_blocks, QB)
    pos_tiles = positions.reshape(query_blocks, QB)

    def scores_of(query_blk, seg_blk, pos_blk, key_mem):
        local_scores = jnp.einsum(
            "qhd,khd->hqk", query_blk, keys_all, preferred_element_type=jnp.float32
        )
        memory_scores = jnp.einsum(
            "qhd,khd->hqk", query_blk, key_mem, preferred_element_type=jnp.float32
        )
        raw_scores = jnp.concatenate([local_scores, memory_scores], axis=-1) * score_scale
        allowed = (seg_blk[:, None] == seg_row[None, :]) & (positions[None, :] <= pos_blk[:, None])
        allowed = jnp.concatenate(
            [allowed, jnp.ones((query_blk.shape[0], key_mem.shape[0]), dtype=jnp.bool_)], axis=1
        )
        return (raw_scores, allowed)

    def forward_block(pieces):
        query_blk, seg_blk, pos_blk, key_mem, value_mem = pieces
        raw_scores, allowed = scores_of(query_blk, seg_blk, pos_blk, key_mem)
        masked = jnp.where(allowed[None], raw_scores, MASKED)
        row_max = jnp.max(masked, axis=-1, keepdims=True)
        expo = jnp.exp(masked - row_max)
        row_total = jnp.sum(expo, axis=-1, keepdims=True)
        weights_soft = (expo / row_total).astype(jnp.bfloat16)
        values_both = jnp.concatenate([values_all, value_mem], axis=0)
        result = jnp.einsum(
            "hqk,khd->qhd", weights_soft, values_both, preferred_element_type=jnp.float32
        )
        return (result, (row_max + jnp.log(row_total))[..., 0])

    attended, log_totals = lax.map(
        forward_block, (query_tiles, seg_tiles, pos_tiles, memory_k, memory_v)
    )
    mixed = attended.reshape(seq_len, head_width).astype(jnp.bfloat16)
    stream = stream_in + reduce_rows(mixed, out_w)
    normed_ffn = normalize(stream, gain_two.astype(jnp.float32)).astype(jnp.bfloat16)
    gate_up = spread_rows(normed_ffn, [gate_w, up_w])
    hidden_width = gate_w.shape[1]
    gate_pre = gate_up[:, :hidden_width]
    up_pre = gate_up[:, hidden_width:]
    hidden = (jax.nn.silu(gate_pre) * up_pre).astype(jnp.bfloat16)
    block_out = stream + reduce_rows(hidden, down_w)
    gathered_back = (
        lax.all_gather(gain_attn, "dp", axis=0, tiled=True),
        lax.all_gather(w_query, "dp", axis=0, tiled=True),
        lax.all_gather(w_key, "dp", axis=0, tiled=True),
        lax.all_gather(w_value, "dp", axis=0, tiled=True),
        lax.all_gather(w_out, "dp", axis=1, tiled=True),
        lax.all_gather(gain_ffn, "dp", axis=0, tiled=True),
        lax.all_gather(w_gate, "dp", axis=0, tiled=True),
        lax.all_gather(w_up, "dp", axis=0, tiled=True),
        lax.all_gather(w_down, "dp", axis=1, tiled=True),
    )
    gain_one, query_w, key_w, value_w, out_w, gain_two, gate_w, up_w, down_w = gathered_back
    dout_rows = cotangent[0]

    def gated(gate_in, up_in):
        return jax.nn.silu(gate_in) * up_in

    dout_full = all_rows(dout_rows)
    grad_down = contract_rows(hidden, dout_full)
    d_hidden = against(dout_full, down_w)
    gated_value, pull_gated = jax.vjp(gated, gate_pre, up_pre)
    d_gate, d_up = pull_gated(d_hidden)
    d_gate = d_gate.astype(jnp.bfloat16)
    d_up = d_up.astype(jnp.bfloat16)
    d_norm_ffn = return_rows([(d_gate, gate_w), (d_up, up_w)])
    grad_gate, grad_up = weight_grads(normed_ffn, [d_gate, d_up])
    norm_value, pull_norm_ffn = jax.vjp(normalize, stream, gain_two.astype(jnp.float32))
    d_stream_norm, grad_gain_ffn = pull_norm_ffn(d_norm_ffn)
    d_stream = dout_rows.astype(jnp.float32) + d_stream_norm
    d_stream_full = all_rows(d_stream.astype(jnp.bfloat16))
    grad_out = contract_rows(mixed, d_stream_full)
    d_mixed = against(d_stream_full, out_w).astype(jnp.bfloat16)
    d_mixed_tiles = d_mixed.reshape(query_blocks, QB, heads_here, HD)

    def backward_block(carry_sums, pieces):
        key_sum, value_sum = carry_sums
        query_blk, seg_blk, pos_blk, key_mem, value_mem, log_blk, grad_blk = pieces
        raw_scores, allowed = scores_of(query_blk, seg_blk, pos_blk, key_mem)
        probs = jnp.where(allowed[None], jnp.exp(raw_scores - log_blk[..., None]), 0.0)
        values_both = jnp.concatenate([values_all, value_mem], axis=0)
        d_probs = jnp.einsum(
            "qhd,khd->hqk", grad_blk, values_both, preferred_element_type=jnp.float32
        )
        shared = jnp.sum(probs * d_probs, axis=-1, keepdims=True)
        d_scores = (probs * (d_probs - shared)).astype(jnp.bfloat16)
        probs_low = probs.astype(jnp.bfloat16)
        keys_both = jnp.concatenate([keys_all, key_mem], axis=0)
        d_query = (
            jnp.einsum("hqk,khd->qhd", d_scores, keys_both, preferred_element_type=jnp.float32)
            * score_scale
        )
        key_sum = (
            key_sum
            + jnp.einsum(
                "hqk,qhd->khd",
                d_scores[..., :seq_len],
                query_blk,
                preferred_element_type=jnp.float32,
            )
            * score_scale
        )
        value_sum = value_sum + jnp.einsum(
            "hqk,qhd->khd", probs_low[..., :seq_len], grad_blk, preferred_element_type=jnp.float32
        )
        return ((key_sum, value_sum), d_query)

    zero_grads = jnp.zeros((seq_len, heads_here, HD), jnp.float32)
    (d_keys, d_values), d_queries = lax.scan(
        backward_block,
        (zero_grads, zero_grads),
        (query_tiles, seg_tiles, pos_tiles, memory_k, memory_v, log_totals, d_mixed_tiles),
    )

    def turn(field):
        return rotate(field, heads_here)

    turned_value, pull_turn = jax.vjp(turn, query_raw)
    d_query_raw = pull_turn(d_queries.reshape(seq_len, head_width))[0].astype(jnp.bfloat16)
    d_key_raw = pull_turn(d_keys.reshape(seq_len, head_width))[0].astype(jnp.bfloat16)
    d_value_raw = d_values.reshape(seq_len, head_width).astype(jnp.bfloat16)
    d_norm_attn = return_rows([(d_query_raw, query_w), (d_key_raw, key_w), (d_value_raw, value_w)])
    grad_query, grad_key, grad_value = weight_grads(normed, [d_query_raw, d_key_raw, d_value_raw])
    norm_first, pull_norm_attn = jax.vjp(normalize, stream_in, gain_one.astype(jnp.float32))
    d_input_norm, grad_gain_attn = pull_norm_attn(d_norm_attn)
    grad_in = d_stream + d_input_norm
    grad_gain_attn, grad_gain_ffn = lax.psum((grad_gain_attn, grad_gain_ffn), "tensor")
    results = (
        lax.psum_scatter(
            grad_gain_attn.astype(jnp.bfloat16), "dp", scatter_dimension=0, tiled=True
        ).astype(jnp.float32),
        lax.psum_scatter(
            grad_query.astype(jnp.bfloat16), "dp", scatter_dimension=0, tiled=True
        ).astype(jnp.float32),
        lax.psum_scatter(
            grad_key.astype(jnp.bfloat16), "dp", scatter_dimension=0, tiled=True
        ).astype(jnp.float32),
        lax.psum_scatter(
            grad_value.astype(jnp.bfloat16), "dp", scatter_dimension=0, tiled=True
        ).astype(jnp.float32),
        lax.psum_scatter(
            grad_out.astype(jnp.bfloat16), "dp", scatter_dimension=1, tiled=True
        ).astype(jnp.float32),
        lax.psum_scatter(
            grad_gain_ffn.astype(jnp.bfloat16), "dp", scatter_dimension=0, tiled=True
        ).astype(jnp.float32),
        lax.psum_scatter(
            grad_gate.astype(jnp.bfloat16), "dp", scatter_dimension=0, tiled=True
        ).astype(jnp.float32),
        lax.psum_scatter(
            grad_up.astype(jnp.bfloat16), "dp", scatter_dimension=0, tiled=True
        ).astype(jnp.float32),
        lax.psum_scatter(
            grad_down.astype(jnp.bfloat16), "dp", scatter_dimension=1, tiled=True
        ).astype(jnp.float32),
    )
    return (block_out[None], grad_in[None]) + results


def on_device(*args):
    x, dp = args[0], lax.axis_size("dp")
    side = math.isqrt(dp // 2)
    if 2 * side * side == dp and x.shape[2] % (128 * dp) == 0:
        return on_device_rows(*args)
    return on_device_any(*args)


def on_device_rows(
    block_in, segments, retrieved, partner, memory_keys, memory_values,
    gain_attn, w_query, w_key, w_value, w_out, gain_ffn, w_gate, w_up, w_down, cotangent,
):
    g = Grid(lax.axis_size("dp"), lax.axis_size("tensor"))
    t, me = lax.axis_index("tensor"), lax.axis_index("dp")
    x, c = block_in[0], cotangent[0]
    r, d = x.shape
    seq_len = segments.shape[1]
    window = seq_len // 4
    halo = -(-window // r)
    nq, ksel = retrieved.shape[1:]
    cap = max(2, -(-2 * nq * ksel // g.dp))
    req, sel = plan_requests(retrieved[0], partner[0], g.dp, memory_keys.shape[1], cap)
    gains = jnp.stack([gain_attn, gain_ffn]).astype(F32)
    flat = lambda m: m.reshape((-1,) + m.shape[2:])
    shards = [w_query, w_key, w_value, w_out, w_gate.T, w_up.T, w_down]
    gout, o_gate, o_up, o_down, o_out, o_q, o_k, o_v, block_out, grad_in = run_layer(
        g, cap, halo, window, req, sel, segments, x, gains, flat(memory_keys), flat(memory_values), c, shards, nq, ksel
    )[:10]
    g_attn, g_ffn, block_out, grad_in, o_q, o_k, o_v, o_out, o_gate, o_up, o_down = hand_out(
        gout, (block_out, grad_in, o_q, o_k, o_v, o_out, o_gate, o_up, o_down)
    )
    return (
        block_out[None], grad_in[None], g_attn.reshape(-1), o_q, o_k, o_v, o_out, g_ffn.reshape(-1), o_gate.T, o_up.T, o_down,
    )


def solution(mesh):
    return jax.shard_map(
        on_device,
        mesh=mesh,
        in_specs=(
            P("dp", "tensor", None), P("dp", None), P("dp", None, None), P("dp"),
            P(None, "dp", None, "tensor"), P(None, "dp", None, "tensor"),
            P("dp"), P("dp", "tensor"), P("dp", "tensor"), P("dp", "tensor"), P("tensor", "dp"),
            P("dp"), P("dp", "tensor"), P("dp", "tensor"), P("tensor", "dp"), P("dp", "tensor", None),
        ),
        out_specs=(
            P("dp", "tensor", None), P("dp", "tensor", None),
            P("dp"), P("dp", "tensor"), P("dp", "tensor"), P("dp", "tensor"), P("tensor", "dp"),
            P("dp"), P("dp", "tensor"), P("dp", "tensor"), P("tensor", "dp"),
        ),
        check_vma=False,
    )
```
